32 devices in a mesh: dp: 4 (over x, core), context: 4 (over z), tensor: 2 (over y).
Axes of the slice: x: 2, y: 2, z: 4, core: 2. Of those that a mesh axis runs over, the one named last changes fastest.
Arguments:
- tokens: bfloat16 [4, 1024, 1536], P('dp', 'context'), may hold values from -6 to 6
- lengths: int32 [4], P('dp'), may hold values from 256 to 1024, as said below
- gain_one: bfloat16 [1536], replicated, may hold values from 0.5 to 1.5
- w_query: bfloat16 [1536, 1536], P('dp', 'tensor'), may hold values from -0.15625 to 0.15625
- b_query: bfloat16 [1536], P('tensor'), may hold values from -3 to 3
- key_weight: bfloat16 [1536, 256], P('dp', 'tensor'), may hold values from -0.15625 to 0.15625
- key_bias: bfloat16 [256], P('tensor'), may hold values from -3 to 3
- value_weight: bfloat16 [1536, 256], P('dp', 'tensor'), may hold values from -0.15625 to 0.15625
- value_bias: bfloat16 [256], P('tensor'), may hold values from -3 to 3
- w_out: bfloat16 [1536, 1536], P('dp', 'tensor'), may hold values from -1.25 to 1.25
- gain_two: bfloat16 [1536], replicated, may hold values from 0.5 to 1.5
- w_gate: bfloat16 [1536, 8960], P('dp', 'tensor'), may hold values from -0.15625 to 0.15625
- w_up: bfloat16 [1536, 8960], P('dp', 'tensor'), may hold values from -0.15625 to 0.15625
- w_down: bfloat16 [1536, 8960], P('dp', 'tensor'), may hold values from -0.0625 to 0.0625
- grad_out: bfloat16 [4, 1024, 1536], P('dp', 'context'), may hold values from -6 to 6
Outputs:
- output: bfloat16 [4, 1024, 1536], P('dp', 'context')
- grad_tokens: bfloat16 [4, 1024, 1536], P('dp', 'context')
- grad_gain_one: float32 [1536], replicated
- grad_w_query: float32 [1536, 1536], P('dp', 'tensor')
- grad_b_query: float32 [1536], P('tensor')
- grad_w_key: float32 [1536, 256], P('dp', 'tensor')
- grad_b_key: float32 [256], P('tensor')
- grad_w_value: float32 [1536, 256], P('dp', 'tensor')
- grad_b_value: float32 [256], P('tensor')
- grad_w_out: float32 [1536, 1536], P('dp', 'tensor')
- grad_gain_two: float32 [1536], replicated
- grad_w_gate: float32 [1536, 8960], P('dp', 'tensor')
- grad_w_up: float32 [1536, 8960], P('dp', 'tensor')
- grad_w_down: float32 [1536, 8960], P('dp', 'tensor')
The draws below stay inside these ranges and needn't reach their ends.
Inputs may be any that keep to these rules, and one draw needn't show every extreme that they name: `lengths`: each sequence's valid tokens fill its first slots; one sequence fills all 1024 slots and one holds exactly 256.
All inputs are finite; a program needn't handle non-finite values.
Results may differ from the reference program's by a relative error of at most 0.022.
Values may be sent and summed in bfloat16 or wider, within the bound.
A program may use at most 448 MiB of HBM per device.

```python
import math
import jax
import jax.numpy as jnp
from jax import lax

MODEL_DIM = 1536
QUERY_HEADS = 12
KEY_VALUE_HEADS = 2
HEAD_DIM = 128
FF = 8960
SLOTS = 1024
SEQS = 4


def draw_lengths(key, part):
    first, second = jax.random.split(key)
    spread = jax.random.randint(first, (SEQS,), SLOTS // 4, SLOTS + 1)
    order = jax.random.permutation(second, SEQS)
    spread = jnp.where(order == 0, SLOTS, spread)
    spread = jnp.where(order == 1, SLOTS // 4, spread)
    return spread.astype(jnp.int32)


def levels(rng, extent, pieces, smallest, top_value):
    factor_of, own = 1.0, jax.random.fold_in(rng, 6)
    for axis_at, blocks in pieces:
        steps = jnp.exp(jax.random.uniform(jax.random.fold_in(own, axis_at), (blocks,), jnp.float32, smallest / len(pieces), top_value / len(pieces)))
        factor_of = factor_of * jnp.repeat(steps, extent[axis_at] // blocks).reshape([-1 if axis == axis_at else 1 for axis in range(len(extent))])
    return factor_of


def normal_values(own_key, shape, scale, limit, pieces=(), kind=jnp.bfloat16):
    result = jax.random.normal(own_key, shape, jnp.float32) * scale
    if len(pieces) > 0:
        result = levels(own_key, shape, pieces, -0.22, 0.18) * result
    return jnp.clip(result, min=-limit, max=limit).astype(kind)


def setup_inputs(seed: int = 0) -> dict:
    streams_of = jax.random.split(jax.random.key(seed), 16)
    tokens = normal_values(streams_of[0], (SEQS, SLOTS, MODEL_DIM), 1.0, 6.0, ((0, 4), (1, 4)))
    lengths = draw_lengths(jax.random.fold_in(streams_of[15], 71), 0)
    gain_one = jnp.clip(1.0 + 0.1 * jax.random.normal(streams_of[2], (MODEL_DIM,), jnp.float32), 0.5, 1.5).astype(jnp.bfloat16)
    w_query = normal_values(streams_of[3], (MODEL_DIM, QUERY_HEADS * HEAD_DIM), MODEL_DIM ** -0.5, 0.15625, ((0, 4), (1, 2)))
    b_query = normal_values(streams_of[4], (QUERY_HEADS * HEAD_DIM,), 0.5, 3.0, ((0, 2),))
    key_weight = normal_values(streams_of[5], (MODEL_DIM, KEY_VALUE_HEADS * HEAD_DIM), MODEL_DIM ** -0.5, 0.15625, ((0, 4), (1, 2)))
    key_bias = normal_values(streams_of[6], (KEY_VALUE_HEADS * HEAD_DIM,), 0.5, 3.0, ((0, 2),))
    value_weight = normal_values(streams_of[7], (MODEL_DIM, KEY_VALUE_HEADS * HEAD_DIM), MODEL_DIM ** -0.5, 0.15625, ((0, 4), (1, 2)))
    value_bias = normal_values(streams_of[8], (KEY_VALUE_HEADS * HEAD_DIM,), 0.5, 3.0, ((0, 2),))
    w_out = normal_values(streams_of[9], (MODEL_DIM, QUERY_HEADS * HEAD_DIM), (QUERY_HEADS * HEAD_DIM // 64) ** -0.5, 1.25, ((0, 4), (1, 2)))
    gain_two = jnp.clip(1.0 + 0.1 * jax.random.normal(streams_of[10], (MODEL_DIM,), jnp.float32), 0.5, 1.5).astype(jnp.bfloat16)
    w_gate = normal_values(streams_of[11], (MODEL_DIM, FF), MODEL_DIM ** -0.5, 0.15625, ((0, 4), (1, 2)))
    w_up = normal_values(streams_of[12], (MODEL_DIM, FF), MODEL_DIM ** -0.5, 0.15625, ((0, 4), (1, 2)))
    w_down = normal_values(streams_of[13], (MODEL_DIM, FF), FF ** -0.5, 0.0625, ((0, 4), (1, 2)))
    grad_out = normal_values(streams_of[14], (SEQS, SLOTS, MODEL_DIM), 1.0, 6.0, ((0, 4), (1, 4)))
    return dict(tokens=tokens, lengths=lengths, gain_one=gain_one, w_query=w_query, b_query=b_query, key_weight=key_weight, key_bias=key_bias, value_weight=value_weight, value_bias=value_bias, w_out=w_out, gain_two=gain_two, w_gate=w_gate, w_up=w_up, w_down=w_down, grad_out=grad_out)


EPSILON = 1e-06
ROPE_BASE = 1000000.0

@jax.custom_vjp
def low(v):
    return lax.optimization_barrier(v.astype(jnp.bfloat16)).astype(jnp.float32)

@jax.custom_vjp
def low_back(v):
    return v

def low_keep(v):
    return (low(v), None)

def low_pass(kept, grad):
    return (grad,)

def back_keep(v):
    return (v, None)

def back_low(kept, grad):
    return (low(grad),)
low.defvjp(low_keep, low_pass)
low_back.defvjp(back_keep, back_low)

def product_exact(left, right):
    return jnp.dot(left, right, precision=lax.Precision.HIGHEST, preferred_element_type=jnp.float32)

def rms_norm(field, gain):
    return field * lax.rsqrt(lax.optimization_barrier(jnp.mean(field * field, -1, keepdims=True)) + EPSILON) * gain

def apply_rotation(field, cosine_rows, sine_table):
    half = field.shape[-1] // 2
    first = field[..., :half]
    second = field[..., half:]
    return jnp.concatenate([first * cosine_rows - second * sine_table, second * cosine_rows + first * sine_table], -1)

def sequence_layer(tokens, length, gain_one, w_query, b_query, key_weight, key_bias, value_weight, value_bias, w_out, gain_two, w_gate, w_up, w_down):
    position_count = tokens.shape[0]
    positions = jnp.arange(position_count, dtype=jnp.int32)
    valid_rows = (positions < length).astype(jnp.float32)[:, None]
    allowed = (positions[None, :] <= positions[:, None]) & (positions[None, :] < length)
    half = HEAD_DIM // 2
    inverse = jnp.exp(jnp.arange(half, dtype=jnp.float32) * (-2.0 * math.log(ROPE_BASE) / HEAD_DIM))
    angles = positions.astype(jnp.float32)[:, None] * inverse[None, :]
    cosine_rows = jnp.cos(angles)[:, None, :]
    sine_table = jnp.sin(angles)[:, None, :]
    query_group_width = QUERY_HEADS // KEY_VALUE_HEADS
    score_scale = 1.0 / math.sqrt(HEAD_DIM)
    normalized_input = low(rms_norm(tokens, gain_one))
    query_rows = low_back(product_exact(normalized_input, w_query) + b_query)
    keys_before_rotation = low_back(product_exact(normalized_input, key_weight) + key_bias)
    values_reduced = low(low_back(product_exact(normalized_input, value_weight) + value_bias)).reshape(position_count, KEY_VALUE_HEADS, HEAD_DIM)
    query_rows = low(apply_rotation(query_rows.reshape(position_count, QUERY_HEADS, HEAD_DIM), cosine_rows, sine_table))
    query_rows = query_rows.reshape(position_count, KEY_VALUE_HEADS, query_group_width, HEAD_DIM)
    keys_reduced = low(apply_rotation(keys_before_rotation.reshape(position_count, KEY_VALUE_HEADS, HEAD_DIM), cosine_rows, sine_table))
    scores = jnp.einsum('qkgd,skd->kgqs', query_rows, keys_reduced, precision=lax.Precision.HIGHEST) * score_scale
    scores = jnp.where(allowed, low_back(scores), -1e+30)
    row_max = lax.optimization_barrier(jnp.max(scores, -1, keepdims=True))
    exp_scores = jnp.exp(scores - row_max)
    attention = exp_scores / lax.optimization_barrier(jnp.sum(exp_scores, -1, keepdims=True))
    mixed_heads = jnp.einsum('kgqs,skd->qkgd', low(attention), values_reduced, precision=lax.Precision.HIGHEST)
    mixed_heads = low(low_back(mixed_heads.reshape(position_count, QUERY_HEADS * HEAD_DIM)))
    hidden = tokens + low_back(product_exact(mixed_heads, w_out.T))
    normed_two = low(rms_norm(hidden, gain_two))
    gate_act = low_back(product_exact(normed_two, w_gate))
    up_act = low_back(product_exact(normed_two, w_up))
    active = low(jax.nn.silu(gate_act) * up_act)
    return valid_rows * (hidden + low_back(product_exact(active, w_down.T)))

def reference(tokens, lengths, gain_one, w_query, b_query, key_weight, key_bias, value_weight, value_bias, w_out, gain_two, w_gate, w_up, w_down, grad_out):
    params = tuple((item.astype(jnp.float32) for item in (gain_one, w_query, b_query, key_weight, key_bias, value_weight, value_bias, w_out, gain_two, w_gate, w_up, w_down)))

    def forward(inputs, *weights):

        def per_sequence(pair_in):
            return jax.checkpoint(sequence_layer)(pair_in[0], pair_in[1], *weights)
        return lax.map(per_sequence, (inputs, lengths))
    output, pull = jax.vjp(forward, tokens.astype(jnp.float32), *params)
    grads = pull(grad_out.astype(jnp.float32))
    return (output.astype(jnp.bfloat16), grads[0].astype(jnp.bfloat16), grads[1], grads[2], grads[3], grads[4], grads[5], grads[6], grads[7], grads[8], grads[9], grads[10], grads[11], grads[12])
```

```python
import math

import jax
import jax.numpy as jnp
from jax import lax
from jax.sharding import PartitionSpec as P

HEAD_DIM = 128


EPSILON = 1e-06
ROPE_BASE = 1000000.0


def xor_pairs(size, mask):
    return [(i, i ^ mask) for i in range(size)]


def far_masks(size):
    masks, mask = [], 2
    while mask < size:
        masks.append(mask)
        mask *= 2
    return masks


def swap_blocks(blocks, me):
    mask = 1
    while mask < len(blocks):
        flag = (me & mask) != 0
        blocks = [jnp.where(flag, blocks[r ^ mask], blocks[r]) for r in range(len(blocks))]
        mask *= 2
    return blocks


def far_half(piece, mask, size, parity):
    half = piece.shape[0] // 2
    sent = lax.dynamic_slice_in_dim(piece, half * parity, half, 0)
    straight = lax.ppermute(sent, "dp", xor_pairs(size, mask))
    other = lax.ppermute(straight, "context", xor_pairs(lax.axis_size("context"), 1))
    first = jnp.where(parity == 0, straight, other)
    second = jnp.where(parity == 0, other, straight)
    return jnp.concatenate([first, second], 0)


def gather_pieces(own, size, parity=None):
    pieces = {0: own}
    for mask in far_masks(size):
        for r in list(pieces):
            if parity is None:
                pieces[r ^ mask] = lax.ppermute(pieces[r], "dp", xor_pairs(size, mask))
            else:
                pieces[r ^ mask] = far_half(pieces[r], mask, size, parity)
    if size > 1:
        for r in list(pieces):
            pieces[r ^ 1] = lax.ppermute(pieces[r], "dp", xor_pairs(size, 1))
    return [pieces[r] for r in range(size)]


def trade_blocks(blocks, size):
    return [blocks[0]] + [
        lax.ppermute(blocks[r], "dp", xor_pairs(size, r)) for r in range(1, size)
    ]


def tensor_sum(part):
    sent = part.astype(jnp.bfloat16)
    size = lax.axis_size("tensor")
    if size == 2:
        other = lax.ppermute(sent, "tensor", [(0, 1), (1, 0)])
        return sent.astype(jnp.float32) + other.astype(jnp.float32)
    return lax.psum(part, "tensor")


def line_sum(part):
    place = lax.axis_index("context")
    if lax.axis_size("context") != 4:
        return lax.psum(part.astype(jnp.float32), "context")
    got = lax.ppermute(part, "context", [(0, 1), (3, 2)])
    pair = (part.astype(jnp.float32) + got.astype(jnp.float32)).astype(jnp.bfloat16)
    got = lax.ppermute(pair, "context", [(1, 2), (2, 1)])
    total = (pair.astype(jnp.float32) + got.astype(jnp.float32)).astype(jnp.bfloat16)
    got = lax.ppermute(total, "context", [(1, 0), (2, 3)])
    ends = (place == 0) | (place == 3)
    return jnp.where(ends, got, total).astype(jnp.float32)


def small_total(vector):
    for axis in ("dp", "context"):
        size, mask = lax.axis_size(axis), 1
        while mask < size:
            vector = vector + lax.ppermute(vector, axis, xor_pairs(size, mask))
            mask *= 2
    return vector


def contract_last(left, right):
    return lax.dot_general(
        left, right, (((1,), (1,)), ((), ())), preferred_element_type=jnp.float32
    )


def contract_first(left, right):
    return lax.dot_general(
        left, right, (((0,), (0,)), ((), ())), preferred_element_type=jnp.float32
    )


def apply_rotation(field, cosine_rows, sine_table):
    half = field.shape[-1] // 2
    first = field[..., :half]
    second = field[..., half:]
    return jnp.concatenate(
        [first * cosine_rows - second * sine_table, second * cosine_rows + first * sine_table], -1
    )


def rotate_back(field, cosine_rows, sine_table):
    half = field.shape[-1] // 2
    first = field[..., :half]
    second = field[..., half:]
    return jnp.concatenate(
        [first * cosine_rows + second * sine_table, second * cosine_rows - first * sine_table], -1
    )


def norm_back(field, scale_rows, gain, d_normed):
    weighted = d_normed * gain
    cubed = scale_rows * scale_rows * scale_rows
    return scale_rows * weighted - field * cubed * jnp.mean(field * weighted, -1, keepdims=True)


def chunk_edges(columns):
    tiles = columns // 128
    count = next((n for n in (5, 4, 7, 6, 3, 2) if tiles % n == 0), 1)
    width = columns // count
    return [(n * width, width) for n in range(count)]


def local(
    tokens,
    lengths,
    gain_one,
    w_query,
    b_query,
    key_weight,
    key_bias,
    value_weight,
    value_bias,
    w_out,
    gain_two,
    w_gate,
    w_up,
    w_down,
    grad_out,
):
    bf16, f32 = jnp.bfloat16, jnp.float32
    seq_count, block_len, model_width = tokens.shape
    row_count = seq_count * block_len
    query_cols = w_query.shape[1]
    key_cols = key_weight.shape[1]
    unit_cols = w_gate.shape[1]
    own_rows = w_query.shape[0]
    head_count = query_cols // HEAD_DIM
    kv_count = key_cols // HEAD_DIM
    query_group_width = head_count // kv_count
    size = lax.axis_size("dp")
    me = lax.axis_index("dp")
    blocks_along = lax.axis_size("context")
    place = lax.axis_index("context")
    parity = place % 2 if blocks_along % 2 == 0 and own_rows % 32 == 0 else None

    def relative(field):
        return swap_blocks([field[:, n * own_rows : (n + 1) * own_rows] for n in range(size)], me)

    def absolute(blocks):
        return jnp.concatenate(swap_blocks(blocks, me), 1)

    def dot_rows(blocks, weights):
        return jnp.dot(
            jnp.concatenate(blocks, 1), jnp.concatenate(weights, 0), preferred_element_type=f32
        )

    attention_weights = gather_pieces(
        jnp.concatenate([w_query, key_weight, value_weight], 1), size
    )
    out_weights = gather_pieces(w_out, size, parity)
    edges = chunk_edges(unit_cols)
    feed_weights = []
    for start, width in edges:
        own = jnp.concatenate(
            [w[:, start : start + width] for w in (w_gate, w_up, w_down)], 1
        )
        feed_weights.append(gather_pieces(own, size, parity))

    positions = place * block_len + jnp.arange(block_len, dtype=jnp.int32)
    key_places = jnp.concatenate(
        [
            (place - shift) * block_len + jnp.arange(block_len, dtype=jnp.int32)
            for shift in range(blocks_along)
        ]
    )
    position_count = block_len * blocks_along
    valid_rows = (positions[None, :] < lengths[:, None]).astype(f32).reshape(row_count, 1)
    allowed = (
        (key_places[None, None, :] <= positions[None, :, None])
        & (key_places[None, None, :] < lengths[:, None, None])
        & (key_places[None, None, :] >= 0)
    )
    allowed = allowed[:, None, None]
    half = HEAD_DIM // 2
    inverse = jnp.exp(jnp.arange(half, dtype=f32) * (-2.0 * math.log(ROPE_BASE) / HEAD_DIM))
    angles = positions.astype(f32)[:, None] * inverse[None, :]
    cosine_rows = jnp.tile(jnp.cos(angles)[:, None, :], (seq_count, 1, 1))
    sine_table = jnp.tile(jnp.sin(angles)[:, None, :], (seq_count, 1, 1))
    score_scale = 1.0 / math.sqrt(HEAD_DIM)
    gain_first = gain_one.astype(f32)
    gain_second = gain_two.astype(f32)
    inputs = tokens.reshape(row_count, model_width).astype(f32)
    scale_one = lax.rsqrt(jnp.mean(inputs * inputs, -1, keepdims=True) + EPSILON)
    normalized_input = (inputs * scale_one * gain_first).astype(bf16)
    normed_blocks = relative(normalized_input)
    projected = dot_rows(normed_blocks, attention_weights)
    query_rows = projected[:, :query_cols] + b_query.astype(f32)
    keys_before_rotation = projected[:, query_cols : query_cols + key_cols] + key_bias.astype(f32)
    values_pre = projected[:, query_cols + key_cols :] + value_bias.astype(f32)
    query_rot = apply_rotation(
        query_rows.reshape(row_count, head_count, HEAD_DIM), cosine_rows, sine_table
    ).astype(bf16)
    key_rot = apply_rotation(
        keys_before_rotation.reshape(row_count, kv_count, HEAD_DIM), cosine_rows, sine_table
    ).astype(bf16)
    value_low = values_pre.astype(bf16)
    pair_rows = jnp.concatenate(
        [key_rot.reshape(seq_count, block_len, key_cols), value_low.reshape(seq_count, block_len, key_cols)], 2
    )
    pair_all = [pair_rows]
    for shift in range(1, blocks_along):
        pair_all.append(
            lax.ppermute(
                pair_rows, "context", [(n, n + shift) for n in range(blocks_along - shift)]
            )
        )
    pair_all = jnp.concatenate(pair_all, 1)
    query_grid = query_rot.reshape(seq_count, block_len, kv_count, query_group_width, HEAD_DIM)
    key_grid = pair_all[:, :, :key_cols].reshape(seq_count, position_count, kv_count, HEAD_DIM)
    value_grid = pair_all[:, :, key_cols:].reshape(seq_count, position_count, kv_count, HEAD_DIM)

    def masked_scores():
        raw = (
            jnp.einsum(
                "sqkgd,stkd->skgqt", query_grid, key_grid, preferred_element_type=f32
            )
            * score_scale
        )
        return jnp.where(allowed, raw, -1e30)

    scores = masked_scores()
    row_max = jnp.max(scores, -1, keepdims=True)
    exp_scores = jnp.exp(scores - row_max)
    row_sums = jnp.sum(exp_scores, -1, keepdims=True)
    logsum = row_max + jnp.log(row_sums)
    attention = (exp_scores / row_sums).astype(bf16)
    mixed_heads = jnp.einsum(
        "skgqt,stkd->sqkgd", attention, value_grid, preferred_element_type=f32
    )
    mixed_heads = mixed_heads.reshape(row_count, head_count * HEAD_DIM).astype(bf16)
    full_out = jnp.concatenate(out_weights, 0)
    branch = contract_last(mixed_heads, full_out)
    branch = absolute([branch[:, r * own_rows : (r + 1) * own_rows] for r in range(size)])
    hidden = inputs + tensor_sum(branch)
    scale_two = lax.rsqrt(jnp.mean(hidden * hidden, -1, keepdims=True) + EPSILON)
    normed_two = (hidden * scale_two * gain_second).astype(bf16)
    fall_grad = grad_out.reshape(row_count, model_width).astype(f32) * valid_rows
    fall_low = fall_grad.astype(bf16)
    fall_blocks = relative(fall_low)
    two_blocks = relative(normed_two)
    traded_early = trade_blocks(
        [jnp.concatenate([a, b], 1) for a, b in zip(normed_blocks, fall_blocks)], size
    )
    traded_early = jnp.concatenate(traded_early, 0)
    normed_features, fall_features = traded_early[:, :own_rows], traded_early[:, own_rows:]
    two_features = jnp.concatenate(trade_blocks(two_blocks, size), 0)

    feed_out = 0.0
    d_normed_two = 0.0
    feed_grads = []
    for (start, width), pieces in zip(edges, feed_weights):
        stacked = jnp.concatenate(pieces, 0)
        gate_part, up_part, down_part = (
            stacked[:, :width],
            stacked[:, width : 2 * width],
            stacked[:, 2 * width :],
        )
        two_row = jnp.concatenate(two_blocks, 1)
        fall_row = jnp.concatenate(fall_blocks, 1)
        gate_act = jnp.dot(two_row, gate_part, preferred_element_type=f32)
        up_act = jnp.dot(two_row, up_part, preferred_element_type=f32)
        d_active = jnp.dot(fall_row, down_part, preferred_element_type=f32)
        sigmoid_gate = jax.nn.sigmoid(gate_act)
        swish_gate = gate_act * sigmoid_gate
        active = (swish_gate * up_act).astype(bf16)
        d_gate = (
            d_active * up_act * sigmoid_gate * (1.0 + gate_act * (1.0 - sigmoid_gate))
        ).astype(bf16)
        d_up = (d_active * swish_gate).astype(bf16)
        feed_out = feed_out + contract_last(active, down_part)
        d_normed_two = (
            d_normed_two + contract_last(d_gate, gate_part) + contract_last(d_up, up_part)
        )
        acts = jnp.concatenate(
            gather_pieces(jnp.concatenate([d_gate, d_up, active], 1), size), 0
        )
        part = jnp.concatenate(
            [
                contract_first(two_features, acts[:, : 2 * width]),
                contract_first(fall_features, acts[:, 2 * width :]),
            ],
            1,
        ).astype(bf16)
        feed_grads.append(line_sum(part))

    def split(field):
        return [field[:, r * own_rows : (r + 1) * own_rows] for r in range(size)]

    d_normed_two = tensor_sum(absolute(split(d_normed_two)))
    result = valid_rows * (hidden + tensor_sum(absolute(split(feed_out))))
    output = result.astype(bf16).reshape(seq_count, block_len, model_width)
    gain_two_grad = jnp.sum(d_normed_two * hidden * scale_two, 0)
    d_hidden = fall_grad + norm_back(hidden, scale_two, gain_second, d_normed_two)
    d_branch = d_hidden.astype(bf16)
    branch_blocks = relative(d_branch)
    branch_features = jnp.concatenate(trade_blocks(branch_blocks, size), 0)
    d_mixed = jnp.dot(
        jnp.concatenate(branch_blocks, 1), full_out, preferred_element_type=f32
    ).astype(bf16)
    mixed_grid = d_mixed.reshape(seq_count, block_len, kv_count, query_group_width, HEAD_DIM)
    scores = masked_scores()
    attention_full = jnp.exp(scores - logsum)
    attention = attention_full.astype(bf16)
    d_probs = jnp.einsum(
        "sqkgd,stkd->skgqt", mixed_grid, value_grid, preferred_element_type=f32
    )
    d_scores = (
        attention_full * (d_probs - jnp.sum(d_probs * attention_full, -1, keepdims=True))
    ).astype(bf16)
    d_query_rot = (
        jnp.einsum("skgqt,stkd->sqkgd", d_scores, key_grid, preferred_element_type=f32)
        * score_scale
    )
    d_keys_all = (
        jnp.einsum("skgqt,sqkgd->stkd", d_scores, query_grid, preferred_element_type=f32)
        * score_scale
    )
    d_values_all = jnp.einsum(
        "skgqt,sqkgd->stkd", attention, mixed_grid, preferred_element_type=f32
    )
    d_pair = jnp.concatenate(
        [
            d_keys_all.reshape(seq_count, position_count, key_cols),
            d_values_all.reshape(seq_count, position_count, key_cols),
        ],
        2,
    )
    d_own = d_pair[:, :block_len]
    for shift in range(1, blocks_along):
        sent = d_pair[:, shift * block_len : (shift + 1) * block_len].astype(bf16)
        d_own = d_own + lax.ppermute(
            sent, "context", [(n, n - shift) for n in range(shift, blocks_along)]
        ).astype(f32)
    d_own = d_own.reshape(row_count, 2 * key_cols)
    d_query_low = (
        rotate_back(d_query_rot.reshape(row_count, head_count, HEAD_DIM), cosine_rows, sine_table)
        .reshape(row_count, head_count * HEAD_DIM)
        .astype(bf16)
    )
    d_key_low = (
        rotate_back(
            d_own[:, :key_cols].reshape(row_count, kv_count, HEAD_DIM), cosine_rows, sine_table
        )
        .reshape(row_count, key_cols)
        .astype(bf16)
    )
    d_value_low = d_own[:, key_cols:].astype(bf16)
    d_projected = jnp.concatenate([d_query_low, d_key_low, d_value_low], 1)
    d_normed = contract_last(d_projected, jnp.concatenate(attention_weights, 0))
    d_normed = tensor_sum(absolute(split(d_normed)))
    gain_one_grad = jnp.sum(d_normed * inputs * scale_one, 0)
    d_inputs = d_hidden + norm_back(inputs, scale_one, gain_first, d_normed)
    grad_tokens = d_inputs.astype(bf16).reshape(seq_count, block_len, model_width)
    gain_two_grad = small_total(gain_two_grad)
    small = small_total(
        jnp.concatenate([gain_one_grad, jnp.sum(d_projected.astype(f32), 0)])
    )
    mixed_all = jnp.concatenate(gather_pieces(mixed_heads, size), 0)
    out_grad = line_sum(contract_first(branch_features, mixed_all).astype(bf16))
    projected_all = jnp.concatenate(gather_pieces(d_projected, size), 0)
    projected_grad = line_sum(contract_first(normed_features, projected_all).astype(bf16))

    def columns(which):
        return jnp.concatenate(
            [g[:, which * w : (which + 1) * w] for g, (_, w) in zip(feed_grads, edges)], 1
        )

    low, high = model_width + query_cols, model_width + query_cols + key_cols
    return (
        output,
        grad_tokens,
        small[:model_width],
        projected_grad[:, :query_cols],
        small[model_width:low],
        projected_grad[:, query_cols : query_cols + key_cols],
        small[low:high],
        projected_grad[:, query_cols + key_cols :],
        small[high:],
        out_grad,
        gain_two_grad,
        columns(0),
        columns(1),
        columns(2),
    )


def solution(mesh):
    in_specs = (
        P("dp", "context", None),
        P("dp"),
        P(),
        P("dp", "tensor"),
        P("tensor"),
        P("dp", "tensor"),
        P("tensor"),
        P("dp", "tensor"),
        P("tensor"),
        P("dp", "tensor"),
        P(),
        P("dp", "tensor"),
        P("dp", "tensor"),
        P("dp", "tensor"),
        P("dp", "context", None),
    )
    out_specs = (
        P("dp", "context", None),
        P("dp", "context", None),
        P(),
        P("dp", "tensor"),
        P("tensor"),
        P("dp", "tensor"),
        P("tensor"),
        P("dp", "tensor"),
        P("tensor"),
        P("dp", "tensor"),
        P(),
        P("dp", "tensor"),
        P("dp", "tensor"),
        P("dp", "tensor"),
    )
    return jax.shard_map(local, mesh=mesh, in_specs=in_specs, out_specs=out_specs, check_vma=False)
```

```python
import math

import jax
import jax.numpy as jnp
from jax import lax
from jax.experimental import pallas as pl
from jax.experimental.pallas import tpu as pltpu
from jax.sharding import PartitionSpec as P

HEAD_DIM = 128


EPSILON = 1e-06
ROPE_BASE = 1000000.0


def xor_pairs(size, mask):
    return [(i, i ^ mask) for i in range(size)]


class Lane:
    def __init__(self, depth=1):
        self.sent = []
        self.depth = depth

    def send(self, array, axis, pairs):
        if len(self.sent) >= self.depth:
            array, _ = lax.optimization_barrier((array, self.sent[-self.depth]))
        got = lax.ppermute(array, axis, pairs)
        self.sent.append(got)
        return got


def far_masks(size):
    masks, mask = [], 2
    while mask < size:
        masks.append(mask)
        mask *= 2
    return masks


def swap_blocks(blocks, me):
    mask = 1
    while mask < len(blocks):
        flag = (me & mask) != 0
        blocks = [jnp.where(flag, blocks[r ^ mask], blocks[r]) for r in range(len(blocks))]
        mask *= 2
    return blocks


def far_half(piece, mask, size, parity, lanes):
    half = piece.shape[0] // 2
    sent = lax.dynamic_slice_in_dim(piece, half * parity, half, 0)
    straight = lanes["x"].send(sent, "dp", xor_pairs(size, mask))
    other = lanes["z"].send(straight, "context", xor_pairs(lax.axis_size("context"), 1))
    first = jnp.where(parity == 0, straight, other)
    second = jnp.where(parity == 0, other, straight)
    return jnp.concatenate([first, second], 0)


def far_pieces(own, size, lanes, parity=None):
    pieces = {0: own}
    for mask in far_masks(size):
        for r in list(pieces):
            if parity is None:
                pieces[r ^ mask] = lanes["x"].send(pieces[r], "dp", xor_pairs(size, mask))
            else:
                pieces[r ^ mask] = far_half(pieces[r], mask, size, parity, lanes)
    return pieces


def gather_pieces(own, size, lanes, parity=None):
    pieces = far_pieces(own, size, lanes, parity)
    for r in list(pieces):
        pieces[r ^ 1] = lax.ppermute(pieces[r], "dp", xor_pairs(size, 1))
    return [pieces[r] for r in range(size)]


def trade_blocks(blocks, size):
    return [blocks[0]] + [
        lax.ppermute(blocks[r], "dp", xor_pairs(size, r)) for r in range(1, size)
    ]


def tensor_sum(part):
    sent = part.astype(jnp.bfloat16)
    size = lax.axis_size("tensor")
    if size == 2:
        other = lax.ppermute(sent, "tensor", [(0, 1), (1, 0)])
        return sent.astype(jnp.float32) + other.astype(jnp.float32)
    return lax.psum(part, "tensor")


def line_sum(part, lanes):
    place = lax.axis_index("context")
    if lax.axis_size("context") != 4:
        return lax.psum(part.astype(jnp.float32), "context")
    got = lanes["hop1"].send(part, "context", [(0, 1), (3, 2)])
    pair = (part.astype(jnp.float32) + got.astype(jnp.float32)).astype(jnp.bfloat16)
    got = lanes["hop2"].send(pair, "context", [(1, 2), (2, 1)])
    total = (pair.astype(jnp.float32) + got.astype(jnp.float32)).astype(jnp.bfloat16)
    got = lanes["hop3"].send(total, "context", [(1, 0), (2, 3)])
    ends = (place == 0) | (place == 3)
    return jnp.where(ends, got, total).astype(jnp.float32)


def small_total(vector):
    for axis in ("dp", "context"):
        size, mask = lax.axis_size(axis), 1
        while mask < size:
            vector = vector + lax.ppermute(vector, axis, xor_pairs(size, mask))
            mask *= 2
    return vector


def contract_last(left, right):
    return lax.dot_general(
        left, right, (((1,), (1,)), ((), ())), preferred_element_type=jnp.float32
    )


def norm_back(field, scale_rows, gain, d_normed):
    weighted = d_normed * gain
    cubed = scale_rows * scale_rows * scale_rows
    return scale_rows * weighted - field * cubed * jnp.mean(field * weighted, -1, keepdims=True)


ANY = pl.BlockSpec(memory_space=pl.ANY)
VMEM = pl.BlockSpec(memory_space=pltpu.VMEM)
SMEM = pl.BlockSpec(memory_space=pltpu.SMEM)


def plain_params(limit):
    return pltpu.CompilerParams(vmem_limit_bytes=limit)


def dot_nn(left, right):
    return jnp.dot(left, right, preferred_element_type=jnp.float32)


def feed_chunk(two_row, fall_row, sources, start, width, d_sum, out_sum):
    rows, features = two_row.shape
    bf16, f32 = jnp.bfloat16, jnp.float32
    flat, layout = [], []
    for source in sources:
        layout.append(len(source))
        flat.extend(source)
    first = d_sum is None
    held = [] if first else [d_sum, out_sum]

    def kernel(*refs):
        refs = list(refs)
        two_ref, fall_ref = refs[:2]
        given = refs[2 : 2 + len(flat)]
        at = 2 + len(flat)
        sums = refs[at : at + len(held)]
        at += len(held)
        acts_ref, d_ref, out_ref, gate_w, up_w, down_w, sems = refs[at:]
        copies = [[], [], []]
        place, taken = 0, 0
        for kind in layout:
            depth = given[taken].shape[0]
            for which, scratch in enumerate((gate_w, up_w, down_w)):
                if kind == 3:
                    view = given[taken + which].at[:, pl.ds(start, width)]
                else:
                    view = given[taken].at[:, pl.ds(which * width, width)]
                copy = pltpu.make_async_copy(
                    view,
                    scratch.at[pl.ds(place, depth), :],
                    sems.at[which, len(copies[which])],
                )
                copies[which].append(copy)
            place += depth
            taken += kind
        for group in copies:
            for copy in group:
                copy.start()
        for copy in copies[0]:
            copy.wait()
        gate = dot_nn(two_ref[...], gate_w[...])
        for copy in copies[1]:
            copy.wait()
        up = dot_nn(two_ref[...], up_w[...])
        for copy in copies[2]:
            copy.wait()
        d_active = dot_nn(fall_ref[...], down_w[...])
        sigmoid = jax.nn.sigmoid(gate)
        swish = gate * sigmoid
        acts_ref[:, 2 * width :] = (swish * up).astype(bf16)
        acts_ref[:, :width] = (d_active * up * sigmoid * (1.0 + gate * (1.0 - sigmoid))).astype(bf16)
        acts_ref[:, width : 2 * width] = (d_active * swish).astype(bf16)
        d_part = contract_last(acts_ref[:, :width], gate_w[...]) + contract_last(
            acts_ref[:, width : 2 * width], up_w[...]
        )
        out_part = contract_last(acts_ref[:, 2 * width :], down_w[...])
        if first:
            d_ref[...] = d_part
            out_ref[...] = out_part
        else:
            d_ref[...] = sums[0][...] + d_part
            out_ref[...] = sums[1][...] + out_part

    weight_bytes = 6 * features * width
    return pl.pallas_call(
        kernel,
        out_shape=(
            jax.ShapeDtypeStruct((rows, 3 * width), bf16),
            jax.ShapeDtypeStruct((rows, features), f32),
            jax.ShapeDtypeStruct((rows, features), f32),
        ),
        in_specs=[VMEM, VMEM] + [ANY] * len(flat) + [VMEM] * len(held),
        out_specs=(VMEM, VMEM, VMEM),
        scratch_shapes=[pltpu.VMEM((features, width), bf16)] * 3
        + [pltpu.SemaphoreType.DMA((3, len(sources)))],
        compiler_params=plain_params(40 << 20),
        cost_estimate=pl.CostEstimate(
            flops=12 * rows * features * width,
            bytes_accessed=weight_bytes + 20 * rows * features + 6 * rows * width,
            transcendentals=rows * width,
        ),
        name="feed_chunk",
    )(two_row, fall_row, *flat, *held)


def grad_block(features, pieces, spans):
    bf16 = jnp.bfloat16
    depth, columns = pieces[0].shape
    tokens = features[0].shape[1]
    own = features[0].shape[0]
    total = sum(w for _, w in spans)

    def kernel(*refs):
        refs = list(refs)
        feature_refs = refs[: len(features)]
        given = refs[len(features) : len(features) + len(pieces)]
        out_ref, held, sems = refs[len(features) + len(pieces) :]
        copies = [
            pltpu.make_async_copy(ref, held.at[pl.ds(n * depth, depth), :], sems.at[n])
            for n, ref in enumerate(given)
        ]
        for copy in copies:
            copy.start()
        for copy in copies:
            copy.wait()
        for ref, (start, width) in zip(feature_refs, spans):
            out_ref[:, start : start + width] = dot_nn(
                ref[...], held[:, start : start + width]
            ).astype(bf16)

    return pl.pallas_call(
        kernel,
        out_shape=jax.ShapeDtypeStruct((own, total), bf16),
        in_specs=[VMEM] * len(features) + [ANY] * len(pieces),
        out_specs=VMEM,
        scratch_shapes=[
            pltpu.VMEM((tokens, columns), bf16),
            pltpu.SemaphoreType.DMA((len(pieces),)),
        ],
        compiler_params=plain_params(40 << 20),
        cost_estimate=pl.CostEstimate(
            flops=2 * own * tokens * total,
            bytes_accessed=2 * (tokens * columns + own * total + own * tokens),
            transcendentals=0,
        ),
        name="grad_block",
    )(*features, *pieces)


def key_bias_table(place, length, keys, block_len):
    key_at = lax.broadcasted_iota(jnp.int32, (keys, block_len), 0)
    query_at = lax.broadcasted_iota(jnp.int32, (keys, block_len), 1) + place * block_len
    shift = key_at // block_len
    key_at = key_at - shift * block_len + (place - shift) * block_len
    seen = (key_at <= query_at) & (key_at < length) & (key_at >= 0)
    return jnp.where(seen, 0.0, -1e30).astype(jnp.float32)


def attend(facts, query, pair):
    rows, width = query.shape
    keys = pair.shape[0]
    heads = width // HEAD_DIM
    bf16, f32 = jnp.bfloat16, jnp.float32
    scale = 1.0 / math.sqrt(HEAD_DIM)

    def kernel(facts_ref, query_ref, pair_ref, mixed_ref, lse_ref, bias, value_t):
        bias[...] = key_bias_table(facts_ref[0], facts_ref[1], keys, rows)
        value_t[...] = pair_ref[:, HEAD_DIM:].T
        lse_ref[...] = jnp.zeros_like(lse_ref)
        for head in range(heads):
            cols = slice(head * HEAD_DIM, (head + 1) * HEAD_DIM)
            scores = contract_last(pair_ref[:, :HEAD_DIM], query_ref[:, cols]) * scale + bias[...]
            top = jnp.max(scores, 0, keepdims=True)
            raised = jnp.exp(scores - top)
            total = jnp.sum(raised, 0, keepdims=True)
            lse_ref[head : head + 1, :] = top + jnp.log(total)
            probs = (raised * (1.0 / total)).astype(bf16)
            mixed_ref[:, cols] = dot_nn(value_t[...], probs).T.astype(bf16)

    return pl.pallas_call(
        kernel,
        out_shape=(
            jax.ShapeDtypeStruct((rows, width), bf16),
            jax.ShapeDtypeStruct((8, rows), f32),
        ),
        in_specs=[SMEM, VMEM, VMEM],
        out_specs=(VMEM, VMEM),
        scratch_shapes=[pltpu.VMEM((keys, rows), f32), pltpu.VMEM((HEAD_DIM, keys), bf16)],
        compiler_params=plain_params(40 << 20),
        cost_estimate=pl.CostEstimate(
            flops=4 * rows * keys * width + 12 * heads * rows * keys * 100,
            bytes_accessed=4 * rows * width + 4 * keys * HEAD_DIM,
            transcendentals=heads * rows * keys,
        ),
        name="attend",
    )(facts, query, pair)


def turn(field, cosine, sine):
    return field * cosine + pltpu.roll(field, HEAD_DIM // 2, 1) * sine


def attend_back(facts, query, pair, lse, d_mixed, cosine, sine):
    rows, width = query.shape
    keys = pair.shape[0]
    heads = width // HEAD_DIM
    bf16, f32 = jnp.bfloat16, jnp.float32
    scale = 1.0 / math.sqrt(HEAD_DIM)

    def kernel(facts_ref, query_ref, pair_ref, lse_ref, d_mixed_ref, cos_ref, sin_ref, d_query_ref, d_own_ref, d_rest_ref, bias, key_t, d_key, d_value):
        bias[...] = key_bias_table(facts_ref[0], facts_ref[1], keys, rows)
        key_t[...] = pair_ref[:, :HEAD_DIM].T
        for head in range(heads):
            cols = slice(head * HEAD_DIM, (head + 1) * HEAD_DIM)
            scores = contract_last(pair_ref[:, :HEAD_DIM], query_ref[:, cols]) * scale + bias[...]
            probs = jnp.exp(scores - lse_ref[head : head + 1, :])
            d_probs = contract_last(pair_ref[:, HEAD_DIM:], d_mixed_ref[:, cols])
            inner = jnp.sum(d_probs * probs, 0, keepdims=True)
            d_scores = (probs * (d_probs - inner)).astype(bf16)
            d_query = (dot_nn(key_t[...], d_scores) * scale).T
            d_query_ref[:, cols] = turn(d_query, cos_ref[...], -sin_ref[...]).astype(bf16)
            more_key = dot_nn(d_scores, query_ref[:, cols])
            more_value = dot_nn(probs.astype(bf16), d_mixed_ref[:, cols])
            if head == 0:
                d_key[...] = more_key
                d_value[...] = more_value
            else:
                d_key[...] += more_key
                d_value[...] += more_value
        d_own_ref[:, :HEAD_DIM] = d_key[:rows, :] * scale
        d_own_ref[:, HEAD_DIM:] = d_value[:rows, :]
        d_rest_ref[:, :HEAD_DIM] = (d_key[rows:, :] * scale).astype(bf16)
        d_rest_ref[:, HEAD_DIM:] = d_value[rows:, :].astype(bf16)

    return pl.pallas_call(
        kernel,
        out_shape=(
            jax.ShapeDtypeStruct((rows, width), bf16),
            jax.ShapeDtypeStruct((rows, 2 * HEAD_DIM), f32),
            jax.ShapeDtypeStruct((keys - rows, 2 * HEAD_DIM), bf16),
        ),
        in_specs=[SMEM] + [VMEM] * 6,
        out_specs=(VMEM, VMEM, VMEM),
        scratch_shapes=[
            pltpu.VMEM((keys, rows), f32),
            pltpu.VMEM((HEAD_DIM, keys), bf16),
            pltpu.VMEM((keys, HEAD_DIM), f32),
            pltpu.VMEM((keys, HEAD_DIM), f32),
        ],
        compiler_params=plain_params(40 << 20),
        cost_estimate=pl.CostEstimate(
            flops=10 * rows * keys * width + 12 * heads * rows * keys * 200,
            bytes_accessed=8 * rows * width + 8 * keys * HEAD_DIM,
            transcendentals=heads * rows * keys,
        ),
        name="attend_back",
    )(facts, query, pair, lse, d_mixed, cosine, sine)


MESH = pl.DeviceIdType.MESH


def flipped(index, mask):
    return index + mask - 2 * mask * ((index // mask) % 2)


def gather_and_sum(units, features, blocks, size):
    bf16, f32 = jnp.bfloat16, jnp.float32
    count = len(units)
    gathered = [isinstance(u, (list, tuple)) for u in units]
    flat = [a for u in units for a in (u if isinstance(u, (list, tuple)) else [u])]
    starts, at = [], 0
    for u in units:
        starts.append(at)
        at += len(u) if isinstance(u, (list, tuple)) else 1
    rows = flat[0].shape[0]
    widest = max(a.shape[1] for a in flat)
    own_rows, tokens = features[0].shape
    widths = []
    where = []
    counts = {}
    for u, group in enumerate(blocks):
        for spans in group:
            width = sum(w for _, _, w in spans)
            if width not in counts:
                counts[width] = 0
                widths.append(width)
            where.append((u, spans, widths.index(width), counts[width]))
            counts[width] += 1
    block_count = len(where)
    steps = []
    held = [0]
    for mask in far_masks(size):
        for r in list(held):
            steps.append((r, mask))
            held.append(r ^ mask)
    for r in list(held):
        steps.append((r, 1))
    arrival = {r ^ mask: n for n, (r, mask) in enumerate(steps)}
    ahead = 2

    def kernel(*refs):
        refs = list(refs)
        unit_refs, refs = refs[: len(flat)], refs[len(flat) :]
        feature_refs, refs = refs[: len(features)], refs[len(features) :]
        outs, refs = refs[: len(widths)], refs[len(widths) :]
        land, refs = refs[0], refs[1:]
        mine, refs = refs[: len(widths)], refs[len(widths) :]
        first, refs = refs[: len(widths)], refs[len(widths) :]
        second, refs = refs[: len(widths)], refs[len(widths) :]
        table, send_g, recv_g, send_a, recv_a, send_b, recv_b, load, store = refs
        me = lax.axis_index("dp")
        place = lax.axis_index("context")
        middle = place * (3 - place) == 2
        inner = 1 + place // 2
        across = 3 - place
        outer = 3 * (place - 1)

        barrier = pltpu.get_barrier_semaphore()
        partners = sorted(set(mask for _, mask in steps))
        for mask in partners:
            pl.semaphore_signal(barrier, 1, device_id={"dp": flipped(me, mask)}, device_id_type=MESH)

        @pl.when(middle)
        def _():
            pl.semaphore_signal(barrier, 1, device_id={"context": across}, device_id_type=MESH)
            pl.semaphore_signal(barrier, 1, device_id={"context": outer}, device_id_type=MESH)
            pl.semaphore_wait(barrier, len(partners) + 2)

        @pl.when(jnp.logical_not(middle))
        def _():
            pl.semaphore_signal(barrier, 1, device_id={"context": inner}, device_id_type=MESH)
            pl.semaphore_wait(barrier, len(partners) + 1)

        def piece(u, r):
            if gathered[u]:
                return unit_refs[starts[u] + r]
            if r == 0:
                return unit_refs[starts[u]]
            return land.at[r - 1, u, :, pl.ds(0, flat[starts[u]].shape[1])]

        def transfer(u, n):
            r, mask = steps[n]
            target = r ^ mask
            return pltpu.make_async_remote_copy(
                src_ref=piece(u, r),
                dst_ref=land.at[target - 1, u, :, pl.ds(0, flat[starts[u]].shape[1])],
                send_sem=send_g.at[n, u],
                recv_sem=recv_g.at[n, u],
                device_id={"dp": flipped(me, mask)},
                device_id_type=MESH,
            )

        wanted = [u for u in range(count) if not gathered[u]]

        def begin(u):
            for n, (r, _) in enumerate(steps):
                if r == 0:
                    transfer(u, n).start()

        def loads(u, slot):
            width = flat[starts[u]].shape[1]
            return [
                pltpu.make_async_copy(
                    piece(u, r),
                    table.at[slot, pl.ds(r * rows, rows), pl.ds(0, width)],
                    load.at[slot, r],
                )
                for r in range(size)
            ]

        def forward(u):
            waited = set()
            for n, (r, mask) in enumerate(steps):
                if r != 0:
                    if r not in waited:
                        transfer(u, arrival[r]).wait_recv()
                        waited.add(r)
                    transfer(u, n).start()
            for r in range(1, size):
                if r not in waited:
                    transfer(u, arrival[r]).wait_recv()

        def hop(j, source, target, place_to, send, recv):
            _, _, kind, index = where[j]
            return pltpu.make_async_remote_copy(
                src_ref=source[kind].at[index],
                dst_ref=target[kind].at[index],
                send_sem=send.at[j],
                recv_sem=recv.at[j],
                device_id={"context": place_to},
                device_id_type=MESH,
            )

        def hop_in(j):
            return hop(j, mine, first, inner, send_a, recv_a)

        def hop_across(j):
            return hop(j, mine, second, across, send_b, recv_b)

        def hop_out(j):
            return hop(j, first, first, outer, send_a, recv_a)

        def keep(j):
            _, _, kind, index = where[j]
            return pltpu.make_async_copy(first[kind].at[index], outs[kind].at[index], store.at[j])

        def total_in(j):
            _, _, kind, index = where[j]
            hop_in(j).wait_recv()
            mine[kind][index] = (
                mine[kind][index].astype(f32) + first[kind][index].astype(f32)
            ).astype(bf16)
            hop_across(j).start()

        def total_across(j):
            _, _, kind, index = where[j]
            hop_across(j).wait_recv()
            first[kind][index] = (
                mine[kind][index].astype(f32) + second[kind][index].astype(f32)
            ).astype(bf16)
            hop_out(j).start()
            keep(j).start()

        of_unit = [[j for j in range(block_count) if where[j][0] == u] for u in range(count)]
        for u in wanted[:ahead]:
            begin(u)
        for copy in loads(0, 0) if gathered[0] else []:
            copy.start()
        middle_in = []
        for u in range(count):
            slot = u % 2
            if not gathered[u]:
                forward(u)
                later = [v for v in wanted if v > u]
                if len(later) >= ahead:
                    begin(later[ahead - 1])
            if not (u == 0 and gathered[0]):
                for copy in loads(u, slot):
                    copy.start()
            for copy in loads(u, slot):
                copy.wait()
            for j in of_unit[u]:
                _, spans, kind, index = where[j]
                filled = 0
                for which, start, width in spans:
                    mine[kind][index, :, filled : filled + width] = dot_nn(
                        feature_refs[which][...], table[slot, :, start : start + width]
                    ).astype(bf16)
                    filled += width

                @pl.when(jnp.logical_not(middle))
                def _(j=j):
                    if j >= 3:
                        hop_in(j - 3).wait_send()
                    hop_in(j).start()

            if u >= 1:

                @pl.when(middle)
                def _(u=u):
                    for j in of_unit[u - 1]:
                        total_in(j)
                        if j >= 1:
                            total_across(j - 1)

        @pl.when(middle)
        def _():
            for j in of_unit[count - 1]:
                total_in(j)
                total_across(j - 1)
            total_across(block_count - 1)
            for j in range(block_count):
                hop_across(j).wait_send()
                hop_out(j).wait_send()
                keep(j).wait()

        @pl.when(jnp.logical_not(middle))
        def _():
            for j in range(max(block_count - 3, 0), block_count):
                hop_in(j).wait_send()
            for j in range(block_count):
                hop_out(j).wait_recv()
                keep(j).start()
            for j in range(block_count):
                keep(j).wait()

        for u in wanted:
            for n in range(len(steps)):
                transfer(u, n).wait_send()

    def stacks(kind_memory):
        return [kind_memory((counts[w], own_rows, w), bf16) for w in widths]

    columns = sum(counts[w] * w for w in widths)
    results = pl.pallas_call(
        kernel,
        out_shape=[jax.ShapeDtypeStruct((counts[w], own_rows, w), bf16) for w in widths]
        + [jax.ShapeDtypeStruct((size - 1, count, rows, widest), bf16)],
        in_specs=[ANY] * len(flat) + [VMEM] * len(features),
        out_specs=[ANY] * (len(widths) + 1),
        scratch_shapes=stacks(pltpu.VMEM) * 3
        + [
            pltpu.VMEM((2, tokens, widest), bf16),
            pltpu.SemaphoreType.DMA((len(steps), count)),
            pltpu.SemaphoreType.DMA((len(steps), count)),
            pltpu.SemaphoreType.DMA((block_count,)),
            pltpu.SemaphoreType.DMA((block_count,)),
            pltpu.SemaphoreType.DMA((block_count,)),
            pltpu.SemaphoreType.DMA((block_count,)),
            pltpu.SemaphoreType.DMA((2, size)),
            pltpu.SemaphoreType.DMA((block_count,)),
        ],
        compiler_params=pltpu.CompilerParams(
            collective_id=0, has_side_effects=True, vmem_limit_bytes=60 << 20
        ),
        cost_estimate=pl.CostEstimate(
            flops=2 * own_rows * tokens * columns,
            bytes_accessed=2 * tokens * columns + 12 * own_rows * columns,
            transcendentals=0,
        ),
        name="gather_and_sum",
    )(*flat, *features)
    return [(results[kind], index) for _, _, kind, index in where]


def chunk_edges(columns):
    tiles = columns // 128
    count = next((n for n in (7, 5, 4, 6, 3, 2) if tiles % n == 0), 1)
    width = columns // count
    return [(n * width, width) for n in range(count)]


def local(
    tokens,
    lengths,
    gain_one,
    w_query,
    b_query,
    key_weight,
    key_bias,
    value_weight,
    value_bias,
    w_out,
    gain_two,
    w_gate,
    w_up,
    w_down,
    grad_out,
):
    bf16, f32 = jnp.bfloat16, jnp.float32
    seq_count, block_len, model_width = tokens.shape
    row_count = seq_count * block_len
    query_cols = w_query.shape[1]
    key_cols = key_weight.shape[1]
    unit_cols = w_gate.shape[1]
    own_rows = w_query.shape[0]
    head_count = query_cols // HEAD_DIM
    kv_count = key_cols // HEAD_DIM
    query_group_width = head_count // kv_count
    size = lax.axis_size("dp")
    me = lax.axis_index("dp")
    blocks_along = lax.axis_size("context")
    place = lax.axis_index("context")
    parity = place % 2 if blocks_along % 2 == 0 and own_rows % 32 == 0 else None

    def relative(field):
        return swap_blocks([field[:, n * own_rows : (n + 1) * own_rows] for n in range(size)], me)

    def absolute(blocks):
        return jnp.concatenate(swap_blocks(blocks, me), 1)

    def dot_rows(blocks, weights):
        return jnp.dot(
            jnp.concatenate(blocks, 1), jnp.concatenate(weights, 0), preferred_element_type=f32
        )

    lanes = {name: Lane() for name in ("x", "z", "hop1", "hop2", "hop3")}
    attention_weights = gather_pieces(
        jnp.concatenate([w_query, key_weight, value_weight], 1), size, lanes
    )
    out_weights = gather_pieces(w_out, size, lanes, parity)
    edges = chunk_edges(unit_cols)
    feed_weights = []
    early = len(edges) - 2

    feed_own = (w_gate, w_up, w_down)
    feed_near = tuple(lax.ppermute(w, "dp", xor_pairs(size, 1)) for w in feed_own)

    def fetch(start, width):
        own = jnp.concatenate([w[:, start : start + width] for w in feed_own], 1)
        far = far_pieces(own, size, lanes, parity)
        sources = []
        for r in range(size):
            if r < 2:
                sources.append(feed_own if r == 0 else feed_near)
            elif r % 2 == 0:
                sources.append((far[r],))
            else:
                sources.append((lax.ppermute(far[r - 1], "dp", xor_pairs(size, 1)),))
        feed_weights.append(sources)

    for start, width in edges[:early]:
        fetch(start, width)

    positions = place * block_len + jnp.arange(block_len, dtype=jnp.int32)
    position_count = block_len * blocks_along
    valid_rows = (positions[None, :] < lengths[:, None]).astype(f32).reshape(row_count, 1)
    facts = jnp.stack([place.astype(jnp.int32), lengths[0]])
    half = HEAD_DIM // 2
    inverse = jnp.exp(jnp.arange(half, dtype=f32) * (-2.0 * math.log(ROPE_BASE) / HEAD_DIM))
    angles = positions.astype(f32)[:, None] * inverse[None, :]
    cosine = jnp.concatenate([jnp.cos(angles)] * 2, 1)
    sine = jnp.concatenate([-jnp.sin(angles), jnp.sin(angles)], 1)
    gain_first = gain_one.astype(f32)
    gain_second = gain_two.astype(f32)
    inputs = tokens.reshape(row_count, model_width).astype(f32)
    scale_one = lax.rsqrt(jnp.mean(inputs * inputs, -1, keepdims=True) + EPSILON)
    normalized_input = (inputs * scale_one * gain_first).astype(bf16)
    normed_blocks = relative(normalized_input)
    projected = dot_rows(normed_blocks, attention_weights) + jnp.concatenate(
        [b_query, key_bias, value_bias]
    ).astype(f32)
    turned = query_cols + key_cols

    def turn_heads(field, sine_rows):
        grid = field.reshape(row_count, field.shape[1] // HEAD_DIM, HEAD_DIM)
        swapped = jnp.concatenate([grid[..., half:], grid[..., :half]], -1)
        grid = grid * cosine[:, None, :] + swapped * sine_rows[:, None, :]
        return grid.reshape(field.shape).astype(bf16)

    turned_rows = turn_heads(projected[:, :turned], sine)
    query_rot = turned_rows[:, :query_cols]
    pair_rows = jnp.concatenate([turned_rows[:, query_cols:], projected[:, turned:].astype(bf16)], 1)
    pair_all = [pair_rows]
    for shift in range(1, blocks_along):
        pair_all.append(
            lax.ppermute(
                pair_rows, "context", [(n, n + shift) for n in range(blocks_along - shift)]
            )
        )
    pair_all = jnp.concatenate(pair_all, 0)
    mixed_heads, lse = attend(facts, query_rot, pair_all)
    full_out = jnp.concatenate(out_weights, 0)
    branch = contract_last(mixed_heads, full_out)
    branch = absolute([branch[:, r * own_rows : (r + 1) * own_rows] for r in range(size)])
    hidden = inputs + tensor_sum(branch)
    scale_two = lax.rsqrt(jnp.mean(hidden * hidden, -1, keepdims=True) + EPSILON)
    normed_two = (hidden * scale_two * gain_second).astype(bf16)
    fall_grad = grad_out.reshape(row_count, model_width).astype(f32) * valid_rows
    fall_low = fall_grad.astype(bf16)
    fall_blocks = relative(fall_low)
    two_blocks = relative(normed_two)
    traded_early = trade_blocks(
        [jnp.concatenate([a, b], 1) for a, b in zip(normed_blocks, fall_blocks)], size
    )
    traded_early = jnp.concatenate(traded_early, 0).T
    normed_features, fall_features = traded_early[:own_rows], traded_early[own_rows:]
    two_features = jnp.concatenate(trade_blocks(two_blocks, size), 0).T
    two_row = jnp.concatenate(two_blocks, 1)
    fall_row = jnp.concatenate(fall_blocks, 1)

    feed_out, d_normed_two = None, None
    feed_units = []
    for turn_at, (start, width) in enumerate(edges):
        acts, d_normed_two, feed_out = feed_chunk(
            two_row, fall_row, feed_weights[turn_at], start, width, d_normed_two, feed_out
        )
        if turn_at < 0:
            acts = gather_pieces(acts, size, lanes)
        feed_units.append(acts)
        if turn_at == 0:
            for edge in edges[early:]:
                fetch(*edge)

    def split(field):
        return [field[:, r * own_rows : (r + 1) * own_rows] for r in range(size)]

    d_normed_two = tensor_sum(absolute(split(d_normed_two)))
    result = valid_rows * (hidden + tensor_sum(absolute(split(feed_out))))
    output = result.astype(bf16).reshape(seq_count, block_len, model_width)
    gain_two_grad = jnp.sum(d_normed_two * hidden * scale_two, 0)
    d_hidden = fall_grad + norm_back(hidden, scale_two, gain_second, d_normed_two)
    d_branch = d_hidden.astype(bf16)
    branch_blocks = relative(d_branch)
    branch_features = jnp.concatenate(trade_blocks(branch_blocks, size), 0).T
    d_mixed = jnp.dot(
        jnp.concatenate(branch_blocks, 1), full_out, preferred_element_type=f32
    ).astype(bf16)
    d_query_low, d_own, d_rest = attend_back(
        facts, query_rot, pair_all, lse, d_mixed, cosine, sine
    )
    for shift in range(1, blocks_along):
        d_own = d_own + lax.ppermute(
            d_rest[(shift - 1) * block_len : shift * block_len],
            "context",
            [(n, n - shift) for n in range(shift, blocks_along)],
        ).astype(f32)
    d_key_low = turn_heads(d_own[:, :key_cols], -sine)
    d_value_low = d_own[:, key_cols:].astype(bf16)
    d_projected = jnp.concatenate([d_query_low, d_key_low, d_value_low], 1)
    d_normed = contract_last(d_projected, jnp.concatenate(attention_weights, 0))
    d_normed = tensor_sum(absolute(split(d_normed)))
    gain_one_grad = jnp.sum(d_normed * inputs * scale_one, 0)
    d_inputs = d_hidden + norm_back(inputs, scale_one, gain_first, d_normed)
    grad_tokens = d_inputs.astype(bf16).reshape(seq_count, block_len, model_width)
    gain_two_grad = small_total(gain_two_grad)
    small = small_total(
        jnp.concatenate([gain_one_grad, jnp.sum(d_projected.astype(f32), 0)])
    )
    projected_width = d_projected.shape[1]
    last = jnp.concatenate([d_projected, mixed_heads], 1)
    halfway = last.shape[1] // 2
    blocks = [
        [[(0, 0, width)], [(0, width, width)], [(1, 2 * width, width)]] for _, width in edges
    ] + [
        [
            [(2, 0, halfway)],
            [(2, halfway, projected_width - halfway), (3, projected_width, query_cols)],
        ]
    ]
    sums = gather_and_sum(
        feed_units + [last],
        [two_features, fall_features, normed_features, branch_features],
        blocks,
        size,
    )

    def columns(which):
        stack = sums[which][0]
        return jnp.concatenate(
            [stack[3 * n + which].astype(f32) for n in range(len(edges))], 1
        )

    stack = sums[-1][0]
    last_grad = jnp.concatenate([stack[0], stack[1]], 1).astype(f32)
    projected_grad, out_grad = last_grad[:, :projected_width], last_grad[:, projected_width:]

    low, high = model_width + query_cols, model_width + query_cols + key_cols
    return (
        output,
        grad_tokens,
        small[:model_width],
        projected_grad[:, :query_cols],
        small[model_width:low],
        projected_grad[:, query_cols : query_cols + key_cols],
        small[low:high],
        projected_grad[:, query_cols + key_cols :],
        small[high:],
        out_grad,
        gain_two_grad,
        columns(0),
        columns(1),
        columns(2),
    )


def solution(mesh):
    in_specs = (
        P("dp", "context", None),
        P("dp"),
        P(),
        P("dp", "tensor"),
        P("tensor"),
        P("dp", "tensor"),
        P("tensor"),
        P("dp", "tensor"),
        P("tensor"),
        P("dp", "tensor"),
        P(),
        P("dp", "tensor"),
        P("dp", "tensor"),
        P("dp", "tensor"),
        P("dp", "context", None),
    )
    out_specs = (
        P("dp", "context", None),
        P("dp", "context", None),
        P(),
        P("dp", "tensor"),
        P("tensor"),
        P("dp", "tensor"),
        P("tensor"),
        P("dp", "tensor"),
        P("tensor"),
        P("dp", "tensor"),
        P(),
        P("dp", "tensor"),
        P("dp", "tensor"),
        P("dp", "tensor"),
    )
    return jax.shard_map(local, mesh=mesh, in_specs=in_specs, out_specs=out_specs, check_vma=False)
```

```python
import math

import jax
import jax.numpy as jnp
from jax import lax
from jax.experimental import pallas as pl
from jax.experimental.pallas import tpu as pltpu
from jax.sharding import PartitionSpec as P

HEAD_DIM = 128


EPSILON = 1e-06
ROPE_BASE = 1000000.0


def xor_pairs(size, mask):
    return [(i, i ^ mask) for i in range(size)]


class Lane:
    def __init__(self, depth=1):
        self.sent = []
        self.depth = depth

    def send(self, array, axis, pairs):
        if len(self.sent) >= self.depth:
            array, _ = lax.optimization_barrier((array, self.sent[-self.depth]))
        got = lax.ppermute(array, axis, pairs)
        self.sent.append(got)
        return got


def far_masks(size):
    masks, mask = [], 2
    while mask < size:
        masks.append(mask)
        mask *= 2
    return masks


def swap_blocks(blocks, me):
    mask = 1
    while mask < len(blocks):
        flag = (me & mask) != 0
        blocks = [jnp.where(flag, blocks[r ^ mask], blocks[r]) for r in range(len(blocks))]
        mask *= 2
    return blocks


def far_half(piece, mask, size, parity, lanes):
    half = piece.shape[0] // 2
    sent = lax.dynamic_slice_in_dim(piece, half * parity, half, 0)
    straight = lanes["x"].send(sent, "dp", xor_pairs(size, mask))
    other = lanes["z"].send(straight, "context", xor_pairs(lax.axis_size("context"), 1))
    first = jnp.where(parity == 0, straight, other)
    second = jnp.where(parity == 0, other, straight)
    return jnp.concatenate([first, second], 0)


def far_pieces(own, size, lanes, parity=None):
    pieces = {0: own}
    for mask in far_masks(size):
        for r in list(pieces):
            if parity is None:
                pieces[r ^ mask] = lanes["x"].send(pieces[r], "dp", xor_pairs(size, mask))
            else:
                pieces[r ^ mask] = far_half(pieces[r], mask, size, parity, lanes)
    return pieces


def gather_pieces(own, size, lanes, parity=None):
    pieces = far_pieces(own, size, lanes, parity)
    for r in list(pieces):
        pieces[r ^ 1] = lax.ppermute(pieces[r], "dp", xor_pairs(size, 1))
    return [pieces[r] for r in range(size)]


def trade_blocks(blocks, size):
    return [blocks[0]] + [
        lax.ppermute(blocks[r], "dp", xor_pairs(size, r)) for r in range(1, size)
    ]


def tensor_sum(part):
    sent = part.astype(jnp.bfloat16)
    size = lax.axis_size("tensor")
    if size == 2:
        other = lax.ppermute(sent, "tensor", [(0, 1), (1, 0)])
        return sent.astype(jnp.float32) + other.astype(jnp.float32)
    return lax.psum(part, "tensor")


def line_sum(part, lanes):
    place = lax.axis_index("context")
    if lax.axis_size("context") != 4:
        return lax.psum(part.astype(jnp.float32), "context")
    got = lanes["hop1"].send(part, "context", [(0, 1), (3, 2)])
    pair = (part.astype(jnp.float32) + got.astype(jnp.float32)).astype(jnp.bfloat16)
    got = lanes["hop2"].send(pair, "context", [(1, 2), (2, 1)])
    total = (pair.astype(jnp.float32) + got.astype(jnp.float32)).astype(jnp.bfloat16)
    got = lanes["hop3"].send(total, "context", [(1, 0), (2, 3)])
    ends = (place == 0) | (place == 3)
    return jnp.where(ends, got, total).astype(jnp.float32)


def small_total(vector):
    for axis in ("dp", "context"):
        size, mask = lax.axis_size(axis), 1
        while mask < size:
            vector = vector + lax.ppermute(vector, axis, xor_pairs(size, mask))
            mask *= 2
    return vector


def contract_last(left, right):
    return lax.dot_general(
        left, right, (((1,), (1,)), ((), ())), preferred_element_type=jnp.float32
    )


def norm_back(field, scale_rows, gain, d_normed):
    weighted = d_normed * gain
    cubed = scale_rows * scale_rows * scale_rows
    return scale_rows * weighted - field * cubed * jnp.mean(field * weighted, -1, keepdims=True)


ANY = pl.BlockSpec(memory_space=pl.ANY)
VMEM = pl.BlockSpec(memory_space=pltpu.VMEM)
SMEM = pl.BlockSpec(memory_space=pltpu.SMEM)


def plain_params(limit):
    return pltpu.CompilerParams(vmem_limit_bytes=limit)


def dot_nn(left, right):
    return jnp.dot(left, right, preferred_element_type=jnp.float32)


def feed_chunk(two_row, fall_row, sources, start, width, d_sum, out_sum):
    rows, features = two_row.shape
    bf16, f32 = jnp.bfloat16, jnp.float32
    flat, layout = [], []
    for source in sources:
        layout.append(len(source))
        flat.extend(source)
    first = d_sum is None
    held = [] if first else [d_sum, out_sum]

    def kernel(*refs):
        refs = list(refs)
        two_ref, fall_ref = refs[:2]
        given = refs[2 : 2 + len(flat)]
        at = 2 + len(flat)
        sums = refs[at : at + len(held)]
        at += len(held)
        acts_ref, d_ref, out_ref, gate_w, up_w, down_w, sems = refs[at:]
        copies = [[], [], []]
        place, taken = 0, 0
        for kind in layout:
            depth = given[taken].shape[0]
            for which, scratch in enumerate((gate_w, up_w, down_w)):
                if kind == 3:
                    view = given[taken + which].at[:, pl.ds(start, width)]
                else:
                    view = given[taken].at[:, pl.ds(which * width, width)]
                copy = pltpu.make_async_copy(
                    view,
                    scratch.at[pl.ds(place, depth), :],
                    sems.at[which, len(copies[which])],
                )
                copies[which].append(copy)
            place += depth
            taken += kind
        for group in copies:
            for copy in group:
                copy.start()
        for copy in copies[0]:
            copy.wait()
        gate = dot_nn(two_ref[...], gate_w[...])
        for copy in copies[1]:
            copy.wait()
        up = dot_nn(two_ref[...], up_w[...])
        for copy in copies[2]:
            copy.wait()
        d_active = dot_nn(fall_ref[...], down_w[...])
        sigmoid = jax.nn.sigmoid(gate)
        swish = gate * sigmoid
        acts_ref[:, 2 * width :] = (swish * up).astype(bf16)
        acts_ref[:, :width] = (d_active * up * sigmoid * (1.0 + gate * (1.0 - sigmoid))).astype(bf16)
        acts_ref[:, width : 2 * width] = (d_active * swish).astype(bf16)
        d_part = contract_last(acts_ref[:, :width], gate_w[...]) + contract_last(
            acts_ref[:, width : 2 * width], up_w[...]
        )
        out_part = contract_last(acts_ref[:, 2 * width :], down_w[...])
        if first:
            d_ref[...] = d_part
            out_ref[...] = out_part
        else:
            d_ref[...] = sums[0][...] + d_part
            out_ref[...] = sums[1][...] + out_part

    weight_bytes = 6 * features * width
    return pl.pallas_call(
        kernel,
        out_shape=(
            jax.ShapeDtypeStruct((rows, 3 * width), bf16),
            jax.ShapeDtypeStruct((rows, features), f32),
            jax.ShapeDtypeStruct((rows, features), f32),
        ),
        in_specs=[VMEM, VMEM] + [ANY] * len(flat) + [VMEM] * len(held),
        out_specs=(VMEM, VMEM, VMEM),
        scratch_shapes=[pltpu.VMEM((features, width), bf16)] * 3
        + [pltpu.SemaphoreType.DMA((3, len(sources)))],
        compiler_params=plain_params(40 << 20),
        cost_estimate=pl.CostEstimate(
            flops=12 * rows * features * width,
            bytes_accessed=weight_bytes + 20 * rows * features + 6 * rows * width,
            transcendentals=rows * width,
        ),
        name="feed_chunk",
    )(two_row, fall_row, *flat, *held)


def grad_block(features, pieces, spans):
    bf16 = jnp.bfloat16
    depth, columns = pieces[0].shape
    tokens = features[0].shape[1]
    own = features[0].shape[0]
    total = sum(w for _, w in spans)

    def kernel(*refs):
        refs = list(refs)
        feature_refs = refs[: len(features)]
        given = refs[len(features) : len(features) + len(pieces)]
        out_ref, held, sems = refs[len(features) + len(pieces) :]
        copies = [
            pltpu.make_async_copy(ref, held.at[pl.ds(n * depth, depth), :], sems.at[n])
            for n, ref in enumerate(given)
        ]
        for copy in copies:
            copy.start()
        for copy in copies:
            copy.wait()
        for ref, (start, width) in zip(feature_refs, spans):
            out_ref[:, start : start + width] = dot_nn(
                ref[...], held[:, start : start + width]
            ).astype(bf16)

    return pl.pallas_call(
        kernel,
        out_shape=jax.ShapeDtypeStruct((own, total), bf16),
        in_specs=[VMEM] * len(features) + [ANY] * len(pieces),
        out_specs=VMEM,
        scratch_shapes=[
            pltpu.VMEM((tokens, columns), bf16),
            pltpu.SemaphoreType.DMA((len(pieces),)),
        ],
        compiler_params=plain_params(40 << 20),
        cost_estimate=pl.CostEstimate(
            flops=2 * own * tokens * total,
            bytes_accessed=2 * (tokens * columns + own * total + own * tokens),
            transcendentals=0,
        ),
        name="grad_block",
    )(*features, *pieces)


def key_bias_table(place, length, keys, block_len):
    key_at = lax.broadcasted_iota(jnp.int32, (keys, block_len), 0)
    query_at = lax.broadcasted_iota(jnp.int32, (keys, block_len), 1) + place * block_len
    shift = key_at // block_len
    key_at = key_at - shift * block_len + (place - shift) * block_len
    seen = (key_at <= query_at) & (key_at < length) & (key_at >= 0)
    return jnp.where(seen, 0.0, -1e30).astype(jnp.float32)


def attend(facts, query, pair):
    rows, width = query.shape
    keys = pair.shape[0]
    heads = width // HEAD_DIM
    bf16, f32 = jnp.bfloat16, jnp.float32
    scale = 1.0 / math.sqrt(HEAD_DIM)

    def kernel(facts_ref, query_ref, pair_ref, mixed_ref, lse_ref, bias, value_t):
        bias[...] = key_bias_table(facts_ref[0], facts_ref[1], keys, rows)
        value_t[...] = pair_ref[:, HEAD_DIM:].T
        lse_ref[...] = jnp.zeros_like(lse_ref)
        for head in range(heads):
            cols = slice(head * HEAD_DIM, (head + 1) * HEAD_DIM)
            scores = contract_last(pair_ref[:, :HEAD_DIM], query_ref[:, cols]) * scale + bias[...]
            top = jnp.max(scores, 0, keepdims=True)
            raised = jnp.exp(scores - top)
            total = jnp.sum(raised, 0, keepdims=True)
            lse_ref[head : head + 1, :] = top + jnp.log(total)
            probs = (raised * (1.0 / total)).astype(bf16)
            mixed_ref[:, cols] = dot_nn(value_t[...], probs).T.astype(bf16)

    return pl.pallas_call(
        kernel,
        out_shape=(
            jax.ShapeDtypeStruct((rows, width), bf16),
            jax.ShapeDtypeStruct((8, rows), f32),
        ),
        in_specs=[SMEM, VMEM, VMEM],
        out_specs=(VMEM, VMEM),
        scratch_shapes=[pltpu.VMEM((keys, rows), f32), pltpu.VMEM((HEAD_DIM, keys), bf16)],
        compiler_params=plain_params(40 << 20),
        cost_estimate=pl.CostEstimate(
            flops=4 * rows * keys * width + 12 * heads * rows * keys * 100,
            bytes_accessed=4 * rows * width + 4 * keys * HEAD_DIM,
            transcendentals=heads * rows * keys,
        ),
        name="attend",
    )(facts, query, pair)


def turn(field, cosine, sine):
    return field * cosine + pltpu.roll(field, HEAD_DIM // 2, 1) * sine


def attend_back(facts, query, pair, lse, d_mixed, cosine, sine):
    rows, width = query.shape
    keys = pair.shape[0]
    heads = width // HEAD_DIM
    bf16, f32 = jnp.bfloat16, jnp.float32
    scale = 1.0 / math.sqrt(HEAD_DIM)

    def kernel(facts_ref, query_ref, pair_ref, lse_ref, d_mixed_ref, cos_ref, sin_ref, d_query_ref, d_own_ref, d_rest_ref, bias, key_t, d_key, d_value):
        bias[...] = key_bias_table(facts_ref[0], facts_ref[1], keys, rows)
        key_t[...] = pair_ref[:, :HEAD_DIM].T
        for head in range(heads):
            cols = slice(head * HEAD_DIM, (head + 1) * HEAD_DIM)
            scores = contract_last(pair_ref[:, :HEAD_DIM], query_ref[:, cols]) * scale + bias[...]
            probs = jnp.exp(scores - lse_ref[head : head + 1, :])
            d_probs = contract_last(pair_ref[:, HEAD_DIM:], d_mixed_ref[:, cols])
            inner = jnp.sum(d_probs * probs, 0, keepdims=True)
            d_scores = (probs * (d_probs - inner)).astype(bf16)
            d_query = (dot_nn(key_t[...], d_scores) * scale).T
            d_query_ref[:, cols] = turn(d_query, cos_ref[...], -sin_ref[...]).astype(bf16)
            more_key = dot_nn(d_scores, query_ref[:, cols])
            more_value = dot_nn(probs.astype(bf16), d_mixed_ref[:, cols])
            if head == 0:
                d_key[...] = more_key
                d_value[...] = more_value
            else:
                d_key[...] += more_key
                d_value[...] += more_value
        d_own_ref[:, :HEAD_DIM] = d_key[:rows, :] * scale
        d_own_ref[:, HEAD_DIM:] = d_value[:rows, :]
        d_rest_ref[:, :HEAD_DIM] = (d_key[rows:, :] * scale).astype(bf16)
        d_rest_ref[:, HEAD_DIM:] = d_value[rows:, :].astype(bf16)

    return pl.pallas_call(
        kernel,
        out_shape=(
            jax.ShapeDtypeStruct((rows, width), bf16),
            jax.ShapeDtypeStruct((rows, 2 * HEAD_DIM), f32),
            jax.ShapeDtypeStruct((keys - rows, 2 * HEAD_DIM), bf16),
        ),
        in_specs=[SMEM] + [VMEM] * 6,
        out_specs=(VMEM, VMEM, VMEM),
        scratch_shapes=[
            pltpu.VMEM((keys, rows), f32),
            pltpu.VMEM((HEAD_DIM, keys), bf16),
            pltpu.VMEM((keys, HEAD_DIM), f32),
            pltpu.VMEM((keys, HEAD_DIM), f32),
        ],
        compiler_params=plain_params(40 << 20),
        cost_estimate=pl.CostEstimate(
            flops=10 * rows * keys * width + 12 * heads * rows * keys * 200,
            bytes_accessed=8 * rows * width + 8 * keys * HEAD_DIM,
            transcendentals=heads * rows * keys,
        ),
        name="attend_back",
    )(facts, query, pair, lse, d_mixed, cosine, sine)


MESH = pl.DeviceIdType.MESH


def flipped(index, mask):
    return index + mask - 2 * mask * ((index // mask) % 2)


def gather_and_sum(units, features, blocks, size):
    bf16, f32 = jnp.bfloat16, jnp.float32
    count = len(units)
    gathered = [isinstance(u, (list, tuple)) for u in units]
    flat = [a for u in units for a in (u if isinstance(u, (list, tuple)) else [u])]
    starts, at = [], 0
    for u in units:
        starts.append(at)
        at += len(u) if isinstance(u, (list, tuple)) else 1
    rows = flat[0].shape[0]
    widest = max(a.shape[1] for a in flat)
    own_rows, tokens = features[0].shape
    widths = []
    where = []
    counts = {}
    for u, group in enumerate(blocks):
        for spans in group:
            width = sum(w for _, _, w in spans)
            if width not in counts:
                counts[width] = 0
                widths.append(width)
            where.append((u, spans, widths.index(width), counts[width]))
            counts[width] += 1
    block_count = len(where)
    steps = []
    held = [0]
    for mask in far_masks(size):
        for r in list(held):
            steps.append((r, mask))
            held.append(r ^ mask)
    for r in list(held):
        steps.append((r, 1))
    arrival = {r ^ mask: n for n, (r, mask) in enumerate(steps)}
    ahead = 2

    def kernel(*refs):
        refs = list(refs)
        unit_refs, refs = refs[: len(flat)], refs[len(flat) :]
        feature_refs, refs = refs[: len(features)], refs[len(features) :]
        outs, refs = refs[: len(widths)], refs[len(widths) :]
        land, refs = refs[0], refs[1:]
        mine, refs = refs[: len(widths)], refs[len(widths) :]
        first, refs = refs[: len(widths)], refs[len(widths) :]
        second, refs = refs[: len(widths)], refs[len(widths) :]
        table, send_g, recv_g, send_a, recv_a, send_b, recv_b, load, store = refs
        me = lax.axis_index("dp")
        place = lax.axis_index("context")
        middle = place * (3 - place) == 2
        inner = 1 + place // 2
        across = 3 - place
        outer = 3 * (place - 1)

        barrier = pltpu.get_barrier_semaphore()
        partners = sorted(set(mask for _, mask in steps))
        for mask in partners:
            pl.semaphore_signal(barrier, 1, device_id={"dp": flipped(me, mask)}, device_id_type=MESH)

        @pl.when(middle)
        def _():
            pl.semaphore_signal(barrier, 1, device_id={"context": across}, device_id_type=MESH)
            pl.semaphore_signal(barrier, 1, device_id={"context": outer}, device_id_type=MESH)
            pl.semaphore_wait(barrier, len(partners) + 2)

        @pl.when(jnp.logical_not(middle))
        def _():
            pl.semaphore_signal(barrier, 1, device_id={"context": inner}, device_id_type=MESH)
            pl.semaphore_wait(barrier, len(partners) + 1)

        def piece(u, r):
            if gathered[u]:
                return unit_refs[starts[u] + r]
            if r == 0:
                return unit_refs[starts[u]]
            return land.at[r - 1, u, :, pl.ds(0, flat[starts[u]].shape[1])]

        def transfer(u, n):
            r, mask = steps[n]
            target = r ^ mask
            return pltpu.make_async_remote_copy(
                src_ref=piece(u, r),
                dst_ref=land.at[target - 1, u, :, pl.ds(0, flat[starts[u]].shape[1])],
                send_sem=send_g.at[n, u],
                recv_sem=recv_g.at[n, u],
                device_id={"dp": flipped(me, mask)},
                device_id_type=MESH,
            )

        wanted = [u for u in range(count) if not gathered[u]]

        def begin(u):
            for n, (r, _) in enumerate(steps):
                if r == 0:
                    transfer(u, n).start()

        def loads(u, slot):
            width = flat[starts[u]].shape[1]
            return [
                pltpu.make_async_copy(
                    piece(u, r),
                    table.at[slot, pl.ds(r * rows, rows), pl.ds(0, width)],
                    load.at[slot, r],
                )
                for r in range(size)
            ]

        def forward(u):
            waited = set()
            for n, (r, mask) in enumerate(steps):
                if r != 0:
                    if r not in waited:
                        transfer(u, arrival[r]).wait_recv()
                        waited.add(r)
                    transfer(u, n).start()
            for r in range(1, size):
                if r not in waited:
                    transfer(u, arrival[r]).wait_recv()

        def hop(j, source, target, place_to, send, recv):
            _, _, kind, index = where[j]
            return pltpu.make_async_remote_copy(
                src_ref=source[kind].at[index],
                dst_ref=target[kind].at[index],
                send_sem=send.at[j],
                recv_sem=recv.at[j],
                device_id={"context": place_to},
                device_id_type=MESH,
            )

        def hop_in(j):
            return hop(j, mine, first, inner, send_a, recv_a)

        def hop_across(j):
            return hop(j, mine, second, across, send_b, recv_b)

        def hop_out(j):
            return hop(j, first, first, outer, send_a, recv_a)

        def keep(j):
            _, _, kind, index = where[j]
            return pltpu.make_async_copy(first[kind].at[index], outs[kind].at[index], store.at[j])

        def total_in(j):
            _, _, kind, index = where[j]
            hop_in(j).wait_recv()
            mine[kind][index] = (
                mine[kind][index].astype(f32) + first[kind][index].astype(f32)
            ).astype(bf16)
            hop_across(j).start()

        def total_across(j):
            _, _, kind, index = where[j]
            hop_across(j).wait_recv()
            first[kind][index] = (
                mine[kind][index].astype(f32) + second[kind][index].astype(f32)
            ).astype(bf16)
            hop_out(j).start()
            keep(j).start()

        of_unit = [[j for j in range(block_count) if where[j][0] == u] for u in range(count)]
        for u in wanted[:ahead]:
            begin(u)
        for copy in loads(0, 0) if gathered[0] else []:
            copy.start()
        middle_in = []
        for u in range(count):
            slot = u % 2
            if not gathered[u]:
                forward(u)
                later = [v for v in wanted if v > u]
                if len(later) >= ahead:
                    begin(later[ahead - 1])
            if not (u == 0 and gathered[0]):
                for copy in loads(u, slot):
                    copy.start()
            for copy in loads(u, slot):
                copy.wait()
            for j in of_unit[u]:
                _, spans, kind, index = where[j]
                filled = 0
                for which, start, width in spans:
                    mine[kind][index, :, filled : filled + width] = dot_nn(
                        feature_refs[which][...], table[slot, :, start : start + width]
                    ).astype(bf16)
                    filled += width

                @pl.when(jnp.logical_not(middle))
                def _(j=j):
                    if j >= 3:
                        hop_in(j - 3).wait_send()
                    hop_in(j).start()

            if u >= 1:

                @pl.when(middle)
                def _(u=u):
                    for j in of_unit[u - 1]:
                        total_in(j)
                        if j >= 1:
                            total_across(j - 1)

        @pl.when(middle)
        def _():
            for j in of_unit[count - 1]:
                total_in(j)
                total_across(j - 1)
            total_across(block_count - 1)
            for j in range(block_count):
                hop_across(j).wait_send()
                hop_out(j).wait_send()
                keep(j).wait()

        @pl.when(jnp.logical_not(middle))
        def _():
            for j in range(max(block_count - 3, 0), block_count):
                hop_in(j).wait_send()
            for j in range(block_count):
                hop_out(j).wait_recv()
                keep(j).start()
            for j in range(block_count):
                keep(j).wait()

        for u in wanted:
            for n in range(len(steps)):
                transfer(u, n).wait_send()

    def stacks(kind_memory):
        return [kind_memory((counts[w], own_rows, w), bf16) for w in widths]

    columns = sum(counts[w] * w for w in widths)
    results = pl.pallas_call(
        kernel,
        out_shape=[jax.ShapeDtypeStruct((counts[w], own_rows, w), bf16) for w in widths]
        + [jax.ShapeDtypeStruct((size - 1, count, rows, widest), bf16)],
        in_specs=[ANY] * len(flat) + [VMEM] * len(features),
        out_specs=[ANY] * (len(widths) + 1),
        scratch_shapes=stacks(pltpu.VMEM) * 3
        + [
            pltpu.VMEM((2, tokens, widest), bf16),
            pltpu.SemaphoreType.DMA((len(steps), count)),
            pltpu.SemaphoreType.DMA((len(steps), count)),
            pltpu.SemaphoreType.DMA((block_count,)),
            pltpu.SemaphoreType.DMA((block_count,)),
            pltpu.SemaphoreType.DMA((block_count,)),
            pltpu.SemaphoreType.DMA((block_count,)),
            pltpu.SemaphoreType.DMA((2, size)),
            pltpu.SemaphoreType.DMA((block_count,)),
        ],
        compiler_params=pltpu.CompilerParams(
            collective_id=0, has_side_effects=True, vmem_limit_bytes=60 << 20
        ),
        cost_estimate=pl.CostEstimate(
            flops=2 * own_rows * tokens * columns,
            bytes_accessed=2 * tokens * columns + 12 * own_rows * columns,
            transcendentals=0,
        ),
        name="gather_and_sum",
    )(*flat, *features)
    return [(results[kind], index) for _, _, kind, index in where]


def layer_back(
    length, hidden, tokens, grad_out, gains, feed_own, feed_near, feed_far, out_pieces, pair_pieces,
    query, pair, lse, mixed, cosine, sine,
):
    bf16, f32 = jnp.bfloat16, jnp.float32
    rows, features = hidden.shape
    own_rows = feed_own[0].shape[0]
    chunks = len(feed_far)
    width = feed_far[0][0].shape[1] // 3
    heads_width = query.shape[1]
    heads = heads_width // HEAD_DIM
    keys = pair.shape[0]
    pair_width = pair.shape[1]
    projected = heads_width + pair_width
    last_width = projected + heads_width
    halfway = last_width // 2
    size = features // own_rows
    units = chunks + 1
    tokens_all = size * rows
    small_width = 2 * features + projected
    scale = 1.0 / math.sqrt(HEAD_DIM)
    part = 64
    where = []
    for k in range(chunks):
        where.append((k, [(0, 0, width)], 0, 3 * k))
        where.append((k, [(0, width, width)], 0, 3 * k + 1))
        where.append((k, [(1, 2 * width, width)], 0, 3 * k + 2))
    where.append((chunks, [(2, 0, halfway)], 1, 0))
    where.append(
        (chunks, [(2, halfway, projected - halfway), (3, projected, heads_width)], 1, 1)
    )
    count = len(where)
    widths = (width, halfway)
    far_flat = [a for pieces in feed_far for a in pieces]

    def kernel(*refs):
        refs = list(refs)

        def take(n):
            taken = refs[:n]
            del refs[:n]
            return taken

        (length_ref, gains_ref, lse_ref, cos_ref, sin_ref) = take(5)
        (hidden_hbm, tokens_hbm, grad_hbm, query_hbm, pair_hbm, mixed_hbm) = take(6)
        own_hbm, near_hbm, far_hbm = take(3), take(3), take(2 * chunks)
        out_hbm, pairw_hbm = take(size), take(size)
        output_hbm, grad_tokens_hbm, small_ref, sum_wide, sum_last, land, acts_hbm, across_wide, across_last = take(9)
        (mine_wide, mine_last, stage_in, stage_across, table, weights, feature_t, feature_land) = take(8)
        (row_two, row_fall, row_normed, row_branch, hidden_rel, tokens_rel, d_sum, out_sum) = take(8)
        (y_send, y_land, acts_stage, query_v, pair_v, last_v, bias, key_t, d_key, d_value) = take(10)
        (d_mixed, d_rest, d_land, vec, vec_land, total_land) = take(6)
        (s_in, s_weights, s_acts, s_rest, send_g, recv_g, send_a, recv_a, send_b, recv_b) = take(10)
        (s_stage, s_keep, s_table, send_t, recv_t, send_y, recv_y, send_k, recv_k) = take(9)
        (send_v, recv_v, send_w, recv_w, s_store) = take(5)
        sums, mines, acrosses = (sum_wide, sum_last), (mine_wide, mine_last), (across_wide, across_last)
        rows_of = (row_two, row_fall, row_normed, row_branch)

        me = lax.axis_index("dp")
        place = lax.axis_index("context")
        side = lax.axis_index("tensor")
        middle = place * (3 - place) == 2
        inner = 1 + place // 2
        across = 3 - place
        outer = 3 * (place - 1)
        one = flipped(me, 1)
        partner = (me, one, flipped(me, 2), flipped(one, 2))

        barrier = pltpu.get_barrier_semaphore()
        for r in range(1, size):
            pl.semaphore_signal(barrier, 1, device_id={"dp": partner[r]}, device_id_type=MESH)
        for s in range(1, 4):
            pl.semaphore_signal(barrier, 1, device_id={"context": lax.rem(place + s, 4)}, device_id_type=MESH)
        pl.semaphore_signal(barrier, 1, device_id={"tensor": 1 - side}, device_id_type=MESH)

        def block_of(r):
            return pl.ds(pl.multiple_of(partner[r] * own_rows, 128), own_rows)

        def local(source, target, sem):
            return pltpu.make_async_copy(source, target, sem)

        def remote(source, target, send, recv, axis, index):
            return pltpu.make_async_remote_copy(
                src_ref=source, dst_ref=target, send_sem=send, recv_sem=recv,
                device_id={axis: index}, device_id_type=MESH,
            )

        def cols(r):
            return pl.ds(r * own_rows, own_rows)

        ins = []
        for n, (source, target) in enumerate(
            ((hidden_hbm, hidden_rel), (grad_hbm, row_fall), (tokens_hbm, tokens_rel))
        ):
            ins.append(
                [local(source.at[:, block_of(r)], target.at[:, cols(r)], s_in.at[n, r]) for r in range(size)]
            )
        rest = [
            local(query_hbm, query_v, s_rest.at[0]),
            local(pair_hbm, pair_v, s_rest.at[1]),
            local(mixed_hbm, last_v.at[:, pl.ds(projected, heads_width)], s_rest.at[2]),
        ]

        def weight_copies(k, which):
            view = pl.ds(which * width, width)
            sources = [
                own_hbm[which].at[:, pl.ds(k * width, width)],
                near_hbm[which].at[:, pl.ds(k * width, width)],
                far_hbm[2 * k].at[:, view],
                far_hbm[2 * k + 1].at[:, view],
            ]
            return [
                local(source, weights.at[pl.ds(r * own_rows, own_rows), view], s_weights.at[which, r])
                for r, source in enumerate(sources)
            ]

        def side_copies():
            return [
                local(out_hbm[r], weights.at[pl.ds(r * own_rows, own_rows), pl.ds(0, heads_width)], s_weights.at[0, r])
                for r in range(size)
            ] + [
                local(pairw_hbm[r], weights.at[pl.ds(r * own_rows, own_rows), pl.ds(heads_width, projected)], s_weights.at[1, r])
                for r in range(size)
            ]

        def start(copies):
            for copy in copies:
                copy.start()

        def wait(copies):
            for copy in copies:
                copy.wait()

        for copies in ins:
            start(copies)
        for which in range(3):
            start(weight_copies(0, which))
        start(rest)

        def trade(w, r):
            return remote(
                rows_of[w].at[:, cols(r)], feature_land.at[w, r - 1], send_t.at[w, r - 1], recv_t.at[w, r - 1],
                "dp", partner[r],
            )

        def turn_features(w):
            feature_t[w, :, 0:rows] = rows_of[w][:, 0:own_rows].T
            for r in range(1, size):
                trade(w, r).wait_recv()
                feature_t[w, :, r * rows : (r + 1) * rows] = feature_land[w, r - 1].T

        steps = ((0, 2), (0, 1), (2, 1))

        def unit_width(u):
            return 3 * width if u < chunks else last_width

        def piece(u, r):
            view = pl.ds(0, unit_width(u))
            return acts_hbm.at[u, :, view] if r == 0 else land.at[r - 1, u, :, view]

        def transfer(u, n):
            r, mask = steps[n]
            return remote(
                piece(u, r), land.at[(r ^ mask) - 1, u, :, pl.ds(0, unit_width(u))],
                send_g.at[n, u], recv_g.at[n, u], "dp", partner[mask],
            )

        def own_copy(u):
            if u < chunks:
                return local(acts_stage.at[u % 2], piece(u, 0), s_acts.at[u])
            return local(last_v, piece(u, 0), s_acts.at[u])

        def begin(u):
            own_copy(u).wait()
            transfer(u, 0).start()
            transfer(u, 1).start()

        def table_copies(u):
            return [
                local(
                    piece(u, r), table.at[pl.ds(r * rows, rows), pl.ds(0, unit_width(u))], s_table.at[r]
                )
                for r in range(size)
            ]

        def hop(j, source, target, to, send, recv):
            _, _, kind, index = where[j]
            return remote(
                source[kind].at[index], target[kind].at[index], send.at[j], recv.at[j], "context", to
            )

        def hop_in(j):
            return hop(j, mines, sums, inner, send_a, recv_a)

        def hop_across(j):
            return hop(j, mines, acrosses, across, send_b, recv_b)

        def hop_out(j):
            return hop(j, mines, sums, outer, send_a, recv_a)

        def staged(j, source, stage, n):
            _, _, kind, index = where[j]
            return local(
                source[kind].at[index], stage.at[j % 2, :, pl.ds(0, widths[kind])], s_stage.at[n, j % 2]
            )

        def keep(j):
            _, _, kind, index = where[j]
            return local(mines[kind].at[index], sums[kind].at[index], s_keep.at[j])

        def add_stage(j, stage):
            _, _, kind, index = where[j]
            mines[kind][index] = (
                mines[kind][index].astype(f32) + stage[j % 2, :, 0 : widths[kind]].astype(f32)
            ).astype(bf16)

        def line_step(j):
            if j < count:
                hop_in(j).wait_recv()
                staged(j, sums, stage_in, 0).start()
            if j >= 1:
                hop_across(j - 1).wait_recv()
                staged(j - 1, acrosses, stage_across, 1).start()
            if j < count:
                staged(j, sums, stage_in, 0).wait()
                add_stage(j, stage_in)
                hop_across(j).start()
            if j >= 1:
                staged(j - 1, acrosses, stage_across, 1).wait()
                hop_across(j - 1).wait_send()
                add_stage(j - 1, stage_across)
                hop_out(j - 1).start()
                keep(j - 1).start()

        of_unit = [[j for j in range(count) if where[j][0] == u] for u in range(units)]

        def gradients(u):
            transfer(u, 0).wait_recv()
            transfer(u, 2).start()
            transfer(u, 1).wait_recv()
            transfer(u, 2).wait_recv()
            start(table_copies(u))
            wait(table_copies(u))
            for j in of_unit[u]:
                _, spans, kind, index = where[j]
                filled = 0
                for which, at, w in spans:
                    mines[kind][index, :, filled : filled + w] = dot_nn(
                        feature_t[which], table[:, at : at + w]
                    ).astype(bf16)
                    filled += w

                @pl.when(jnp.logical_not(middle))
                def _(j=j):
                    if j >= 3:
                        hop_in(j - 3).wait_send()
                    hop_in(j).start()

        def line(u):
            @pl.when(middle)
            def _():
                for j in of_unit[u]:
                    line_step(j)

        def feed(k):
            if k >= 2:
                own_copy(k - 2).wait() if k - 2 >= begun[0] else None
            wait(weight_copies(k, 0))
            gate_w, up_w, down_w = (weights.at[:, pl.ds(n * width, width)] for n in range(3))
            gate = dot_nn(row_two[...], gate_w[...])
            wait(weight_copies(k, 1))
            up = dot_nn(row_two[...], up_w[...])
            wait(weight_copies(k, 2))
            d_active = dot_nn(row_fall[...], down_w[...])
            sigmoid = jax.nn.sigmoid(gate)
            swish = gate * sigmoid
            stage = acts_stage.at[k % 2]
            stage[:, 2 * width :] = (swish * up).astype(bf16)
            stage[:, :width] = (d_active * up * sigmoid * (1.0 + gate * (1.0 - sigmoid))).astype(bf16)
            stage[:, width : 2 * width] = (d_active * swish).astype(bf16)
            own_copy(k).start()
            d_part = contract_last(stage[:, :width], gate_w[...]) + contract_last(
                stage[:, width : 2 * width], up_w[...]
            )
            out_part = contract_last(stage[:, 2 * width :], down_w[...])
            if k == 0:
                d_sum[...] = d_part
                out_sum[...] = out_part
            else:
                d_sum[...] += d_part
                out_sum[...] += out_part
            if k + 1 < chunks:
                for which in range(3):
                    start(weight_copies(k + 1, which))
            else:
                start(side_copies())

        def swap(n):
            return remote(y_send.at[n], y_land.at[n], send_y.at[n], recv_y.at[n], "tensor", 1 - side)

        gain_one, gain_two = gains_ref[0:1, :], gains_ref[1:2, :]

        def mean_scale(field):
            return lax.rsqrt(jnp.mean(field * field, -1, keepdims=True) + EPSILON)

        spans_of_rows = [slice(n, n + part) for n in range(0, rows, part)]

        def row_valid(span):
            at = lax.broadcasted_iota(jnp.int32, (part, 1), 0) + (place * rows + span.start)
            return (at < length_ref[0]).astype(f32)

        def keep_gain(which, value):
            for r in range(size):
                at = pl.multiple_of(partner[r] * own_rows + which * features, 128)
                vec[:, pl.ds(at, own_rows)] = value[:, r * own_rows : (r + 1) * own_rows]

        wait(ins[0])
        for span in spans_of_rows:
            field = hidden_rel[span, :]
            row_two[span, :] = (field * mean_scale(field) * gain_two).astype(bf16)
        wait(ins[1])
        for span in spans_of_rows:
            row_fall[span, :] = (row_fall[span, :].astype(f32) * row_valid(span)).astype(bf16)
        pl.semaphore_wait(barrier, size - 1 + 3 + 1)
        for r in (2, 3, 1):
            for w in (0, 1):
                trade(w, r).start()
        begun = [0]

        feed(0)
        begin(0)
        begun[0] = 1
        feed(1)
        begin(1)
        begun[0] = 2
        wait(ins[2])
        for span in spans_of_rows:
            field = tokens_rel[span, :].astype(f32)
            row_normed[span, :] = (field * mean_scale(field) * gain_one).astype(bf16)
        turn_features(0)
        turn_features(1)
        feed(2)
        feed(3)
        gradients(0)
        begin(2)
        begin(3)
        begun[0] = 4
        feed(4)
        feed(5)
        line(0)
        gradients(1)
        begin(4)
        begun[0] = 5
        feed(6)
        y_send[0] = d_sum[...].astype(bf16)
        swap(0).start()
        y_send[1] = out_sum[...].astype(bf16)
        line(1)
        swap(1).start()
        for r in (2, 3, 1):
            trade(2, r).start()
        gradients(2)
        begin(5)
        swap(0).wait_recv()
        gain_sum = jnp.zeros((1, features), f32)
        for span in spans_of_rows:
            d_normed = y_send[0, span, :].astype(f32) + y_land[0, span, :].astype(f32)
            field = hidden_rel[span, :]
            r2 = mean_scale(field)
            gain_sum = gain_sum + jnp.sum(d_normed * field * r2, 0, keepdims=True)
            weighted = d_normed * gain_two
            d_hidden = (
                row_fall[span, :].astype(f32)
                + r2 * weighted
                - field * (r2 * r2 * r2) * jnp.mean(field * weighted, -1, keepdims=True)
            )
            d_sum[span, :] = d_hidden
            row_branch[span, :] = d_hidden.astype(bf16)
        keep_gain(1, gain_sum)
        for r in (2, 3, 1):
            trade(3, r).start()
        wait(side_copies())
        d_mixed[...] = dot_nn(row_branch[...], weights[:, 0:heads_width]).astype(bf16)
        line(2)
        gradients(3)
        begin(6)
        wait(rest)
        bias[...] = key_bias_table(place, length_ref[0], keys, rows)
        key_t[...] = pair_v[:, :HEAD_DIM].T
        for head in range(heads):
            at = slice(head * HEAD_DIM, (head + 1) * HEAD_DIM)
            scores = contract_last(pair_v[:, :HEAD_DIM], query_v[:, at]) * scale + bias[...]
            probs = jnp.exp(scores - lse_ref[head : head + 1, :])
            d_probs = contract_last(pair_v[:, HEAD_DIM:], d_mixed[:, at])
            inside = jnp.sum(d_probs * probs, 0, keepdims=True)
            d_scores = (probs * (d_probs - inside)).astype(bf16)
            d_query = (dot_nn(key_t[...], d_scores) * scale).T
            last_v[:, at] = turn(d_query, cos_ref[...], -sin_ref[...]).astype(bf16)
            more_key = dot_nn(d_scores, query_v[:, at])
            more_value = dot_nn(probs.astype(bf16), d_mixed[:, at])
            if head == 0:
                d_key[...] = more_key
                d_value[...] = more_value
            else:
                d_key[...] += more_key
                d_value[...] += more_value
        d_rest[:, :HEAD_DIM] = (d_key[rows:, :] * scale).astype(bf16)
        d_rest[:, HEAD_DIM:] = d_value[rows:, :].astype(bf16)

        def give(s):
            return remote(
                d_rest.at[pl.ds((s - 1) * rows, rows), :], d_land.at[s - 1], send_k.at[s - 1], recv_k.at[s - 1],
                "context", place - s,
            )

        for s in range(1, 4):
            pl.when(place >= s)(give(s).start)
        line(3)
        gradients(4)
        d_key[0:rows, :] = d_key[0:rows, :] * scale
        for s in range(1, 4):

            @pl.when(place + s <= 3)
            def _(s=s):
                give(s).wait_recv()
                d_key[0:rows, :] += d_land[s - 1, :, :HEAD_DIM].astype(f32)
                d_value[0:rows, :] += d_land[s - 1, :, HEAD_DIM:].astype(f32)

        last_v[:, heads_width : heads_width + HEAD_DIM] = turn(
            d_key[0:rows, :], cos_ref[...], -sin_ref[...]
        ).astype(bf16)
        last_v[:, heads_width + HEAD_DIM : projected] = d_value[0:rows, :].astype(bf16)
        own_copy(chunks).start()
        y_send[2] = contract_last(
            last_v[:, 0:projected], weights[:, heads_width : heads_width + projected]
        ).astype(bf16)
        swap(2).start()
        vec[:, 2 * features :] = jnp.sum(last_v[:, 0:projected].astype(f32), 0, keepdims=True)
        begin(chunks)
        turn_features(2)
        turn_features(3)
        swap(1).wait_recv()
        swap(1).wait_send()
        for span in spans_of_rows:
            whole = y_send[1, span, :].astype(f32) + y_land[1, span, :].astype(f32)
            y_land[1, span, :] = (row_valid(span) * (hidden_rel[span, :] + whole)).astype(bf16)

        def stored(n, target):
            return [
                local(y_land.at[n, :, cols(r)], target.at[:, block_of(r)], s_store.at[n, r]) for r in range(size)
            ]

        start(stored(1, output_hbm))
        line(4)
        gradients(5)
        swap(2).wait_recv()
        swap(2).wait_send()
        gain_sum = jnp.zeros((1, features), f32)
        for span in spans_of_rows:
            d_normed = y_send[2, span, :].astype(f32) + y_land[2, span, :].astype(f32)
            field = tokens_rel[span, :].astype(f32)
            r1 = mean_scale(field)
            gain_sum = gain_sum + jnp.sum(d_normed * field * r1, 0, keepdims=True)
            weighted = d_normed * gain_one
            y_land[2, span, :] = (
                d_sum[span, :]
                + r1 * weighted
                - field * (r1 * r1 * r1) * jnp.mean(field * weighted, -1, keepdims=True)
            ).astype(bf16)
        start(stored(2, grad_tokens_hbm))
        keep_gain(0, gain_sum)

        def share(r):
            return remote(vec, vec_land.at[me], send_v.at[r - 1], recv_v.at[r - 1], "dp", partner[r])

        def spread(s):
            return remote(
                vec, total_land.at[place], send_w.at[s - 1], recv_w.at[s - 1], "context", lax.rem(place + s, 4)
            )

        for r in range(1, size):
            share(r).start()
        vec_land[me] = vec[...]
        line(5)
        gradients(6)
        for r in range(1, size):
            share(r).wait()
        vec[...] = vec_land[0] + vec_land[1] + vec_land[2] + vec_land[3]
        for s in range(1, 4):
            spread(s).start()
        total_land[place] = vec[...]
        line(6)
        gradients(7)
        for s in range(1, 4):
            spread(s).wait()
        small_ref[...] = total_land[0] + total_land[1] + total_land[2] + total_land[3]
        line(7)

        @pl.when(middle)
        def _():
            line_step(count)
            for j in range(count):
                hop_out(j).wait_send()
                keep(j).wait()

        @pl.when(jnp.logical_not(middle))
        def _():
            for j in range(count - 3, count):
                hop_in(j).wait_send()
            for j in range(count):
                hop_out(j).wait_recv()

        wait(stored(1, output_hbm))
        wait(stored(2, grad_tokens_hbm))
        swap(0).wait_send()
        for s in range(1, 4):
            pl.when(place >= s)(give(s).wait_send)
        for w in range(4):
            for r in range(1, size):
                trade(w, r).wait_send()
        for u in range(units):
            for n in range(3):
                transfer(u, n).wait_send()

    dma = pltpu.SemaphoreType.DMA
    shape = jax.ShapeDtypeStruct
    wide, last = (3 * chunks, own_rows, width), (2, own_rows, halfway)
    results = pl.pallas_call(
        kernel,
        out_shape=(
            shape((rows, features), bf16),
            shape((rows, features), bf16),
            shape((1, small_width), f32),
            shape(wide, bf16),
            shape(last, bf16),
            shape((size - 1, units, rows, 3 * width), bf16),
            shape((units, rows, 3 * width), bf16),
            shape(wide, bf16),
            shape(last, bf16),
        ),
        in_specs=[SMEM, VMEM, VMEM, VMEM, VMEM] + [ANY] * (6 + 6 + 2 * chunks + 2 * size),
        out_specs=(ANY, ANY, VMEM) + (ANY,) * 6,
        scratch_shapes=[
            pltpu.VMEM(wide, bf16),
            pltpu.VMEM(last, bf16),
            pltpu.VMEM((2, own_rows, max(widths)), bf16),
            pltpu.VMEM((2, own_rows, max(widths)), bf16),
            pltpu.VMEM((tokens_all, 3 * width), bf16),
            pltpu.VMEM((features, 3 * width), bf16),
            pltpu.VMEM((4, own_rows, tokens_all), bf16),
            pltpu.VMEM((4, size - 1, rows, own_rows), bf16),
            pltpu.VMEM((rows, features), bf16),
            pltpu.VMEM((rows, features), bf16),
            pltpu.VMEM((rows, features), bf16),
            pltpu.VMEM((rows, features), bf16),
            pltpu.VMEM((rows, features), f32),
            pltpu.VMEM((rows, features), bf16),
            pltpu.VMEM((rows, features), f32),
            pltpu.VMEM((rows, features), f32),
            pltpu.VMEM((3, rows, features), bf16),
            pltpu.VMEM((3, rows, features), bf16),
            pltpu.VMEM((2, rows, 3 * width), bf16),
            pltpu.VMEM((rows, heads_width), bf16),
            pltpu.VMEM((keys, pair_width), bf16),
            pltpu.VMEM((rows, last_width), bf16),
            pltpu.VMEM((keys, rows), f32),
            pltpu.VMEM((HEAD_DIM, keys), bf16),
            pltpu.VMEM((keys, HEAD_DIM), f32),
            pltpu.VMEM((keys, HEAD_DIM), f32),
            pltpu.VMEM((rows, heads_width), bf16),
            pltpu.VMEM((keys - rows, pair_width), bf16),
            pltpu.VMEM((3, rows, pair_width), bf16),
            pltpu.VMEM((1, small_width), f32),
            pltpu.VMEM((4, 1, small_width), f32),
            pltpu.VMEM((4, 1, small_width), f32),
            dma((3, size)),
            dma((3, size)),
            dma((units,)),
            dma((3,)),
            dma((3, units)),
            dma((3, units)),
            dma((count,)),
            dma((count,)),
            dma((count,)),
            dma((count,)),
            dma((2, 2)),
            dma((count,)),
            dma((size,)),
            dma((4, size - 1)),
            dma((4, size - 1)),
            dma((3,)),
            dma((3,)),
            dma((3,)),
            dma((3,)),
            dma((size - 1,)),
            dma((size - 1,)),
            dma((3,)),
            dma((3,)),
            dma((3, size)),
        ],
        compiler_params=pltpu.CompilerParams(
            collective_id=0, has_side_effects=True, vmem_limit_bytes=60 << 20
        ),
        name="layer_back",
    )(
        length, gains, lse, cosine, sine, hidden, tokens, grad_out, query, pair, mixed,
        *feed_own, *feed_near, *far_flat, *out_pieces, *pair_pieces,
    )
    return results[:5]


def chunk_edges(columns):
    tiles = columns // 128
    count = next((n for n in (7, 5, 4, 6, 3, 2) if tiles % n == 0), 1)
    width = columns // count
    return [(n * width, width) for n in range(count)]


def local(
    tokens,
    lengths,
    gain_one,
    w_query,
    b_query,
    key_weight,
    key_bias,
    value_weight,
    value_bias,
    w_out,
    gain_two,
    w_gate,
    w_up,
    w_down,
    grad_out,
):
    bf16, f32 = jnp.bfloat16, jnp.float32
    seq_count, block_len, model_width = tokens.shape
    row_count = seq_count * block_len
    query_cols = w_query.shape[1]
    key_cols = key_weight.shape[1]
    unit_cols = w_gate.shape[1]
    own_rows = w_query.shape[0]
    head_count = query_cols // HEAD_DIM
    kv_count = key_cols // HEAD_DIM
    query_group_width = head_count // kv_count
    size = lax.axis_size("dp")
    me = lax.axis_index("dp")
    blocks_along = lax.axis_size("context")
    place = lax.axis_index("context")
    parity = place % 2 if blocks_along % 2 == 0 and own_rows % 32 == 0 else None

    def relative(field):
        return swap_blocks([field[:, n * own_rows : (n + 1) * own_rows] for n in range(size)], me)

    def absolute(blocks):
        return jnp.concatenate(swap_blocks(blocks, me), 1)

    def dot_rows(blocks, weights):
        return jnp.dot(
            jnp.concatenate(blocks, 1), jnp.concatenate(weights, 0), preferred_element_type=f32
        )

    lanes = {name: Lane() for name in ("x", "z", "hop1", "hop2", "hop3")}
    attention_weights = gather_pieces(
        jnp.concatenate([w_query, key_weight, value_weight], 1), size, lanes
    )
    out_weights = gather_pieces(w_out, size, lanes, parity)
    edges = chunk_edges(unit_cols)
    feed_weights = []
    mega = (
        size == 4
        and blocks_along == 4
        and lax.axis_size("tensor") == 2
        and own_rows % 128 == 0
        and row_count % 64 == 0
        and len(set(w for _, w in edges)) == 1
        and kv_count == 1
        and seq_count == 1
    )
    early = len(edges) if mega else len(edges) - 2

    feed_own = (w_gate, w_up, w_down)
    feed_near = tuple(lax.ppermute(w, "dp", xor_pairs(size, 1)) for w in feed_own)

    def fetch(start, width):
        own = jnp.concatenate([w[:, start : start + width] for w in feed_own], 1)
        far = far_pieces(own, size, lanes, parity)
        sources = []
        for r in range(size):
            if r < 2:
                sources.append(feed_own if r == 0 else feed_near)
            elif r % 2 == 0:
                sources.append((far[r],))
            else:
                sources.append((lax.ppermute(far[r - 1], "dp", xor_pairs(size, 1)),))
        feed_weights.append(sources)

    for start, width in edges[:early]:
        fetch(start, width)

    positions = place * block_len + jnp.arange(block_len, dtype=jnp.int32)
    position_count = block_len * blocks_along
    valid_rows = (positions[None, :] < lengths[:, None]).astype(f32).reshape(row_count, 1)
    facts = jnp.stack([place.astype(jnp.int32), lengths[0]])
    half = HEAD_DIM // 2
    inverse = jnp.exp(jnp.arange(half, dtype=f32) * (-2.0 * math.log(ROPE_BASE) / HEAD_DIM))
    angles = positions.astype(f32)[:, None] * inverse[None, :]
    cosine = jnp.concatenate([jnp.cos(angles)] * 2, 1)
    sine = jnp.concatenate([-jnp.sin(angles), jnp.sin(angles)], 1)
    gain_first = gain_one.astype(f32)
    gain_second = gain_two.astype(f32)
    inputs = tokens.reshape(row_count, model_width).astype(f32)
    scale_one = lax.rsqrt(jnp.mean(inputs * inputs, -1, keepdims=True) + EPSILON)
    normalized_input = (inputs * scale_one * gain_first).astype(bf16)
    normed_blocks = relative(normalized_input)
    projected = dot_rows(normed_blocks, attention_weights) + jnp.concatenate(
        [b_query, key_bias, value_bias]
    ).astype(f32)
    turned = query_cols + key_cols

    def turn_heads(field, sine_rows):
        grid = field.reshape(row_count, field.shape[1] // HEAD_DIM, HEAD_DIM)
        swapped = jnp.concatenate([grid[..., half:], grid[..., :half]], -1)
        grid = grid * cosine[:, None, :] + swapped * sine_rows[:, None, :]
        return grid.reshape(field.shape).astype(bf16)

    turned_rows = turn_heads(projected[:, :turned], sine)
    query_rot = turned_rows[:, :query_cols]
    pair_rows = jnp.concatenate([turned_rows[:, query_cols:], projected[:, turned:].astype(bf16)], 1)
    pair_all = [pair_rows]
    for shift in range(1, blocks_along):
        pair_all.append(
            lax.ppermute(
                pair_rows, "context", [(n, n + shift) for n in range(blocks_along - shift)]
            )
        )
    pair_all = jnp.concatenate(pair_all, 0)
    mixed_heads, lse = attend(facts, query_rot, pair_all)
    full_out = jnp.concatenate(out_weights, 0)
    branch = contract_last(mixed_heads, full_out)
    branch = absolute([branch[:, r * own_rows : (r + 1) * own_rows] for r in range(size)])
    hidden = inputs + tensor_sum(branch)
    scale_two = lax.rsqrt(jnp.mean(hidden * hidden, -1, keepdims=True) + EPSILON)
    if mega:
        gains = jnp.concatenate(
            [jnp.concatenate(relative(g[None, :]), 1) for g in (gain_first, gain_second)], 0
        )
        output, grad_tokens, small, feed_sums, last_sums = layer_back(
            lengths,
            hidden,
            tokens.reshape(row_count, model_width),
            grad_out.reshape(row_count, model_width),
            gains,
            feed_own,
            feed_near,
            [(sources[2][0], sources[3][0]) for sources in feed_weights],
            out_weights,
            attention_weights,
            query_rot,
            pair_all,
            lse,
            mixed_heads,
            cosine,
            sine,
        )
        small = small[0]
        feed_grads = [
            jnp.concatenate([feed_sums[3 * n + w].astype(f32) for n in range(len(edges))], 1)
            for w in range(3)
        ]
        last_grad = jnp.concatenate([last_sums[0], last_sums[1]], 1).astype(f32)
        turned_at = query_cols + key_cols
        at = 2 * model_width
        return (
            output.reshape(seq_count, block_len, model_width),
            grad_tokens.reshape(seq_count, block_len, model_width),
            small[:model_width],
            last_grad[:, :query_cols],
            small[at : at + query_cols],
            last_grad[:, query_cols:turned_at],
            small[at + query_cols : at + turned_at],
            last_grad[:, turned_at : turned_at + key_cols],
            small[at + turned_at :],
            last_grad[:, turned_at + key_cols :],
            small[model_width:at],
            *feed_grads,
        )
    normed_two = (hidden * scale_two * gain_second).astype(bf16)
    fall_grad = grad_out.reshape(row_count, model_width).astype(f32) * valid_rows
    fall_low = fall_grad.astype(bf16)
    fall_blocks = relative(fall_low)
    two_blocks = relative(normed_two)
    traded_early = trade_blocks(
        [jnp.concatenate([a, b], 1) for a, b in zip(normed_blocks, fall_blocks)], size
    )
    traded_early = jnp.concatenate(traded_early, 0).T
    normed_features, fall_features = traded_early[:own_rows], traded_early[own_rows:]
    two_features = jnp.concatenate(trade_blocks(two_blocks, size), 0).T
    two_row = jnp.concatenate(two_blocks, 1)
    fall_row = jnp.concatenate(fall_blocks, 1)

    feed_out, d_normed_two = None, None
    feed_units = []
    for turn_at, (start, width) in enumerate(edges):
        acts, d_normed_two, feed_out = feed_chunk(
            two_row, fall_row, feed_weights[turn_at], start, width, d_normed_two, feed_out
        )
        if turn_at < 0:
            acts = gather_pieces(acts, size, lanes)
        feed_units.append(acts)
        if turn_at == 0:
            for edge in edges[early:]:
                fetch(*edge)

    def split(field):
        return [field[:, r * own_rows : (r + 1) * own_rows] for r in range(size)]

    d_normed_two = tensor_sum(absolute(split(d_normed_two)))
    result = valid_rows * (hidden + tensor_sum(absolute(split(feed_out))))
    output = result.astype(bf16).reshape(seq_count, block_len, model_width)
    gain_two_grad = jnp.sum(d_normed_two * hidden * scale_two, 0)
    d_hidden = fall_grad + norm_back(hidden, scale_two, gain_second, d_normed_two)
    d_branch = d_hidden.astype(bf16)
    branch_blocks = relative(d_branch)
    branch_features = jnp.concatenate(trade_blocks(branch_blocks, size), 0).T
    d_mixed = jnp.dot(
        jnp.concatenate(branch_blocks, 1), full_out, preferred_element_type=f32
    ).astype(bf16)
    d_query_low, d_own, d_rest = attend_back(
        facts, query_rot, pair_all, lse, d_mixed, cosine, sine
    )
    for shift in range(1, blocks_along):
        d_own = d_own + lax.ppermute(
            d_rest[(shift - 1) * block_len : shift * block_len],
            "context",
            [(n, n - shift) for n in range(shift, blocks_along)],
        ).astype(f32)
    d_key_low = turn_heads(d_own[:, :key_cols], -sine)
    d_value_low = d_own[:, key_cols:].astype(bf16)
    d_projected = jnp.concatenate([d_query_low, d_key_low, d_value_low], 1)
    d_normed = contract_last(d_projected, jnp.concatenate(attention_weights, 0))
    d_normed = tensor_sum(absolute(split(d_normed)))
    gain_one_grad = jnp.sum(d_normed * inputs * scale_one, 0)
    d_inputs = d_hidden + norm_back(inputs, scale_one, gain_first, d_normed)
    grad_tokens = d_inputs.astype(bf16).reshape(seq_count, block_len, model_width)
    gain_two_grad = small_total(gain_two_grad)
    small = small_total(
        jnp.concatenate([gain_one_grad, jnp.sum(d_projected.astype(f32), 0)])
    )
    projected_width = d_projected.shape[1]
    last = jnp.concatenate([d_projected, mixed_heads], 1)
    halfway = last.shape[1] // 2
    blocks = [
        [[(0, 0, width)], [(0, width, width)], [(1, 2 * width, width)]] for _, width in edges
    ] + [
        [
            [(2, 0, halfway)],
            [(2, halfway, projected_width - halfway), (3, projected_width, query_cols)],
        ]
    ]
    sums = gather_and_sum(
        feed_units + [last],
        [two_features, fall_features, normed_features, branch_features],
        blocks,
        size,
    )

    def columns(which):
        stack = sums[which][0]
        return jnp.concatenate(
            [stack[3 * n + which].astype(f32) for n in range(len(edges))], 1
        )

    stack = sums[-1][0]
    last_grad = jnp.concatenate([stack[0], stack[1]], 1).astype(f32)
    projected_grad, out_grad = last_grad[:, :projected_width], last_grad[:, projected_width:]

    low, high = model_width + query_cols, model_width + query_cols + key_cols
    return (
        output,
        grad_tokens,
        small[:model_width],
        projected_grad[:, :query_cols],
        small[model_width:low],
        projected_grad[:, query_cols : query_cols + key_cols],
        small[low:high],
        projected_grad[:, query_cols + key_cols :],
        small[high:],
        out_grad,
        gain_two_grad,
        columns(0),
        columns(1),
        columns(2),
    )


def solution(mesh):
    in_specs = (
        P("dp", "context", None),
        P("dp"),
        P(),
        P("dp", "tensor"),
        P("tensor"),
        P("dp", "tensor"),
        P("tensor"),
        P("dp", "tensor"),
        P("tensor"),
        P("dp", "tensor"),
        P(),
        P("dp", "tensor"),
        P("dp", "tensor"),
        P("dp", "tensor"),
        P("dp", "context", None),
    )
    out_specs = (
        P("dp", "context", None),
        P("dp", "context", None),
        P(),
        P("dp", "tensor"),
        P("tensor"),
        P("dp", "tensor"),
        P("tensor"),
        P("dp", "tensor"),
        P("tensor"),
        P("dp", "tensor"),
        P(),
        P("dp", "tensor"),
        P("dp", "tensor"),
        P("dp", "tensor"),
    )
    return jax.shard_map(local, mesh=mesh, in_specs=in_specs, out_specs=out_specs, check_vma=False)
```

```python
import math

import jax
import jax.numpy as jnp
import numpy as np
from jax import lax
from jax.experimental import pallas as pl
from jax.experimental.pallas import tpu as pltpu
from jax.sharding import PartitionSpec as P

HEAD_DIM = 128


EPSILON = 1e-06
ROPE_BASE = 1000000.0


def xor_pairs(size, mask):
    return [(i, i ^ mask) for i in range(size)]


class Lane:
    def __init__(self, depth=1):
        self.sent = []
        self.depth = depth

    def send(self, array, axis, pairs):
        if len(self.sent) >= self.depth:
            array, _ = lax.optimization_barrier((array, self.sent[-self.depth]))
        got = lax.ppermute(array, axis, pairs)
        self.sent.append(got)
        return got


def far_masks(size):
    masks, mask = [], 2
    while mask < size:
        masks.append(mask)
        mask *= 2
    return masks


def swap_blocks(blocks, me):
    mask = 1
    while mask < len(blocks):
        flag = (me & mask) != 0
        blocks = [jnp.where(flag, blocks[r ^ mask], blocks[r]) for r in range(len(blocks))]
        mask *= 2
    return blocks


def far_half(piece, mask, size, parity, lanes):
    half = piece.shape[0] // 2
    sent = lax.dynamic_slice_in_dim(piece, half * parity, half, 0)
    straight = lanes["x"].send(sent, "dp", xor_pairs(size, mask))
    other = lanes["z"].send(straight, "context", xor_pairs(lax.axis_size("context"), 1))
    first = jnp.where(parity == 0, straight, other)
    second = jnp.where(parity == 0, other, straight)
    return jnp.concatenate([first, second], 0)


def far_pieces(own, size, lanes, parity=None):
    pieces = {0: own}
    for mask in far_masks(size):
        for r in list(pieces):
            if parity is None:
                pieces[r ^ mask] = lanes["x"].send(pieces[r], "dp", xor_pairs(size, mask))
            else:
                pieces[r ^ mask] = far_half(pieces[r], mask, size, parity, lanes)
    return pieces


def gather_pieces(own, size, lanes, parity=None):
    pieces = far_pieces(own, size, lanes, parity)
    for r in list(pieces):
        pieces[r ^ 1] = lax.ppermute(pieces[r], "dp", xor_pairs(size, 1))
    return [pieces[r] for r in range(size)]


def trade_blocks(blocks, size):
    return [blocks[0]] + [
        lax.ppermute(blocks[r], "dp", xor_pairs(size, r)) for r in range(1, size)
    ]


def tensor_sum(part):
    sent = part.astype(jnp.bfloat16)
    size = lax.axis_size("tensor")
    if size == 2:
        other = lax.ppermute(sent, "tensor", [(0, 1), (1, 0)])
        return sent.astype(jnp.float32) + other.astype(jnp.float32)
    return lax.psum(part, "tensor")


def line_sum(part, lanes):
    place = lax.axis_index("context")
    if lax.axis_size("context") != 4:
        return lax.psum(part.astype(jnp.float32), "context")
    got = lanes["hop1"].send(part, "context", [(0, 1), (3, 2)])
    pair = (part.astype(jnp.float32) + got.astype(jnp.float32)).astype(jnp.bfloat16)
    got = lanes["hop2"].send(pair, "context", [(1, 2), (2, 1)])
    total = (pair.astype(jnp.float32) + got.astype(jnp.float32)).astype(jnp.bfloat16)
    got = lanes["hop3"].send(total, "context", [(1, 0), (2, 3)])
    ends = (place == 0) | (place == 3)
    return jnp.where(ends, got, total).astype(jnp.float32)


def small_total(vector):
    for axis in ("dp", "context"):
        size, mask = lax.axis_size(axis), 1
        while mask < size:
            vector = vector + lax.ppermute(vector, axis, xor_pairs(size, mask))
            mask *= 2
    return vector


def contract_last(left, right):
    return lax.dot_general(
        left, right, (((1,), (1,)), ((), ())), preferred_element_type=jnp.float32
    )


def norm_back(field, scale_rows, gain, d_normed):
    weighted = d_normed * gain
    cubed = scale_rows * scale_rows * scale_rows
    return scale_rows * weighted - field * cubed * jnp.mean(field * weighted, -1, keepdims=True)


ANY = pl.BlockSpec(memory_space=pl.ANY)
VMEM = pl.BlockSpec(memory_space=pltpu.VMEM)
SMEM = pl.BlockSpec(memory_space=pltpu.SMEM)


def plain_params(limit):
    return pltpu.CompilerParams(vmem_limit_bytes=limit)


def dot_nn(left, right):
    return jnp.dot(left, right, preferred_element_type=jnp.float32)


def feed_chunk(two_row, fall_row, sources, start, width, d_sum, out_sum):
    rows, features = two_row.shape
    bf16, f32 = jnp.bfloat16, jnp.float32
    flat, layout = [], []
    for source in sources:
        layout.append(len(source))
        flat.extend(source)
    first = d_sum is None
    held = [] if first else [d_sum, out_sum]

    def kernel(*refs):
        refs = list(refs)
        two_ref, fall_ref = refs[:2]
        given = refs[2 : 2 + len(flat)]
        at = 2 + len(flat)
        sums = refs[at : at + len(held)]
        at += len(held)
        acts_ref, d_ref, out_ref, gate_w, up_w, down_w, sems = refs[at:]
        copies = [[], [], []]
        place, taken = 0, 0
        for kind in layout:
            depth = given[taken].shape[0]
            for which, scratch in enumerate((gate_w, up_w, down_w)):
                if kind == 3:
                    view = given[taken + which].at[:, pl.ds(start, width)]
                else:
                    view = given[taken].at[:, pl.ds(which * width, width)]
                copy = pltpu.make_async_copy(
                    view,
                    scratch.at[pl.ds(place, depth), :],
                    sems.at[which, len(copies[which])],
                )
                copies[which].append(copy)
            place += depth
            taken += kind
        for group in copies:
            for copy in group:
                copy.start()
        for copy in copies[0]:
            copy.wait()
        gate = dot_nn(two_ref[...], gate_w[...])
        for copy in copies[1]:
            copy.wait()
        up = dot_nn(two_ref[...], up_w[...])
        for copy in copies[2]:
            copy.wait()
        d_active = dot_nn(fall_ref[...], down_w[...])
        sigmoid = jax.nn.sigmoid(gate)
        swish = gate * sigmoid
        acts_ref[:, 2 * width :] = (swish * up).astype(bf16)
        acts_ref[:, :width] = (d_active * up * sigmoid * (1.0 + gate * (1.0 - sigmoid))).astype(bf16)
        acts_ref[:, width : 2 * width] = (d_active * swish).astype(bf16)
        d_part = contract_last(acts_ref[:, :width], gate_w[...]) + contract_last(
            acts_ref[:, width : 2 * width], up_w[...]
        )
        out_part = contract_last(acts_ref[:, 2 * width :], down_w[...])
        if first:
            d_ref[...] = d_part
            out_ref[...] = out_part
        else:
            d_ref[...] = sums[0][...] + d_part
            out_ref[...] = sums[1][...] + out_part

    weight_bytes = 6 * features * width
    return pl.pallas_call(
        kernel,
        out_shape=(
            jax.ShapeDtypeStruct((rows, 3 * width), bf16),
            jax.ShapeDtypeStruct((rows, features), f32),
            jax.ShapeDtypeStruct((rows, features), f32),
        ),
        in_specs=[VMEM, VMEM] + [ANY] * len(flat) + [VMEM] * len(held),
        out_specs=(VMEM, VMEM, VMEM),
        scratch_shapes=[pltpu.VMEM((features, width), bf16)] * 3
        + [pltpu.SemaphoreType.DMA((3, len(sources)))],
        compiler_params=plain_params(40 << 20),
        cost_estimate=pl.CostEstimate(
            flops=12 * rows * features * width,
            bytes_accessed=weight_bytes + 20 * rows * features + 6 * rows * width,
            transcendentals=rows * width,
        ),
        name="feed_chunk",
    )(two_row, fall_row, *flat, *held)


def grad_block(features, pieces, spans):
    bf16 = jnp.bfloat16
    depth, columns = pieces[0].shape
    tokens = features[0].shape[1]
    own = features[0].shape[0]
    total = sum(w for _, w in spans)

    def kernel(*refs):
        refs = list(refs)
        feature_refs = refs[: len(features)]
        given = refs[len(features) : len(features) + len(pieces)]
        out_ref, held, sems = refs[len(features) + len(pieces) :]
        copies = [
            pltpu.make_async_copy(ref, held.at[pl.ds(n * depth, depth), :], sems.at[n])
            for n, ref in enumerate(given)
        ]
        for copy in copies:
            copy.start()
        for copy in copies:
            copy.wait()
        for ref, (start, width) in zip(feature_refs, spans):
            out_ref[:, start : start + width] = dot_nn(
                ref[...], held[:, start : start + width]
            ).astype(bf16)

    return pl.pallas_call(
        kernel,
        out_shape=jax.ShapeDtypeStruct((own, total), bf16),
        in_specs=[VMEM] * len(features) + [ANY] * len(pieces),
        out_specs=VMEM,
        scratch_shapes=[
            pltpu.VMEM((tokens, columns), bf16),
            pltpu.SemaphoreType.DMA((len(pieces),)),
        ],
        compiler_params=plain_params(40 << 20),
        cost_estimate=pl.CostEstimate(
            flops=2 * own * tokens * total,
            bytes_accessed=2 * (tokens * columns + own * total + own * tokens),
            transcendentals=0,
        ),
        name="grad_block",
    )(*features, *pieces)


def key_bias_table(place, length, keys, block_len):
    key_at = lax.broadcasted_iota(jnp.int32, (keys, block_len), 0)
    query_at = lax.broadcasted_iota(jnp.int32, (keys, block_len), 1) + place * block_len
    shift = key_at // block_len
    key_at = key_at - shift * block_len + (place - shift) * block_len
    seen = (key_at <= query_at) & (key_at < length) & (key_at >= 0)
    return jnp.where(seen, 0.0, -1e30).astype(jnp.float32)


def attend(facts, query, pair):
    rows, width = query.shape
    keys = pair.shape[0]
    heads = width // HEAD_DIM
    bf16, f32 = jnp.bfloat16, jnp.float32
    scale = 1.0 / math.sqrt(HEAD_DIM)

    def kernel(facts_ref, query_ref, pair_ref, mixed_ref, lse_ref, bias, value_t):
        bias[...] = key_bias_table(facts_ref[0], facts_ref[1], keys, rows)
        value_t[...] = pair_ref[:, HEAD_DIM:].T
        lse_ref[...] = jnp.zeros_like(lse_ref)
        for head in range(heads):
            cols = slice(head * HEAD_DIM, (head + 1) * HEAD_DIM)
            scores = contract_last(pair_ref[:, :HEAD_DIM], query_ref[:, cols]) * scale + bias[...]
            top = jnp.max(scores, 0, keepdims=True)
            raised = jnp.exp(scores - top)
            total = jnp.sum(raised, 0, keepdims=True)
            lse_ref[head : head + 1, :] = top + jnp.log(total)
            probs = (raised * (1.0 / total)).astype(bf16)
            mixed_ref[:, cols] = dot_nn(value_t[...], probs).T.astype(bf16)

    return pl.pallas_call(
        kernel,
        out_shape=(
            jax.ShapeDtypeStruct((rows, width), bf16),
            jax.ShapeDtypeStruct((8, rows), f32),
        ),
        in_specs=[SMEM, VMEM, VMEM],
        out_specs=(VMEM, VMEM),
        scratch_shapes=[pltpu.VMEM((keys, rows), f32), pltpu.VMEM((HEAD_DIM, keys), bf16)],
        compiler_params=plain_params(40 << 20),
        cost_estimate=pl.CostEstimate(
            flops=4 * rows * keys * width + 12 * heads * rows * keys * 100,
            bytes_accessed=4 * rows * width + 4 * keys * HEAD_DIM,
            transcendentals=heads * rows * keys,
        ),
        name="attend",
    )(facts, query, pair)


def turn(field, cosine, sine):
    return field * cosine + pltpu.roll(field, HEAD_DIM // 2, 1) * sine


def attend_back(facts, query, pair, lse, d_mixed, cosine, sine):
    rows, width = query.shape
    keys = pair.shape[0]
    heads = width // HEAD_DIM
    bf16, f32 = jnp.bfloat16, jnp.float32
    scale = 1.0 / math.sqrt(HEAD_DIM)

    def kernel(facts_ref, query_ref, pair_ref, lse_ref, d_mixed_ref, cos_ref, sin_ref, d_query_ref, d_own_ref, d_rest_ref, bias, key_t, d_key, d_value):
        bias[...] = key_bias_table(facts_ref[0], facts_ref[1], keys, rows)
        key_t[...] = pair_ref[:, :HEAD_DIM].T
        for head in range(heads):
            cols = slice(head * HEAD_DIM, (head + 1) * HEAD_DIM)
            scores = contract_last(pair_ref[:, :HEAD_DIM], query_ref[:, cols]) * scale + bias[...]
            probs = jnp.exp(scores - lse_ref[head : head + 1, :])
            d_probs = contract_last(pair_ref[:, HEAD_DIM:], d_mixed_ref[:, cols])
            inner = jnp.sum(d_probs * probs, 0, keepdims=True)
            d_scores = (probs * (d_probs - inner)).astype(bf16)
            d_query = (dot_nn(key_t[...], d_scores) * scale).T
            d_query_ref[:, cols] = turn(d_query, cos_ref[...], -sin_ref[...]).astype(bf16)
            more_key = dot_nn(d_scores, query_ref[:, cols])
            more_value = dot_nn(probs.astype(bf16), d_mixed_ref[:, cols])
            if head == 0:
                d_key[...] = more_key
                d_value[...] = more_value
            else:
                d_key[...] += more_key
                d_value[...] += more_value
        d_own_ref[:, :HEAD_DIM] = d_key[:rows, :] * scale
        d_own_ref[:, HEAD_DIM:] = d_value[:rows, :]
        d_rest_ref[:, :HEAD_DIM] = (d_key[rows:, :] * scale).astype(bf16)
        d_rest_ref[:, HEAD_DIM:] = d_value[rows:, :].astype(bf16)

    return pl.pallas_call(
        kernel,
        out_shape=(
            jax.ShapeDtypeStruct((rows, width), bf16),
            jax.ShapeDtypeStruct((rows, 2 * HEAD_DIM), f32),
            jax.ShapeDtypeStruct((keys - rows, 2 * HEAD_DIM), bf16),
        ),
        in_specs=[SMEM] + [VMEM] * 6,
        out_specs=(VMEM, VMEM, VMEM),
        scratch_shapes=[
            pltpu.VMEM((keys, rows), f32),
            pltpu.VMEM((HEAD_DIM, keys), bf16),
            pltpu.VMEM((keys, HEAD_DIM), f32),
            pltpu.VMEM((keys, HEAD_DIM), f32),
        ],
        compiler_params=plain_params(40 << 20),
        cost_estimate=pl.CostEstimate(
            flops=10 * rows * keys * width + 12 * heads * rows * keys * 200,
            bytes_accessed=8 * rows * width + 8 * keys * HEAD_DIM,
            transcendentals=heads * rows * keys,
        ),
        name="attend_back",
    )(facts, query, pair, lse, d_mixed, cosine, sine)


MESH = pl.DeviceIdType.MESH


def flipped(index, mask):
    return index + mask - 2 * mask * ((index // mask) % 2)


def gather_and_sum(units, features, blocks, size):
    bf16, f32 = jnp.bfloat16, jnp.float32
    count = len(units)
    gathered = [isinstance(u, (list, tuple)) for u in units]
    flat = [a for u in units for a in (u if isinstance(u, (list, tuple)) else [u])]
    starts, at = [], 0
    for u in units:
        starts.append(at)
        at += len(u) if isinstance(u, (list, tuple)) else 1
    rows = flat[0].shape[0]
    widest = max(a.shape[1] for a in flat)
    own_rows, tokens = features[0].shape
    widths = []
    where = []
    counts = {}
    for u, group in enumerate(blocks):
        for spans in group:
            width = sum(w for _, _, w in spans)
            if width not in counts:
                counts[width] = 0
                widths.append(width)
            where.append((u, spans, widths.index(width), counts[width]))
            counts[width] += 1
    block_count = len(where)
    steps = []
    held = [0]
    for mask in far_masks(size):
        for r in list(held):
            steps.append((r, mask))
            held.append(r ^ mask)
    for r in list(held):
        steps.append((r, 1))
    arrival = {r ^ mask: n for n, (r, mask) in enumerate(steps)}
    ahead = 2

    def kernel(*refs):
        refs = list(refs)
        unit_refs, refs = refs[: len(flat)], refs[len(flat) :]
        feature_refs, refs = refs[: len(features)], refs[len(features) :]
        outs, refs = refs[: len(widths)], refs[len(widths) :]
        land, refs = refs[0], refs[1:]
        mine, refs = refs[: len(widths)], refs[len(widths) :]
        first, refs = refs[: len(widths)], refs[len(widths) :]
        second, refs = refs[: len(widths)], refs[len(widths) :]
        table, send_g, recv_g, send_a, recv_a, send_b, recv_b, load, store = refs
        me = lax.axis_index("dp")
        place = lax.axis_index("context")
        middle = place * (3 - place) == 2
        inner = 1 + place // 2
        across = 3 - place
        outer = 3 * (place - 1)

        barrier = pltpu.get_barrier_semaphore()
        partners = sorted(set(mask for _, mask in steps))
        for mask in partners:
            pl.semaphore_signal(barrier, 1, device_id={"dp": flipped(me, mask)}, device_id_type=MESH)

        @pl.when(middle)
        def _():
            pl.semaphore_signal(barrier, 1, device_id={"context": across}, device_id_type=MESH)
            pl.semaphore_signal(barrier, 1, device_id={"context": outer}, device_id_type=MESH)
            pl.semaphore_wait(barrier, len(partners) + 2)

        @pl.when(jnp.logical_not(middle))
        def _():
            pl.semaphore_signal(barrier, 1, device_id={"context": inner}, device_id_type=MESH)
            pl.semaphore_wait(barrier, len(partners) + 1)

        def piece(u, r):
            if gathered[u]:
                return unit_refs[starts[u] + r]
            if r == 0:
                return unit_refs[starts[u]]
            return land.at[r - 1, u, :, pl.ds(0, flat[starts[u]].shape[1])]

        def transfer(u, n):
            r, mask = steps[n]
            target = r ^ mask
            return pltpu.make_async_remote_copy(
                src_ref=piece(u, r),
                dst_ref=land.at[target - 1, u, :, pl.ds(0, flat[starts[u]].shape[1])],
                send_sem=send_g.at[n, u],
                recv_sem=recv_g.at[n, u],
                device_id={"dp": flipped(me, mask)},
                device_id_type=MESH,
            )

        wanted = [u for u in range(count) if not gathered[u]]

        def begin(u):
            for n, (r, _) in enumerate(steps):
                if r == 0:
                    transfer(u, n).start()

        def loads(u, slot):
            width = flat[starts[u]].shape[1]
            return [
                pltpu.make_async_copy(
                    piece(u, r),
                    table.at[slot, pl.ds(r * rows, rows), pl.ds(0, width)],
                    load.at[slot, r],
                )
                for r in range(size)
            ]

        def forward(u):
            waited = set()
            for n, (r, mask) in enumerate(steps):
                if r != 0:
                    if r not in waited:
                        transfer(u, arrival[r]).wait_recv()
                        waited.add(r)
                    transfer(u, n).start()
            for r in range(1, size):
                if r not in waited:
                    transfer(u, arrival[r]).wait_recv()

        def hop(j, source, target, place_to, send, recv):
            _, _, kind, index = where[j]
            return pltpu.make_async_remote_copy(
                src_ref=source[kind].at[index],
                dst_ref=target[kind].at[index],
                send_sem=send.at[j],
                recv_sem=recv.at[j],
                device_id={"context": place_to},
                device_id_type=MESH,
            )

        def hop_in(j):
            return hop(j, mine, first, inner, send_a, recv_a)

        def hop_across(j):
            return hop(j, mine, second, across, send_b, recv_b)

        def hop_out(j):
            return hop(j, first, first, outer, send_a, recv_a)

        def keep(j):
            _, _, kind, index = where[j]
            return pltpu.make_async_copy(first[kind].at[index], outs[kind].at[index], store.at[j])

        def total_in(j):
            _, _, kind, index = where[j]
            hop_in(j).wait_recv()
            mine[kind][index] = (
                mine[kind][index].astype(f32) + first[kind][index].astype(f32)
            ).astype(bf16)
            hop_across(j).start()

        def total_across(j):
            _, _, kind, index = where[j]
            hop_across(j).wait_recv()
            first[kind][index] = (
                mine[kind][index].astype(f32) + second[kind][index].astype(f32)
            ).astype(bf16)
            hop_out(j).start()
            keep(j).start()

        of_unit = [[j for j in range(block_count) if where[j][0] == u] for u in range(count)]
        for u in wanted[:ahead]:
            begin(u)
        for copy in loads(0, 0) if gathered[0] else []:
            copy.start()
        middle_in = []
        for u in range(count):
            slot = u % 2
            if not gathered[u]:
                forward(u)
                later = [v for v in wanted if v > u]
                if len(later) >= ahead:
                    begin(later[ahead - 1])
            if not (u == 0 and gathered[0]):
                for copy in loads(u, slot):
                    copy.start()
            for copy in loads(u, slot):
                copy.wait()
            for j in of_unit[u]:
                _, spans, kind, index = where[j]
                filled = 0
                for which, start, width in spans:
                    mine[kind][index, :, filled : filled + width] = dot_nn(
                        feature_refs[which][...], table[slot, :, start : start + width]
                    ).astype(bf16)
                    filled += width

                @pl.when(jnp.logical_not(middle))
                def _(j=j):
                    if j >= 3:
                        hop_in(j - 3).wait_send()
                    hop_in(j).start()

            if u >= 1:

                @pl.when(middle)
                def _(u=u):
                    for j in of_unit[u - 1]:
                        total_in(j)
                        if j >= 1:
                            total_across(j - 1)

        @pl.when(middle)
        def _():
            for j in of_unit[count - 1]:
                total_in(j)
                total_across(j - 1)
            total_across(block_count - 1)
            for j in range(block_count):
                hop_across(j).wait_send()
                hop_out(j).wait_send()
                keep(j).wait()

        @pl.when(jnp.logical_not(middle))
        def _():
            for j in range(max(block_count - 3, 0), block_count):
                hop_in(j).wait_send()
            for j in range(block_count):
                hop_out(j).wait_recv()
                keep(j).start()
            for j in range(block_count):
                keep(j).wait()

        for u in wanted:
            for n in range(len(steps)):
                transfer(u, n).wait_send()

    def stacks(kind_memory):
        return [kind_memory((counts[w], own_rows, w), bf16) for w in widths]

    columns = sum(counts[w] * w for w in widths)
    results = pl.pallas_call(
        kernel,
        out_shape=[jax.ShapeDtypeStruct((counts[w], own_rows, w), bf16) for w in widths]
        + [jax.ShapeDtypeStruct((size - 1, count, rows, widest), bf16)],
        in_specs=[ANY] * len(flat) + [VMEM] * len(features),
        out_specs=[ANY] * (len(widths) + 1),
        scratch_shapes=stacks(pltpu.VMEM) * 3
        + [
            pltpu.VMEM((2, tokens, widest), bf16),
            pltpu.SemaphoreType.DMA((len(steps), count)),
            pltpu.SemaphoreType.DMA((len(steps), count)),
            pltpu.SemaphoreType.DMA((block_count,)),
            pltpu.SemaphoreType.DMA((block_count,)),
            pltpu.SemaphoreType.DMA((block_count,)),
            pltpu.SemaphoreType.DMA((block_count,)),
            pltpu.SemaphoreType.DMA((2, size)),
            pltpu.SemaphoreType.DMA((block_count,)),
        ],
        compiler_params=pltpu.CompilerParams(
            collective_id=0, has_side_effects=True, vmem_limit_bytes=60 << 20
        ),
        cost_estimate=pl.CostEstimate(
            flops=2 * own_rows * tokens * columns,
            bytes_accessed=2 * tokens * columns + 12 * own_rows * columns,
            transcendentals=0,
        ),
        name="gather_and_sum",
    )(*flat, *features)
    return [(results[kind], index) for _, _, kind, index in where]


def layer(
    length, tokens, grad_out, gains, biases, tables, attention_own, feed_own, width, parts_of_x,
):
    bf16, f32 = jnp.bfloat16, jnp.float32
    rows, features = tokens.shape
    own_rows, units_all = feed_own[0].shape
    chunks = units_all // width
    heads_width = attention_own[0].shape[1]
    heads = heads_width // HEAD_DIM
    keys = tables.shape[1]
    pair_width = attention_own[1].shape[1] + attention_own[2].shape[1]
    projected = heads_width + pair_width
    last_width = projected + heads_width
    halfway = last_width // 2
    size = features // own_rows
    units = chunks + 1
    tokens_all = size * rows
    small_width = 2 * features + projected
    scale = 1.0 / math.sqrt(HEAD_DIM)
    part = 64
    where = []
    for k in range(chunks):
        where.append((k, [(0, 0, width)], 0, 3 * k))
        where.append((k, [(0, width, width)], 0, 3 * k + 1))
        where.append((k, [(1, 2 * width, width)], 0, 3 * k + 2))
    where.append((chunks, [(2, 0, halfway)], 1, 0))
    where.append(
        (chunks, [(2, halfway, projected - halfway), (3, projected, heads_width)], 1, 1)
    )
    count = len(where)
    widths = (width, halfway)
    attention_width = projected + heads_width
    attention_spans = []
    for array in attention_own:
        attention_spans.append((sum(w for _, w in attention_spans), array.shape[1]))

    def kernel(*refs):
        refs = list(refs)

        def take(n):
            taken = refs[:n]
            del refs[:n]
            return taken

        (length_ref, gains_ref, biases_ref) = take(3)
        (tokens_hbm, grad_hbm, tables_hbm) = take(3)
        attention_hbm, own_hbm = take(4), take(3)
        output_hbm, grad_tokens_hbm, small_ref, sum_wide, sum_last, land, acts_hbm, across_wide, across_last = take(9)
        attention_land, near_land, far_land = take(3)
        (mine_wide, mine_last, stage_in, stage_across, table, weights, feature_t, feature_land) = take(8)
        (row_two, row_fall, row_normed, row_branch, hidden_rel, tokens_rel, d_sum, out_sum) = take(8)
        (y_send, y_land, acts_stage, query_v, pair_v, last_v, bias, key_t, d_key, d_value) = take(10)
        (d_mixed, d_rest, d_land, vec, vec_land, total_land) = take(6)
        (gains_v, tables_v, lse_ref) = take(3)
        (s_in, s_weights, s_acts, s_rest, send_g, recv_g, send_a, recv_a, send_b, recv_b) = take(10)
        (s_stage, s_keep, s_table, send_t, recv_t, send_y, recv_y, send_k, recv_k) = take(9)
        (send_v, recv_v, send_w, recv_w, s_store) = take(5)
        (send_m, recv_m, send_near, recv_near, send_x, recv_x, send_z, recv_z, send_c, recv_c, send_p, recv_p) = take(12)
        (s_attention,) = take(1)
        cos_ref, sin_ref = tables_v.at[0], tables_v.at[1]
        sums, mines, acrosses = (sum_wide, sum_last), (mine_wide, mine_last), (across_wide, across_last)
        rows_of = (row_two, row_fall, row_normed, row_branch)

        me = lax.axis_index("dp")
        place = lax.axis_index("context")
        side = lax.axis_index("tensor")
        middle = place * (3 - place) == 2
        inner = 1 + place // 2
        across = 3 - place
        outer = 3 * (place - 1)
        one = flipped(me, 1)
        partner = (me, one, flipped(me, 2), flipped(one, 2))
        parity = lax.rem(place, 2)
        beside = flipped(place, 1)

        barrier = pltpu.get_barrier_semaphore()
        for r in range(1, size):
            pl.semaphore_signal(barrier, 1, device_id={"dp": partner[r]}, device_id_type=MESH)
        for s in range(1, 4):
            pl.semaphore_signal(barrier, 1, device_id={"context": lax.rem(place + s, 4)}, device_id_type=MESH)
        pl.semaphore_signal(barrier, 1, device_id={"tensor": 1 - side}, device_id_type=MESH)

        def block_of(r):
            return pl.ds(pl.multiple_of(partner[r] * own_rows, 128), own_rows)

        def local(source, target, sem):
            return pltpu.make_async_copy(source, target, sem)

        def remote(source, target, send, recv, axis, index):
            return pltpu.make_async_remote_copy(
                src_ref=source, dst_ref=target, send_sem=send, recv_sem=recv,
                device_id={axis: index}, device_id_type=MESH,
            )

        def cols(r):
            return pl.ds(r * own_rows, own_rows)

        ins = []
        for n, (source, target) in enumerate(((tokens_hbm, tokens_rel), (grad_hbm, row_fall))):
            ins.append(
                [local(source.at[:, block_of(r)], target.at[:, cols(r)], s_in.at[n, r]) for r in range(size)]
            )
        rest = [
            local(tables_hbm.at[:, pl.ds(pl.multiple_of(place * rows, rows), rows), :], tables_v, s_rest.at[0])
        ]

        attention_parts = ((0, 3, 0, projected), (3, 4, projected, heads_width))

        def attention_send(n):
            first, last, at, _ = attention_parts[n % 2]
            if n >= 4:
                attention_wait(n).start()
                return
            for m in range(first, last):
                at, wide = attention_spans[m]
                remote(
                    attention_hbm[m], attention_land.at[1 if n < 2 else 0, :, pl.ds(at, wide)],
                    send_m.at[n], recv_m.at[n], "dp", partner[2 if n < 2 else 1],
                ).start()

        def attention_wait(n):
            _, _, at, wide = attention_parts[n % 2]
            source = attention_land.at[1, :, pl.ds(at, wide)]
            target = attention_land.at[(1, 0, 2)[n // 2], :, pl.ds(at, wide)]
            return remote(source, target, send_m.at[n], recv_m.at[n], "dp", partner[2 if n < 2 else 1])

        def attention_copies(n):
            first, last, at, wide = attention_parts[n]
            return [
                local(
                    attention_hbm[m],
                    weights.at[pl.ds(0, own_rows), pl.ds(attention_spans[m][0], attention_spans[m][1])],
                    s_attention.at[m],
                )
                for m in range(first, last)
            ] + [
                local(
                    attention_land.at[r - 1, :, pl.ds(at, wide)],
                    weights.at[pl.ds(r * own_rows, own_rows), pl.ds(at, wide)],
                    s_weights.at[n, r],
                )
                for r in range(1, size)
            ]

        def near(which):
            return remote(
                own_hbm[which], near_land.at[which], send_near.at[which], recv_near.at[which], "dp", partner[1]
            )

        def straight_rows(k):
            wide = own_rows * parts_of_x[k] // 6
            return pl.ds(pl.multiple_of((own_rows - wide) * parity, 64), wide)

        def round_rows(k):
            short = own_rows - own_rows * parts_of_x[k] // 6
            return pl.ds(pl.multiple_of((own_rows - short) * parity, 64), short)

        def far_send(k):
            for which in range(3):
                remote(
                    own_hbm[which].at[straight_rows(k), pl.ds(k * width, width)],
                    far_land.at[0, k, straight_rows(k), pl.ds(which * width, width)],
                    send_x.at[k], recv_x.at[k], "dp", partner[2],
                ).start()

        def far_wait(k):
            view = far_land.at[0, k, straight_rows(k), :]
            return remote(view, view, send_x.at[k], recv_x.at[k], "dp", partner[2])

        def far_round(k):
            view = far_land.at[0, k, round_rows(k), :]
            return remote(view, view, send_z.at[k], recv_z.at[k], "context", beside)

        def missing_rows(k):
            short = own_rows - own_rows * parts_of_x[k] // 6
            return pl.ds(pl.multiple_of((own_rows - short) * (1 - parity), 64), short)

        def far_round_wait(k):
            view = far_land.at[0, k, missing_rows(k), :]
            return remote(view, view, send_z.at[k], recv_z.at[k], "context", beside)

        def far_near(k):
            return remote(far_land.at[0, k], far_land.at[1, k], send_c.at[k], recv_c.at[k], "dp", partner[1])

        def weight_straight(k):
            far_wait(k).wait_recv()
            if parts_of_x[k] < 6:
                far_round(k).start()
            else:
                far_near(k).start()

        def weight_round(k):
            if parts_of_x[k] < 6:
                far_round_wait(k).wait_recv()
                far_near(k).start()

        def weight_copies(k, which):
            view = pl.ds(which * width, width)
            sources = [
                own_hbm[which].at[:, pl.ds(k * width, width)],
                near_land.at[which, :, pl.ds(k * width, width)],
                far_land.at[0, k, :, view],
                far_land.at[1, k, :, view],
            ]
            return [
                local(source, weights.at[pl.ds(r * own_rows, own_rows), view], s_weights.at[which, r])
                for r, source in enumerate(sources)
            ]

        def start(copies):
            for copy in copies:
                copy.start()

        def wait(copies):
            for copy in copies:
                copy.wait()

        for copies in ins:
            start(copies)
        start(rest)

        def trade(w, r):
            return remote(
                rows_of[w].at[:, cols(r)], feature_land.at[w, r - 1], send_t.at[w, r - 1], recv_t.at[w, r - 1],
                "dp", partner[r],
            )

        def turn_features(w):
            feature_t[w, :, 0:rows] = rows_of[w][:, 0:own_rows].T
            for r in range(1, size):
                trade(w, r).wait_recv()
                feature_t[w, :, r * rows : (r + 1) * rows] = feature_land[w, r - 1].T

        steps = ((0, 2), (0, 1), (2, 1))

        def unit_width(u):
            return 3 * width if u < chunks else last_width

        def piece(u, r):
            view = pl.ds(0, unit_width(u))
            return acts_hbm.at[u, :, view] if r == 0 else land.at[r - 1, u, :, view]

        def transfer(u, n):
            r, mask = steps[n]
            return remote(
                piece(u, r), land.at[(r ^ mask) - 1, u, :, pl.ds(0, unit_width(u))],
                send_g.at[n, u], recv_g.at[n, u], "dp", partner[mask],
            )

        def own_copy(u):
            if u < chunks:
                return local(acts_stage.at[u % 2], piece(u, 0), s_acts.at[u])
            return local(last_v, piece(u, 0), s_acts.at[u])

        def begin(u):
            own_copy(u).wait()
            transfer(u, 0).start()
            transfer(u, 1).start()

        def table_copies(u):
            return [
                local(
                    piece(u, r), table.at[pl.ds(r * rows, rows), pl.ds(0, unit_width(u))], s_table.at[r]
                )
                for r in range(size)
            ]

        def hop(j, source, target, to, send, recv):
            _, _, kind, index = where[j]
            return remote(
                source[kind].at[index], target[kind].at[index], send.at[j], recv.at[j], "context", to
            )

        def hop_in(j):
            return hop(j, mines, sums, inner, send_a, recv_a)

        def hop_across(j):
            return hop(j, mines, acrosses, across, send_b, recv_b)

        def hop_out(j):
            return hop(j, mines, sums, outer, send_a, recv_a)

        def staged(j, source, stage, n):
            _, _, kind, index = where[j]
            return local(
                source[kind].at[index], stage.at[j % 2, :, pl.ds(0, widths[kind])], s_stage.at[n, j % 2]
            )

        def keep(j):
            _, _, kind, index = where[j]
            return local(mines[kind].at[index], sums[kind].at[index], s_keep.at[j])

        def add_stage(j, stage):
            _, _, kind, index = where[j]
            mines[kind][index] = (
                mines[kind][index].astype(f32) + stage[j % 2, :, 0 : widths[kind]].astype(f32)
            ).astype(bf16)

        def line_step(j):
            if j < count:
                hop_in(j).wait_recv()
                staged(j, sums, stage_in, 0).start()
            if j >= 1:
                hop_across(j - 1).wait_recv()
                staged(j - 1, acrosses, stage_across, 1).start()
            if j < count:
                staged(j, sums, stage_in, 0).wait()
                add_stage(j, stage_in)
                hop_across(j).start()
            if j >= 1:
                staged(j - 1, acrosses, stage_across, 1).wait()
                hop_across(j - 1).wait_send()
                add_stage(j - 1, stage_across)
                hop_out(j - 1).start()
                keep(j - 1).start()

        of_unit = [[j for j in range(count) if where[j][0] == u] for u in range(units)]

        def gradients(u):
            transfer(u, 0).wait_recv()
            transfer(u, 2).start()
            transfer(u, 1).wait_recv()
            transfer(u, 2).wait_recv()
            start(table_copies(u))
            wait(table_copies(u))
            for j in of_unit[u]:
                _, spans, kind, index = where[j]
                filled = 0
                for which, at, w in spans:
                    mines[kind][index, :, filled : filled + w] = dot_nn(
                        feature_t[which], table[:, at : at + w]
                    ).astype(bf16)
                    filled += w

                @pl.when(jnp.logical_not(middle))
                def _(j=j):
                    if j >= 3:
                        hop_in(j - 3).wait_send()
                    hop_in(j).start()

        def line(u):
            @pl.when(middle)
            def _():
                for j in of_unit[u]:
                    line_step(j)

        def feed(k):
            far_near(k).wait_recv()
            for which in range(3):
                if k == 0:
                    near(which).wait_recv()
                start(weight_copies(k, which))
            wait(weight_copies(k, 0))
            gate_w, up_w, down_w = (weights.at[:, pl.ds(n * width, width)] for n in range(3))
            gate = dot_nn(row_two[...], gate_w[...])
            wait(weight_copies(k, 1))
            up = dot_nn(row_two[...], up_w[...])
            wait(weight_copies(k, 2))
            d_active = dot_nn(row_fall[...], down_w[...])
            sigmoid = jax.nn.sigmoid(gate)
            swish = gate * sigmoid
            stage = acts_stage.at[k % 2]
            stage[:, 2 * width :] = (swish * up).astype(bf16)
            stage[:, :width] = (d_active * up * sigmoid * (1.0 + gate * (1.0 - sigmoid))).astype(bf16)
            stage[:, width : 2 * width] = (d_active * swish).astype(bf16)
            own_copy(k).start()
            d_part = contract_last(stage[:, :width], gate_w[...]) + contract_last(
                stage[:, width : 2 * width], up_w[...]
            )
            out_part = contract_last(stage[:, 2 * width :], down_w[...])
            if k == 0:
                d_sum[...] = d_part
                out_sum[...] = out_part
            else:
                d_sum[...] += d_part
                out_sum[...] += out_part

        def swap(n):
            return remote(y_send.at[n], y_land.at[n], send_y.at[n], recv_y.at[n], "tensor", 1 - side)

        for r in range(size):
            gains_v[:, r * own_rows : (r + 1) * own_rows] = gains_ref[:, block_of(r)]
        gain_one, gain_two = gains_v[0:1, :], gains_v[1:2, :]

        def mean_scale(field):
            return lax.rsqrt(jnp.mean(field * field, -1, keepdims=True) + EPSILON)

        spans_of_rows = [slice(n, n + part) for n in range(0, rows, part)]

        def row_valid(span):
            at = lax.broadcasted_iota(jnp.int32, (part, 1), 0) + (place * rows + span.start)
            return (at < length_ref[0]).astype(f32)

        def keep_gain(which, value):
            for r in range(size):
                at = pl.multiple_of(partner[r] * own_rows + which * features, 128)
                vec[:, pl.ds(at, own_rows)] = value[:, r * own_rows : (r + 1) * own_rows]

        wait(ins[0])
        for span in spans_of_rows:
            field = tokens_rel[span, :].astype(f32)
            row_normed[span, :] = (field * mean_scale(field) * gain_one).astype(bf16)
        pl.semaphore_wait(barrier, size - 1 + 3 + 1)
        attention_send(0)
        attention_send(2)
        wait(ins[1])
        for span in spans_of_rows:
            row_fall[span, :] = (row_fall[span, :].astype(f32) * row_valid(span)).astype(bf16)
        bias[...] = key_bias_table(place, length_ref[0], keys, rows)
        attention_send(1)
        attention_send(3)
        attention_wait(0).wait_recv()
        attention_send(4)
        far_send(0)
        near(0).start()
        attention_wait(2).wait_recv()
        attention_wait(4).wait_recv()
        start(attention_copies(0))
        wait(rest)
        wait(attention_copies(0))
        queries = dot_nn(row_normed[...], weights[:, 0:heads_width]) + biases_ref[:, 0:heads_width]
        for head in range(heads):
            at = slice(head * HEAD_DIM, (head + 1) * HEAD_DIM)
            query_v[:, at] = turn(queries[:, at], cos_ref[...], sin_ref[...]).astype(bf16)
        others = dot_nn(row_normed[...], weights[:, heads_width:projected]) + biases_ref[:, heads_width:projected]
        pair_v[0:rows, :HEAD_DIM] = turn(others[:, :HEAD_DIM], cos_ref[...], sin_ref[...]).astype(bf16)
        pair_v[0:rows, HEAD_DIM:] = others[:, HEAD_DIM:].astype(bf16)

        def lend(s):
            return remote(
                pair_v.at[pl.ds(0, rows), :], pair_v.at[pl.ds(s * rows, rows), :], send_p.at[s - 1], recv_p.at[s - 1],
                "context", place + s,
            )

        for s in range(1, 4):
            pl.when(place + s <= 3)(lend(s).start)

            @pl.when(place < s)
            def _(s=s):
                pair_v[s * rows : (s + 1) * rows, :] = jnp.zeros((rows, pair_width), bf16)

        attention_wait(1).wait_recv()
        attention_send(5)
        for r in (2, 3, 1):
            trade(1, r).start()
        near(1).start()
        near(2).start()
        for s in range(1, 4):
            pl.when(place >= s)(lend(s).wait_recv)
        key_t[...] = pair_v[:, HEAD_DIM:].T
        for head in range(heads):
            at = slice(head * HEAD_DIM, (head + 1) * HEAD_DIM)
            scores = contract_last(pair_v[:, :HEAD_DIM], query_v[:, at]) * scale + bias[...]
            top = jnp.max(scores, 0, keepdims=True)
            raised = jnp.exp(scores - top)
            total = jnp.sum(raised, 0, keepdims=True)
            lse_ref[head : head + 1, :] = top + jnp.log(total)
            probs = (raised * (1.0 / total)).astype(bf16)
            mixed_at = slice(projected + head * HEAD_DIM, projected + (head + 1) * HEAD_DIM)
            last_v[:, mixed_at] = dot_nn(key_t[...], probs).T.astype(bf16)
        attention_wait(3).wait_recv()
        attention_wait(5).wait_recv()
        start(attention_copies(1))
        wait(attention_copies(1))
        y_send[3] = contract_last(last_v[:, projected:], weights[:, projected:attention_width]).astype(bf16)
        swap(3).start()
        weight_straight(0)
        far_send(1)
        swap(3).wait_recv()
        for span in spans_of_rows:
            field = tokens_rel[span, :].astype(f32) + (
                y_send[3, span, :].astype(f32) + y_land[3, span, :].astype(f32)
            )
            hidden_rel[span, :] = field
            row_two[span, :] = (field * mean_scale(field) * gain_two).astype(bf16)
        for r in (2, 3, 1):
            trade(0, r).start()
        weight_round(0)
        feed(0)
        begin(0)
        far_send(2)
        weight_straight(1)
        turn_features(1)
        weight_round(1)
        turn_features(0)
        feed(1)
        begin(1)
        far_send(3)
        gradients(0)

        def line_step_at(j):
            pl.when(middle)(lambda: line_step(j))

        for k in range(2, chunks):
            weight_straight(k)
            line_step_at(3 * (k - 2))
            weight_round(k)
            line_step_at(3 * (k - 2) + 1)
            feed(k)
            begin(k)
            if k + 2 < chunks:
                far_send(k + 2)
            if k == chunks - 1:
                y_send[0] = d_sum[...].astype(bf16)
                swap(0).start()
                start(attention_copies(0) + attention_copies(1))
                for r in (2, 3, 1):
                    trade(2, r).start()
            line_step_at(3 * (k - 2) + 2)
            gradients(k - 1)
        at_block = 3 * (chunks - 2)
        y_send[1] = out_sum[...].astype(bf16)
        swap(0).wait_recv()
        swap(1).start()
        gain_sum = jnp.zeros((1, features), f32)
        for span in spans_of_rows:
            d_normed = y_send[0, span, :].astype(f32) + y_land[0, span, :].astype(f32)
            field = hidden_rel[span, :]
            r2 = mean_scale(field)
            gain_sum = gain_sum + jnp.sum(d_normed * field * r2, 0, keepdims=True)
            weighted = d_normed * gain_two
            d_hidden = (
                row_fall[span, :].astype(f32)
                + r2 * weighted
                - field * (r2 * r2 * r2) * jnp.mean(field * weighted, -1, keepdims=True)
            )
            d_sum[span, :] = d_hidden
            row_branch[span, :] = d_hidden.astype(bf16)
        keep_gain(1, gain_sum)
        for r in (2, 3, 1):
            trade(3, r).start()
        wait(attention_copies(0) + attention_copies(1))
        d_mixed[...] = dot_nn(row_branch[...], weights[:, projected:attention_width]).astype(bf16)
        line_step_at(at_block)
        key_t[...] = pair_v[:, :HEAD_DIM].T
        for head in range(heads):
            at = slice(head * HEAD_DIM, (head + 1) * HEAD_DIM)
            scores = contract_last(pair_v[:, :HEAD_DIM], query_v[:, at]) * scale + bias[...]
            probs = jnp.exp(scores - lse_ref[head : head + 1, :])
            d_probs = contract_last(pair_v[:, HEAD_DIM:], d_mixed[:, at])
            inside = jnp.sum(d_probs * probs, 0, keepdims=True)
            d_scores = (probs * (d_probs - inside)).astype(bf16)
            d_query = (dot_nn(key_t[...], d_scores) * scale).T
            last_v[:, at] = turn(d_query, cos_ref[...], -sin_ref[...]).astype(bf16)
            more_key = dot_nn(d_scores, query_v[:, at])
            more_value = dot_nn(probs.astype(bf16), d_mixed[:, at])
            if head == 0:
                d_key[...] = more_key
                d_value[...] = more_value
            else:
                d_key[...] += more_key
                d_value[...] += more_value
        d_rest[:, :HEAD_DIM] = (d_key[rows:, :] * scale).astype(bf16)
        d_rest[:, HEAD_DIM:] = d_value[rows:, :].astype(bf16)

        def give(s):
            return remote(
                d_rest.at[pl.ds((s - 1) * rows, rows), :], d_land.at[s - 1], send_k.at[s - 1], recv_k.at[s - 1],
                "context", place - s,
            )

        for s in range(1, 4):
            pl.when(place >= s)(give(s).start)
        line_step_at(at_block + 1)
        d_key[0:rows, :] = d_key[0:rows, :] * scale
        gradients(chunks - 1)
        for s in range(1, 4):

            @pl.when(place + s <= 3)
            def _(s=s):
                give(s).wait_recv()
                d_key[0:rows, :] += d_land[s - 1, :, :HEAD_DIM].astype(f32)
                d_value[0:rows, :] += d_land[s - 1, :, HEAD_DIM:].astype(f32)

        last_v[:, heads_width : heads_width + HEAD_DIM] = turn(
            d_key[0:rows, :], cos_ref[...], -sin_ref[...]
        ).astype(bf16)
        last_v[:, heads_width + HEAD_DIM : projected] = d_value[0:rows, :].astype(bf16)
        own_copy(chunks).start()
        begin(chunks)
        line_step_at(at_block + 2)
        y_send[2] = contract_last(last_v[:, 0:projected], weights[:, 0:projected]).astype(bf16)
        swap(2).start()
        vec[:, 2 * features :] = jnp.sum(last_v[:, 0:projected].astype(f32), 0, keepdims=True)
        line_step_at(at_block + 3)
        turn_features(2)
        turn_features(3)
        swap(1).wait_recv()
        swap(1).wait_send()
        for span in spans_of_rows:
            whole = y_send[1, span, :].astype(f32) + y_land[1, span, :].astype(f32)
            y_land[1, span, :] = (row_valid(span) * (hidden_rel[span, :] + whole)).astype(bf16)

        def stored(n, target):
            return [
                local(y_land.at[n, :, cols(r)], target.at[:, block_of(r)], s_store.at[n, r]) for r in range(size)
            ]

        start(stored(1, output_hbm))
        line_step_at(at_block + 4)
        gradients(chunks)
        line_step_at(at_block + 5)
        swap(2).wait_recv()
        swap(2).wait_send()
        gain_sum = jnp.zeros((1, features), f32)
        for span in spans_of_rows:
            d_normed = y_send[2, span, :].astype(f32) + y_land[2, span, :].astype(f32)
            field = tokens_rel[span, :].astype(f32)
            r1 = mean_scale(field)
            gain_sum = gain_sum + jnp.sum(d_normed * field * r1, 0, keepdims=True)
            weighted = d_normed * gain_one
            y_land[2, span, :] = (
                d_sum[span, :]
                + r1 * weighted
                - field * (r1 * r1 * r1) * jnp.mean(field * weighted, -1, keepdims=True)
            ).astype(bf16)
        start(stored(2, grad_tokens_hbm))
        keep_gain(0, gain_sum)

        def share(r):
            return remote(vec, vec_land.at[me], send_v.at[r - 1], recv_v.at[r - 1], "dp", partner[r])

        def spread(s):
            return remote(
                vec, total_land.at[place], send_w.at[s - 1], recv_w.at[s - 1], "context", lax.rem(place + s, 4)
            )

        for r in range(1, size):
            share(r).start()
        vec_land[me] = vec[...]
        for r in range(1, size):
            share(r).wait()
        vec[...] = vec_land[0] + vec_land[1] + vec_land[2] + vec_land[3]
        for s in range(1, 4):
            spread(s).start()
        total_land[place] = vec[...]
        line_step_at(at_block + 6)
        line_step_at(at_block + 7)
        line_step_at(at_block + 8)
        for s in range(1, 4):
            spread(s).wait()
        small_ref[...] = total_land[0] + total_land[1] + total_land[2] + total_land[3]

        @pl.when(middle)
        def _():
            for j in range(count):
                hop_out(j).wait_send()
                keep(j).wait()

        @pl.when(jnp.logical_not(middle))
        def _():
            for j in range(count - 3, count):
                hop_in(j).wait_send()
            for j in range(count):
                hop_out(j).wait_recv()

        wait(stored(1, output_hbm))
        wait(stored(2, grad_tokens_hbm))
        swap(0).wait_send()
        swap(3).wait_send()
        for n in range(6):
            attention_wait(n).wait_send()
        for which in range(3):
            near(which).wait_send()
        for k in range(chunks):
            far_wait(k).wait_send()
            if parts_of_x[k] < 6:
                far_round(k).wait_send()
            far_near(k).wait_send()
        for s in range(1, 4):
            pl.when(place >= s)(give(s).wait_send)
            pl.when(place + s <= 3)(lend(s).wait_send)
        for w in range(4):
            for r in range(1, size):
                trade(w, r).wait_send()
        for u in range(units):
            for n in range(3):
                transfer(u, n).wait_send()

    dma = pltpu.SemaphoreType.DMA
    shape = jax.ShapeDtypeStruct
    wide, last = (3 * chunks, own_rows, width), (2, own_rows, halfway)
    results = pl.pallas_call(
        kernel,
        out_shape=(
            shape((rows, features), bf16),
            shape((rows, features), bf16),
            shape((1, small_width), f32),
            shape(wide, bf16),
            shape(last, bf16),
            shape((size - 1, units, rows, 3 * width), bf16),
            shape((units, rows, 3 * width), bf16),
            shape(wide, bf16),
            shape(last, bf16),
            shape((size - 1, own_rows, attention_width), bf16),
            shape((3, own_rows, units_all), bf16),
            shape((2, chunks, own_rows, 3 * width), bf16),
        ),
        in_specs=[SMEM, VMEM, VMEM] + [ANY] * (3 + 4 + 3),
        out_specs=(ANY, ANY, VMEM) + (ANY,) * 9,
        scratch_shapes=[
            pltpu.VMEM(wide, bf16),
            pltpu.VMEM(last, bf16),
            pltpu.VMEM((2, own_rows, max(widths)), bf16),
            pltpu.VMEM((2, own_rows, max(widths)), bf16),
            pltpu.VMEM((tokens_all, 3 * width), bf16),
            pltpu.VMEM((features, 3 * width), bf16),
            pltpu.VMEM((4, own_rows, tokens_all), bf16),
            pltpu.VMEM((4, size - 1, rows, own_rows), bf16),
            pltpu.VMEM((rows, features), bf16),
            pltpu.VMEM((rows, features), bf16),
            pltpu.VMEM((rows, features), bf16),
            pltpu.VMEM((rows, features), bf16),
            pltpu.VMEM((rows, features), f32),
            pltpu.VMEM((rows, features), bf16),
            pltpu.VMEM((rows, features), f32),
            pltpu.VMEM((rows, features), f32),
            pltpu.VMEM((4, rows, features), bf16),
            pltpu.VMEM((4, rows, features), bf16),
            pltpu.VMEM((2, rows, 3 * width), bf16),
            pltpu.VMEM((rows, heads_width), bf16),
            pltpu.VMEM((keys, pair_width), bf16),
            pltpu.VMEM((rows, last_width), bf16),
            pltpu.VMEM((keys, rows), f32),
            pltpu.VMEM((HEAD_DIM, keys), bf16),
            pltpu.VMEM((keys, HEAD_DIM), f32),
            pltpu.VMEM((keys, HEAD_DIM), f32),
            pltpu.VMEM((rows, heads_width), bf16),
            pltpu.VMEM((keys - rows, pair_width), bf16),
            pltpu.VMEM((3, rows, pair_width), bf16),
            pltpu.VMEM((1, small_width), f32),
            pltpu.VMEM((4, 1, small_width), f32),
            pltpu.VMEM((4, 1, small_width), f32),
            pltpu.VMEM((2, features), f32),
            pltpu.VMEM((2, rows, HEAD_DIM), f32),
            pltpu.VMEM((8, rows), f32),
            dma((2, size)),
            dma((3, size)),
            dma((units,)),
            dma((1,)),
            dma((3, units)),
            dma((3, units)),
            dma((count,)),
            dma((count,)),
            dma((count,)),
            dma((count,)),
            dma((2, 2)),
            dma((count,)),
            dma((size,)),
            dma((4, size - 1)),
            dma((4, size - 1)),
            dma((4,)),
            dma((4,)),
            dma((3,)),
            dma((3,)),
            dma((size - 1,)),
            dma((size - 1,)),
            dma((3,)),
            dma((3,)),
            dma((3, size)),
            dma((6,)),
            dma((6,)),
            dma((3,)),
            dma((3,)),
            dma((chunks,)),
            dma((chunks,)),
            dma((chunks,)),
            dma((chunks,)),
            dma((chunks,)),
            dma((chunks,)),
            dma((3,)),
            dma((3,)),
            dma((4,)),
        ],
        compiler_params=pltpu.CompilerParams(
            collective_id=0, has_side_effects=True, vmem_limit_bytes=60 << 20
        ),
        name="layer",
    )(
        length, gains, biases, tokens, grad_out, tables, *attention_own, *feed_own,
    )
    return results[:5]


def finish(wide, last, output, grad_tokens, spans):
    blocks, own_rows, width = wide.shape
    halfway = last.shape[2]
    chunks = blocks // 3
    f32 = jnp.float32

    def kernel(wide_ref, last_ref, output_ref, tokens_ref, *outs):
        for n in range(3):
            outs[n][...] = wide_ref[n].astype(f32)

        @pl.when(pl.program_id(0) == 0)
        def _():
            for (start, size), out in zip(spans, outs[3:-2]):
                done = 0
                while done < size:
                    half, at = divmod(start + done, halfway)
                    step = min(size - done, halfway - at)
                    out[:, done : done + step] = last_ref[half, :, at : at + step].astype(f32)
                    done += step
            outs[-2][...] = output_ref[...]
            outs[-1][...] = tokens_ref[...]

    def whole(shape):
        return pl.BlockSpec(shape, lambda k: (0,) * len(shape))

    shape = jax.ShapeDtypeStruct
    return pl.pallas_call(
        kernel,
        grid=(chunks,),
        out_shape=[shape((own_rows, chunks * width), f32)] * 3
        + [shape((own_rows, size), f32) for _, size in spans]
        + [shape(output.shape, output.dtype)] * 2,
        in_specs=[
            pl.BlockSpec((3, own_rows, width), lambda k: (k, 0, 0)),
            whole(last.shape),
            whole(output.shape),
            whole(output.shape),
        ],
        out_specs=[pl.BlockSpec((own_rows, width), lambda k: (0, k))] * 3
        + [whole((own_rows, size)) for _, size in spans]
        + [whole(output.shape)] * 2,
        compiler_params=plain_params(48 << 20),
        name="finish",
    )(wide, last, output, grad_tokens)


def rotary_tables(position_count):
    half = HEAD_DIM // 2
    inverse = np.exp(np.arange(half) * (-2.0 * math.log(ROPE_BASE) / HEAD_DIM))
    angles = np.arange(position_count)[:, None] * inverse[None, :]
    cosine, sine = np.cos(angles), np.sin(angles)
    return np.stack(
        [np.concatenate([cosine, cosine], 1), np.concatenate([-sine, sine], 1)]
    ).astype(np.float32)


PARTS_OF_X = (3, 3, 4, 4, 4, 4, 4)


def chunk_edges(columns):
    tiles = columns // 128
    count = next((n for n in (7, 5, 4, 6, 3, 2) if tiles % n == 0), 1)
    width = columns // count
    return [(n * width, width) for n in range(count)]


def local(
    tokens,
    lengths,
    gain_one,
    w_query,
    b_query,
    key_weight,
    key_bias,
    value_weight,
    value_bias,
    w_out,
    gain_two,
    w_gate,
    w_up,
    w_down,
    grad_out,
):
    bf16, f32 = jnp.bfloat16, jnp.float32
    seq_count, block_len, model_width = tokens.shape
    row_count = seq_count * block_len
    query_cols = w_query.shape[1]
    key_cols = key_weight.shape[1]
    unit_cols = w_gate.shape[1]
    own_rows = w_query.shape[0]
    head_count = query_cols // HEAD_DIM
    kv_count = key_cols // HEAD_DIM
    query_group_width = head_count // kv_count
    size = lax.axis_size("dp")
    me = lax.axis_index("dp")
    blocks_along = lax.axis_size("context")
    place = lax.axis_index("context")
    parity = place % 2 if blocks_along % 2 == 0 and own_rows % 32 == 0 else None

    edges = chunk_edges(unit_cols)
    if (
        size == 4
        and blocks_along == 4
        and lax.axis_size("tensor") == 2
        and own_rows % 384 == 0
        and row_count % 64 == 0
        and len(edges) == len(PARTS_OF_X)
        and kv_count == 1
        and seq_count == 1
    ):
        f32 = jnp.float32
        output, grad_tokens, small, feed_sums, last_sums = layer(
            lengths,
            tokens.reshape(row_count, model_width),
            grad_out.reshape(row_count, model_width),
            jnp.stack([gain_one, gain_two]).astype(f32),
            jnp.concatenate([b_query, key_bias, value_bias]).astype(f32)[None, :],
            rotary_tables(block_len * blocks_along),
            (w_query, key_weight, value_weight, w_out),
            (w_gate, w_up, w_down),
            edges[0][1],
            PARTS_OF_X,
        )
        small = small[0]
        turned_at, at = query_cols + key_cols, 2 * model_width
        *grads, output, grad_tokens = finish(
            feed_sums,
            last_sums,
            output,
            grad_tokens,
            [(0, query_cols), (query_cols, key_cols), (turned_at, key_cols), (turned_at + key_cols, query_cols)],
        )
        return (
            output.reshape(seq_count, block_len, model_width),
            grad_tokens.reshape(seq_count, block_len, model_width),
            small[:model_width],
            grads[3],
            small[at : at + query_cols],
            grads[4],
            small[at + query_cols : at + turned_at],
            grads[5],
            small[at + turned_at :],
            grads[6],
            small[model_width:at],
            *grads[:3],
        )

    def relative(field):
        return swap_blocks([field[:, n * own_rows : (n + 1) * own_rows] for n in range(size)], me)

    def absolute(blocks):
        return jnp.concatenate(swap_blocks(blocks, me), 1)

    def dot_rows(blocks, weights):
        return jnp.dot(
            jnp.concatenate(blocks, 1), jnp.concatenate(weights, 0), preferred_element_type=f32
        )

    lanes = {name: Lane() for name in ("x", "z", "hop1", "hop2", "hop3")}
    attention_weights = gather_pieces(
        jnp.concatenate([w_query, key_weight, value_weight], 1), size, lanes
    )
    out_weights = gather_pieces(w_out, size, lanes, parity)
    edges = chunk_edges(unit_cols)
    feed_weights = []
    early = len(edges) - 2

    feed_own = (w_gate, w_up, w_down)
    feed_near = tuple(lax.ppermute(w, "dp", xor_pairs(size, 1)) for w in feed_own)

    def fetch(start, width):
        own = jnp.concatenate([w[:, start : start + width] for w in feed_own], 1)
        far = far_pieces(own, size, lanes, parity)
        sources = []
        for r in range(size):
            if r < 2:
                sources.append(feed_own if r == 0 else feed_near)
            elif r % 2 == 0:
                sources.append((far[r],))
            else:
                sources.append((lax.ppermute(far[r - 1], "dp", xor_pairs(size, 1)),))
        feed_weights.append(sources)

    for start, width in edges[:early]:
        fetch(start, width)

    positions = place * block_len + jnp.arange(block_len, dtype=jnp.int32)
    position_count = block_len * blocks_along
    valid_rows = (positions[None, :] < lengths[:, None]).astype(f32).reshape(row_count, 1)
    facts = jnp.stack([place.astype(jnp.int32), lengths[0]])
    half = HEAD_DIM // 2
    inverse = jnp.exp(jnp.arange(half, dtype=f32) * (-2.0 * math.log(ROPE_BASE) / HEAD_DIM))
    angles = positions.astype(f32)[:, None] * inverse[None, :]
    cosine = jnp.concatenate([jnp.cos(angles)] * 2, 1)
    sine = jnp.concatenate([-jnp.sin(angles), jnp.sin(angles)], 1)
    gain_first = gain_one.astype(f32)
    gain_second = gain_two.astype(f32)
    inputs = tokens.reshape(row_count, model_width).astype(f32)
    scale_one = lax.rsqrt(jnp.mean(inputs * inputs, -1, keepdims=True) + EPSILON)
    normalized_input = (inputs * scale_one * gain_first).astype(bf16)
    normed_blocks = relative(normalized_input)
    projected = dot_rows(normed_blocks, attention_weights) + jnp.concatenate(
        [b_query, key_bias, value_bias]
    ).astype(f32)
    turned = query_cols + key_cols

    def turn_heads(field, sine_rows):
        grid = field.reshape(row_count, field.shape[1] // HEAD_DIM, HEAD_DIM)
        swapped = jnp.concatenate([grid[..., half:], grid[..., :half]], -1)
        grid = grid * cosine[:, None, :] + swapped * sine_rows[:, None, :]
        return grid.reshape(field.shape).astype(bf16)

    turned_rows = turn_heads(projected[:, :turned], sine)
    query_rot = turned_rows[:, :query_cols]
    pair_rows = jnp.concatenate([turned_rows[:, query_cols:], projected[:, turned:].astype(bf16)], 1)
    pair_all = [pair_rows]
    for shift in range(1, blocks_along):
        pair_all.append(
            lax.ppermute(
                pair_rows, "context", [(n, n + shift) for n in range(blocks_along - shift)]
            )
        )
    pair_all = jnp.concatenate(pair_all, 0)
    mixed_heads, lse = attend(facts, query_rot, pair_all)
    full_out = jnp.concatenate(out_weights, 0)
    branch = contract_last(mixed_heads, full_out)
    branch = absolute([branch[:, r * own_rows : (r + 1) * own_rows] for r in range(size)])
    hidden = inputs + tensor_sum(branch)
    scale_two = lax.rsqrt(jnp.mean(hidden * hidden, -1, keepdims=True) + EPSILON)
    normed_two = (hidden * scale_two * gain_second).astype(bf16)
    fall_grad = grad_out.reshape(row_count, model_width).astype(f32) * valid_rows
    fall_low = fall_grad.astype(bf16)
    fall_blocks = relative(fall_low)
    two_blocks = relative(normed_two)
    traded_early = trade_blocks(
        [jnp.concatenate([a, b], 1) for a, b in zip(normed_blocks, fall_blocks)], size
    )
    traded_early = jnp.concatenate(traded_early, 0).T
    normed_features, fall_features = traded_early[:own_rows], traded_early[own_rows:]
    two_features = jnp.concatenate(trade_blocks(two_blocks, size), 0).T
    two_row = jnp.concatenate(two_blocks, 1)
    fall_row = jnp.concatenate(fall_blocks, 1)

    feed_out, d_normed_two = None, None
    feed_units = []
    for turn_at, (start, width) in enumerate(edges):
        acts, d_normed_two, feed_out = feed_chunk(
            two_row, fall_row, feed_weights[turn_at], start, width, d_normed_two, feed_out
        )
        if turn_at < 0:
            acts = gather_pieces(acts, size, lanes)
        feed_units.append(acts)
        if turn_at == 0:
            for edge in edges[early:]:
                fetch(*edge)

    def split(field):
        return [field[:, r * own_rows : (r + 1) * own_rows] for r in range(size)]

    d_normed_two = tensor_sum(absolute(split(d_normed_two)))
    result = valid_rows * (hidden + tensor_sum(absolute(split(feed_out))))
    output = result.astype(bf16).reshape(seq_count, block_len, model_width)
    gain_two_grad = jnp.sum(d_normed_two * hidden * scale_two, 0)
    d_hidden = fall_grad + norm_back(hidden, scale_two, gain_second, d_normed_two)
    d_branch = d_hidden.astype(bf16)
    branch_blocks = relative(d_branch)
    branch_features = jnp.concatenate(trade_blocks(branch_blocks, size), 0).T
    d_mixed = jnp.dot(
        jnp.concatenate(branch_blocks, 1), full_out, preferred_element_type=f32
    ).astype(bf16)
    d_query_low, d_own, d_rest = attend_back(
        facts, query_rot, pair_all, lse, d_mixed, cosine, sine
    )
    for shift in range(1, blocks_along):
        d_own = d_own + lax.ppermute(
            d_rest[(shift - 1) * block_len : shift * block_len],
            "context",
            [(n, n - shift) for n in range(shift, blocks_along)],
        ).astype(f32)
    d_key_low = turn_heads(d_own[:, :key_cols], -sine)
    d_value_low = d_own[:, key_cols:].astype(bf16)
    d_projected = jnp.concatenate([d_query_low, d_key_low, d_value_low], 1)
    d_normed = contract_last(d_projected, jnp.concatenate(attention_weights, 0))
    d_normed = tensor_sum(absolute(split(d_normed)))
    gain_one_grad = jnp.sum(d_normed * inputs * scale_one, 0)
    d_inputs = d_hidden + norm_back(inputs, scale_one, gain_first, d_normed)
    grad_tokens = d_inputs.astype(bf16).reshape(seq_count, block_len, model_width)
    gain_two_grad = small_total(gain_two_grad)
    small = small_total(
        jnp.concatenate([gain_one_grad, jnp.sum(d_projected.astype(f32), 0)])
    )
    projected_width = d_projected.shape[1]
    last = jnp.concatenate([d_projected, mixed_heads], 1)
    halfway = last.shape[1] // 2
    blocks = [
        [[(0, 0, width)], [(0, width, width)], [(1, 2 * width, width)]] for _, width in edges
    ] + [
        [
            [(2, 0, halfway)],
            [(2, halfway, projected_width - halfway), (3, projected_width, query_cols)],
        ]
    ]
    sums = gather_and_sum(
        feed_units + [last],
        [two_features, fall_features, normed_features, branch_features],
        blocks,
        size,
    )

    def columns(which):
        stack = sums[which][0]
        return jnp.concatenate(
            [stack[3 * n + which].astype(f32) for n in range(len(edges))], 1
        )

    stack = sums[-1][0]
    last_grad = jnp.concatenate([stack[0], stack[1]], 1).astype(f32)
    projected_grad, out_grad = last_grad[:, :projected_width], last_grad[:, projected_width:]

    low, high = model_width + query_cols, model_width + query_cols + key_cols
    return (
        output,
        grad_tokens,
        small[:model_width],
        projected_grad[:, :query_cols],
        small[model_width:low],
        projected_grad[:, query_cols : query_cols + key_cols],
        small[low:high],
        projected_grad[:, query_cols + key_cols :],
        small[high:],
        out_grad,
        gain_two_grad,
        columns(0),
        columns(1),
        columns(2),
    )


def solution(mesh):
    in_specs = (
        P("dp", "context", None),
        P("dp"),
        P(),
        P("dp", "tensor"),
        P("tensor"),
        P("dp", "tensor"),
        P("tensor"),
        P("dp", "tensor"),
        P("tensor"),
        P("dp", "tensor"),
        P(),
        P("dp", "tensor"),
        P("dp", "tensor"),
        P("dp", "tensor"),
        P("dp", "context", None),
    )
    out_specs = (
        P("dp", "context", None),
        P("dp", "context", None),
        P(),
        P("dp", "tensor"),
        P("tensor"),
        P("dp", "tensor"),
        P("tensor"),
        P("dp", "tensor"),
        P("tensor"),
        P("dp", "tensor"),
        P(),
        P("dp", "tensor"),
        P("dp", "tensor"),
        P("dp", "tensor"),
    )
    return jax.shard_map(local, mesh=mesh, in_specs=in_specs, out_specs=out_specs, check_vma=False)
```

```python
import math

import jax
import jax.numpy as jnp
import numpy as np
from jax import lax
from jax.experimental import pallas as pl
from jax.experimental.pallas import tpu as pltpu
from jax.sharding import PartitionSpec as P

HEAD_DIM = 128


EPSILON = 1e-06
ROPE_BASE = 1000000.0


def xor_pairs(size, mask):
    return [(i, i ^ mask) for i in range(size)]


class Lane:
    def __init__(self, depth=1):
        self.sent = []
        self.depth = depth

    def send(self, array, axis, pairs):
        if len(self.sent) >= self.depth:
            array, _ = lax.optimization_barrier((array, self.sent[-self.depth]))
        got = lax.ppermute(array, axis, pairs)
        self.sent.append(got)
        return got


def far_masks(size):
    masks, mask = [], 2
    while mask < size:
        masks.append(mask)
        mask *= 2
    return masks


def swap_blocks(blocks, me):
    mask = 1
    while mask < len(blocks):
        flag = (me & mask) != 0
        blocks = [jnp.where(flag, blocks[r ^ mask], blocks[r]) for r in range(len(blocks))]
        mask *= 2
    return blocks


def far_half(piece, mask, size, parity, lanes):
    half = piece.shape[0] // 2
    sent = lax.dynamic_slice_in_dim(piece, half * parity, half, 0)
    straight = lanes["x"].send(sent, "dp", xor_pairs(size, mask))
    other = lanes["z"].send(straight, "context", xor_pairs(lax.axis_size("context"), 1))
    first = jnp.where(parity == 0, straight, other)
    second = jnp.where(parity == 0, other, straight)
    return jnp.concatenate([first, second], 0)


def far_pieces(own, size, lanes, parity=None):
    pieces = {0: own}
    for mask in far_masks(size):
        for r in list(pieces):
            if parity is None:
                pieces[r ^ mask] = lanes["x"].send(pieces[r], "dp", xor_pairs(size, mask))
            else:
                pieces[r ^ mask] = far_half(pieces[r], mask, size, parity, lanes)
    return pieces


def gather_pieces(own, size, lanes, parity=None):
    pieces = far_pieces(own, size, lanes, parity)
    for r in list(pieces):
        pieces[r ^ 1] = lax.ppermute(pieces[r], "dp", xor_pairs(size, 1))
    return [pieces[r] for r in range(size)]


def trade_blocks(blocks, size):
    return [blocks[0]] + [
        lax.ppermute(blocks[r], "dp", xor_pairs(size, r)) for r in range(1, size)
    ]


def tensor_sum(part):
    sent = part.astype(jnp.bfloat16)
    size = lax.axis_size("tensor")
    if size == 2:
        other = lax.ppermute(sent, "tensor", [(0, 1), (1, 0)])
        return sent.astype(jnp.float32) + other.astype(jnp.float32)
    return lax.psum(part, "tensor")


def line_sum(part, lanes):
    place = lax.axis_index("context")
    if lax.axis_size("context") != 4:
        return lax.psum(part.astype(jnp.float32), "context")
    got = lanes["hop1"].send(part, "context", [(0, 1), (3, 2)])
    pair = (part.astype(jnp.float32) + got.astype(jnp.float32)).astype(jnp.bfloat16)
    got = lanes["hop2"].send(pair, "context", [(1, 2), (2, 1)])
    total = (pair.astype(jnp.float32) + got.astype(jnp.float32)).astype(jnp.bfloat16)
    got = lanes["hop3"].send(total, "context", [(1, 0), (2, 3)])
    ends = (place == 0) | (place == 3)
    return jnp.where(ends, got, total).astype(jnp.float32)


def small_total(vector):
    for axis in ("dp", "context"):
        size, mask = lax.axis_size(axis), 1
        while mask < size:
            vector = vector + lax.ppermute(vector, axis, xor_pairs(size, mask))
            mask *= 2
    return vector


def contract_last(left, right):
    return lax.dot_general(
        left, right, (((1,), (1,)), ((), ())), preferred_element_type=jnp.float32
    )


def norm_back(field, scale_rows, gain, d_normed):
    weighted = d_normed * gain
    cubed = scale_rows * scale_rows * scale_rows
    return scale_rows * weighted - field * cubed * jnp.mean(field * weighted, -1, keepdims=True)


ANY = pl.BlockSpec(memory_space=pl.ANY)
VMEM = pl.BlockSpec(memory_space=pltpu.VMEM)
SMEM = pl.BlockSpec(memory_space=pltpu.SMEM)


def plain_params(limit):
    return pltpu.CompilerParams(vmem_limit_bytes=limit)


def dot_nn(left, right):
    return jnp.dot(left, right, preferred_element_type=jnp.float32)


def feed_chunk(two_row, fall_row, sources, start, width, d_sum, out_sum):
    rows, features = two_row.shape
    bf16, f32 = jnp.bfloat16, jnp.float32
    flat, layout = [], []
    for source in sources:
        layout.append(len(source))
        flat.extend(source)
    first = d_sum is None
    held = [] if first else [d_sum, out_sum]

    def kernel(*refs):
        refs = list(refs)
        two_ref, fall_ref = refs[:2]
        given = refs[2 : 2 + len(flat)]
        at = 2 + len(flat)
        sums = refs[at : at + len(held)]
        at += len(held)
        acts_ref, d_ref, out_ref, gate_w, up_w, down_w, sems = refs[at:]
        copies = [[], [], []]
        place, taken = 0, 0
        for kind in layout:
            depth = given[taken].shape[0]
            for which, scratch in enumerate((gate_w, up_w, down_w)):
                if kind == 3:
                    view = given[taken + which].at[:, pl.ds(start, width)]
                else:
                    view = given[taken].at[:, pl.ds(which * width, width)]
                copy = pltpu.make_async_copy(
                    view,
                    scratch.at[pl.ds(place, depth), :],
                    sems.at[which, len(copies[which])],
                )
                copies[which].append(copy)
            place += depth
            taken += kind
        for group in copies:
            for copy in group:
                copy.start()
        for copy in copies[0]:
            copy.wait()
        gate = dot_nn(two_ref[...], gate_w[...])
        for copy in copies[1]:
            copy.wait()
        up = dot_nn(two_ref[...], up_w[...])
        for copy in copies[2]:
            copy.wait()
        d_active = dot_nn(fall_ref[...], down_w[...])
        sigmoid = jax.nn.sigmoid(gate)
        swish = gate * sigmoid
        acts_ref[:, 2 * width :] = (swish * up).astype(bf16)
        acts_ref[:, :width] = (d_active * up * sigmoid * (1.0 + gate * (1.0 - sigmoid))).astype(bf16)
        acts_ref[:, width : 2 * width] = (d_active * swish).astype(bf16)
        d_part = contract_last(acts_ref[:, :width], gate_w[...]) + contract_last(
            acts_ref[:, width : 2 * width], up_w[...]
        )
        out_part = contract_last(acts_ref[:, 2 * width :], down_w[...])
        if first:
            d_ref[...] = d_part
            out_ref[...] = out_part
        else:
            d_ref[...] = sums[0][...] + d_part
            out_ref[...] = sums[1][...] + out_part

    weight_bytes = 6 * features * width
    return pl.pallas_call(
        kernel,
        out_shape=(
            jax.ShapeDtypeStruct((rows, 3 * width), bf16),
            jax.ShapeDtypeStruct((rows, features), f32),
            jax.ShapeDtypeStruct((rows, features), f32),
        ),
        in_specs=[VMEM, VMEM] + [ANY] * len(flat) + [VMEM] * len(held),
        out_specs=(VMEM, VMEM, VMEM),
        scratch_shapes=[pltpu.VMEM((features, width), bf16)] * 3
        + [pltpu.SemaphoreType.DMA((3, len(sources)))],
        compiler_params=plain_params(40 << 20),
        cost_estimate=pl.CostEstimate(
            flops=12 * rows * features * width,
            bytes_accessed=weight_bytes + 20 * rows * features + 6 * rows * width,
            transcendentals=rows * width,
        ),
        name="feed_chunk",
    )(two_row, fall_row, *flat, *held)


def grad_block(features, pieces, spans):
    bf16 = jnp.bfloat16
    depth, columns = pieces[0].shape
    tokens = features[0].shape[1]
    own = features[0].shape[0]
    total = sum(w for _, w in spans)

    def kernel(*refs):
        refs = list(refs)
        feature_refs = refs[: len(features)]
        given = refs[len(features) : len(features) + len(pieces)]
        out_ref, held, sems = refs[len(features) + len(pieces) :]
        copies = [
            pltpu.make_async_copy(ref, held.at[pl.ds(n * depth, depth), :], sems.at[n])
            for n, ref in enumerate(given)
        ]
        for copy in copies:
            copy.start()
        for copy in copies:
            copy.wait()
        for ref, (start, width) in zip(feature_refs, spans):
            out_ref[:, start : start + width] = dot_nn(
                ref[...], held[:, start : start + width]
            ).astype(bf16)

    return pl.pallas_call(
        kernel,
        out_shape=jax.ShapeDtypeStruct((own, total), bf16),
        in_specs=[VMEM] * len(features) + [ANY] * len(pieces),
        out_specs=VMEM,
        scratch_shapes=[
            pltpu.VMEM((tokens, columns), bf16),
            pltpu.SemaphoreType.DMA((len(pieces),)),
        ],
        compiler_params=plain_params(40 << 20),
        cost_estimate=pl.CostEstimate(
            flops=2 * own * tokens * total,
            bytes_accessed=2 * (tokens * columns + own * total + own * tokens),
            transcendentals=0,
        ),
        name="grad_block",
    )(*features, *pieces)


def key_bias_table(place, length, keys, block_len):
    key_at = lax.broadcasted_iota(jnp.int32, (keys, block_len), 0)
    query_at = lax.broadcasted_iota(jnp.int32, (keys, block_len), 1) + place * block_len
    shift = key_at // block_len
    key_at = key_at - shift * block_len + (place - shift) * block_len
    seen = (key_at <= query_at) & (key_at < length) & (key_at >= 0)
    return jnp.where(seen, 0.0, -1e30).astype(jnp.float32)


def attend(facts, query, pair):
    rows, width = query.shape
    keys = pair.shape[0]
    heads = width // HEAD_DIM
    bf16, f32 = jnp.bfloat16, jnp.float32
    scale = 1.0 / math.sqrt(HEAD_DIM)

    def kernel(facts_ref, query_ref, pair_ref, mixed_ref, lse_ref, bias, value_t):
        bias[...] = key_bias_table(facts_ref[0], facts_ref[1], keys, rows)
        value_t[...] = pair_ref[:, HEAD_DIM:].T
        lse_ref[...] = jnp.zeros_like(lse_ref)
        for head in range(heads):
            cols = slice(head * HEAD_DIM, (head + 1) * HEAD_DIM)
            scores = contract_last(pair_ref[:, :HEAD_DIM], query_ref[:, cols]) * scale + bias[...]
            top = jnp.max(scores, 0, keepdims=True)
            raised = jnp.exp(scores - top)
            total = jnp.sum(raised, 0, keepdims=True)
            lse_ref[head : head + 1, :] = top + jnp.log(total)
            probs = (raised * (1.0 / total)).astype(bf16)
            mixed_ref[:, cols] = dot_nn(value_t[...], probs).T.astype(bf16)

    return pl.pallas_call(
        kernel,
        out_shape=(
            jax.ShapeDtypeStruct((rows, width), bf16),
            jax.ShapeDtypeStruct((8, rows), f32),
        ),
        in_specs=[SMEM, VMEM, VMEM],
        out_specs=(VMEM, VMEM),
        scratch_shapes=[pltpu.VMEM((keys, rows), f32), pltpu.VMEM((HEAD_DIM, keys), bf16)],
        compiler_params=plain_params(40 << 20),
        cost_estimate=pl.CostEstimate(
            flops=4 * rows * keys * width + 12 * heads * rows * keys * 100,
            bytes_accessed=4 * rows * width + 4 * keys * HEAD_DIM,
            transcendentals=heads * rows * keys,
        ),
        name="attend",
    )(facts, query, pair)


def turn(field, cosine, sine):
    return field * cosine + pltpu.roll(field, HEAD_DIM // 2, 1) * sine


def attend_back(facts, query, pair, lse, d_mixed, cosine, sine):
    rows, width = query.shape
    keys = pair.shape[0]
    heads = width // HEAD_DIM
    bf16, f32 = jnp.bfloat16, jnp.float32
    scale = 1.0 / math.sqrt(HEAD_DIM)

    def kernel(facts_ref, query_ref, pair_ref, lse_ref, d_mixed_ref, cos_ref, sin_ref, d_query_ref, d_own_ref, d_rest_ref, bias, key_t, d_key, d_value):
        bias[...] = key_bias_table(facts_ref[0], facts_ref[1], keys, rows)
        key_t[...] = pair_ref[:, :HEAD_DIM].T
        for head in range(heads):
            cols = slice(head * HEAD_DIM, (head + 1) * HEAD_DIM)
            scores = contract_last(pair_ref[:, :HEAD_DIM], query_ref[:, cols]) * scale + bias[...]
            probs = jnp.exp(scores - lse_ref[head : head + 1, :])
            d_probs = contract_last(pair_ref[:, HEAD_DIM:], d_mixed_ref[:, cols])
            inner = jnp.sum(d_probs * probs, 0, keepdims=True)
            d_scores = (probs * (d_probs - inner)).astype(bf16)
            d_query = (dot_nn(key_t[...], d_scores) * scale).T
            d_query_ref[:, cols] = turn(d_query, cos_ref[...], -sin_ref[...]).astype(bf16)
            more_key = dot_nn(d_scores, query_ref[:, cols])
            more_value = dot_nn(probs.astype(bf16), d_mixed_ref[:, cols])
            if head == 0:
                d_key[...] = more_key
                d_value[...] = more_value
            else:
                d_key[...] += more_key
                d_value[...] += more_value
        d_own_ref[:, :HEAD_DIM] = d_key[:rows, :] * scale
        d_own_ref[:, HEAD_DIM:] = d_value[:rows, :]
        d_rest_ref[:, :HEAD_DIM] = (d_key[rows:, :] * scale).astype(bf16)
        d_rest_ref[:, HEAD_DIM:] = d_value[rows:, :].astype(bf16)

    return pl.pallas_call(
        kernel,
        out_shape=(
            jax.ShapeDtypeStruct((rows, width), bf16),
            jax.ShapeDtypeStruct((rows, 2 * HEAD_DIM), f32),
            jax.ShapeDtypeStruct((keys - rows, 2 * HEAD_DIM), bf16),
        ),
        in_specs=[SMEM] + [VMEM] * 6,
        out_specs=(VMEM, VMEM, VMEM),
        scratch_shapes=[
            pltpu.VMEM((keys, rows), f32),
            pltpu.VMEM((HEAD_DIM, keys), bf16),
            pltpu.VMEM((keys, HEAD_DIM), f32),
            pltpu.VMEM((keys, HEAD_DIM), f32),
        ],
        compiler_params=plain_params(40 << 20),
        cost_estimate=pl.CostEstimate(
            flops=10 * rows * keys * width + 12 * heads * rows * keys * 200,
            bytes_accessed=8 * rows * width + 8 * keys * HEAD_DIM,
            transcendentals=heads * rows * keys,
        ),
        name="attend_back",
    )(facts, query, pair, lse, d_mixed, cosine, sine)


MESH = pl.DeviceIdType.MESH


def flipped(index, mask):
    return index + mask - 2 * mask * ((index // mask) % 2)


def gather_and_sum(units, features, blocks, size):
    bf16, f32 = jnp.bfloat16, jnp.float32
    count = len(units)
    gathered = [isinstance(u, (list, tuple)) for u in units]
    flat = [a for u in units for a in (u if isinstance(u, (list, tuple)) else [u])]
    starts, at = [], 0
    for u in units:
        starts.append(at)
        at += len(u) if isinstance(u, (list, tuple)) else 1
    rows = flat[0].shape[0]
    widest = max(a.shape[1] for a in flat)
    own_rows, tokens = features[0].shape
    widths = []
    where = []
    counts = {}
    for u, group in enumerate(blocks):
        for spans in group:
            width = sum(w for _, _, w in spans)
            if width not in counts:
                counts[width] = 0
                widths.append(width)
            where.append((u, spans, widths.index(width), counts[width]))
            counts[width] += 1
    block_count = len(where)
    steps = []
    held = [0]
    for mask in far_masks(size):
        for r in list(held):
            steps.append((r, mask))
            held.append(r ^ mask)
    for r in list(held):
        steps.append((r, 1))
    arrival = {r ^ mask: n for n, (r, mask) in enumerate(steps)}
    ahead = 2

    def kernel(*refs):
        refs = list(refs)
        unit_refs, refs = refs[: len(flat)], refs[len(flat) :]
        feature_refs, refs = refs[: len(features)], refs[len(features) :]
        outs, refs = refs[: len(widths)], refs[len(widths) :]
        land, refs = refs[0], refs[1:]
        mine, refs = refs[: len(widths)], refs[len(widths) :]
        first, refs = refs[: len(widths)], refs[len(widths) :]
        second, refs = refs[: len(widths)], refs[len(widths) :]
        table, send_g, recv_g, send_a, recv_a, send_b, recv_b, load, store = refs
        me = lax.axis_index("dp")
        place = lax.axis_index("context")
        middle = place * (3 - place) == 2
        inner = 1 + place // 2
        across = 3 - place
        outer = 3 * (place - 1)

        barrier = pltpu.get_barrier_semaphore()
        partners = sorted(set(mask for _, mask in steps))
        for mask in partners:
            pl.semaphore_signal(barrier, 1, device_id={"dp": flipped(me, mask)}, device_id_type=MESH)

        @pl.when(middle)
        def _():
            pl.semaphore_signal(barrier, 1, device_id={"context": across}, device_id_type=MESH)
            pl.semaphore_signal(barrier, 1, device_id={"context": outer}, device_id_type=MESH)
            pl.semaphore_wait(barrier, len(partners) + 2)

        @pl.when(jnp.logical_not(middle))
        def _():
            pl.semaphore_signal(barrier, 1, device_id={"context": inner}, device_id_type=MESH)
            pl.semaphore_wait(barrier, len(partners) + 1)

        def piece(u, r):
            if gathered[u]:
                return unit_refs[starts[u] + r]
            if r == 0:
                return unit_refs[starts[u]]
            return land.at[r - 1, u, :, pl.ds(0, flat[starts[u]].shape[1])]

        def transfer(u, n):
            r, mask = steps[n]
            target = r ^ mask
            return pltpu.make_async_remote_copy(
                src_ref=piece(u, r),
                dst_ref=land.at[target - 1, u, :, pl.ds(0, flat[starts[u]].shape[1])],
                send_sem=send_g.at[n, u],
                recv_sem=recv_g.at[n, u],
                device_id={"dp": flipped(me, mask)},
                device_id_type=MESH,
            )

        wanted = [u for u in range(count) if not gathered[u]]

        def begin(u):
            for n, (r, _) in enumerate(steps):
                if r == 0:
                    transfer(u, n).start()

        def loads(u, slot):
            width = flat[starts[u]].shape[1]
            return [
                pltpu.make_async_copy(
                    piece(u, r),
                    table.at[slot, pl.ds(r * rows, rows), pl.ds(0, width)],
                    load.at[slot, r],
                )
                for r in range(size)
            ]

        def forward(u):
            waited = set()
            for n, (r, mask) in enumerate(steps):
                if r != 0:
                    if r not in waited:
                        transfer(u, arrival[r]).wait_recv()
                        waited.add(r)
                    transfer(u, n).start()
            for r in range(1, size):
                if r not in waited:
                    transfer(u, arrival[r]).wait_recv()

        def hop(j, source, target, place_to, send, recv):
            _, _, kind, index = where[j]
            return pltpu.make_async_remote_copy(
                src_ref=source[kind].at[index],
                dst_ref=target[kind].at[index],
                send_sem=send.at[j],
                recv_sem=recv.at[j],
                device_id={"context": place_to},
                device_id_type=MESH,
            )

        def hop_in(j):
            return hop(j, mine, first, inner, send_a, recv_a)

        def hop_across(j):
            return hop(j, mine, second, across, send_b, recv_b)

        def hop_out(j):
            return hop(j, first, first, outer, send_a, recv_a)

        def keep(j):
            _, _, kind, index = where[j]
            return pltpu.make_async_copy(first[kind].at[index], outs[kind].at[index], store.at[j])

        def total_in(j):
            _, _, kind, index = where[j]
            hop_in(j).wait_recv()
            mine[kind][index] = (
                mine[kind][index].astype(f32) + first[kind][index].astype(f32)
            ).astype(bf16)
            hop_across(j).start()

        def total_across(j):
            _, _, kind, index = where[j]
            hop_across(j).wait_recv()
            first[kind][index] = (
                mine[kind][index].astype(f32) + second[kind][index].astype(f32)
            ).astype(bf16)
            hop_out(j).start()
            keep(j).start()

        of_unit = [[j for j in range(block_count) if where[j][0] == u] for u in range(count)]
        for u in wanted[:ahead]:
            begin(u)
        for copy in loads(0, 0) if gathered[0] else []:
            copy.start()
        middle_in = []
        for u in range(count):
            slot = u % 2
            if not gathered[u]:
                forward(u)
                later = [v for v in wanted if v > u]
                if len(later) >= ahead:
                    begin(later[ahead - 1])
            if not (u == 0 and gathered[0]):
                for copy in loads(u, slot):
                    copy.start()
            for copy in loads(u, slot):
                copy.wait()
            for j in of_unit[u]:
                _, spans, kind, index = where[j]
                filled = 0
                for which, start, width in spans:
                    mine[kind][index, :, filled : filled + width] = dot_nn(
                        feature_refs[which][...], table[slot, :, start : start + width]
                    ).astype(bf16)
                    filled += width

                @pl.when(jnp.logical_not(middle))
                def _(j=j):
                    if j >= 3:
                        hop_in(j - 3).wait_send()
                    hop_in(j).start()

            if u >= 1:

                @pl.when(middle)
                def _(u=u):
                    for j in of_unit[u - 1]:
                        total_in(j)
                        if j >= 1:
                            total_across(j - 1)

        @pl.when(middle)
        def _():
            for j in of_unit[count - 1]:
                total_in(j)
                total_across(j - 1)
            total_across(block_count - 1)
            for j in range(block_count):
                hop_across(j).wait_send()
                hop_out(j).wait_send()
                keep(j).wait()

        @pl.when(jnp.logical_not(middle))
        def _():
            for j in range(max(block_count - 3, 0), block_count):
                hop_in(j).wait_send()
            for j in range(block_count):
                hop_out(j).wait_recv()
                keep(j).start()
            for j in range(block_count):
                keep(j).wait()

        for u in wanted:
            for n in range(len(steps)):
                transfer(u, n).wait_send()

    def stacks(kind_memory):
        return [kind_memory((counts[w], own_rows, w), bf16) for w in widths]

    columns = sum(counts[w] * w for w in widths)
    results = pl.pallas_call(
        kernel,
        out_shape=[jax.ShapeDtypeStruct((counts[w], own_rows, w), bf16) for w in widths]
        + [jax.ShapeDtypeStruct((size - 1, count, rows, widest), bf16)],
        in_specs=[ANY] * len(flat) + [VMEM] * len(features),
        out_specs=[ANY] * (len(widths) + 1),
        scratch_shapes=stacks(pltpu.VMEM) * 3
        + [
            pltpu.VMEM((2, tokens, widest), bf16),
            pltpu.SemaphoreType.DMA((len(steps), count)),
            pltpu.SemaphoreType.DMA((len(steps), count)),
            pltpu.SemaphoreType.DMA((block_count,)),
            pltpu.SemaphoreType.DMA((block_count,)),
            pltpu.SemaphoreType.DMA((block_count,)),
            pltpu.SemaphoreType.DMA((block_count,)),
            pltpu.SemaphoreType.DMA((2, size)),
            pltpu.SemaphoreType.DMA((block_count,)),
        ],
        compiler_params=pltpu.CompilerParams(
            collective_id=0, has_side_effects=True, vmem_limit_bytes=60 << 20
        ),
        cost_estimate=pl.CostEstimate(
            flops=2 * own_rows * tokens * columns,
            bytes_accessed=2 * tokens * columns + 12 * own_rows * columns,
            transcendentals=0,
        ),
        name="gather_and_sum",
    )(*flat, *features)
    return [(results[kind], index) for _, _, kind, index in where]


def layer(
    length, tokens, grad_out, gains, biases, tables, attention_own, feed_own, width, parts_of_x,
):
    bf16, f32 = jnp.bfloat16, jnp.float32
    rows, features = tokens.shape
    own_rows, units_all = feed_own[0].shape
    chunks = units_all // width
    heads_width = attention_own[0].shape[1]
    heads = heads_width // HEAD_DIM
    keys = tables.shape[1]
    pair_width = attention_own[1].shape[1] + attention_own[2].shape[1]
    projected = heads_width + pair_width
    last_width = projected + heads_width
    halfway = 2 * HEAD_DIM
    size = features // own_rows
    units = chunks + 1
    tokens_all = size * rows
    small_width = 2 * features + projected
    scale = 1.0 / math.sqrt(HEAD_DIM)
    part = 64
    where = []
    for k in range(chunks):
        where.append((k, [(0, 0, width)], 0, 3 * k))
        where.append((k, [(0, width, width)], 0, 3 * k + 1))
        where.append((k, [(1, 2 * width, width)], 0, 3 * k + 2))
    for n in range(last_width // halfway):
        where.append((chunks, [(2 if n * halfway < projected else 3, n * halfway, halfway)], 1, n))
    count = len(where)
    widths = (width, halfway)
    attention_width = projected + heads_width
    attention_spans = []
    for array in attention_own:
        attention_spans.append((sum(w for _, w in attention_spans), array.shape[1]))

    def kernel(*refs):
        refs = list(refs)

        def take(n):
            taken = refs[:n]
            del refs[:n]
            return taken

        (length_ref, gains_ref, biases_ref) = take(3)
        (tokens_hbm, grad_hbm, tables_hbm) = take(3)
        attention_hbm, own_hbm = take(4), take(3)
        output_hbm, grad_tokens_hbm, small_ref, sum_wide, sum_last, land, acts_hbm, across_wide, across_last = take(9)
        attention_land, near_land, far_land = take(3)
        (mine_wide, mine_last, stage_in, stage_across, table, weights, feature_t, feature_land) = take(8)
        (row_two, row_fall, row_normed, row_branch, hidden_rel, tokens_rel, d_sum, out_sum) = take(8)
        (y_send, y_land, acts_stage, query_v, pair_v, last_v, bias, key_t, d_key, d_value) = take(10)
        (d_mixed, d_rest, d_land, vec, vec_land, total_land) = take(6)
        (gains_v, tables_v, lse_ref) = take(3)
        (s_in, s_weights, s_acts, s_rest, send_g, recv_g, send_a, recv_a, send_b, recv_b) = take(10)
        (s_stage, s_keep, s_table, send_t, recv_t, send_y, recv_y, send_k, recv_k) = take(9)
        (send_v, recv_v, send_w, recv_w, s_store) = take(5)
        (send_m, recv_m, send_near, recv_near, send_x, recv_x, send_z, recv_z, send_c, recv_c, send_p, recv_p) = take(12)
        (s_attention,) = take(1)
        cos_ref, sin_ref = tables_v.at[0], tables_v.at[1]
        sums, mines, acrosses = (sum_wide, sum_last), (mine_wide, mine_last), (across_wide, across_last)
        rows_of = (row_two, row_fall, row_normed, row_branch)

        me = lax.axis_index("dp")
        place = lax.axis_index("context")
        side = lax.axis_index("tensor")
        middle = place * (3 - place) == 2
        inner = 1 + place // 2
        across = 3 - place
        outer = 3 * (place - 1)
        one = flipped(me, 1)
        partner = (me, one, flipped(me, 2), flipped(one, 2))
        parity = lax.rem(place, 2)
        beside = flipped(place, 1)

        barrier = pltpu.get_barrier_semaphore()
        for r in range(1, size):
            pl.semaphore_signal(barrier, 1, device_id={"dp": partner[r]}, device_id_type=MESH)
        for s in range(1, 4):
            pl.semaphore_signal(barrier, 1, device_id={"context": lax.rem(place + s, 4)}, device_id_type=MESH)
        pl.semaphore_signal(barrier, 1, device_id={"tensor": 1 - side}, device_id_type=MESH)

        def block_of(r):
            return pl.ds(pl.multiple_of(partner[r] * own_rows, 128), own_rows)

        def local(source, target, sem):
            return pltpu.make_async_copy(source, target, sem)

        def remote(source, target, send, recv, axis, index):
            return pltpu.make_async_remote_copy(
                src_ref=source, dst_ref=target, send_sem=send, recv_sem=recv,
                device_id={axis: index}, device_id_type=MESH,
            )

        def cols(r):
            return pl.ds(r * own_rows, own_rows)

        ins = []
        for n, (source, target) in enumerate(((tokens_hbm, tokens_rel), (grad_hbm, row_fall))):
            ins.append(
                [local(source.at[:, block_of(r)], target.at[:, cols(r)], s_in.at[n, r]) for r in range(size)]
            )
        rest = [
            local(tables_hbm.at[:, pl.ds(pl.multiple_of(place * rows, rows), rows), :], tables_v, s_rest.at[0])
        ]

        attention_parts = ((0, 3, 0, projected), (3, 4, projected, heads_width))
        half_rows = pl.ds(pl.multiple_of(own_rows // 2 * parity, 64), own_rows // 2)

        def attention_send(n):
            first, last, _, _ = attention_parts[n % 2]
            if n >= 4:
                attention_wait(n).start()
                return
            rows_sent = half_rows if n < 2 else pl.ds(0, own_rows)
            for m in range(first, last):
                at, wide = attention_spans[m]
                remote(
                    attention_hbm[m].at[rows_sent, :],
                    attention_land.at[1 if n < 2 else 0, rows_sent, pl.ds(at, wide)],
                    send_m.at[n], recv_m.at[n], "dp", partner[2 if n < 2 else 1],
                ).start()

        def attention_wait(n):
            _, _, at, wide = attention_parts[n % 2]
            rows_sent = half_rows if n < 2 or n >= 6 else pl.ds(0, own_rows)
            source = attention_land.at[1, rows_sent, pl.ds(at, wide)]
            target = attention_land.at[(1, 0, 2, 1)[n // 2], rows_sent, pl.ds(at, wide)]
            axis, to = ("context", beside) if n >= 6 else ("dp", partner[2 if n < 2 else 1])
            return remote(source, target, send_m.at[n], recv_m.at[n], axis, to)

        def attention_arrived(n):
            _, _, at, wide = attention_parts[n % 2]
            half = pl.ds(pl.multiple_of(own_rows // 2 * (1 - parity), 64), own_rows // 2)
            view = attention_land.at[1, half, pl.ds(at, wide)]
            remote(view, view, send_m.at[n], recv_m.at[n], "context", beside).wait_recv()

        def attention_copies(n):
            first, last, at, wide = attention_parts[n]
            return [
                local(
                    attention_hbm[m],
                    weights.at[pl.ds(0, own_rows), pl.ds(attention_spans[m][0], attention_spans[m][1])],
                    s_attention.at[m],
                )
                for m in range(first, last)
            ] + [
                local(
                    attention_land.at[r - 1, :, pl.ds(at, wide)],
                    weights.at[pl.ds(r * own_rows, own_rows), pl.ds(at, wide)],
                    s_weights.at[n, r],
                )
                for r in range(1, size)
            ]

        def near(which):
            return remote(
                own_hbm[which], near_land.at[which], send_near.at[which], recv_near.at[which], "dp", partner[1]
            )

        def straight_rows(k):
            wide = own_rows * parts_of_x[k] // 6
            return pl.ds(pl.multiple_of((own_rows - wide) * parity, 64), wide)

        def round_rows(k):
            short = own_rows - own_rows * parts_of_x[k] // 6
            return pl.ds(pl.multiple_of((own_rows - short) * parity, 64), short)

        def far_send(k):
            for which in range(3):
                remote(
                    own_hbm[which].at[straight_rows(k), pl.ds(k * width, width)],
                    far_land.at[0, k, straight_rows(k), pl.ds(which * width, width)],
                    send_x.at[k], recv_x.at[k], "dp", partner[2],
                ).start()

        def far_wait(k):
            view = far_land.at[0, k, straight_rows(k), :]
            return remote(view, view, send_x.at[k], recv_x.at[k], "dp", partner[2])

        def far_round(k):
            view = far_land.at[0, k, round_rows(k), :]
            return remote(view, view, send_z.at[k], recv_z.at[k], "context", beside)

        def missing_rows(k):
            short = own_rows - own_rows * parts_of_x[k] // 6
            return pl.ds(pl.multiple_of((own_rows - short) * (1 - parity), 64), short)

        def far_round_wait(k):
            view = far_land.at[0, k, missing_rows(k), :]
            return remote(view, view, send_z.at[k], recv_z.at[k], "context", beside)

        def far_near(k):
            return remote(far_land.at[0, k], far_land.at[1, k], send_c.at[k], recv_c.at[k], "dp", partner[1])

        def weight_straight(k):
            far_wait(k).wait_recv()
            if parts_of_x[k] < 6:
                far_round(k).start()
            else:
                far_near(k).start()

        def weight_round(k):
            if parts_of_x[k] < 6:
                far_round_wait(k).wait_recv()
                far_near(k).start()

        def weight_copies(k, which):
            view = pl.ds(which * width, width)
            sources = [
                own_hbm[which].at[:, pl.ds(k * width, width)],
                near_land.at[which, :, pl.ds(k * width, width)],
                far_land.at[0, k, :, view],
                far_land.at[1, k, :, view],
            ]
            return [
                local(source, weights.at[pl.ds(r * own_rows, own_rows), view], s_weights.at[which, r])
                for r, source in enumerate(sources)
            ]

        def start(copies):
            for copy in copies:
                copy.start()

        def wait(copies):
            for copy in copies:
                copy.wait()

        for copies in ins:
            start(copies)
        start(rest)

        def trade(w, r):
            return remote(
                rows_of[w].at[:, cols(r)], feature_land.at[w, r - 1], send_t.at[w, r - 1], recv_t.at[w, r - 1],
                "dp", partner[r],
            )

        def turn_features(w):
            feature_t[w, :, 0:rows] = rows_of[w][:, 0:own_rows].T
            for r in range(1, size):
                trade(w, r).wait_recv()
                feature_t[w, :, r * rows : (r + 1) * rows] = feature_land[w, r - 1].T

        steps = ((0, 2), (0, 1), (2, 1))

        def unit_width(u):
            return 3 * width if u < chunks else last_width

        def piece(u, r):
            view = pl.ds(0, unit_width(u))
            return acts_hbm.at[u, :, view] if r == 0 else land.at[r - 1, u, :, view]

        def transfer(u, n):
            r, mask = steps[n]
            return remote(
                piece(u, r), land.at[(r ^ mask) - 1, u, :, pl.ds(0, unit_width(u))],
                send_g.at[n, u], recv_g.at[n, u], "dp", partner[mask],
            )

        def own_copy(u):
            if u < chunks:
                return local(acts_stage.at[u % 2], piece(u, 0), s_acts.at[u])
            return local(last_v, piece(u, 0), s_acts.at[u])

        def begin(u):
            own_copy(u).wait()
            transfer(u, 0).start()
            transfer(u, 1).start()

        def table_copies(u):
            return [
                local(
                    piece(u, r), table.at[pl.ds(r * rows, rows), pl.ds(0, unit_width(u))], s_table.at[r]
                )
                for r in range(size)
            ]

        def hop(j, source, target, to, send, recv):
            _, _, kind, index = where[j]
            return remote(
                source[kind].at[index], target[kind].at[index], send.at[j], recv.at[j], "context", to
            )

        def hop_in(j):
            return hop(j, mines, sums, inner, send_a, recv_a)

        def hop_across(j):
            return hop(j, mines, acrosses, across, send_b, recv_b)

        def hop_out(j):
            return hop(j, mines, sums, outer, send_a, recv_a)

        def staged(j, source, stage, n):
            _, _, kind, index = where[j]
            return local(
                source[kind].at[index], stage.at[j % 2, :, pl.ds(0, widths[kind])], s_stage.at[n, j % 2]
            )

        def keep(j):
            _, _, kind, index = where[j]
            return local(mines[kind].at[index], sums[kind].at[index], s_keep.at[j])

        def add_stage(j, stage):
            _, _, kind, index = where[j]
            mines[kind][index] = (
                mines[kind][index].astype(f32) + stage[j % 2, :, 0 : widths[kind]].astype(f32)
            ).astype(bf16)

        def line_in(j):
            hop_in(j).wait_recv()
            staged(j, sums, stage_in, 0).start()
            staged(j, sums, stage_in, 0).wait()
            add_stage(j, stage_in)
            hop_across(j).start()

        def line_out(j):
            hop_across(j).wait_recv()
            staged(j, acrosses, stage_across, 1).start()
            staged(j, acrosses, stage_across, 1).wait()
            hop_across(j).wait_send()
            add_stage(j, stage_across)
            hop_out(j).start()
            keep(j).start()

        of_unit = [[j for j in range(count) if where[j][0] == u] for u in range(units)]

        def gradients(u):
            transfer(u, 0).wait_recv()
            transfer(u, 2).start()
            transfer(u, 1).wait_recv()
            transfer(u, 2).wait_recv()
            start(table_copies(u))
            wait(table_copies(u))
            for j in of_unit[u]:
                _, spans, kind, index = where[j]
                filled = 0
                for which, at, w in spans:
                    mines[kind][index, :, filled : filled + w] = dot_nn(
                        feature_t[which], table[:, at : at + w]
                    ).astype(bf16)
                    filled += w

                @pl.when(jnp.logical_not(middle))
                def _(j=j):
                    if j >= 3:
                        hop_in(j - 3).wait_send()
                    hop_in(j).start()

        def feed(k):
            far_near(k).wait_recv()
            for which in range(3):
                if k == 0:
                    near(which).wait_recv()
                start(weight_copies(k, which))
            wait(weight_copies(k, 0))
            gate_w, up_w, down_w = (weights.at[:, pl.ds(n * width, width)] for n in range(3))
            gate = dot_nn(row_two[...], gate_w[...])
            wait(weight_copies(k, 1))
            up = dot_nn(row_two[...], up_w[...])
            wait(weight_copies(k, 2))
            d_active = dot_nn(row_fall[...], down_w[...])
            sigmoid = jax.nn.sigmoid(gate)
            swish = gate * sigmoid
            stage = acts_stage.at[k % 2]
            stage[:, 2 * width :] = (swish * up).astype(bf16)
            stage[:, :width] = (d_active * up * sigmoid * (1.0 + gate * (1.0 - sigmoid))).astype(bf16)
            stage[:, width : 2 * width] = (d_active * swish).astype(bf16)
            own_copy(k).start()
            d_part = contract_last(stage[:, :width], gate_w[...]) + contract_last(
                stage[:, width : 2 * width], up_w[...]
            )
            out_part = contract_last(stage[:, 2 * width :], down_w[...])
            if k == 0:
                d_sum[...] = d_part
                out_sum[...] = out_part
            else:
                d_sum[...] += d_part
                out_sum[...] += out_part

        def swap(n):
            return remote(y_send.at[n], y_land.at[n], send_y.at[n], recv_y.at[n], "tensor", 1 - side)

        for r in range(size):
            gains_v[:, r * own_rows : (r + 1) * own_rows] = gains_ref[:, block_of(r)]
        gain_one, gain_two = gains_v[0:1, :], gains_v[1:2, :]

        def mean_scale(field):
            return lax.rsqrt(jnp.mean(field * field, -1, keepdims=True) + EPSILON)

        spans_of_rows = [slice(n, n + part) for n in range(0, rows, part)]

        def row_valid(span):
            at = lax.broadcasted_iota(jnp.int32, (part, 1), 0) + (place * rows + span.start)
            return (at < length_ref[0]).astype(f32)

        def keep_gain(which, value):
            for r in range(size):
                at = pl.multiple_of(partner[r] * own_rows + which * features, 128)
                vec[:, pl.ds(at, own_rows)] = value[:, r * own_rows : (r + 1) * own_rows]

        wait(ins[0])
        for span in spans_of_rows:
            field = tokens_rel[span, :].astype(f32)
            row_normed[span, :] = (field * mean_scale(field) * gain_one).astype(bf16)
        pl.semaphore_wait(barrier, size - 1 + 3 + 1)
        attention_send(0)
        attention_send(2)
        attention_send(1)
        attention_send(3)
        far_send(0)
        wait(ins[1])
        for span in spans_of_rows:
            row_fall[span, :] = (row_fall[span, :].astype(f32) * row_valid(span)).astype(bf16)
        for r in (2, 3, 1):
            trade(1, r).start()
        far_send(1)
        far_send(2)
        attention_wait(0).wait_recv()
        attention_send(6)
        bias[...] = key_bias_table(place, length_ref[0], keys, rows)
        attention_wait(1).wait_recv()
        attention_send(7)
        attention_arrived(6)
        attention_send(4)
        near(0).start()
        attention_wait(2).wait_recv()
        attention_wait(4).wait_recv()
        start(attention_copies(0))
        wait(rest)
        wait(attention_copies(0))
        queries = dot_nn(row_normed[...], weights[:, 0:heads_width]) + biases_ref[:, 0:heads_width]
        for head in range(heads):
            at = slice(head * HEAD_DIM, (head + 1) * HEAD_DIM)
            query_v[:, at] = turn(queries[:, at], cos_ref[...], sin_ref[...]).astype(bf16)
        others = dot_nn(row_normed[...], weights[:, heads_width:projected]) + biases_ref[:, heads_width:projected]
        pair_v[0:rows, :HEAD_DIM] = turn(others[:, :HEAD_DIM], cos_ref[...], sin_ref[...]).astype(bf16)
        pair_v[0:rows, HEAD_DIM:] = others[:, HEAD_DIM:].astype(bf16)

        def lend(s):
            return remote(
                pair_v.at[pl.ds(0, rows), :], pair_v.at[pl.ds(s * rows, rows), :], send_p.at[s - 1], recv_p.at[s - 1],
                "context", place + s,
            )

        for s in range(1, 4):
            pl.when(place + s <= 3)(lend(s).start)

            @pl.when(place < s)
            def _(s=s):
                pair_v[s * rows : (s + 1) * rows, :] = jnp.zeros((rows, pair_width), bf16)

        attention_arrived(7)
        attention_send(5)
        near(1).start()
        near(2).start()
        for s in range(1, 4):
            pl.when(place >= s)(lend(s).wait_recv)
        weight_straight(0)
        key_t[...] = pair_v[:, HEAD_DIM:].T
        for head in range(heads):
            at = slice(head * HEAD_DIM, (head + 1) * HEAD_DIM)
            scores = contract_last(pair_v[:, :HEAD_DIM], query_v[:, at]) * scale + bias[...]
            top = jnp.max(scores, 0, keepdims=True)
            raised = jnp.exp(scores - top)
            total = jnp.sum(raised, 0, keepdims=True)
            lse_ref[head : head + 1, :] = top + jnp.log(total)
            probs = (raised * (1.0 / total)).astype(bf16)
            mixed_at = slice(projected + head * HEAD_DIM, projected + (head + 1) * HEAD_DIM)
            last_v[:, mixed_at] = dot_nn(key_t[...], probs).T.astype(bf16)
        attention_wait(3).wait_recv()
        attention_wait(5).wait_recv()
        start(attention_copies(1))
        wait(attention_copies(1))
        y_send[3] = contract_last(last_v[:, projected:], weights[:, projected:attention_width]).astype(bf16)
        swap(3).start()
        weight_round(0)
        weight_straight(1)
        swap(3).wait_recv()
        for span in spans_of_rows:
            field = tokens_rel[span, :].astype(f32) + (
                y_send[3, span, :].astype(f32) + y_land[3, span, :].astype(f32)
            )
            hidden_rel[span, :] = field
            row_two[span, :] = (field * mean_scale(field) * gain_two).astype(bf16)
        def share(r):
            return remote(vec, vec_land.at[me], send_v.at[r - 1], recv_v.at[r - 1], "dp", partner[r])

        def spread(s):
            return remote(
                vec, total_land.at[place], send_w.at[s - 1], recv_w.at[s - 1], "context", lax.rem(place + s, 4)
            )

        far_send(3)
        feed(0)
        for r in (2, 3, 1):
            trade(0, r).start()
        weight_round(1)
        begin(0)
        weight_straight(2)
        weight_round(2)
        feed(1)
        turn_features(0)
        far_send(4)
        feed(2)
        turn_features(1)
        begin(1)
        weight_straight(3)
        gradients(0)
        weight_straight(4)

        @pl.when(middle)
        def _():
            line_in(0)
            line_in(1)

        weight_round(3)
        far_send(5)

        @pl.when(middle)
        def _():
            line_out(0)

        gradients(1)

        @pl.when(middle)
        def _():
            line_in(2)

        feed(3)

        @pl.when(middle)
        def _():
            line_out(1)
            line_in(3)

        begin(2)
        weight_straight(5)

        @pl.when(middle)
        def _():
            line_in(4)

        begin(3)

        @pl.when(middle)
        def _():
            line_in(5)

        weight_round(4)

        @pl.when(middle)
        def _():
            line_out(2)
            line_out(3)

        feed(4)

        @pl.when(middle)
        def _():
            line_out(4)

        gradients(2)

        @pl.when(middle)
        def _():
            line_out(5)

        far_send(6)

        @pl.when(middle)
        def _():
            line_in(6)
            line_in(7)

        begin(4)
        gradients(3)

        @pl.when(middle)
        def _():
            line_out(6)
            line_in(8)
            line_in(9)
            line_out(7)

        weight_round(5)
        weight_straight(6)

        @pl.when(middle)
        def _():
            line_out(8)

        feed(5)
        weight_round(6)

        @pl.when(middle)
        def _():
            line_in(10)

        feed(6)

        @pl.when(middle)
        def _():
            line_out(9)
            line_in(11)

        y_send[0] = d_sum[...].astype(bf16)
        swap(0).start()
        start(attention_copies(0) + attention_copies(1))

        @pl.when(middle)
        def _():
            line_out(10)

        begin(5)
        gradients(4)
        for r in (2, 3, 1):
            trade(2, r).start()

        @pl.when(middle)
        def _():
            line_out(11)
            line_in(12)

        y_send[1] = out_sum[...].astype(bf16)
        swap(0).wait_recv()
        swap(1).start()
        gain_sum = jnp.zeros((1, features), f32)
        for span in spans_of_rows:
            d_normed = y_send[0, span, :].astype(f32) + y_land[0, span, :].astype(f32)
            field = hidden_rel[span, :]
            r2 = mean_scale(field)
            gain_sum = gain_sum + jnp.sum(d_normed * field * r2, 0, keepdims=True)
            weighted = d_normed * gain_two
            d_hidden = (
                row_fall[span, :].astype(f32)
                + r2 * weighted
                - field * (r2 * r2 * r2) * jnp.mean(field * weighted, -1, keepdims=True)
            )
            d_sum[span, :] = d_hidden
            row_branch[span, :] = d_hidden.astype(bf16)
        keep_gain(1, gain_sum)
        for r in (2, 3, 1):
            trade(3, r).start()
        wait(attention_copies(0) + attention_copies(1))
        d_mixed[...] = dot_nn(row_branch[...], weights[:, projected:attention_width]).astype(bf16)

        @pl.when(middle)
        def _():
            line_in(13)
            line_out(12)

        key_t[...] = pair_v[:, :HEAD_DIM].T
        for head in range(heads):
            at = slice(head * HEAD_DIM, (head + 1) * HEAD_DIM)
            scores = contract_last(pair_v[:, :HEAD_DIM], query_v[:, at]) * scale + bias[...]
            probs = jnp.exp(scores - lse_ref[head : head + 1, :])
            d_probs = contract_last(pair_v[:, HEAD_DIM:], d_mixed[:, at])
            inside = jnp.sum(d_probs * probs, 0, keepdims=True)
            d_scores = (probs * (d_probs - inside)).astype(bf16)
            d_query = (dot_nn(key_t[...], d_scores) * scale).T
            last_v[:, at] = turn(d_query, cos_ref[...], -sin_ref[...]).astype(bf16)
            more_key = dot_nn(d_scores, query_v[:, at])
            more_value = dot_nn(probs.astype(bf16), d_mixed[:, at])
            if head == 0:
                d_key[...] = more_key
                d_value[...] = more_value
            else:
                d_key[...] += more_key
                d_value[...] += more_value
        d_rest[:, :HEAD_DIM] = (d_key[rows:, :] * scale).astype(bf16)
        d_rest[:, HEAD_DIM:] = d_value[rows:, :].astype(bf16)

        def give(s):
            return remote(
                d_rest.at[pl.ds((s - 1) * rows, rows), :], d_land.at[s - 1], send_k.at[s - 1], recv_k.at[s - 1],
                "context", place - s,
            )

        for s in range(1, 4):
            pl.when(place >= s)(give(s).start)

        @pl.when(middle)
        def _():
            line_in(14)

        begin(6)

        @pl.when(middle)
        def _():
            line_out(13)

        gradients(5)

        @pl.when(middle)
        def _():
            line_in(15)
            line_out(14)

        d_key[0:rows, :] = d_key[0:rows, :] * scale
        for s in range(1, 4):

            @pl.when(place + s <= 3)
            def _(s=s):
                give(s).wait_recv()
                d_key[0:rows, :] += d_land[s - 1, :, :HEAD_DIM].astype(f32)
                d_value[0:rows, :] += d_land[s - 1, :, HEAD_DIM:].astype(f32)

        last_v[:, heads_width : heads_width + HEAD_DIM] = turn(
            d_key[0:rows, :], cos_ref[...], -sin_ref[...]
        ).astype(bf16)
        last_v[:, heads_width + HEAD_DIM : projected] = d_value[0:rows, :].astype(bf16)
        own_copy(chunks).start()
        begin(chunks)
        swap(1).wait_recv()
        swap(1).wait_send()
        for span in spans_of_rows:
            whole = y_send[1, span, :].astype(f32) + y_land[1, span, :].astype(f32)
            y_land[1, span, :] = (row_valid(span) * (hidden_rel[span, :] + whole)).astype(bf16)

        def stored(n, target):
            return [
                local(y_land.at[n, :, cols(r)], target.at[:, block_of(r)], s_store.at[n, r]) for r in range(size)
            ]

        start(stored(1, output_hbm))

        @pl.when(middle)
        def _():
            line_in(16)
            line_out(15)

        turn_features(3)
        y_send[2] = contract_last(last_v[:, 0:projected], weights[:, 0:projected]).astype(bf16)
        swap(2).start()
        vec[:, 2 * features :] = jnp.sum(last_v[:, 0:projected].astype(f32), 0, keepdims=True)

        @pl.when(middle)
        def _():
            line_in(17)
            line_out(16)

        gradients(6)

        @pl.when(middle)
        def _():
            line_in(18)
            line_out(17)

        swap(2).wait_recv()
        swap(2).wait_send()
        gain_sum = jnp.zeros((1, features), f32)
        for span in spans_of_rows:
            d_normed = y_send[2, span, :].astype(f32) + y_land[2, span, :].astype(f32)
            field = tokens_rel[span, :].astype(f32)
            r1 = mean_scale(field)
            gain_sum = gain_sum + jnp.sum(d_normed * field * r1, 0, keepdims=True)
            weighted = d_normed * gain_one
            y_land[2, span, :] = (
                d_sum[span, :]
                + r1 * weighted
                - field * (r1 * r1 * r1) * jnp.mean(field * weighted, -1, keepdims=True)
            ).astype(bf16)
        start(stored(2, grad_tokens_hbm))
        keep_gain(0, gain_sum)


        @pl.when(middle)
        def _():
            line_in(19)
            line_out(18)

        turn_features(2)

        @pl.when(middle)
        def _():
            line_in(20)
            line_out(19)

        gradients(7)

        @pl.when(middle)
        def _():
            line_in(21)
            line_out(20)
            line_in(22)

        for r in range(1, size):
            share(r).start()
        vec_land[me] = vec[...]

        @pl.when(middle)
        def _():
            line_in(23)
            line_in(24)
            line_out(21)
            line_out(22)

        for r in range(1, size):
            share(r).wait()
        vec[...] = vec_land[0] + vec_land[1] + vec_land[2] + vec_land[3]
        for s in range(1, 4):
            spread(s).start()
        total_land[place] = vec[...]

        @pl.when(middle)
        def _():
            line_in(25)
            line_out(23)
            line_out(24)
            line_in(26)
            line_out(25)
            line_out(26)
            line_in(27)
            line_out(27)

        for s in range(1, 4):
            spread(s).wait()
        small_ref[...] = total_land[0] + total_land[1] + total_land[2] + total_land[3]

        @pl.when(middle)
        def _():
            for j in range(count):
                hop_out(j).wait_send()
                keep(j).wait()

        @pl.when(jnp.logical_not(middle))
        def _():
            for j in range(count - 3, count):
                hop_in(j).wait_send()
            for j in range(count):
                hop_out(j).wait_recv()

        wait(stored(1, output_hbm))
        wait(stored(2, grad_tokens_hbm))
        swap(0).wait_send()
        swap(3).wait_send()
        for n in range(8):
            attention_wait(n).wait_send()
        for which in range(3):
            near(which).wait_send()
        for k in range(chunks):
            far_wait(k).wait_send()
            if parts_of_x[k] < 6:
                far_round(k).wait_send()
            far_near(k).wait_send()
        for s in range(1, 4):
            pl.when(place >= s)(give(s).wait_send)
            pl.when(place + s <= 3)(lend(s).wait_send)
        for w in range(4):
            for r in range(1, size):
                trade(w, r).wait_send()
        for u in range(units):
            for n in range(3):
                transfer(u, n).wait_send()

    dma = pltpu.SemaphoreType.DMA
    shape = jax.ShapeDtypeStruct
    wide, last = (3 * chunks, own_rows, width), (last_width // halfway, own_rows, halfway)
    results = pl.pallas_call(
        kernel,
        out_shape=(
            shape((rows, features), bf16),
            shape((rows, features), bf16),
            shape((1, small_width), f32),
            shape(wide, bf16),
            shape(last, bf16),
            shape((size - 1, units, rows, 3 * width), bf16),
            shape((units, rows, 3 * width), bf16),
            shape(wide, bf16),
            shape(last, bf16),
            shape((size - 1, own_rows, attention_width), bf16),
            shape((3, own_rows, units_all), bf16),
            shape((2, chunks, own_rows, 3 * width), bf16),
        ),
        in_specs=[SMEM, VMEM, VMEM] + [ANY] * (3 + 4 + 3),
        out_specs=(ANY, ANY, VMEM) + (ANY,) * 9,
        scratch_shapes=[
            pltpu.VMEM(wide, bf16),
            pltpu.VMEM(last, bf16),
            pltpu.VMEM((2, own_rows, max(widths)), bf16),
            pltpu.VMEM((2, own_rows, max(widths)), bf16),
            pltpu.VMEM((tokens_all, 3 * width), bf16),
            pltpu.VMEM((features, 3 * width), bf16),
            pltpu.VMEM((4, own_rows, tokens_all), bf16),
            pltpu.VMEM((4, size - 1, rows, own_rows), bf16),
            pltpu.VMEM((rows, features), bf16),
            pltpu.VMEM((rows, features), bf16),
            pltpu.VMEM((rows, features), bf16),
            pltpu.VMEM((rows, features), bf16),
            pltpu.VMEM((rows, features), f32),
            pltpu.VMEM((rows, features), bf16),
            pltpu.VMEM((rows, features), f32),
            pltpu.VMEM((rows, features), f32),
            pltpu.VMEM((4, rows, features), bf16),
            pltpu.VMEM((4, rows, features), bf16),
            pltpu.VMEM((2, rows, 3 * width), bf16),
            pltpu.VMEM((rows, heads_width), bf16),
            pltpu.VMEM((keys, pair_width), bf16),
            pltpu.VMEM((rows, last_width), bf16),
            pltpu.VMEM((keys, rows), f32),
            pltpu.VMEM((HEAD_DIM, keys), bf16),
            pltpu.VMEM((keys, HEAD_DIM), f32),
            pltpu.VMEM((keys, HEAD_DIM), f32),
            pltpu.VMEM((rows, heads_width), bf16),
            pltpu.VMEM((keys - rows, pair_width), bf16),
            pltpu.VMEM((3, rows, pair_width), bf16),
            pltpu.VMEM((1, small_width), f32),
            pltpu.VMEM((4, 1, small_width), f32),
            pltpu.VMEM((4, 1, small_width), f32),
            pltpu.VMEM((2, features), f32),
            pltpu.VMEM((2, rows, HEAD_DIM), f32),
            pltpu.VMEM((8, rows), f32),
            dma((2, size)),
            dma((3, size)),
            dma((units,)),
            dma((1,)),
            dma((3, units)),
            dma((3, units)),
            dma((count,)),
            dma((count,)),
            dma((count,)),
            dma((count,)),
            dma((2, 2)),
            dma((count,)),
            dma((size,)),
            dma((4, size - 1)),
            dma((4, size - 1)),
            dma((4,)),
            dma((4,)),
            dma((3,)),
            dma((3,)),
            dma((size - 1,)),
            dma((size - 1,)),
            dma((3,)),
            dma((3,)),
            dma((3, size)),
            dma((8,)),
            dma((8,)),
            dma((3,)),
            dma((3,)),
            dma((chunks,)),
            dma((chunks,)),
            dma((chunks,)),
            dma((chunks,)),
            dma((chunks,)),
            dma((chunks,)),
            dma((3,)),
            dma((3,)),
            dma((4,)),
        ],
        compiler_params=pltpu.CompilerParams(
            collective_id=0, has_side_effects=True, vmem_limit_bytes=60 << 20
        ),
        name="layer",
    )(
        length, gains, biases, tokens, grad_out, tables, *attention_own, *feed_own,
    )
    return results[:5]


def finish(wide, last, output, grad_tokens, small, spans, small_spans):
    blocks, own_rows, width = wide.shape
    halfway = last.shape[2]
    chunks = blocks // 3
    f32 = jnp.float32

    def kernel(wide_ref, last_ref, small_ref, output_ref, tokens_ref, *refs):
        outs = refs

        @pl.when(pl.program_id(0) == 0)
        def _():
            outs[-2][...] = output_ref[...]
            outs[-1][...] = tokens_ref[...]
            for (start, size), out in zip(spans, outs[3:]):
                done = 0
                while done < size:
                    half, at = divmod(start + done, halfway)
                    step = min(size - done, halfway - at)
                    out[:, done : done + step] = last_ref[half, :, at : at + step].astype(f32)
                    done += step
            for (start, size), out in zip(small_spans, outs[3 + len(spans) :]):
                out[...] = small_ref[0, start : start + size]

        for n in range(3):
            outs[n][...] = wide_ref[n].astype(f32)

    def whole(shape):
        return pl.BlockSpec(shape, lambda k: (0,) * len(shape))

    shape = jax.ShapeDtypeStruct
    return pl.pallas_call(
        kernel,
        grid=(chunks,),
        out_shape=[shape((own_rows, chunks * width), f32)] * 3
        + [shape((own_rows, size), f32) for _, size in spans]
        + [shape((size,), f32) for _, size in small_spans]
        + [shape(output.shape, output.dtype)] * 2,
        in_specs=[
            pl.BlockSpec((3, own_rows, width), lambda k: (k, 0, 0)),
            whole(last.shape),
            whole(small.shape),
            whole(output.shape),
            whole(output.shape),
        ],
        out_specs=[pl.BlockSpec((own_rows, width), lambda k: (0, k))] * 3
        + [whole((own_rows, size)) for _, size in spans]
        + [whole((size,)) for _, size in small_spans]
        + [whole(output.shape)] * 2,
        compiler_params=plain_params(60 << 20),
        name="finish",
    )(wide, last, small, output, grad_tokens)


def rotary_tables(position_count):
    half = HEAD_DIM // 2
    inverse = np.exp(np.arange(half) * (-2.0 * math.log(ROPE_BASE) / HEAD_DIM))
    angles = np.arange(position_count)[:, None] * inverse[None, :]
    cosine, sine = np.cos(angles), np.sin(angles)
    return np.stack(
        [np.concatenate([cosine, cosine], 1), np.concatenate([-sine, sine], 1)]
    ).astype(np.float32)


PARTS_OF_X = (3, 3, 3, 3, 4, 4, 6)


def chunk_edges(columns):
    tiles = columns // 128
    count = next((n for n in (7, 5, 4, 6, 3, 2) if tiles % n == 0), 1)
    width = columns // count
    return [(n * width, width) for n in range(count)]


def local(
    tokens,
    lengths,
    gain_one,
    w_query,
    b_query,
    key_weight,
    key_bias,
    value_weight,
    value_bias,
    w_out,
    gain_two,
    w_gate,
    w_up,
    w_down,
    grad_out,
):
    bf16, f32 = jnp.bfloat16, jnp.float32
    seq_count, block_len, model_width = tokens.shape
    row_count = seq_count * block_len
    query_cols = w_query.shape[1]
    key_cols = key_weight.shape[1]
    unit_cols = w_gate.shape[1]
    own_rows = w_query.shape[0]
    head_count = query_cols // HEAD_DIM
    kv_count = key_cols // HEAD_DIM
    query_group_width = head_count // kv_count
    size = lax.axis_size("dp")
    me = lax.axis_index("dp")
    blocks_along = lax.axis_size("context")
    place = lax.axis_index("context")
    parity = place % 2 if blocks_along % 2 == 0 and own_rows % 32 == 0 else None

    edges = chunk_edges(unit_cols)
    if (
        size == 4
        and blocks_along == 4
        and lax.axis_size("tensor") == 2
        and own_rows % 384 == 0
        and row_count % 64 == 0
        and len(edges) == len(PARTS_OF_X)
        and kv_count == 1
        and seq_count == 1
    ):
        f32 = jnp.float32
        output, grad_tokens, small, feed_sums, last_sums = layer(
            lengths,
            tokens.reshape(row_count, model_width),
            grad_out.reshape(row_count, model_width),
            jnp.stack([gain_one, gain_two]).astype(f32),
            jnp.concatenate([b_query, key_bias, value_bias]).astype(f32)[None, :],
            rotary_tables(block_len * blocks_along),
            (w_query, key_weight, value_weight, w_out),
            (w_gate, w_up, w_down),
            edges[0][1],
            PARTS_OF_X,
        )
        turned_at, at = query_cols + key_cols, 2 * model_width
        *grads, output, grad_tokens = finish(
            feed_sums,
            last_sums,
            output,
            grad_tokens,
            small,
            [(0, query_cols), (query_cols, key_cols), (turned_at, key_cols), (turned_at + key_cols, query_cols)],
            [
                (0, model_width),
                (at, query_cols),
                (at + query_cols, key_cols),
                (at + turned_at, key_cols),
                (model_width, model_width),
            ],
        )
        return (
            output.reshape(seq_count, block_len, model_width),
            grad_tokens.reshape(seq_count, block_len, model_width),
            grads[7],
            grads[3],
            grads[8],
            grads[4],
            grads[9],
            grads[5],
            grads[10],
            grads[6],
            grads[11],
            *grads[:3],
        )

    def relative(field):
        return swap_blocks([field[:, n * own_rows : (n + 1) * own_rows] for n in range(size)], me)

    def absolute(blocks):
        return jnp.concatenate(swap_blocks(blocks, me), 1)

    def dot_rows(blocks, weights):
        return jnp.dot(
            jnp.concatenate(blocks, 1), jnp.concatenate(weights, 0), preferred_element_type=f32
        )

    lanes = {name: Lane() for name in ("x", "z", "hop1", "hop2", "hop3")}
    attention_weights = gather_pieces(
        jnp.concatenate([w_query, key_weight, value_weight], 1), size, lanes
    )
    out_weights = gather_pieces(w_out, size, lanes, parity)
    edges = chunk_edges(unit_cols)
    feed_weights = []
    early = len(edges) - 2

    feed_own = (w_gate, w_up, w_down)
    feed_near = tuple(lax.ppermute(w, "dp", xor_pairs(size, 1)) for w in feed_own)

    def fetch(start, width):
        own = jnp.concatenate([w[:, start : start + width] for w in feed_own], 1)
        far = far_pieces(own, size, lanes, parity)
        sources = []
        for r in range(size):
            if r < 2:
                sources.append(feed_own if r == 0 else feed_near)
            elif r % 2 == 0:
                sources.append((far[r],))
            else:
                sources.append((lax.ppermute(far[r - 1], "dp", xor_pairs(size, 1)),))
        feed_weights.append(sources)

    for start, width in edges[:early]:
        fetch(start, width)

    positions = place * block_len + jnp.arange(block_len, dtype=jnp.int32)
    position_count = block_len * blocks_along
    valid_rows = (positions[None, :] < lengths[:, None]).astype(f32).reshape(row_count, 1)
    facts = jnp.stack([place.astype(jnp.int32), lengths[0]])
    half = HEAD_DIM // 2
    inverse = jnp.exp(jnp.arange(half, dtype=f32) * (-2.0 * math.log(ROPE_BASE) / HEAD_DIM))
    angles = positions.astype(f32)[:, None] * inverse[None, :]
    cosine = jnp.concatenate([jnp.cos(angles)] * 2, 1)
    sine = jnp.concatenate([-jnp.sin(angles), jnp.sin(angles)], 1)
    gain_first = gain_one.astype(f32)
    gain_second = gain_two.astype(f32)
    inputs = tokens.reshape(row_count, model_width).astype(f32)
    scale_one = lax.rsqrt(jnp.mean(inputs * inputs, -1, keepdims=True) + EPSILON)
    normalized_input = (inputs * scale_one * gain_first).astype(bf16)
    normed_blocks = relative(normalized_input)
    projected = dot_rows(normed_blocks, attention_weights) + jnp.concatenate(
        [b_query, key_bias, value_bias]
    ).astype(f32)
    turned = query_cols + key_cols

    def turn_heads(field, sine_rows):
        grid = field.reshape(row_count, field.shape[1] // HEAD_DIM, HEAD_DIM)
        swapped = jnp.concatenate([grid[..., half:], grid[..., :half]], -1)
        grid = grid * cosine[:, None, :] + swapped * sine_rows[:, None, :]
        return grid.reshape(field.shape).astype(bf16)

    turned_rows = turn_heads(projected[:, :turned], sine)
    query_rot = turned_rows[:, :query_cols]
    pair_rows = jnp.concatenate([turned_rows[:, query_cols:], projected[:, turned:].astype(bf16)], 1)
    pair_all = [pair_rows]
    for shift in range(1, blocks_along):
        pair_all.append(
            lax.ppermute(
                pair_rows, "context", [(n, n + shift) for n in range(blocks_along - shift)]
            )
        )
    pair_all = jnp.concatenate(pair_all, 0)
    mixed_heads, lse = attend(facts, query_rot, pair_all)
    full_out = jnp.concatenate(out_weights, 0)
    branch = contract_last(mixed_heads, full_out)
    branch = absolute([branch[:, r * own_rows : (r + 1) * own_rows] for r in range(size)])
    hidden = inputs + tensor_sum(branch)
    scale_two = lax.rsqrt(jnp.mean(hidden * hidden, -1, keepdims=True) + EPSILON)
    normed_two = (hidden * scale_two * gain_second).astype(bf16)
    fall_grad = grad_out.reshape(row_count, model_width).astype(f32) * valid_rows
    fall_low = fall_grad.astype(bf16)
    fall_blocks = relative(fall_low)
    two_blocks = relative(normed_two)
    traded_early = trade_blocks(
        [jnp.concatenate([a, b], 1) for a, b in zip(normed_blocks, fall_blocks)], size
    )
    traded_early = jnp.concatenate(traded_early, 0).T
    normed_features, fall_features = traded_early[:own_rows], traded_early[own_rows:]
    two_features = jnp.concatenate(trade_blocks(two_blocks, size), 0).T
    two_row = jnp.concatenate(two_blocks, 1)
    fall_row = jnp.concatenate(fall_blocks, 1)

    feed_out, d_normed_two = None, None
    feed_units = []
    for turn_at, (start, width) in enumerate(edges):
        acts, d_normed_two, feed_out = feed_chunk(
            two_row, fall_row, feed_weights[turn_at], start, width, d_normed_two, feed_out
        )
        if turn_at < 0:
            acts = gather_pieces(acts, size, lanes)
        feed_units.append(acts)
        if turn_at == 0:
            for edge in edges[early:]:
                fetch(*edge)

    def split(field):
        return [field[:, r * own_rows : (r + 1) * own_rows] for r in range(size)]

    d_normed_two = tensor_sum(absolute(split(d_normed_two)))
    result = valid_rows * (hidden + tensor_sum(absolute(split(feed_out))))
    output = result.astype(bf16).reshape(seq_count, block_len, model_width)
    gain_two_grad = jnp.sum(d_normed_two * hidden * scale_two, 0)
    d_hidden = fall_grad + norm_back(hidden, scale_two, gain_second, d_normed_two)
    d_branch = d_hidden.astype(bf16)
    branch_blocks = relative(d_branch)
    branch_features = jnp.concatenate(trade_blocks(branch_blocks, size), 0).T
    d_mixed = jnp.dot(
        jnp.concatenate(branch_blocks, 1), full_out, preferred_element_type=f32
    ).astype(bf16)
    d_query_low, d_own, d_rest = attend_back(
        facts, query_rot, pair_all, lse, d_mixed, cosine, sine
    )
    for shift in range(1, blocks_along):
        d_own = d_own + lax.ppermute(
            d_rest[(shift - 1) * block_len : shift * block_len],
            "context",
            [(n, n - shift) for n in range(shift, blocks_along)],
        ).astype(f32)
    d_key_low = turn_heads(d_own[:, :key_cols], -sine)
    d_value_low = d_own[:, key_cols:].astype(bf16)
    d_projected = jnp.concatenate([d_query_low, d_key_low, d_value_low], 1)
    d_normed = contract_last(d_projected, jnp.concatenate(attention_weights, 0))
    d_normed = tensor_sum(absolute(split(d_normed)))
    gain_one_grad = jnp.sum(d_normed * inputs * scale_one, 0)
    d_inputs = d_hidden + norm_back(inputs, scale_one, gain_first, d_normed)
    grad_tokens = d_inputs.astype(bf16).reshape(seq_count, block_len, model_width)
    gain_two_grad = small_total(gain_two_grad)
    small = small_total(
        jnp.concatenate([gain_one_grad, jnp.sum(d_projected.astype(f32), 0)])
    )
    projected_width = d_projected.shape[1]
    last = jnp.concatenate([d_projected, mixed_heads], 1)
    halfway = last.shape[1] // 2
    blocks = [
        [[(0, 0, width)], [(0, width, width)], [(1, 2 * width, width)]] for _, width in edges
    ] + [
        [
            [(2, 0, halfway)],
            [(2, halfway, projected_width - halfway), (3, projected_width, query_cols)],
        ]
    ]
    sums = gather_and_sum(
        feed_units + [last],
        [two_features, fall_features, normed_features, branch_features],
        blocks,
        size,
    )

    def columns(which):
        stack = sums[which][0]
        return jnp.concatenate(
            [stack[3 * n + which].astype(f32) for n in range(len(edges))], 1
        )

    stack = sums[-1][0]
    last_grad = jnp.concatenate([stack[0], stack[1]], 1).astype(f32)
    projected_grad, out_grad = last_grad[:, :projected_width], last_grad[:, projected_width:]

    low, high = model_width + query_cols, model_width + query_cols + key_cols
    return (
        output,
        grad_tokens,
        small[:model_width],
        projected_grad[:, :query_cols],
        small[model_width:low],
        projected_grad[:, query_cols : query_cols + key_cols],
        small[low:high],
        projected_grad[:, query_cols + key_cols :],
        small[high:],
        out_grad,
        gain_two_grad,
        columns(0),
        columns(1),
        columns(2),
    )


def solution(mesh):
    in_specs = (
        P("dp", "context", None),
        P("dp"),
        P(),
        P("dp", "tensor"),
        P("tensor"),
        P("dp", "tensor"),
        P("tensor"),
        P("dp", "tensor"),
        P("tensor"),
        P("dp", "tensor"),
        P(),
        P("dp", "tensor"),
        P("dp", "tensor"),
        P("dp", "tensor"),
        P("dp", "context", None),
    )
    out_specs = (
        P("dp", "context", None),
        P("dp", "context", None),
        P(),
        P("dp", "tensor"),
        P("tensor"),
        P("dp", "tensor"),
        P("tensor"),
        P("dp", "tensor"),
        P("tensor"),
        P("dp", "tensor"),
        P(),
        P("dp", "tensor"),
        P("dp", "tensor"),
        P("dp", "tensor"),
    )
    return jax.shard_map(local, mesh=mesh, in_specs=in_specs, out_specs=out_specs, check_vma=False)
```

```python
import math

import jax
import jax.numpy as jnp
import numpy as np
from jax import lax
from jax.experimental import pallas as pl
from jax.experimental.pallas import tpu as pltpu
from jax.sharding import PartitionSpec as P

HEAD_DIM = 128


EPSILON = 1e-06
ROPE_BASE = 1000000.0


def xor_pairs(size, mask):
    return [(i, i ^ mask) for i in range(size)]


class Lane:
    def __init__(self, depth=1):
        self.sent = []
        self.depth = depth

    def send(self, array, axis, pairs):
        if len(self.sent) >= self.depth:
            array, _ = lax.optimization_barrier((array, self.sent[-self.depth]))
        got = lax.ppermute(array, axis, pairs)
        self.sent.append(got)
        return got


def far_masks(size):
    masks, mask = [], 2
    while mask < size:
        masks.append(mask)
        mask *= 2
    return masks


def swap_blocks(blocks, me):
    mask = 1
    while mask < len(blocks):
        flag = (me & mask) != 0
        blocks = [jnp.where(flag, blocks[r ^ mask], blocks[r]) for r in range(len(blocks))]
        mask *= 2
    return blocks


def far_half(piece, mask, size, parity, lanes):
    half = piece.shape[0] // 2
    sent = lax.dynamic_slice_in_dim(piece, half * parity, half, 0)
    straight = lanes["x"].send(sent, "dp", xor_pairs(size, mask))
    other = lanes["z"].send(straight, "context", xor_pairs(lax.axis_size("context"), 1))
    first = jnp.where(parity == 0, straight, other)
    second = jnp.where(parity == 0, other, straight)
    return jnp.concatenate([first, second], 0)


def far_pieces(own, size, lanes, parity=None):
    pieces = {0: own}
    for mask in far_masks(size):
        for r in list(pieces):
            if parity is None:
                pieces[r ^ mask] = lanes["x"].send(pieces[r], "dp", xor_pairs(size, mask))
            else:
                pieces[r ^ mask] = far_half(pieces[r], mask, size, parity, lanes)
    return pieces


def gather_pieces(own, size, lanes, parity=None):
    pieces = far_pieces(own, size, lanes, parity)
    for r in list(pieces):
        pieces[r ^ 1] = lax.ppermute(pieces[r], "dp", xor_pairs(size, 1))
    return [pieces[r] for r in range(size)]


def trade_blocks(blocks, size):
    return [blocks[0]] + [
        lax.ppermute(blocks[r], "dp", xor_pairs(size, r)) for r in range(1, size)
    ]


def tensor_sum(part):
    sent = part.astype(jnp.bfloat16)
    size = lax.axis_size("tensor")
    if size == 2:
        other = lax.ppermute(sent, "tensor", [(0, 1), (1, 0)])
        return sent.astype(jnp.float32) + other.astype(jnp.float32)
    return lax.psum(part, "tensor")


def line_sum(part, lanes):
    place = lax.axis_index("context")
    if lax.axis_size("context") != 4:
        return lax.psum(part.astype(jnp.float32), "context")
    got = lanes["hop1"].send(part, "context", [(0, 1), (3, 2)])
    pair = (part.astype(jnp.float32) + got.astype(jnp.float32)).astype(jnp.bfloat16)
    got = lanes["hop2"].send(pair, "context", [(1, 2), (2, 1)])
    total = (pair.astype(jnp.float32) + got.astype(jnp.float32)).astype(jnp.bfloat16)
    got = lanes["hop3"].send(total, "context", [(1, 0), (2, 3)])
    ends = (place == 0) | (place == 3)
    return jnp.where(ends, got, total).astype(jnp.float32)


def small_total(vector):
    for axis in ("dp", "context"):
        size, mask = lax.axis_size(axis), 1
        while mask < size:
            vector = vector + lax.ppermute(vector, axis, xor_pairs(size, mask))
            mask *= 2
    return vector


def contract_last(left, right):
    return lax.dot_general(
        left, right, (((1,), (1,)), ((), ())), preferred_element_type=jnp.float32
    )


def norm_back(field, scale_rows, gain, d_normed):
    weighted = d_normed * gain
    cubed = scale_rows * scale_rows * scale_rows
    return scale_rows * weighted - field * cubed * jnp.mean(field * weighted, -1, keepdims=True)


ANY = pl.BlockSpec(memory_space=pl.ANY)
VMEM = pl.BlockSpec(memory_space=pltpu.VMEM)
SMEM = pl.BlockSpec(memory_space=pltpu.SMEM)


def plain_params(limit):
    return pltpu.CompilerParams(vmem_limit_bytes=limit)


def dot_nn(left, right):
    return jnp.dot(left, right, preferred_element_type=jnp.float32)


def feed_chunk(two_row, fall_row, sources, start, width, d_sum, out_sum):
    rows, features = two_row.shape
    bf16, f32 = jnp.bfloat16, jnp.float32
    flat, layout = [], []
    for source in sources:
        layout.append(len(source))
        flat.extend(source)
    first = d_sum is None
    held = [] if first else [d_sum, out_sum]

    def kernel(*refs):
        refs = list(refs)
        two_ref, fall_ref = refs[:2]
        given = refs[2 : 2 + len(flat)]
        at = 2 + len(flat)
        sums = refs[at : at + len(held)]
        at += len(held)
        acts_ref, d_ref, out_ref, gate_w, up_w, down_w, sems = refs[at:]
        copies = [[], [], []]
        place, taken = 0, 0
        for kind in layout:
            depth = given[taken].shape[0]
            for which, scratch in enumerate((gate_w, up_w, down_w)):
                if kind == 3:
                    view = given[taken + which].at[:, pl.ds(start, width)]
                else:
                    view = given[taken].at[:, pl.ds(which * width, width)]
                copy = pltpu.make_async_copy(
                    view,
                    scratch.at[pl.ds(place, depth), :],
                    sems.at[which, len(copies[which])],
                )
                copies[which].append(copy)
            place += depth
            taken += kind
        for group in copies:
            for copy in group:
                copy.start()
        for copy in copies[0]:
            copy.wait()
        gate = dot_nn(two_ref[...], gate_w[...])
        for copy in copies[1]:
            copy.wait()
        up = dot_nn(two_ref[...], up_w[...])
        for copy in copies[2]:
            copy.wait()
        d_active = dot_nn(fall_ref[...], down_w[...])
        sigmoid = jax.nn.sigmoid(gate)
        swish = gate * sigmoid
        acts_ref[:, 2 * width :] = (swish * up).astype(bf16)
        acts_ref[:, :width] = (d_active * up * sigmoid * (1.0 + gate * (1.0 - sigmoid))).astype(bf16)
        acts_ref[:, width : 2 * width] = (d_active * swish).astype(bf16)
        d_part = contract_last(acts_ref[:, :width], gate_w[...]) + contract_last(
            acts_ref[:, width : 2 * width], up_w[...]
        )
        out_part = contract_last(acts_ref[:, 2 * width :], down_w[...])
        if first:
            d_ref[...] = d_part
            out_ref[...] = out_part
        else:
            d_ref[...] = sums[0][...] + d_part
            out_ref[...] = sums[1][...] + out_part

    weight_bytes = 6 * features * width
    return pl.pallas_call(
        kernel,
        out_shape=(
            jax.ShapeDtypeStruct((rows, 3 * width), bf16),
            jax.ShapeDtypeStruct((rows, features), f32),
            jax.ShapeDtypeStruct((rows, features), f32),
        ),
        in_specs=[VMEM, VMEM] + [ANY] * len(flat) + [VMEM] * len(held),
        out_specs=(VMEM, VMEM, VMEM),
        scratch_shapes=[pltpu.VMEM((features, width), bf16)] * 3
        + [pltpu.SemaphoreType.DMA((3, len(sources)))],
        compiler_params=plain_params(40 << 20),
        cost_estimate=pl.CostEstimate(
            flops=12 * rows * features * width,
            bytes_accessed=weight_bytes + 20 * rows * features + 6 * rows * width,
            transcendentals=rows * width,
        ),
        name="feed_chunk",
    )(two_row, fall_row, *flat, *held)


def grad_block(features, pieces, spans):
    bf16 = jnp.bfloat16
    depth, columns = pieces[0].shape
    tokens = features[0].shape[1]
    own = features[0].shape[0]
    total = sum(w for _, w in spans)

    def kernel(*refs):
        refs = list(refs)
        feature_refs = refs[: len(features)]
        given = refs[len(features) : len(features) + len(pieces)]
        out_ref, held, sems = refs[len(features) + len(pieces) :]
        copies = [
            pltpu.make_async_copy(ref, held.at[pl.ds(n * depth, depth), :], sems.at[n])
            for n, ref in enumerate(given)
        ]
        for copy in copies:
            copy.start()
        for copy in copies:
            copy.wait()
        for ref, (start, width) in zip(feature_refs, spans):
            out_ref[:, start : start + width] = dot_nn(
                ref[...], held[:, start : start + width]
            ).astype(bf16)

    return pl.pallas_call(
        kernel,
        out_shape=jax.ShapeDtypeStruct((own, total), bf16),
        in_specs=[VMEM] * len(features) + [ANY] * len(pieces),
        out_specs=VMEM,
        scratch_shapes=[
            pltpu.VMEM((tokens, columns), bf16),
            pltpu.SemaphoreType.DMA((len(pieces),)),
        ],
        compiler_params=plain_params(40 << 20),
        cost_estimate=pl.CostEstimate(
            flops=2 * own * tokens * total,
            bytes_accessed=2 * (tokens * columns + own * total + own * tokens),
            transcendentals=0,
        ),
        name="grad_block",
    )(*features, *pieces)


def key_bias_table(place, length, keys, block_len):
    key_at = lax.broadcasted_iota(jnp.int32, (keys, block_len), 0)
    query_at = lax.broadcasted_iota(jnp.int32, (keys, block_len), 1) + place * block_len
    shift = key_at // block_len
    key_at = key_at - shift * block_len + (place - shift) * block_len
    seen = (key_at <= query_at) & (key_at < length) & (key_at >= 0)
    return jnp.where(seen, 0.0, -1e30).astype(jnp.float32)


def attend(facts, query, pair):
    rows, width = query.shape
    keys = pair.shape[0]
    heads = width // HEAD_DIM
    bf16, f32 = jnp.bfloat16, jnp.float32
    scale = 1.0 / math.sqrt(HEAD_DIM)

    def kernel(facts_ref, query_ref, pair_ref, mixed_ref, lse_ref, bias, value_t):
        bias[...] = key_bias_table(facts_ref[0], facts_ref[1], keys, rows)
        value_t[...] = pair_ref[:, HEAD_DIM:].T
        lse_ref[...] = jnp.zeros_like(lse_ref)
        for head in range(heads):
            cols = slice(head * HEAD_DIM, (head + 1) * HEAD_DIM)
            scores = contract_last(pair_ref[:, :HEAD_DIM], query_ref[:, cols]) * scale + bias[...]
            top = jnp.max(scores, 0, keepdims=True)
            raised = jnp.exp(scores - top)
            total = jnp.sum(raised, 0, keepdims=True)
            lse_ref[head : head + 1, :] = top + jnp.log(total)
            probs = (raised * (1.0 / total)).astype(bf16)
            mixed_ref[:, cols] = dot_nn(value_t[...], probs).T.astype(bf16)

    return pl.pallas_call(
        kernel,
        out_shape=(
            jax.ShapeDtypeStruct((rows, width), bf16),
            jax.ShapeDtypeStruct((8, rows), f32),
        ),
        in_specs=[SMEM, VMEM, VMEM],
        out_specs=(VMEM, VMEM),
        scratch_shapes=[pltpu.VMEM((keys, rows), f32), pltpu.VMEM((HEAD_DIM, keys), bf16)],
        compiler_params=plain_params(40 << 20),
        cost_estimate=pl.CostEstimate(
            flops=4 * rows * keys * width + 12 * heads * rows * keys * 100,
            bytes_accessed=4 * rows * width + 4 * keys * HEAD_DIM,
            transcendentals=heads * rows * keys,
        ),
        name="attend",
    )(facts, query, pair)


def turn(field, cosine, sine):
    return field * cosine + pltpu.roll(field, HEAD_DIM // 2, 1) * sine


def attend_back(facts, query, pair, lse, d_mixed, cosine, sine):
    rows, width = query.shape
    keys = pair.shape[0]
    heads = width // HEAD_DIM
    bf16, f32 = jnp.bfloat16, jnp.float32
    scale = 1.0 / math.sqrt(HEAD_DIM)

    def kernel(facts_ref, query_ref, pair_ref, lse_ref, d_mixed_ref, cos_ref, sin_ref, d_query_ref, d_own_ref, d_rest_ref, bias, key_t, d_key, d_value):
        bias[...] = key_bias_table(facts_ref[0], facts_ref[1], keys, rows)
        key_t[...] = pair_ref[:, :HEAD_DIM].T
        for head in range(heads):
            cols = slice(head * HEAD_DIM, (head + 1) * HEAD_DIM)
            scores = contract_last(pair_ref[:, :HEAD_DIM], query_ref[:, cols]) * scale + bias[...]
            probs = jnp.exp(scores - lse_ref[head : head + 1, :])
            d_probs = contract_last(pair_ref[:, HEAD_DIM:], d_mixed_ref[:, cols])
            inner = jnp.sum(d_probs * probs, 0, keepdims=True)
            d_scores = (probs * (d_probs - inner)).astype(bf16)
            d_query = (dot_nn(key_t[...], d_scores) * scale).T
            d_query_ref[:, cols] = turn(d_query, cos_ref[...], -sin_ref[...]).astype(bf16)
            more_key = dot_nn(d_scores, query_ref[:, cols])
            more_value = dot_nn(probs.astype(bf16), d_mixed_ref[:, cols])
            if head == 0:
                d_key[...] = more_key
                d_value[...] = more_value
            else:
                d_key[...] += more_key
                d_value[...] += more_value
        d_own_ref[:, :HEAD_DIM] = d_key[:rows, :] * scale
        d_own_ref[:, HEAD_DIM:] = d_value[:rows, :]
        d_rest_ref[:, :HEAD_DIM] = (d_key[rows:, :] * scale).astype(bf16)
        d_rest_ref[:, HEAD_DIM:] = d_value[rows:, :].astype(bf16)

    return pl.pallas_call(
        kernel,
        out_shape=(
            jax.ShapeDtypeStruct((rows, width), bf16),
            jax.ShapeDtypeStruct((rows, 2 * HEAD_DIM), f32),
            jax.ShapeDtypeStruct((keys - rows, 2 * HEAD_DIM), bf16),
        ),
        in_specs=[SMEM] + [VMEM] * 6,
        out_specs=(VMEM, VMEM, VMEM),
        scratch_shapes=[
            pltpu.VMEM((keys, rows), f32),
            pltpu.VMEM((HEAD_DIM, keys), bf16),
            pltpu.VMEM((keys, HEAD_DIM), f32),
            pltpu.VMEM((keys, HEAD_DIM), f32),
        ],
        compiler_params=plain_params(40 << 20),
        cost_estimate=pl.CostEstimate(
            flops=10 * rows * keys * width + 12 * heads * rows * keys * 200,
            bytes_accessed=8 * rows * width + 8 * keys * HEAD_DIM,
            transcendentals=heads * rows * keys,
        ),
        name="attend_back",
    )(facts, query, pair, lse, d_mixed, cosine, sine)


MESH = pl.DeviceIdType.MESH


def flipped(index, mask):
    return index + mask - 2 * mask * ((index // mask) % 2)


def gather_and_sum(units, features, blocks, size):
    bf16, f32 = jnp.bfloat16, jnp.float32
    count = len(units)
    gathered = [isinstance(u, (list, tuple)) for u in units]
    flat = [a for u in units for a in (u if isinstance(u, (list, tuple)) else [u])]
    starts, at = [], 0
    for u in units:
        starts.append(at)
        at += len(u) if isinstance(u, (list, tuple)) else 1
    rows = flat[0].shape[0]
    widest = max(a.shape[1] for a in flat)
    own_rows, tokens = features[0].shape
    widths = []
    where = []
    counts = {}
    for u, group in enumerate(blocks):
        for spans in group:
            width = sum(w for _, _, w in spans)
            if width not in counts:
                counts[width] = 0
                widths.append(width)
            where.append((u, spans, widths.index(width), counts[width]))
            counts[width] += 1
    block_count = len(where)
    steps = []
    held = [0]
    for mask in far_masks(size):
        for r in list(held):
            steps.append((r, mask))
            held.append(r ^ mask)
    for r in list(held):
        steps.append((r, 1))
    arrival = {r ^ mask: n for n, (r, mask) in enumerate(steps)}
    ahead = 2

    def kernel(*refs):
        refs = list(refs)
        unit_refs, refs = refs[: len(flat)], refs[len(flat) :]
        feature_refs, refs = refs[: len(features)], refs[len(features) :]
        outs, refs = refs[: len(widths)], refs[len(widths) :]
        land, refs = refs[0], refs[1:]
        mine, refs = refs[: len(widths)], refs[len(widths) :]
        first, refs = refs[: len(widths)], refs[len(widths) :]
        second, refs = refs[: len(widths)], refs[len(widths) :]
        table, send_g, recv_g, send_a, recv_a, send_b, recv_b, load, store = refs
        me = lax.axis_index("dp")
        place = lax.axis_index("context")
        middle = place * (3 - place) == 2
        inner = 1 + place // 2
        across = 3 - place
        outer = 3 * (place - 1)

        barrier = pltpu.get_barrier_semaphore()
        partners = sorted(set(mask for _, mask in steps))
        for mask in partners:
            pl.semaphore_signal(barrier, 1, device_id={"dp": flipped(me, mask)}, device_id_type=MESH)

        @pl.when(middle)
        def _():
            pl.semaphore_signal(barrier, 1, device_id={"context": across}, device_id_type=MESH)
            pl.semaphore_signal(barrier, 1, device_id={"context": outer}, device_id_type=MESH)
            pl.semaphore_wait(barrier, len(partners) + 2)

        @pl.when(jnp.logical_not(middle))
        def _():
            pl.semaphore_signal(barrier, 1, device_id={"context": inner}, device_id_type=MESH)
            pl.semaphore_wait(barrier, len(partners) + 1)

        def piece(u, r):
            if gathered[u]:
                return unit_refs[starts[u] + r]
            if r == 0:
                return unit_refs[starts[u]]
            return land.at[r - 1, u, :, pl.ds(0, flat[starts[u]].shape[1])]

        def transfer(u, n):
            r, mask = steps[n]
            target = r ^ mask
            return pltpu.make_async_remote_copy(
                src_ref=piece(u, r),
                dst_ref=land.at[target - 1, u, :, pl.ds(0, flat[starts[u]].shape[1])],
                send_sem=send_g.at[n, u],
                recv_sem=recv_g.at[n, u],
                device_id={"dp": flipped(me, mask)},
                device_id_type=MESH,
            )

        wanted = [u for u in range(count) if not gathered[u]]

        def begin(u):
            for n, (r, _) in enumerate(steps):
                if r == 0:
                    transfer(u, n).start()

        def loads(u, slot):
            width = flat[starts[u]].shape[1]
            return [
                pltpu.make_async_copy(
                    piece(u, r),
                    table.at[slot, pl.ds(r * rows, rows), pl.ds(0, width)],
                    load.at[slot, r],
                )
                for r in range(size)
            ]

        def forward(u):
            waited = set()
            for n, (r, mask) in enumerate(steps):
                if r != 0:
                    if r not in waited:
                        transfer(u, arrival[r]).wait_recv()
                        waited.add(r)
                    transfer(u, n).start()
            for r in range(1, size):
                if r not in waited:
                    transfer(u, arrival[r]).wait_recv()

        def hop(j, source, target, place_to, send, recv):
            _, _, kind, index = where[j]
            return pltpu.make_async_remote_copy(
                src_ref=source[kind].at[index],
                dst_ref=target[kind].at[index],
                send_sem=send.at[j],
                recv_sem=recv.at[j],
                device_id={"context": place_to},
                device_id_type=MESH,
            )

        def hop_in(j):
            return hop(j, mine, first, inner, send_a, recv_a)

        def hop_across(j):
            return hop(j, mine, second, across, send_b, recv_b)

        def hop_out(j):
            return hop(j, first, first, outer, send_a, recv_a)

        def keep(j):
            _, _, kind, index = where[j]
            return pltpu.make_async_copy(first[kind].at[index], outs[kind].at[index], store.at[j])

        def total_in(j):
            _, _, kind, index = where[j]
            hop_in(j).wait_recv()
            mine[kind][index] = (
                mine[kind][index].astype(f32) + first[kind][index].astype(f32)
            ).astype(bf16)
            hop_across(j).start()

        def total_across(j):
            _, _, kind, index = where[j]
            hop_across(j).wait_recv()
            first[kind][index] = (
                mine[kind][index].astype(f32) + second[kind][index].astype(f32)
            ).astype(bf16)
            hop_out(j).start()
            keep(j).start()

        of_unit = [[j for j in range(block_count) if where[j][0] == u] for u in range(count)]
        for u in wanted[:ahead]:
            begin(u)
        for copy in loads(0, 0) if gathered[0] else []:
            copy.start()
        middle_in = []
        for u in range(count):
            slot = u % 2
            if not gathered[u]:
                forward(u)
                later = [v for v in wanted if v > u]
                if len(later) >= ahead:
                    begin(later[ahead - 1])
            if not (u == 0 and gathered[0]):
                for copy in loads(u, slot):
                    copy.start()
            for copy in loads(u, slot):
                copy.wait()
            for j in of_unit[u]:
                _, spans, kind, index = where[j]
                filled = 0
                for which, start, width in spans:
                    mine[kind][index, :, filled : filled + width] = dot_nn(
                        feature_refs[which][...], table[slot, :, start : start + width]
                    ).astype(bf16)
                    filled += width

                @pl.when(jnp.logical_not(middle))
                def _(j=j):
                    if j >= 3:
                        hop_in(j - 3).wait_send()
                    hop_in(j).start()

            if u >= 1:

                @pl.when(middle)
                def _(u=u):
                    for j in of_unit[u - 1]:
                        total_in(j)
                        if j >= 1:
                            total_across(j - 1)

        @pl.when(middle)
        def _():
            for j in of_unit[count - 1]:
                total_in(j)
                total_across(j - 1)
            total_across(block_count - 1)
            for j in range(block_count):
                hop_across(j).wait_send()
                hop_out(j).wait_send()
                keep(j).wait()

        @pl.when(jnp.logical_not(middle))
        def _():
            for j in range(max(block_count - 3, 0), block_count):
                hop_in(j).wait_send()
            for j in range(block_count):
                hop_out(j).wait_recv()
                keep(j).start()
            for j in range(block_count):
                keep(j).wait()

        for u in wanted:
            for n in range(len(steps)):
                transfer(u, n).wait_send()

    def stacks(kind_memory):
        return [kind_memory((counts[w], own_rows, w), bf16) for w in widths]

    columns = sum(counts[w] * w for w in widths)
    results = pl.pallas_call(
        kernel,
        out_shape=[jax.ShapeDtypeStruct((counts[w], own_rows, w), bf16) for w in widths]
        + [jax.ShapeDtypeStruct((size - 1, count, rows, widest), bf16)],
        in_specs=[ANY] * len(flat) + [VMEM] * len(features),
        out_specs=[ANY] * (len(widths) + 1),
        scratch_shapes=stacks(pltpu.VMEM) * 3
        + [
            pltpu.VMEM((2, tokens, widest), bf16),
            pltpu.SemaphoreType.DMA((len(steps), count)),
            pltpu.SemaphoreType.DMA((len(steps), count)),
            pltpu.SemaphoreType.DMA((block_count,)),
            pltpu.SemaphoreType.DMA((block_count,)),
            pltpu.SemaphoreType.DMA((block_count,)),
            pltpu.SemaphoreType.DMA((block_count,)),
            pltpu.SemaphoreType.DMA((2, size)),
            pltpu.SemaphoreType.DMA((block_count,)),
        ],
        compiler_params=pltpu.CompilerParams(
            collective_id=0, has_side_effects=True, vmem_limit_bytes=60 << 20
        ),
        cost_estimate=pl.CostEstimate(
            flops=2 * own_rows * tokens * columns,
            bytes_accessed=2 * tokens * columns + 12 * own_rows * columns,
            transcendentals=0,
        ),
        name="gather_and_sum",
    )(*flat, *features)
    return [(results[kind], index) for _, _, kind, index in where]


def layer(
    length, tokens, grad_out, gains, biases, tables, attention_own, feed_own, width, parts_of_x,
):
    bf16, f32 = jnp.bfloat16, jnp.float32
    rows, features = tokens.shape
    own_rows, units_all = feed_own[0].shape
    chunks = units_all // width
    heads_width = attention_own[0].shape[1]
    heads = heads_width // HEAD_DIM
    keys = tables.shape[1]
    pair_width = attention_own[1].shape[1] + attention_own[2].shape[1]
    projected = heads_width + pair_width
    last_width = projected + heads_width
    halfway = 2 * HEAD_DIM
    size = features // own_rows
    units = chunks + 1
    tokens_all = size * rows
    small_width = 2 * features + projected
    scale = 1.0 / math.sqrt(HEAD_DIM)
    part = 64
    where = []
    for k in range(chunks):
        where.append((k, [(0, 0, width)], 0, 3 * k))
        where.append((k, [(0, width, width)], 0, 3 * k + 1))
        where.append((k, [(1, 2 * width, width)], 0, 3 * k + 2))
    for n in range(last_width // halfway):
        where.append((chunks, [(2 if n * halfway < projected else 3, n * halfway, halfway)], 1, n))
    count = len(where)
    widths = (width, halfway)
    attention_width = projected + heads_width
    attention_spans = []
    for array in attention_own:
        attention_spans.append((sum(w for _, w in attention_spans), array.shape[1]))

    def kernel(*refs):
        refs = list(refs)

        def take(n):
            taken = refs[:n]
            del refs[:n]
            return taken

        (length_ref,) = take(1)
        gain_refs, bias_refs = take(2), take(3)
        (tokens_hbm, grad_hbm, tables_hbm) = take(3)
        attention_hbm, own_hbm = take(4), take(3)
        output_hbm, grad_tokens_hbm, small_ref, sum_wide, sum_last, land, acts_hbm, across_wide, across_last = take(9)
        attention_land, near_land, far_land = take(3)
        (mine_wide, mine_last, stage_in, stage_across, table, weights, feature_t, feature_land) = take(8)
        (row_two, row_fall, row_normed, row_branch, hidden_rel, tokens_rel, d_sum, out_sum) = take(8)
        (y_send, y_land, acts_stage, query_v, pair_v, last_v, bias, key_t, d_key, d_value) = take(10)
        (d_mixed, d_rest, d_land, vec, vec_land, total_land) = take(6)
        (gains_v, tables_v, lse_ref, gains_ref, biases_ref) = take(5)
        (s_in, s_weights, s_acts, s_rest, send_g, recv_g, send_a, recv_a, send_b, recv_b) = take(10)
        (s_stage, s_keep, s_table, send_t, recv_t, send_y, recv_y, send_k, recv_k) = take(9)
        (send_v, recv_v, send_w, recv_w, s_store) = take(5)
        (send_m, recv_m, send_near, recv_near, send_x, recv_x, send_z, recv_z, send_c, recv_c, send_p, recv_p) = take(12)
        (s_attention,) = take(1)
        cos_ref, sin_ref = tables_v.at[0], tables_v.at[1]
        sums, mines, acrosses = (sum_wide, sum_last), (mine_wide, mine_last), (across_wide, across_last)
        rows_of = (row_two, row_fall, row_normed, row_branch)

        me = lax.axis_index("dp")
        place = lax.axis_index("context")
        side = lax.axis_index("tensor")
        middle = place * (3 - place) == 2
        inner = 1 + place // 2
        across = 3 - place
        outer = 3 * (place - 1)
        one = flipped(me, 1)
        partner = (me, one, flipped(me, 2), flipped(one, 2))
        parity = lax.rem(place, 2)
        beside = flipped(place, 1)

        barrier = pltpu.get_barrier_semaphore()
        for r in range(1, size):
            pl.semaphore_signal(barrier, 1, device_id={"dp": partner[r]}, device_id_type=MESH)
        for s in range(1, 4):
            pl.semaphore_signal(barrier, 1, device_id={"context": lax.rem(place + s, 4)}, device_id_type=MESH)
        pl.semaphore_signal(barrier, 1, device_id={"tensor": 1 - side}, device_id_type=MESH)

        def block_of(r):
            return pl.ds(pl.multiple_of(partner[r] * own_rows, 128), own_rows)

        def local(source, target, sem):
            return pltpu.make_async_copy(source, target, sem)

        def remote(source, target, send, recv, axis, index):
            return pltpu.make_async_remote_copy(
                src_ref=source, dst_ref=target, send_sem=send, recv_sem=recv,
                device_id={axis: index}, device_id_type=MESH,
            )

        def cols(r):
            return pl.ds(r * own_rows, own_rows)

        ins = []
        for n, (source, target) in enumerate(((tokens_hbm, tokens_rel), (grad_hbm, row_fall))):
            ins.append(
                [local(source.at[:, block_of(r)], target.at[:, cols(r)], s_in.at[n, r]) for r in range(size)]
            )
        rest = [
            local(tables_hbm.at[:, pl.ds(pl.multiple_of(place * rows, rows), rows), :], tables_v, s_rest.at[0])
        ]

        attention_parts = ((0, 3, 0, projected), (3, 4, projected, heads_width))
        half_rows = pl.ds(pl.multiple_of(own_rows // 2 * parity, 64), own_rows // 2)

        def attention_send(n):
            first, last, _, _ = attention_parts[n % 2]
            if n >= 4:
                attention_wait(n).start()
                return
            rows_sent = half_rows if n < 2 else pl.ds(0, own_rows)
            for m in range(first, last):
                at, wide = attention_spans[m]
                remote(
                    attention_hbm[m].at[rows_sent, :],
                    attention_land.at[1 if n < 2 else 0, rows_sent, pl.ds(at, wide)],
                    send_m.at[n], recv_m.at[n], "dp", partner[2 if n < 2 else 1],
                ).start()

        def attention_wait(n):
            _, _, at, wide = attention_parts[n % 2]
            rows_sent = half_rows if n < 2 or n >= 6 else pl.ds(0, own_rows)
            source = attention_land.at[1, rows_sent, pl.ds(at, wide)]
            target = attention_land.at[(1, 0, 2, 1)[n // 2], rows_sent, pl.ds(at, wide)]
            axis, to = ("context", beside) if n >= 6 else ("dp", partner[2 if n < 2 else 1])
            return remote(source, target, send_m.at[n], recv_m.at[n], axis, to)

        def attention_arrived(n):
            _, _, at, wide = attention_parts[n % 2]
            half = pl.ds(pl.multiple_of(own_rows // 2 * (1 - parity), 64), own_rows // 2)
            view = attention_land.at[1, half, pl.ds(at, wide)]
            remote(view, view, send_m.at[n], recv_m.at[n], "context", beside).wait_recv()

        def attention_copies(n):
            first, last, at, wide = attention_parts[n]
            return [
                local(
                    attention_hbm[m],
                    weights.at[pl.ds(0, own_rows), pl.ds(attention_spans[m][0], attention_spans[m][1])],
                    s_attention.at[m],
                )
                for m in range(first, last)
            ] + [
                local(
                    attention_land.at[r - 1, :, pl.ds(at, wide)],
                    weights.at[pl.ds(r * own_rows, own_rows), pl.ds(at, wide)],
                    s_weights.at[n, r],
                )
                for r in range(1, size)
            ]

        def near(which):
            return remote(
                own_hbm[which], near_land.at[which], send_near.at[which], recv_near.at[which], "dp", partner[1]
            )

        def straight_rows(k):
            wide = own_rows * parts_of_x[k] // 6
            return pl.ds(pl.multiple_of((own_rows - wide) * parity, 64), wide)

        def round_rows(k):
            short = own_rows - own_rows * parts_of_x[k] // 6
            return pl.ds(pl.multiple_of((own_rows - short) * parity, 64), short)

        def far_send(k):
            for which in range(3):
                remote(
                    own_hbm[which].at[straight_rows(k), pl.ds(k * width, width)],
                    far_land.at[0, k, straight_rows(k), pl.ds(which * width, width)],
                    send_x.at[k], recv_x.at[k], "dp", partner[2],
                ).start()

        def far_wait(k):
            view = far_land.at[0, k, straight_rows(k), :]
            return remote(view, view, send_x.at[k], recv_x.at[k], "dp", partner[2])

        def far_round(k):
            view = far_land.at[0, k, round_rows(k), :]
            return remote(view, view, send_z.at[k], recv_z.at[k], "context", beside)

        def missing_rows(k):
            short = own_rows - own_rows * parts_of_x[k] // 6
            return pl.ds(pl.multiple_of((own_rows - short) * (1 - parity), 64), short)

        def far_round_wait(k):
            view = far_land.at[0, k, missing_rows(k), :]
            return remote(view, view, send_z.at[k], recv_z.at[k], "context", beside)

        def far_near(k):
            return remote(far_land.at[0, k], far_land.at[1, k], send_c.at[k], recv_c.at[k], "dp", partner[1])

        def weight_straight(k):
            far_wait(k).wait_recv()
            if parts_of_x[k] < 6:
                far_round(k).start()
            else:
                far_near(k).start()

        def weight_round(k):
            if parts_of_x[k] < 6:
                far_round_wait(k).wait_recv()
                far_near(k).start()

        def weight_copies(k, which):
            view = pl.ds(which * width, width)
            sources = [
                own_hbm[which].at[:, pl.ds(k * width, width)],
                near_land.at[which, :, pl.ds(k * width, width)],
                far_land.at[0, k, :, view],
                far_land.at[1, k, :, view],
            ]
            return [
                local(source, weights.at[pl.ds(r * own_rows, own_rows), view], s_weights.at[which, r])
                for r, source in enumerate(sources)
            ]

        def start(copies):
            for copy in copies:
                copy.start()

        def wait(copies):
            for copy in copies:
                copy.wait()

        for copies in ins:
            start(copies)
        start(rest)

        def trade(w, r):
            return remote(
                rows_of[w].at[:, cols(r)], feature_land.at[w, r - 1], send_t.at[w, r - 1], recv_t.at[w, r - 1],
                "dp", partner[r],
            )

        def turn_features(w):
            feature_t[w, :, 0:rows] = rows_of[w][:, 0:own_rows].T
            for r in range(1, size):
                trade(w, r).wait_recv()
                feature_t[w, :, r * rows : (r + 1) * rows] = feature_land[w, r - 1].T

        steps = ((0, 2), (0, 1), (2, 1))

        def unit_width(u):
            return 3 * width if u < chunks else last_width

        def piece(u, r):
            view = pl.ds(0, unit_width(u))
            return acts_hbm.at[u, :, view] if r == 0 else land.at[r - 1, u, :, view]

        def transfer(u, n):
            r, mask = steps[n]
            return remote(
                piece(u, r), land.at[(r ^ mask) - 1, u, :, pl.ds(0, unit_width(u))],
                send_g.at[n, u], recv_g.at[n, u], "dp", partner[mask],
            )

        def own_copy(u):
            if u < chunks:
                return local(acts_stage.at[u % 2], piece(u, 0), s_acts.at[u])
            return local(last_v, piece(u, 0), s_acts.at[u])

        def begin(u):
            own_copy(u).wait()
            transfer(u, 0).start()
            transfer(u, 1).start()

        def table_copies(u):
            return [
                local(
                    piece(u, r), table.at[pl.ds(r * rows, rows), pl.ds(0, unit_width(u))], s_table.at[r]
                )
                for r in range(size)
            ]

        def hop(j, source, target, to, send, recv):
            _, _, kind, index = where[j]
            return remote(
                source[kind].at[index], target[kind].at[index], send.at[j], recv.at[j], "context", to
            )

        def hop_in(j):
            return hop(j, mines, sums, inner, send_a, recv_a)

        def hop_across(j):
            return hop(j, mines, acrosses, across, send_b, recv_b)

        def hop_out(j):
            return hop(j, mines, sums, outer, send_a, recv_a)

        def staged(j, source, stage, n):
            _, _, kind, index = where[j]
            return local(
                source[kind].at[index], stage.at[j % 2, :, pl.ds(0, widths[kind])], s_stage.at[n, j % 2]
            )

        def keep(j):
            _, _, kind, index = where[j]
            return local(mines[kind].at[index], sums[kind].at[index], s_keep.at[j])

        def add_stage(j, stage):
            _, _, kind, index = where[j]
            mines[kind][index] = (
                mines[kind][index].astype(f32) + stage[j % 2, :, 0 : widths[kind]].astype(f32)
            ).astype(bf16)

        def line_in(j):
            hop_in(j).wait_recv()
            staged(j, sums, stage_in, 0).start()
            staged(j, sums, stage_in, 0).wait()
            add_stage(j, stage_in)
            hop_across(j).start()

        def line_out(j):
            hop_across(j).wait_recv()
            staged(j, acrosses, stage_across, 1).start()
            staged(j, acrosses, stage_across, 1).wait()
            hop_across(j).wait_send()
            add_stage(j, stage_across)
            hop_out(j).start()
            keep(j).start()

        of_unit = [[j for j in range(count) if where[j][0] == u] for u in range(units)]

        def gradients(u):
            transfer(u, 0).wait_recv()
            transfer(u, 2).start()
            transfer(u, 1).wait_recv()
            transfer(u, 2).wait_recv()
            start(table_copies(u))
            wait(table_copies(u))
            for j in of_unit[u]:
                _, spans, kind, index = where[j]
                filled = 0
                for which, at, w in spans:
                    mines[kind][index, :, filled : filled + w] = dot_nn(
                        feature_t[which], table[:, at : at + w]
                    ).astype(bf16)
                    filled += w

                @pl.when(jnp.logical_not(middle))
                def _(j=j):
                    if j >= 3:
                        hop_in(j - 3).wait_send()
                    hop_in(j).start()

        def feed(k):
            far_near(k).wait_recv()
            for which in range(3):
                if k == 0:
                    near(which).wait_recv()
                start(weight_copies(k, which))
            wait(weight_copies(k, 0))
            gate_w, up_w, down_w = (weights.at[:, pl.ds(n * width, width)] for n in range(3))
            gate = dot_nn(row_two[...], gate_w[...])
            wait(weight_copies(k, 1))
            up = dot_nn(row_two[...], up_w[...])
            wait(weight_copies(k, 2))
            d_active = dot_nn(row_fall[...], down_w[...])
            sigmoid = jax.nn.sigmoid(gate)
            swish = gate * sigmoid
            stage = acts_stage.at[k % 2]
            stage[:, 2 * width :] = (swish * up).astype(bf16)
            stage[:, :width] = (d_active * up * sigmoid * (1.0 + gate * (1.0 - sigmoid))).astype(bf16)
            stage[:, width : 2 * width] = (d_active * swish).astype(bf16)
            own_copy(k).start()
            d_part = contract_last(stage[:, :width], gate_w[...]) + contract_last(
                stage[:, width : 2 * width], up_w[...]
            )
            out_part = contract_last(stage[:, 2 * width :], down_w[...])
            if k == 0:
                d_sum[...] = d_part
                out_sum[...] = out_part
            else:
                d_sum[...] += d_part
                out_sum[...] += out_part

        def swap(n):
            return remote(y_send.at[n], y_land.at[n], send_y.at[n], recv_y.at[n], "tensor", 1 - side)

        for n, ref in enumerate(gain_refs):
            gains_ref[n : n + 1, :] = ref[...].astype(f32).reshape(1, features)
        at = 0
        for ref in bias_refs:
            biases_ref[:, at : at + ref.shape[0]] = ref[...].astype(f32).reshape(1, ref.shape[0])
            at += ref.shape[0]
        for r in range(size):
            gains_v[:, r * own_rows : (r + 1) * own_rows] = gains_ref[:, block_of(r)]
        gain_one, gain_two = gains_v[0:1, :], gains_v[1:2, :]

        def mean_scale(field):
            return lax.rsqrt(jnp.mean(field * field, -1, keepdims=True) + EPSILON)

        spans_of_rows = [slice(n, n + part) for n in range(0, rows, part)]

        def row_valid(span):
            at = lax.broadcasted_iota(jnp.int32, (part, 1), 0) + (place * rows + span.start)
            return (at < length_ref[0]).astype(f32)

        def keep_gain(which, value):
            for r in range(size):
                at = pl.multiple_of(partner[r] * own_rows + which * features, 128)
                vec[:, pl.ds(at, own_rows)] = value[:, r * own_rows : (r + 1) * own_rows]

        pl.semaphore_wait(barrier, size - 1 + 3 + 1)
        attention_send(0)
        attention_send(2)
        attention_send(1)
        attention_send(3)
        far_send(0)
        wait(ins[0])
        for span in spans_of_rows:
            field = tokens_rel[span, :].astype(f32)
            row_normed[span, :] = (field * mean_scale(field) * gain_one).astype(bf16)
        wait(ins[1])
        for span in spans_of_rows:
            row_fall[span, :] = (row_fall[span, :].astype(f32) * row_valid(span)).astype(bf16)
        for r in (2, 3, 1):
            trade(1, r).start()
        far_send(1)
        far_send(2)
        attention_wait(0).wait_recv()
        attention_send(6)
        bias[...] = key_bias_table(place, length_ref[0], keys, rows)
        attention_wait(1).wait_recv()
        attention_send(7)
        attention_arrived(6)
        attention_send(4)
        near(0).start()
        attention_wait(2).wait_recv()
        attention_wait(4).wait_recv()
        start(attention_copies(0))
        wait(rest)
        wait(attention_copies(0))
        queries = dot_nn(row_normed[...], weights[:, 0:heads_width]) + biases_ref[:, 0:heads_width]
        for head in range(heads):
            at = slice(head * HEAD_DIM, (head + 1) * HEAD_DIM)
            query_v[:, at] = turn(queries[:, at], cos_ref[...], sin_ref[...]).astype(bf16)
        others = dot_nn(row_normed[...], weights[:, heads_width:projected]) + biases_ref[:, heads_width:projected]
        pair_v[0:rows, :HEAD_DIM] = turn(others[:, :HEAD_DIM], cos_ref[...], sin_ref[...]).astype(bf16)
        pair_v[0:rows, HEAD_DIM:] = others[:, HEAD_DIM:].astype(bf16)

        def lend(s):
            return remote(
                pair_v.at[pl.ds(0, rows), :], pair_v.at[pl.ds(s * rows, rows), :], send_p.at[s - 1], recv_p.at[s - 1],
                "context", place + s,
            )

        for s in range(1, 4):
            pl.when(place + s <= 3)(lend(s).start)

            @pl.when(place < s)
            def _(s=s):
                pair_v[s * rows : (s + 1) * rows, :] = jnp.zeros((rows, pair_width), bf16)

        attention_arrived(7)
        attention_send(5)
        near(1).start()
        near(2).start()
        for s in range(1, 4):
            pl.when(place >= s)(lend(s).wait_recv)
        weight_straight(0)
        key_t[...] = pair_v[:, HEAD_DIM:].T
        for head in range(heads):
            at = slice(head * HEAD_DIM, (head + 1) * HEAD_DIM)
            scores = contract_last(pair_v[:, :HEAD_DIM], query_v[:, at]) * scale + bias[...]
            top = jnp.max(scores, 0, keepdims=True)
            raised = jnp.exp(scores - top)
            total = jnp.sum(raised, 0, keepdims=True)
            lse_ref[head : head + 1, :] = top + jnp.log(total)
            probs = (raised * (1.0 / total)).astype(bf16)
            mixed_at = slice(projected + head * HEAD_DIM, projected + (head + 1) * HEAD_DIM)
            last_v[:, mixed_at] = dot_nn(key_t[...], probs).T.astype(bf16)
        attention_wait(3).wait_recv()
        attention_wait(5).wait_recv()
        start(attention_copies(1))
        wait(attention_copies(1))
        y_send[3] = contract_last(last_v[:, projected:], weights[:, projected:attention_width]).astype(bf16)
        swap(3).start()
        weight_round(0)
        weight_straight(1)
        swap(3).wait_recv()
        for span in spans_of_rows:
            field = tokens_rel[span, :].astype(f32) + (
                y_send[3, span, :].astype(f32) + y_land[3, span, :].astype(f32)
            )
            hidden_rel[span, :] = field
            row_two[span, :] = (field * mean_scale(field) * gain_two).astype(bf16)
        def share(r):
            return remote(vec, vec_land.at[me], send_v.at[r - 1], recv_v.at[r - 1], "dp", partner[r])

        def spread(s):
            return remote(
                vec, total_land.at[place], send_w.at[s - 1], recv_w.at[s - 1], "context", lax.rem(place + s, 4)
            )

        for r in (2, 3, 1):
            trade(0, r).start()
        far_send(3)
        feed(0)
        weight_straight(2)
        weight_round(1)
        turn_features(0)
        begin(0)
        turn_features(1)
        feed(1)
        begin(1)
        weight_round(2)
        weight_straight(3)
        far_send(4)
        gradients(0)
        feed(2)
        begin(2)
        far_send(5)

        @pl.when(middle)
        def _():
            line_in(0)

        weight_round(3)
        gradients(1)

        @pl.when(middle)
        def _():
            line_in(1)
            line_out(0)

        weight_straight(4)

        @pl.when(middle)
        def _():
            line_in(2)

        feed(3)

        @pl.when(middle)
        def _():
            line_out(1)
            line_in(3)
            line_in(4)
            line_out(2)

        gradients(2)

        @pl.when(middle)
        def _():
            line_in(5)
            line_out(3)

        begin(3)

        @pl.when(middle)
        def _():
            line_out(4)

        weight_round(4)

        @pl.when(middle)
        def _():
            line_out(5)

        feed(4)
        weight_straight(5)
        begin(4)

        @pl.when(middle)
        def _():
            line_in(6)
            line_in(7)

        far_send(6)

        @pl.when(middle)
        def _():
            line_out(6)
            line_in(8)

        gradients(3)
        weight_round(5)

        @pl.when(middle)
        def _():
            line_out(7)
            line_in(9)
            line_out(8)

        feed(5)

        @pl.when(middle)
        def _():
            line_in(10)
            line_out(9)

        gradients(4)

        @pl.when(middle)
        def _():
            line_in(11)

        begin(5)
        weight_straight(6)

        @pl.when(middle)
        def _():
            line_out(10)

        weight_round(6)

        @pl.when(middle)
        def _():
            line_in(12)

        feed(6)

        @pl.when(middle)
        def _():
            line_out(11)
            line_in(13)

        y_send[0] = d_sum[...].astype(bf16)
        swap(0).start()
        start(attention_copies(0) + attention_copies(1))
        begin(6)

        @pl.when(middle)
        def _():
            line_out(12)

        gradients(5)

        @pl.when(middle)
        def _():
            line_in(14)
            line_out(13)

        y_send[1] = out_sum[...].astype(bf16)
        swap(0).wait_recv()
        swap(1).start()
        gain_sum = jnp.zeros((1, features), f32)
        for span in spans_of_rows:
            d_normed = y_send[0, span, :].astype(f32) + y_land[0, span, :].astype(f32)
            field = hidden_rel[span, :]
            r2 = mean_scale(field)
            gain_sum = gain_sum + jnp.sum(d_normed * field * r2, 0, keepdims=True)
            weighted = d_normed * gain_two
            d_hidden = (
                row_fall[span, :].astype(f32)
                + r2 * weighted
                - field * (r2 * r2 * r2) * jnp.mean(field * weighted, -1, keepdims=True)
            )
            d_sum[span, :] = d_hidden
            row_branch[span, :] = d_hidden.astype(bf16)
        keep_gain(1, gain_sum)
        for r in (2, 3, 1):
            trade(3, r).start()
        wait(attention_copies(0) + attention_copies(1))
        d_mixed[...] = dot_nn(row_branch[...], weights[:, projected:attention_width]).astype(bf16)

        @pl.when(middle)
        def _():
            line_out(14)
            line_in(15)

        key_t[...] = pair_v[:, :HEAD_DIM].T
        for head in range(heads):
            at = slice(head * HEAD_DIM, (head + 1) * HEAD_DIM)
            scores = contract_last(pair_v[:, :HEAD_DIM], query_v[:, at]) * scale + bias[...]
            probs = jnp.exp(scores - lse_ref[head : head + 1, :])
            d_probs = contract_last(pair_v[:, HEAD_DIM:], d_mixed[:, at])
            inside = jnp.sum(d_probs * probs, 0, keepdims=True)
            d_scores = (probs * (d_probs - inside)).astype(bf16)
            d_query = (dot_nn(key_t[...], d_scores) * scale).T
            last_v[:, at] = turn(d_query, cos_ref[...], -sin_ref[...]).astype(bf16)
            more_key = dot_nn(d_scores, query_v[:, at])
            more_value = dot_nn(probs.astype(bf16), d_mixed[:, at])
            if head == 0:
                d_key[...] = more_key
                d_value[...] = more_value
            else:
                d_key[...] += more_key
                d_value[...] += more_value
        d_rest[:, :HEAD_DIM] = (d_key[rows:, :] * scale).astype(bf16)
        d_rest[:, HEAD_DIM:] = d_value[rows:, :].astype(bf16)

        def give(s):
            return remote(
                d_rest.at[pl.ds((s - 1) * rows, rows), :], d_land.at[s - 1], send_k.at[s - 1], recv_k.at[s - 1],
                "context", place - s,
            )

        for s in range(1, 4):
            pl.when(place >= s)(give(s).start)

        @pl.when(middle)
        def _():
            line_in(16)
            line_in(17)

        turn_features(3)

        @pl.when(middle)
        def _():
            line_out(15)

        gradients(6)
        for r in (2, 3, 1):
            trade(2, r).start()

        @pl.when(middle)
        def _():
            line_out(16)

        d_key[0:rows, :] = d_key[0:rows, :] * scale
        for s in range(1, 4):

            @pl.when(place + s <= 3)
            def _(s=s):
                give(s).wait_recv()
                d_key[0:rows, :] += d_land[s - 1, :, :HEAD_DIM].astype(f32)
                d_value[0:rows, :] += d_land[s - 1, :, HEAD_DIM:].astype(f32)

        last_v[:, heads_width : heads_width + HEAD_DIM] = turn(
            d_key[0:rows, :], cos_ref[...], -sin_ref[...]
        ).astype(bf16)
        last_v[:, heads_width + HEAD_DIM : projected] = d_value[0:rows, :].astype(bf16)
        own_copy(chunks).start()
        begin(chunks)

        @pl.when(middle)
        def _():
            line_in(18)
            line_out(17)
            line_in(19)

        turn_features(2)

        @pl.when(middle)
        def _():
            line_out(18)
            line_in(20)

        y_send[2] = contract_last(last_v[:, 0:projected], weights[:, 0:projected]).astype(bf16)
        swap(2).start()
        vec[:, 2 * features :] = jnp.sum(last_v[:, 0:projected].astype(f32), 0, keepdims=True)
        swap(1).wait_recv()
        swap(1).wait_send()
        for span in spans_of_rows:
            whole = y_send[1, span, :].astype(f32) + y_land[1, span, :].astype(f32)
            y_land[1, span, :] = (row_valid(span) * (hidden_rel[span, :] + whole)).astype(bf16)

        def stored(n, target):
            return [
                local(y_land.at[n, :, cols(r)], target.at[:, block_of(r)], s_store.at[n, r]) for r in range(size)
            ]

        start(stored(1, output_hbm))

        @pl.when(middle)
        def _():
            line_out(19)

        gradients(7)

        @pl.when(middle)
        def _():
            line_out(20)
            line_in(21)
            line_in(22)

        swap(2).wait_recv()
        swap(2).wait_send()
        gain_sum = jnp.zeros((1, features), f32)
        for span in spans_of_rows:
            d_normed = y_send[2, span, :].astype(f32) + y_land[2, span, :].astype(f32)
            field = tokens_rel[span, :].astype(f32)
            r1 = mean_scale(field)
            gain_sum = gain_sum + jnp.sum(d_normed * field * r1, 0, keepdims=True)
            weighted = d_normed * gain_one
            y_land[2, span, :] = (
                d_sum[span, :]
                + r1 * weighted
                - field * (r1 * r1 * r1) * jnp.mean(field * weighted, -1, keepdims=True)
            ).astype(bf16)
        start(stored(2, grad_tokens_hbm))
        keep_gain(0, gain_sum)


        @pl.when(middle)
        def _():
            line_out(21)
            line_in(23)
            line_in(24)
            line_out(22)

        for r in range(1, size):
            share(r).start()
        vec_land[me] = vec[...]

        @pl.when(middle)
        def _():
            line_in(25)
            line_out(23)

        for r in range(1, size):
            share(r).wait()
        vec[...] = vec_land[0] + vec_land[1] + vec_land[2] + vec_land[3]
        for s in range(1, 4):
            spread(s).start()
        total_land[place] = vec[...]

        @pl.when(middle)
        def _():
            line_out(24)
            line_in(26)
            line_out(25)
            line_in(27)
            line_out(26)
            line_out(27)

        for s in range(1, 4):
            spread(s).wait()
        small_ref[...] = total_land[0] + total_land[1] + total_land[2] + total_land[3]

        @pl.when(middle)
        def _():
            for j in range(count):
                hop_out(j).wait_send()
                keep(j).wait()

        @pl.when(jnp.logical_not(middle))
        def _():
            for j in range(count - 3, count):
                hop_in(j).wait_send()
            for j in range(count):
                hop_out(j).wait_recv()

        wait(stored(1, output_hbm))
        wait(stored(2, grad_tokens_hbm))
        swap(0).wait_send()
        swap(3).wait_send()
        for n in range(8):
            attention_wait(n).wait_send()
        for which in range(3):
            near(which).wait_send()
        for k in range(chunks):
            far_wait(k).wait_send()
            if parts_of_x[k] < 6:
                far_round(k).wait_send()
            far_near(k).wait_send()
        for s in range(1, 4):
            pl.when(place >= s)(give(s).wait_send)
            pl.when(place + s <= 3)(lend(s).wait_send)
        for w in range(4):
            for r in range(1, size):
                trade(w, r).wait_send()
        for u in range(units):
            for n in range(3):
                transfer(u, n).wait_send()

    dma = pltpu.SemaphoreType.DMA
    shape = jax.ShapeDtypeStruct
    wide, last = (3 * chunks, own_rows, width), (last_width // halfway, own_rows, halfway)
    results = pl.pallas_call(
        kernel,
        out_shape=(
            shape((rows, features), bf16),
            shape((rows, features), bf16),
            shape((1, small_width), f32),
            shape(wide, bf16),
            shape(last, bf16),
            shape((size - 1, units, rows, 3 * width), bf16),
            shape((units, rows, 3 * width), bf16),
            shape(wide, bf16),
            shape(last, bf16),
            shape((size - 1, own_rows, attention_width), bf16),
            shape((3, own_rows, units_all), bf16),
            shape((2, chunks, own_rows, 3 * width), bf16),
        ),
        in_specs=[SMEM] + [VMEM] * 5 + [ANY] * (3 + 4 + 3),
        out_specs=(ANY, ANY, VMEM) + (ANY,) * 9,
        scratch_shapes=[
            pltpu.VMEM(wide, bf16),
            pltpu.VMEM(last, bf16),
            pltpu.VMEM((2, own_rows, max(widths)), bf16),
            pltpu.VMEM((2, own_rows, max(widths)), bf16),
            pltpu.VMEM((tokens_all, 3 * width), bf16),
            pltpu.VMEM((features, 3 * width), bf16),
            pltpu.VMEM((4, own_rows, tokens_all), bf16),
            pltpu.VMEM((4, size - 1, rows, own_rows), bf16),
            pltpu.VMEM((rows, features), bf16),
            pltpu.VMEM((rows, features), bf16),
            pltpu.VMEM((rows, features), bf16),
            pltpu.VMEM((rows, features), bf16),
            pltpu.VMEM((rows, features), f32),
            pltpu.VMEM((rows, features), bf16),
            pltpu.VMEM((rows, features), f32),
            pltpu.VMEM((rows, features), f32),
            pltpu.VMEM((4, rows, features), bf16),
            pltpu.VMEM((4, rows, features), bf16),
            pltpu.VMEM((2, rows, 3 * width), bf16),
            pltpu.VMEM((rows, heads_width), bf16),
            pltpu.VMEM((keys, pair_width), bf16),
            pltpu.VMEM((rows, last_width), bf16),
            pltpu.VMEM((keys, rows), f32),
            pltpu.VMEM((HEAD_DIM, keys), bf16),
            pltpu.VMEM((keys, HEAD_DIM), f32),
            pltpu.VMEM((keys, HEAD_DIM), f32),
            pltpu.VMEM((rows, heads_width), bf16),
            pltpu.VMEM((keys - rows, pair_width), bf16),
            pltpu.VMEM((3, rows, pair_width), bf16),
            pltpu.VMEM((1, small_width), f32),
            pltpu.VMEM((4, 1, small_width), f32),
            pltpu.VMEM((4, 1, small_width), f32),
            pltpu.VMEM((2, features), f32),
            pltpu.VMEM((2, rows, HEAD_DIM), f32),
            pltpu.VMEM((8, rows), f32),
            pltpu.VMEM((2, features), f32),
            pltpu.VMEM((1, projected), f32),
            dma((2, size)),
            dma((3, size)),
            dma((units,)),
            dma((1,)),
            dma((3, units)),
            dma((3, units)),
            dma((count,)),
            dma((count,)),
            dma((count,)),
            dma((count,)),
            dma((2, 2)),
            dma((count,)),
            dma((size,)),
            dma((4, size - 1)),
            dma((4, size - 1)),
            dma((4,)),
            dma((4,)),
            dma((3,)),
            dma((3,)),
            dma((size - 1,)),
            dma((size - 1,)),
            dma((3,)),
            dma((3,)),
            dma((3, size)),
            dma((8,)),
            dma((8,)),
            dma((3,)),
            dma((3,)),
            dma((chunks,)),
            dma((chunks,)),
            dma((chunks,)),
            dma((chunks,)),
            dma((chunks,)),
            dma((chunks,)),
            dma((3,)),
            dma((3,)),
            dma((4,)),
        ],
        compiler_params=pltpu.CompilerParams(
            collective_id=0, has_side_effects=True, vmem_limit_bytes=60 << 20
        ),
        name="layer",
    )(
        length, *gains, *biases, tokens, grad_out, tables, *attention_own, *feed_own,
    )
    return results[:5]


def finish(wide, last, output, grad_tokens, small, spans, small_spans):
    blocks, own_rows, width = wide.shape
    halfway = last.shape[2]
    chunks = blocks // 3
    row_steps = 4
    f32 = jnp.float32

    def kernel(wide_ref, last_ref, small_ref, output_ref, tokens_ref, *refs):
        outs = refs
        at = pl.program_id(0)
        block = last_ref[0].astype(f32)
        for (start, size), out in zip(spans, outs[3:]):
            if size % halfway == 0:
                first, count = start // halfway, size // halfway

                @pl.when((at >= first) & (at < first + count))
                def _(out=out):
                    out[...] = block

            else:

                @pl.when(at == start // halfway)
                def _(out=out, low=start % halfway, size=size):
                    out[...] = block[:, low : low + size]

        @pl.when(at < row_steps)
        def _():
            outs[-2][...] = output_ref[...]
            outs[-1][...] = tokens_ref[...]

        @pl.when(at == 0)
        def _():
            for (start, size), out in zip(small_spans, outs[3 + len(spans) :]):
                out[...] = small_ref[0, start : start + size]

        for n in range(3):
            outs[n][...] = wide_ref[n].astype(f32)

    def whole(shape):
        return pl.BlockSpec(shape, lambda k: (0,) * len(shape))

    def by_span(start, size):
        if size % halfway:
            return whole((own_rows, size))
        first, count = start // halfway, size // halfway
        return pl.BlockSpec((own_rows, halfway), lambda k: (0, jnp.clip(k - first, 0, count - 1)))

    by_rows = pl.BlockSpec(
        (output.shape[0] // row_steps, output.shape[1]), lambda k: (jnp.minimum(k, row_steps - 1), 0)
    )

    shape = jax.ShapeDtypeStruct
    return pl.pallas_call(
        kernel,
        grid=(chunks,),
        out_shape=[shape((own_rows, chunks * width), f32)] * 3
        + [shape((own_rows, size), f32) for _, size in spans]
        + [shape((size,), f32) for _, size in small_spans]
        + [shape(output.shape, output.dtype)] * 2,
        in_specs=[
            pl.BlockSpec((3, own_rows, width), lambda k: (k, 0, 0)),
            pl.BlockSpec((1, own_rows, halfway), lambda k: (jnp.minimum(k, last.shape[0] - 1), 0, 0)),
            whole(small.shape),
            by_rows,
            by_rows,
        ],
        out_specs=[pl.BlockSpec((own_rows, width), lambda k: (0, k))] * 3
        + [by_span(start, size) for start, size in spans]
        + [whole((size,)) for _, size in small_spans]
        + [by_rows] * 2,
        compiler_params=plain_params(60 << 20),
        name="finish",
    )(wide, last, small, output, grad_tokens)


def rotary_tables(position_count):
    half = HEAD_DIM // 2
    inverse = np.exp(np.arange(half) * (-2.0 * math.log(ROPE_BASE) / HEAD_DIM))
    angles = np.arange(position_count)[:, None] * inverse[None, :]
    cosine, sine = np.cos(angles), np.sin(angles)
    return np.stack(
        [np.concatenate([cosine, cosine], 1), np.concatenate([-sine, sine], 1)]
    ).astype(np.float32)


PARTS_OF_X = (3, 3, 3, 3, 4, 4, 6)


def chunk_edges(columns):
    tiles = columns // 128
    count = next((n for n in (7, 5, 4, 6, 3, 2) if tiles % n == 0), 1)
    width = columns // count
    return [(n * width, width) for n in range(count)]


def local(
    tokens,
    lengths,
    gain_one,
    w_query,
    b_query,
    key_weight,
    key_bias,
    value_weight,
    value_bias,
    w_out,
    gain_two,
    w_gate,
    w_up,
    w_down,
    grad_out,
):
    bf16, f32 = jnp.bfloat16, jnp.float32
    seq_count, block_len, model_width = tokens.shape
    row_count = seq_count * block_len
    query_cols = w_query.shape[1]
    key_cols = key_weight.shape[1]
    unit_cols = w_gate.shape[1]
    own_rows = w_query.shape[0]
    head_count = query_cols // HEAD_DIM
    kv_count = key_cols // HEAD_DIM
    query_group_width = head_count // kv_count
    size = lax.axis_size("dp")
    me = lax.axis_index("dp")
    blocks_along = lax.axis_size("context")
    place = lax.axis_index("context")
    parity = place % 2 if blocks_along % 2 == 0 and own_rows % 32 == 0 else None

    edges = chunk_edges(unit_cols)
    if (
        size == 4
        and blocks_along == 4
        and lax.axis_size("tensor") == 2
        and own_rows % 384 == 0
        and row_count % 64 == 0
        and len(edges) == len(PARTS_OF_X)
        and kv_count == 1
        and seq_count == 1
    ):
        output, grad_tokens, small, feed_sums, last_sums = layer(
            lengths,
            tokens.reshape(row_count, model_width),
            grad_out.reshape(row_count, model_width),
            (gain_one, gain_two),
            (b_query, key_bias, value_bias),
            rotary_tables(block_len * blocks_along),
            (w_query, key_weight, value_weight, w_out),
            (w_gate, w_up, w_down),
            edges[0][1],
            PARTS_OF_X,
        )
        turned_at, at = query_cols + key_cols, 2 * model_width
        *grads, output, grad_tokens = finish(
            feed_sums,
            last_sums,
            output,
            grad_tokens,
            small,
            [(0, query_cols), (query_cols, key_cols), (turned_at, key_cols), (turned_at + key_cols, query_cols)],
            [
                (0, model_width),
                (at, query_cols),
                (at + query_cols, key_cols),
                (at + turned_at, key_cols),
                (model_width, model_width),
            ],
        )
        return (
            output.reshape(seq_count, block_len, model_width),
            grad_tokens.reshape(seq_count, block_len, model_width),
            grads[7],
            grads[3],
            grads[8],
            grads[4],
            grads[9],
            grads[5],
            grads[10],
            grads[6],
            grads[11],
            *grads[:3],
        )

    def relative(field):
        return swap_blocks([field[:, n * own_rows : (n + 1) * own_rows] for n in range(size)], me)

    def absolute(blocks):
        return jnp.concatenate(swap_blocks(blocks, me), 1)

    def dot_rows(blocks, weights):
        return jnp.dot(
            jnp.concatenate(blocks, 1), jnp.concatenate(weights, 0), preferred_element_type=f32
        )

    lanes = {name: Lane() for name in ("x", "z", "hop1", "hop2", "hop3")}
    attention_weights = gather_pieces(
        jnp.concatenate([w_query, key_weight, value_weight], 1), size, lanes
    )
    out_weights = gather_pieces(w_out, size, lanes, parity)
    edges = chunk_edges(unit_cols)
    feed_weights = []
    early = len(edges) - 2

    feed_own = (w_gate, w_up, w_down)
    feed_near = tuple(lax.ppermute(w, "dp", xor_pairs(size, 1)) for w in feed_own)

    def fetch(start, width):
        own = jnp.concatenate([w[:, start : start + width] for w in feed_own], 1)
        far = far_pieces(own, size, lanes, parity)
        sources = []
        for r in range(size):
            if r < 2:
                sources.append(feed_own if r == 0 else feed_near)
            elif r % 2 == 0:
                sources.append((far[r],))
            else:
                sources.append((lax.ppermute(far[r - 1], "dp", xor_pairs(size, 1)),))
        feed_weights.append(sources)

    for start, width in edges[:early]:
        fetch(start, width)

    positions = place * block_len + jnp.arange(block_len, dtype=jnp.int32)
    position_count = block_len * blocks_along
    valid_rows = (positions[None, :] < lengths[:, None]).astype(f32).reshape(row_count, 1)
    facts = jnp.stack([place.astype(jnp.int32), lengths[0]])
    half = HEAD_DIM // 2
    inverse = jnp.exp(jnp.arange(half, dtype=f32) * (-2.0 * math.log(ROPE_BASE) / HEAD_DIM))
    angles = positions.astype(f32)[:, None] * inverse[None, :]
    cosine = jnp.concatenate([jnp.cos(angles)] * 2, 1)
    sine = jnp.concatenate([-jnp.sin(angles), jnp.sin(angles)], 1)
    gain_first = gain_one.astype(f32)
    gain_second = gain_two.astype(f32)
    inputs = tokens.reshape(row_count, model_width).astype(f32)
    scale_one = lax.rsqrt(jnp.mean(inputs * inputs, -1, keepdims=True) + EPSILON)
    normalized_input = (inputs * scale_one * gain_first).astype(bf16)
    normed_blocks = relative(normalized_input)
    projected = dot_rows(normed_blocks, attention_weights) + jnp.concatenate(
        [b_query, key_bias, value_bias]
    ).astype(f32)
    turned = query_cols + key_cols

    def turn_heads(field, sine_rows):
        grid = field.reshape(row_count, field.shape[1] // HEAD_DIM, HEAD_DIM)
        swapped = jnp.concatenate([grid[..., half:], grid[..., :half]], -1)
        grid = grid * cosine[:, None, :] + swapped * sine_rows[:, None, :]
        return grid.reshape(field.shape).astype(bf16)

    turned_rows = turn_heads(projected[:, :turned], sine)
    query_rot = turned_rows[:, :query_cols]
    pair_rows = jnp.concatenate([turned_rows[:, query_cols:], projected[:, turned:].astype(bf16)], 1)
    pair_all = [pair_rows]
    for shift in range(1, blocks_along):
        pair_all.append(
            lax.ppermute(
                pair_rows, "context", [(n, n + shift) for n in range(blocks_along - shift)]
            )
        )
    pair_all = jnp.concatenate(pair_all, 0)
    mixed_heads, lse = attend(facts, query_rot, pair_all)
    full_out = jnp.concatenate(out_weights, 0)
    branch = contract_last(mixed_heads, full_out)
    branch = absolute([branch[:, r * own_rows : (r + 1) * own_rows] for r in range(size)])
    hidden = inputs + tensor_sum(branch)
    scale_two = lax.rsqrt(jnp.mean(hidden * hidden, -1, keepdims=True) + EPSILON)
    normed_two = (hidden * scale_two * gain_second).astype(bf16)
    fall_grad = grad_out.reshape(row_count, model_width).astype(f32) * valid_rows
    fall_low = fall_grad.astype(bf16)
    fall_blocks = relative(fall_low)
    two_blocks = relative(normed_two)
    traded_early = trade_blocks(
        [jnp.concatenate([a, b], 1) for a, b in zip(normed_blocks, fall_blocks)], size
    )
    traded_early = jnp.concatenate(traded_early, 0).T
    normed_features, fall_features = traded_early[:own_rows], traded_early[own_rows:]
    two_features = jnp.concatenate(trade_blocks(two_blocks, size), 0).T
    two_row = jnp.concatenate(two_blocks, 1)
    fall_row = jnp.concatenate(fall_blocks, 1)

    feed_out, d_normed_two = None, None
    feed_units = []
    for turn_at, (start, width) in enumerate(edges):
        acts, d_normed_two, feed_out = feed_chunk(
            two_row, fall_row, feed_weights[turn_at], start, width, d_normed_two, feed_out
        )
        if turn_at < 0:
            acts = gather_pieces(acts, size, lanes)
        feed_units.append(acts)
        if turn_at == 0:
            for edge in edges[early:]:
                fetch(*edge)

    def split(field):
        return [field[:, r * own_rows : (r + 1) * own_rows] for r in range(size)]

    d_normed_two = tensor_sum(absolute(split(d_normed_two)))
    result = valid_rows * (hidden + tensor_sum(absolute(split(feed_out))))
    output = result.astype(bf16).reshape(seq_count, block_len, model_width)
    gain_two_grad = jnp.sum(d_normed_two * hidden * scale_two, 0)
    d_hidden = fall_grad + norm_back(hidden, scale_two, gain_second, d_normed_two)
    d_branch = d_hidden.astype(bf16)
    branch_blocks = relative(d_branch)
    branch_features = jnp.concatenate(trade_blocks(branch_blocks, size), 0).T
    d_mixed = jnp.dot(
        jnp.concatenate(branch_blocks, 1), full_out, preferred_element_type=f32
    ).astype(bf16)
    d_query_low, d_own, d_rest = attend_back(
        facts, query_rot, pair_all, lse, d_mixed, cosine, sine
    )
    for shift in range(1, blocks_along):
        d_own = d_own + lax.ppermute(
            d_rest[(shift - 1) * block_len : shift * block_len],
            "context",
            [(n, n - shift) for n in range(shift, blocks_along)],
        ).astype(f32)
    d_key_low = turn_heads(d_own[:, :key_cols], -sine)
    d_value_low = d_own[:, key_cols:].astype(bf16)
    d_projected = jnp.concatenate([d_query_low, d_key_low, d_value_low], 1)
    d_normed = contract_last(d_projected, jnp.concatenate(attention_weights, 0))
    d_normed = tensor_sum(absolute(split(d_normed)))
    gain_one_grad = jnp.sum(d_normed * inputs * scale_one, 0)
    d_inputs = d_hidden + norm_back(inputs, scale_one, gain_first, d_normed)
    grad_tokens = d_inputs.astype(bf16).reshape(seq_count, block_len, model_width)
    gain_two_grad = small_total(gain_two_grad)
    small = small_total(
        jnp.concatenate([gain_one_grad, jnp.sum(d_projected.astype(f32), 0)])
    )
    projected_width = d_projected.shape[1]
    last = jnp.concatenate([d_projected, mixed_heads], 1)
    halfway = last.shape[1] // 2
    blocks = [
        [[(0, 0, width)], [(0, width, width)], [(1, 2 * width, width)]] for _, width in edges
    ] + [
        [
            [(2, 0, halfway)],
            [(2, halfway, projected_width - halfway), (3, projected_width, query_cols)],
        ]
    ]
    sums = gather_and_sum(
        feed_units + [last],
        [two_features, fall_features, normed_features, branch_features],
        blocks,
        size,
    )

    def columns(which):
        stack = sums[which][0]
        return jnp.concatenate(
            [stack[3 * n + which].astype(f32) for n in range(len(edges))], 1
        )

    stack = sums[-1][0]
    last_grad = jnp.concatenate([stack[0], stack[1]], 1).astype(f32)
    projected_grad, out_grad = last_grad[:, :projected_width], last_grad[:, projected_width:]

    low, high = model_width + query_cols, model_width + query_cols + key_cols
    return (
        output,
        grad_tokens,
        small[:model_width],
        projected_grad[:, :query_cols],
        small[model_width:low],
        projected_grad[:, query_cols : query_cols + key_cols],
        small[low:high],
        projected_grad[:, query_cols + key_cols :],
        small[high:],
        out_grad,
        gain_two_grad,
        columns(0),
        columns(1),
        columns(2),
    )


def solution(mesh):
    in_specs = (
        P("dp", "context", None),
        P("dp"),
        P(),
        P("dp", "tensor"),
        P("tensor"),
        P("dp", "tensor"),
        P("tensor"),
        P("dp", "tensor"),
        P("tensor"),
        P("dp", "tensor"),
        P(),
        P("dp", "tensor"),
        P("dp", "tensor"),
        P("dp", "tensor"),
        P("dp", "context", None),
    )
    out_specs = (
        P("dp", "context", None),
        P("dp", "context", None),
        P(),
        P("dp", "tensor"),
        P("tensor"),
        P("dp", "tensor"),
        P("tensor"),
        P("dp", "tensor"),
        P("tensor"),
        P("dp", "tensor"),
        P(),
        P("dp", "tensor"),
        P("dp", "tensor"),
        P("dp", "tensor"),
    )
    return jax.shard_map(local, mesh=mesh, in_specs=in_specs, out_specs=out_specs, check_vma=False)
```

```python
import math

import jax
import jax.numpy as jnp
import numpy as np
from jax import lax
from jax.experimental import pallas as pl
from jax.experimental.pallas import tpu as pltpu
from jax.sharding import PartitionSpec as P

HEAD_DIM = 128


EPSILON = 1e-06
ROPE_BASE = 1000000.0


def xor_pairs(size, mask):
    return [(i, i ^ mask) for i in range(size)]


class Lane:
    def __init__(self, depth=1):
        self.sent = []
        self.depth = depth

    def send(self, array, axis, pairs):
        if len(self.sent) >= self.depth:
            array, _ = lax.optimization_barrier((array, self.sent[-self.depth]))
        got = lax.ppermute(array, axis, pairs)
        self.sent.append(got)
        return got


def far_masks(size):
    masks, mask = [], 2
    while mask < size:
        masks.append(mask)
        mask *= 2
    return masks


def swap_blocks(blocks, me):
    mask = 1
    while mask < len(blocks):
        flag = (me & mask) != 0
        blocks = [jnp.where(flag, blocks[r ^ mask], blocks[r]) for r in range(len(blocks))]
        mask *= 2
    return blocks


def far_half(piece, mask, size, parity, lanes):
    half = piece.shape[0] // 2
    sent = lax.dynamic_slice_in_dim(piece, half * parity, half, 0)
    straight = lanes["x"].send(sent, "dp", xor_pairs(size, mask))
    other = lanes["z"].send(straight, "context", xor_pairs(lax.axis_size("context"), 1))
    first = jnp.where(parity == 0, straight, other)
    second = jnp.where(parity == 0, other, straight)
    return jnp.concatenate([first, second], 0)


def far_pieces(own, size, lanes, parity=None):
    pieces = {0: own}
    for mask in far_masks(size):
        for r in list(pieces):
            if parity is None:
                pieces[r ^ mask] = lanes["x"].send(pieces[r], "dp", xor_pairs(size, mask))
            else:
                pieces[r ^ mask] = far_half(pieces[r], mask, size, parity, lanes)
    return pieces


def gather_pieces(own, size, lanes, parity=None):
    pieces = far_pieces(own, size, lanes, parity)
    for r in list(pieces):
        pieces[r ^ 1] = lax.ppermute(pieces[r], "dp", xor_pairs(size, 1))
    return [pieces[r] for r in range(size)]


def trade_blocks(blocks, size):
    return [blocks[0]] + [
        lax.ppermute(blocks[r], "dp", xor_pairs(size, r)) for r in range(1, size)
    ]


def tensor_sum(part):
    sent = part.astype(jnp.bfloat16)
    size = lax.axis_size("tensor")
    if size == 2:
        other = lax.ppermute(sent, "tensor", [(0, 1), (1, 0)])
        return sent.astype(jnp.float32) + other.astype(jnp.float32)
    return lax.psum(part, "tensor")


def line_sum(part, lanes):
    place = lax.axis_index("context")
    if lax.axis_size("context") != 4:
        return lax.psum(part.astype(jnp.float32), "context")
    got = lanes["hop1"].send(part, "context", [(0, 1), (3, 2)])
    pair = (part.astype(jnp.float32) + got.astype(jnp.float32)).astype(jnp.bfloat16)
    got = lanes["hop2"].send(pair, "context", [(1, 2), (2, 1)])
    total = (pair.astype(jnp.float32) + got.astype(jnp.float32)).astype(jnp.bfloat16)
    got = lanes["hop3"].send(total, "context", [(1, 0), (2, 3)])
    ends = (place == 0) | (place == 3)
    return jnp.where(ends, got, total).astype(jnp.float32)


def small_total(vector):
    for axis in ("dp", "context"):
        size, mask = lax.axis_size(axis), 1
        while mask < size:
            vector = vector + lax.ppermute(vector, axis, xor_pairs(size, mask))
            mask *= 2
    return vector


def contract_last(left, right):
    return lax.dot_general(
        left, right, (((1,), (1,)), ((), ())), preferred_element_type=jnp.float32
    )


def norm_back(field, scale_rows, gain, d_normed):
    weighted = d_normed * gain
    cubed = scale_rows * scale_rows * scale_rows
    return scale_rows * weighted - field * cubed * jnp.mean(field * weighted, -1, keepdims=True)


ANY = pl.BlockSpec(memory_space=pl.ANY)
VMEM = pl.BlockSpec(memory_space=pltpu.VMEM)
SMEM = pl.BlockSpec(memory_space=pltpu.SMEM)


def plain_params(limit):
    return pltpu.CompilerParams(vmem_limit_bytes=limit)


def dot_nn(left, right):
    return jnp.dot(left, right, preferred_element_type=jnp.float32)


def feed_chunk(two_row, fall_row, sources, start, width, d_sum, out_sum):
    rows, features = two_row.shape
    bf16, f32 = jnp.bfloat16, jnp.float32
    flat, layout = [], []
    for source in sources:
        layout.append(len(source))
        flat.extend(source)
    first = d_sum is None
    held = [] if first else [d_sum, out_sum]

    def kernel(*refs):
        refs = list(refs)
        two_ref, fall_ref = refs[:2]
        given = refs[2 : 2 + len(flat)]
        at = 2 + len(flat)
        sums = refs[at : at + len(held)]
        at += len(held)
        acts_ref, d_ref, out_ref, gate_w, up_w, down_w, sems = refs[at:]
        copies = [[], [], []]
        place, taken = 0, 0
        for kind in layout:
            depth = given[taken].shape[0]
            for which, scratch in enumerate((gate_w, up_w, down_w)):
                if kind == 3:
                    view = given[taken + which].at[:, pl.ds(start, width)]
                else:
                    view = given[taken].at[:, pl.ds(which * width, width)]
                copy = pltpu.make_async_copy(
                    view,
                    scratch.at[pl.ds(place, depth), :],
                    sems.at[which, len(copies[which])],
                )
                copies[which].append(copy)
            place += depth
            taken += kind
        for group in copies:
            for copy in group:
                copy.start()
        for copy in copies[0]:
            copy.wait()
        gate = dot_nn(two_ref[...], gate_w[...])
        for copy in copies[1]:
            copy.wait()
        up = dot_nn(two_ref[...], up_w[...])
        for copy in copies[2]:
            copy.wait()
        d_active = dot_nn(fall_ref[...], down_w[...])
        sigmoid = jax.nn.sigmoid(gate)
        swish = gate * sigmoid
        acts_ref[:, 2 * width :] = (swish * up).astype(bf16)
        acts_ref[:, :width] = (d_active * up * sigmoid * (1.0 + gate * (1.0 - sigmoid))).astype(bf16)
        acts_ref[:, width : 2 * width] = (d_active * swish).astype(bf16)
        d_part = contract_last(acts_ref[:, :width], gate_w[...]) + contract_last(
            acts_ref[:, width : 2 * width], up_w[...]
        )
        out_part = contract_last(acts_ref[:, 2 * width :], down_w[...])
        if first:
            d_ref[...] = d_part
            out_ref[...] = out_part
        else:
            d_ref[...] = sums[0][...] + d_part
            out_ref[...] = sums[1][...] + out_part

    weight_bytes = 6 * features * width
    return pl.pallas_call(
        kernel,
        out_shape=(
            jax.ShapeDtypeStruct((rows, 3 * width), bf16),
            jax.ShapeDtypeStruct((rows, features), f32),
            jax.ShapeDtypeStruct((rows, features), f32),
        ),
        in_specs=[VMEM, VMEM] + [ANY] * len(flat) + [VMEM] * len(held),
        out_specs=(VMEM, VMEM, VMEM),
        scratch_shapes=[pltpu.VMEM((features, width), bf16)] * 3
        + [pltpu.SemaphoreType.DMA((3, len(sources)))],
        compiler_params=plain_params(40 << 20),
        cost_estimate=pl.CostEstimate(
            flops=12 * rows * features * width,
            bytes_accessed=weight_bytes + 20 * rows * features + 6 * rows * width,
            transcendentals=rows * width,
        ),
        name="feed_chunk",
    )(two_row, fall_row, *flat, *held)


def grad_block(features, pieces, spans):
    bf16 = jnp.bfloat16
    depth, columns = pieces[0].shape
    tokens = features[0].shape[1]
    own = features[0].shape[0]
    total = sum(w for _, w in spans)

    def kernel(*refs):
        refs = list(refs)
        feature_refs = refs[: len(features)]
        given = refs[len(features) : len(features) + len(pieces)]
        out_ref, held, sems = refs[len(features) + len(pieces) :]
        copies = [
            pltpu.make_async_copy(ref, held.at[pl.ds(n * depth, depth), :], sems.at[n])
            for n, ref in enumerate(given)
        ]
        for copy in copies:
            copy.start()
        for copy in copies:
            copy.wait()
        for ref, (start, width) in zip(feature_refs, spans):
            out_ref[:, start : start + width] = dot_nn(
                ref[...], held[:, start : start + width]
            ).astype(bf16)

    return pl.pallas_call(
        kernel,
        out_shape=jax.ShapeDtypeStruct((own, total), bf16),
        in_specs=[VMEM] * len(features) + [ANY] * len(pieces),
        out_specs=VMEM,
        scratch_shapes=[
            pltpu.VMEM((tokens, columns), bf16),
            pltpu.SemaphoreType.DMA((len(pieces),)),
        ],
        compiler_params=plain_params(40 << 20),
        cost_estimate=pl.CostEstimate(
            flops=2 * own * tokens * total,
            bytes_accessed=2 * (tokens * columns + own * total + own * tokens),
            transcendentals=0,
        ),
        name="grad_block",
    )(*features, *pieces)


def key_bias_table(place, length, keys, block_len):
    key_at = lax.broadcasted_iota(jnp.int32, (keys, block_len), 0)
    query_at = lax.broadcasted_iota(jnp.int32, (keys, block_len), 1) + place * block_len
    shift = key_at // block_len
    key_at = key_at - shift * block_len + (place - shift) * block_len
    seen = (key_at <= query_at) & (key_at < length) & (key_at >= 0)
    return jnp.where(seen, 0.0, -1e30).astype(jnp.float32)


def attend(facts, query, pair):
    rows, width = query.shape
    keys = pair.shape[0]
    heads = width // HEAD_DIM
    bf16, f32 = jnp.bfloat16, jnp.float32
    scale = 1.0 / math.sqrt(HEAD_DIM)

    def kernel(facts_ref, query_ref, pair_ref, mixed_ref, lse_ref, bias, value_t):
        bias[...] = key_bias_table(facts_ref[0], facts_ref[1], keys, rows)
        value_t[...] = pair_ref[:, HEAD_DIM:].T
        lse_ref[...] = jnp.zeros_like(lse_ref)
        for head in range(heads):
            cols = slice(head * HEAD_DIM, (head + 1) * HEAD_DIM)
            scores = contract_last(pair_ref[:, :HEAD_DIM], query_ref[:, cols]) * scale + bias[...]
            top = jnp.max(scores, 0, keepdims=True)
            raised = jnp.exp(scores - top)
            total = jnp.sum(raised, 0, keepdims=True)
            lse_ref[head : head + 1, :] = top + jnp.log(total)
            probs = (raised * (1.0 / total)).astype(bf16)
            mixed_ref[:, cols] = dot_nn(value_t[...], probs).T.astype(bf16)

    return pl.pallas_call(
        kernel,
        out_shape=(
            jax.ShapeDtypeStruct((rows, width), bf16),
            jax.ShapeDtypeStruct((8, rows), f32),
        ),
        in_specs=[SMEM, VMEM, VMEM],
        out_specs=(VMEM, VMEM),
        scratch_shapes=[pltpu.VMEM((keys, rows), f32), pltpu.VMEM((HEAD_DIM, keys), bf16)],
        compiler_params=plain_params(40 << 20),
        cost_estimate=pl.CostEstimate(
            flops=4 * rows * keys * width + 12 * heads * rows * keys * 100,
            bytes_accessed=4 * rows * width + 4 * keys * HEAD_DIM,
            transcendentals=heads * rows * keys,
        ),
        name="attend",
    )(facts, query, pair)


def turn(field, cosine, sine):
    return field * cosine + pltpu.roll(field, HEAD_DIM // 2, 1) * sine


def attend_back(facts, query, pair, lse, d_mixed, cosine, sine):
    rows, width = query.shape
    keys = pair.shape[0]
    heads = width // HEAD_DIM
    bf16, f32 = jnp.bfloat16, jnp.float32
    scale = 1.0 / math.sqrt(HEAD_DIM)

    def kernel(facts_ref, query_ref, pair_ref, lse_ref, d_mixed_ref, cos_ref, sin_ref, d_query_ref, d_own_ref, d_rest_ref, bias, key_t, d_key, d_value):
        bias[...] = key_bias_table(facts_ref[0], facts_ref[1], keys, rows)
        key_t[...] = pair_ref[:, :HEAD_DIM].T
        for head in range(heads):
            cols = slice(head * HEAD_DIM, (head + 1) * HEAD_DIM)
            scores = contract_last(pair_ref[:, :HEAD_DIM], query_ref[:, cols]) * scale + bias[...]
            probs = jnp.exp(scores - lse_ref[head : head + 1, :])
            d_probs = contract_last(pair_ref[:, HEAD_DIM:], d_mixed_ref[:, cols])
            inner = jnp.sum(d_probs * probs, 0, keepdims=True)
            d_scores = (probs * (d_probs - inner)).astype(bf16)
            d_query = (dot_nn(key_t[...], d_scores) * scale).T
            d_query_ref[:, cols] = turn(d_query, cos_ref[...], -sin_ref[...]).astype(bf16)
            more_key = dot_nn(d_scores, query_ref[:, cols])
            more_value = dot_nn(probs.astype(bf16), d_mixed_ref[:, cols])
            if head == 0:
                d_key[...] = more_key
                d_value[...] = more_value
            else:
                d_key[...] += more_key
                d_value[...] += more_value
        d_own_ref[:, :HEAD_DIM] = d_key[:rows, :] * scale
        d_own_ref[:, HEAD_DIM:] = d_value[:rows, :]
        d_rest_ref[:, :HEAD_DIM] = (d_key[rows:, :] * scale).astype(bf16)
        d_rest_ref[:, HEAD_DIM:] = d_value[rows:, :].astype(bf16)

    return pl.pallas_call(
        kernel,
        out_shape=(
            jax.ShapeDtypeStruct((rows, width), bf16),
            jax.ShapeDtypeStruct((rows, 2 * HEAD_DIM), f32),
            jax.ShapeDtypeStruct((keys - rows, 2 * HEAD_DIM), bf16),
        ),
        in_specs=[SMEM] + [VMEM] * 6,
        out_specs=(VMEM, VMEM, VMEM),
        scratch_shapes=[
            pltpu.VMEM((keys, rows), f32),
            pltpu.VMEM((HEAD_DIM, keys), bf16),
            pltpu.VMEM((keys, HEAD_DIM), f32),
            pltpu.VMEM((keys, HEAD_DIM), f32),
        ],
        compiler_params=plain_params(40 << 20),
        cost_estimate=pl.CostEstimate(
            flops=10 * rows * keys * width + 12 * heads * rows * keys * 200,
            bytes_accessed=8 * rows * width + 8 * keys * HEAD_DIM,
            transcendentals=heads * rows * keys,
        ),
        name="attend_back",
    )(facts, query, pair, lse, d_mixed, cosine, sine)


MESH = pl.DeviceIdType.MESH


def flipped(index, mask):
    return index + mask - 2 * mask * ((index // mask) % 2)


def gather_and_sum(units, features, blocks, size):
    bf16, f32 = jnp.bfloat16, jnp.float32
    count = len(units)
    gathered = [isinstance(u, (list, tuple)) for u in units]
    flat = [a for u in units for a in (u if isinstance(u, (list, tuple)) else [u])]
    starts, at = [], 0
    for u in units:
        starts.append(at)
        at += len(u) if isinstance(u, (list, tuple)) else 1
    rows = flat[0].shape[0]
    widest = max(a.shape[1] for a in flat)
    own_rows, tokens = features[0].shape
    widths = []
    where = []
    counts = {}
    for u, group in enumerate(blocks):
        for spans in group:
            width = sum(w for _, _, w in spans)
            if width not in counts:
                counts[width] = 0
                widths.append(width)
            where.append((u, spans, widths.index(width), counts[width]))
            counts[width] += 1
    block_count = len(where)
    steps = []
    held = [0]
    for mask in far_masks(size):
        for r in list(held):
            steps.append((r, mask))
            held.append(r ^ mask)
    for r in list(held):
        steps.append((r, 1))
    arrival = {r ^ mask: n for n, (r, mask) in enumerate(steps)}
    ahead = 2

    def kernel(*refs):
        refs = list(refs)
        unit_refs, refs = refs[: len(flat)], refs[len(flat) :]
        feature_refs, refs = refs[: len(features)], refs[len(features) :]
        outs, refs = refs[: len(widths)], refs[len(widths) :]
        land, refs = refs[0], refs[1:]
        mine, refs = refs[: len(widths)], refs[len(widths) :]
        first, refs = refs[: len(widths)], refs[len(widths) :]
        second, refs = refs[: len(widths)], refs[len(widths) :]
        table, send_g, recv_g, send_a, recv_a, send_b, recv_b, load, store = refs
        me = lax.axis_index("dp")
        place = lax.axis_index("context")
        middle = place * (3 - place) == 2
        inner = 1 + place // 2
        across = 3 - place
        outer = 3 * (place - 1)

        barrier = pltpu.get_barrier_semaphore()
        partners = sorted(set(mask for _, mask in steps))
        for mask in partners:
            pl.semaphore_signal(barrier, 1, device_id={"dp": flipped(me, mask)}, device_id_type=MESH)

        @pl.when(middle)
        def _():
            pl.semaphore_signal(barrier, 1, device_id={"context": across}, device_id_type=MESH)
            pl.semaphore_signal(barrier, 1, device_id={"context": outer}, device_id_type=MESH)
            pl.semaphore_wait(barrier, len(partners) + 2)

        @pl.when(jnp.logical_not(middle))
        def _():
            pl.semaphore_signal(barrier, 1, device_id={"context": inner}, device_id_type=MESH)
            pl.semaphore_wait(barrier, len(partners) + 1)

        def piece(u, r):
            if gathered[u]:
                return unit_refs[starts[u] + r]
            if r == 0:
                return unit_refs[starts[u]]
            return land.at[r - 1, u, :, pl.ds(0, flat[starts[u]].shape[1])]

        def transfer(u, n):
            r, mask = steps[n]
            target = r ^ mask
            return pltpu.make_async_remote_copy(
                src_ref=piece(u, r),
                dst_ref=land.at[target - 1, u, :, pl.ds(0, flat[starts[u]].shape[1])],
                send_sem=send_g.at[n, u],
                recv_sem=recv_g.at[n, u],
                device_id={"dp": flipped(me, mask)},
                device_id_type=MESH,
            )

        wanted = [u for u in range(count) if not gathered[u]]

        def begin(u):
            for n, (r, _) in enumerate(steps):
                if r == 0:
                    transfer(u, n).start()

        def loads(u, slot):
            width = flat[starts[u]].shape[1]
            return [
                pltpu.make_async_copy(
                    piece(u, r),
                    table.at[slot, pl.ds(r * rows, rows), pl.ds(0, width)],
                    load.at[slot, r],
                )
                for r in range(size)
            ]

        def forward(u):
            waited = set()
            for n, (r, mask) in enumerate(steps):
                if r != 0:
                    if r not in waited:
                        transfer(u, arrival[r]).wait_recv()
                        waited.add(r)
                    transfer(u, n).start()
            for r in range(1, size):
                if r not in waited:
                    transfer(u, arrival[r]).wait_recv()

        def hop(j, source, target, place_to, send, recv):
            _, _, kind, index = where[j]
            return pltpu.make_async_remote_copy(
                src_ref=source[kind].at[index],
                dst_ref=target[kind].at[index],
                send_sem=send.at[j],
                recv_sem=recv.at[j],
                device_id={"context": place_to},
                device_id_type=MESH,
            )

        def hop_in(j):
            return hop(j, mine, first, inner, send_a, recv_a)

        def hop_across(j):
            return hop(j, mine, second, across, send_b, recv_b)

        def hop_out(j):
            return hop(j, first, first, outer, send_a, recv_a)

        def keep(j):
            _, _, kind, index = where[j]
            return pltpu.make_async_copy(first[kind].at[index], outs[kind].at[index], store.at[j])

        def total_in(j):
            _, _, kind, index = where[j]
            hop_in(j).wait_recv()
            mine[kind][index] = (
                mine[kind][index].astype(f32) + first[kind][index].astype(f32)
            ).astype(bf16)
            hop_across(j).start()

        def total_across(j):
            _, _, kind, index = where[j]
            hop_across(j).wait_recv()
            first[kind][index] = (
                mine[kind][index].astype(f32) + second[kind][index].astype(f32)
            ).astype(bf16)
            hop_out(j).start()
            keep(j).start()

        of_unit = [[j for j in range(block_count) if where[j][0] == u] for u in range(count)]
        for u in wanted[:ahead]:
            begin(u)
        for copy in loads(0, 0) if gathered[0] else []:
            copy.start()
        middle_in = []
        for u in range(count):
            slot = u % 2
            if not gathered[u]:
                forward(u)
                later = [v for v in wanted if v > u]
                if len(later) >= ahead:
                    begin(later[ahead - 1])
            if not (u == 0 and gathered[0]):
                for copy in loads(u, slot):
                    copy.start()
            for copy in loads(u, slot):
                copy.wait()
            for j in of_unit[u]:
                _, spans, kind, index = where[j]
                filled = 0
                for which, start, width in spans:
                    mine[kind][index, :, filled : filled + width] = dot_nn(
                        feature_refs[which][...], table[slot, :, start : start + width]
                    ).astype(bf16)
                    filled += width

                @pl.when(jnp.logical_not(middle))
                def _(j=j):
                    if j >= 3:
                        hop_in(j - 3).wait_send()
                    hop_in(j).start()

            if u >= 1:

                @pl.when(middle)
                def _(u=u):
                    for j in of_unit[u - 1]:
                        total_in(j)
                        if j >= 1:
                            total_across(j - 1)

        @pl.when(middle)
        def _():
            for j in of_unit[count - 1]:
                total_in(j)
                total_across(j - 1)
            total_across(block_count - 1)
            for j in range(block_count):
                hop_across(j).wait_send()
                hop_out(j).wait_send()
                keep(j).wait()

        @pl.when(jnp.logical_not(middle))
        def _():
            for j in range(max(block_count - 3, 0), block_count):
                hop_in(j).wait_send()
            for j in range(block_count):
                hop_out(j).wait_recv()
                keep(j).start()
            for j in range(block_count):
                keep(j).wait()

        for u in wanted:
            for n in range(len(steps)):
                transfer(u, n).wait_send()

    def stacks(kind_memory):
        return [kind_memory((counts[w], own_rows, w), bf16) for w in widths]

    columns = sum(counts[w] * w for w in widths)
    results = pl.pallas_call(
        kernel,
        out_shape=[jax.ShapeDtypeStruct((counts[w], own_rows, w), bf16) for w in widths]
        + [jax.ShapeDtypeStruct((size - 1, count, rows, widest), bf16)],
        in_specs=[ANY] * len(flat) + [VMEM] * len(features),
        out_specs=[ANY] * (len(widths) + 1),
        scratch_shapes=stacks(pltpu.VMEM) * 3
        + [
            pltpu.VMEM((2, tokens, widest), bf16),
            pltpu.SemaphoreType.DMA((len(steps), count)),
            pltpu.SemaphoreType.DMA((len(steps), count)),
            pltpu.SemaphoreType.DMA((block_count,)),
            pltpu.SemaphoreType.DMA((block_count,)),
            pltpu.SemaphoreType.DMA((block_count,)),
            pltpu.SemaphoreType.DMA((block_count,)),
            pltpu.SemaphoreType.DMA((2, size)),
            pltpu.SemaphoreType.DMA((block_count,)),
        ],
        compiler_params=pltpu.CompilerParams(
            collective_id=0, has_side_effects=True, vmem_limit_bytes=60 << 20
        ),
        cost_estimate=pl.CostEstimate(
            flops=2 * own_rows * tokens * columns,
            bytes_accessed=2 * tokens * columns + 12 * own_rows * columns,
            transcendentals=0,
        ),
        name="gather_and_sum",
    )(*flat, *features)
    return [(results[kind], index) for _, _, kind, index in where]


def layer(
    length, tokens, grad_out, gains, biases, tables, attention_own, feed_own, width, parts_of_x,
):
    bf16, f32 = jnp.bfloat16, jnp.float32
    rows, features = tokens.shape
    own_rows, units_all = feed_own[0].shape
    chunks = units_all // width
    heads_width = attention_own[0].shape[1]
    heads = heads_width // HEAD_DIM
    keys = tables.shape[1]
    pair_width = attention_own[1].shape[1] + attention_own[2].shape[1]
    projected = heads_width + pair_width
    last_width = projected + heads_width
    halfway = 2 * HEAD_DIM
    size = features // own_rows
    units = chunks + 1
    tokens_all = size * rows
    small_width = 2 * features + projected
    scale = 1.0 / math.sqrt(HEAD_DIM)
    part = 64
    where = []
    every = slice(0, own_rows)
    for k in range(chunks):
        cuts = [slice(0, own_rows // 2), slice(own_rows // 2, own_rows)] if k == 0 else [every]
        for n, which in enumerate((0, 0, 1)):
            for cut in cuts:
                where.append((k, [(which, n * width, width)], 0, 3 * k + n, cut))
    for n in range(last_width // halfway):
        where.append((chunks, [(2 if n * halfway < projected else 3, n * halfway, halfway)], 1, n, every))
    count = len(where)
    widths = (width, halfway)
    attention_width = projected + heads_width
    attention_spans = []
    for array in attention_own:
        attention_spans.append((sum(w for _, w in attention_spans), array.shape[1]))

    def kernel(*refs):
        refs = list(refs)

        def take(n):
            taken = refs[:n]
            del refs[:n]
            return taken

        (length_ref,) = take(1)
        gain_refs, bias_refs = take(2), take(3)
        (tokens_hbm, grad_hbm, tables_hbm) = take(3)
        attention_hbm, own_hbm = take(4), take(3)
        output_hbm, grad_tokens_hbm, small_ref, sum_wide, sum_last, land, acts_hbm, across_wide, across_last = take(9)
        attention_land, near_land, far_land = take(3)
        (mine_wide, mine_last, stage_in, stage_across, table, weights, feature_t, feature_land) = take(8)
        (row_two, row_fall, row_normed, row_branch, hidden_rel, tokens_rel, d_sum, out_sum) = take(8)
        (y_send, y_land, acts_stage, query_v, pair_v, last_v, bias, key_t, d_key, d_value) = take(10)
        (d_mixed, d_rest, d_land, vec, vec_land, total_land) = take(6)
        (gains_v, tables_v, lse_ref, gains_ref, biases_ref) = take(5)
        (s_in, s_weights, s_acts, s_rest, send_g, recv_g, send_a, recv_a, send_b, recv_b) = take(10)
        (s_stage, s_keep, s_table, send_t, recv_t, send_y, recv_y, send_k, recv_k) = take(9)
        (send_v, recv_v, send_w, recv_w, s_store) = take(5)
        (send_m, recv_m, send_near, recv_near, send_x, recv_x, send_z, recv_z, send_c, recv_c, send_p, recv_p) = take(12)
        (s_attention,) = take(1)
        cos_ref, sin_ref = tables_v.at[0], tables_v.at[1]
        sums, mines, acrosses = (sum_wide, sum_last), (mine_wide, mine_last), (across_wide, across_last)
        rows_of = (row_two, row_fall, row_normed, row_branch)

        me = lax.axis_index("dp")
        place = lax.axis_index("context")
        side = lax.axis_index("tensor")
        middle = place * (3 - place) == 2
        inner = 1 + place // 2
        across = 3 - place
        outer = 3 * (place - 1)
        one = flipped(me, 1)
        partner = (me, one, flipped(me, 2), flipped(one, 2))
        parity = lax.rem(place, 2)
        beside = flipped(place, 1)

        barrier = pltpu.get_barrier_semaphore()
        for r in range(1, size):
            pl.semaphore_signal(barrier, 1, device_id={"dp": partner[r]}, device_id_type=MESH)
        for s in range(1, 4):
            pl.semaphore_signal(barrier, 1, device_id={"context": lax.rem(place + s, 4)}, device_id_type=MESH)
        pl.semaphore_signal(barrier, 1, device_id={"tensor": 1 - side}, device_id_type=MESH)

        def block_of(r):
            return pl.ds(pl.multiple_of(partner[r] * own_rows, 128), own_rows)

        def local(source, target, sem):
            return pltpu.make_async_copy(source, target, sem)

        def remote(source, target, send, recv, axis, index):
            return pltpu.make_async_remote_copy(
                src_ref=source, dst_ref=target, send_sem=send, recv_sem=recv,
                device_id={axis: index}, device_id_type=MESH,
            )

        def cols(r):
            return pl.ds(r * own_rows, own_rows)

        ins = []
        for n, (source, target) in enumerate(((tokens_hbm, tokens_rel), (grad_hbm, row_fall))):
            ins.append(
                [local(source.at[:, block_of(r)], target.at[:, cols(r)], s_in.at[n, r]) for r in range(size)]
            )
        rest = [
            local(tables_hbm.at[:, pl.ds(pl.multiple_of(place * rows, rows), rows), :], tables_v, s_rest.at[0])
        ]

        attention_parts = ((0, 3, 0, projected), (3, 4, projected, heads_width))
        half_rows = pl.ds(pl.multiple_of(own_rows // 2 * parity, 64), own_rows // 2)

        def attention_send(n):
            first, last, _, _ = attention_parts[n % 2]
            if n >= 4:
                attention_wait(n).start()
                return
            rows_sent = half_rows if n < 2 else pl.ds(0, own_rows)
            for m in range(first, last):
                at, wide = attention_spans[m]
                remote(
                    attention_hbm[m].at[rows_sent, :],
                    attention_land.at[1 if n < 2 else 0, rows_sent, pl.ds(at, wide)],
                    send_m.at[n], recv_m.at[n], "dp", partner[2 if n < 2 else 1],
                ).start()

        def attention_wait(n):
            _, _, at, wide = attention_parts[n % 2]
            rows_sent = half_rows if n < 2 or n >= 6 else pl.ds(0, own_rows)
            source = attention_land.at[1, rows_sent, pl.ds(at, wide)]
            target = attention_land.at[(1, 0, 2, 1)[n // 2], rows_sent, pl.ds(at, wide)]
            axis, to = ("context", beside) if n >= 6 else ("dp", partner[2 if n < 2 else 1])
            return remote(source, target, send_m.at[n], recv_m.at[n], axis, to)

        def attention_arrived(n):
            _, _, at, wide = attention_parts[n % 2]
            half = pl.ds(pl.multiple_of(own_rows // 2 * (1 - parity), 64), own_rows // 2)
            view = attention_land.at[1, half, pl.ds(at, wide)]
            remote(view, view, send_m.at[n], recv_m.at[n], "context", beside).wait_recv()

        def attention_copies(n):
            first, last, at, wide = attention_parts[n]
            return [
                local(
                    attention_hbm[m],
                    weights.at[pl.ds(0, own_rows), pl.ds(attention_spans[m][0], attention_spans[m][1])],
                    s_attention.at[m],
                )
                for m in range(first, last)
            ] + [
                local(
                    attention_land.at[r - 1, :, pl.ds(at, wide)],
                    weights.at[pl.ds(r * own_rows, own_rows), pl.ds(at, wide)],
                    s_weights.at[n, r],
                )
                for r in range(1, size)
            ]

        def near(which):
            return remote(
                own_hbm[which], near_land.at[which], send_near.at[which], recv_near.at[which], "dp", partner[1]
            )

        def straight_rows(k):
            wide = own_rows * parts_of_x[k] // 6
            return pl.ds(pl.multiple_of((own_rows - wide) * parity, 64), wide)

        def round_rows(k):
            short = own_rows - own_rows * parts_of_x[k] // 6
            return pl.ds(pl.multiple_of((own_rows - short) * parity, 64), short)

        def far_send(k):
            for which in range(3):
                remote(
                    own_hbm[which].at[straight_rows(k), pl.ds(k * width, width)],
                    far_land.at[0, k, straight_rows(k), pl.ds(which * width, width)],
                    send_x.at[k], recv_x.at[k], "dp", partner[2],
                ).start()

        def far_wait(k):
            view = far_land.at[0, k, straight_rows(k), :]
            return remote(view, view, send_x.at[k], recv_x.at[k], "dp", partner[2])

        def far_round(k):
            view = far_land.at[0, k, round_rows(k), :]
            return remote(view, view, send_z.at[k], recv_z.at[k], "context", beside)

        def missing_rows(k):
            short = own_rows - own_rows * parts_of_x[k] // 6
            return pl.ds(pl.multiple_of((own_rows - short) * (1 - parity), 64), short)

        def far_round_wait(k):
            view = far_land.at[0, k, missing_rows(k), :]
            return remote(view, view, send_z.at[k], recv_z.at[k], "context", beside)

        def far_near(k):
            return remote(far_land.at[0, k], far_land.at[1, k], send_c.at[k], recv_c.at[k], "dp", partner[1])

        def weight_straight(k):
            far_wait(k).wait_recv()
            if parts_of_x[k] < 6:
                far_round(k).start()
            else:
                far_near(k).start()

        def weight_round(k):
            if parts_of_x[k] < 6:
                far_round_wait(k).wait_recv()
                far_near(k).start()

        def weight_copies(k, which):
            view = pl.ds(which * width, width)
            sources = [
                own_hbm[which].at[:, pl.ds(k * width, width)],
                near_land.at[which, :, pl.ds(k * width, width)],
                far_land.at[0, k, :, view],
                far_land.at[1, k, :, view],
            ]
            return [
                local(source, weights.at[pl.ds(r * own_rows, own_rows), view], s_weights.at[which, r])
                for r, source in enumerate(sources)
            ]

        def start(copies):
            for copy in copies:
                copy.start()

        def wait(copies):
            for copy in copies:
                copy.wait()

        for copies in ins:
            start(copies)
        start(rest)

        def trade(w, r):
            return remote(
                rows_of[w].at[:, cols(r)], feature_land.at[w, r - 1], send_t.at[w, r - 1], recv_t.at[w, r - 1],
                "dp", partner[r],
            )

        def turn_features(w):
            feature_t[w, :, 0:rows] = rows_of[w][:, 0:own_rows].T
            for r in range(1, size):
                trade(w, r).wait_recv()
                feature_t[w, :, r * rows : (r + 1) * rows] = feature_land[w, r - 1].T

        steps = ((0, 2), (0, 1), (2, 1))

        def unit_width(u):
            return 3 * width if u < chunks else last_width

        def piece(u, r):
            view = pl.ds(0, unit_width(u))
            return acts_hbm.at[u, :, view] if r == 0 else land.at[r - 1, u, :, view]

        def transfer(u, n):
            r, mask = steps[n]
            return remote(
                piece(u, r), land.at[(r ^ mask) - 1, u, :, pl.ds(0, unit_width(u))],
                send_g.at[n, u], recv_g.at[n, u], "dp", partner[mask],
            )

        def own_copy(u):
            if u < chunks:
                return local(acts_stage.at[u % 2], piece(u, 0), s_acts.at[u])
            return local(last_v, piece(u, 0), s_acts.at[u])

        def begin(u):
            own_copy(u).wait()
            transfer(u, 0).start()
            transfer(u, 1).start()

        def table_copies(u):
            return [
                local(
                    piece(u, r), table.at[pl.ds(r * rows, rows), pl.ds(0, unit_width(u))], s_table.at[r]
                )
                for r in range(size)
            ]

        def hop(j, source, target, to, send, recv):
            _, _, kind, index, cut = where[j]
            at = (index, pl.ds(cut.start, cut.stop - cut.start))
            return remote(source[kind].at[at], target[kind].at[at], send.at[j], recv.at[j], "context", to)

        def hop_in(j):
            return hop(j, mines, sums, inner, send_a, recv_a)

        def hop_across(j):
            return hop(j, mines, acrosses, across, send_b, recv_b)

        def hop_out(j):
            return hop(j, mines, sums, outer, send_a, recv_a)

        def staged(j, source, stage, n):
            _, _, kind, index, cut = where[j]
            tall = pl.ds(cut.start, cut.stop - cut.start)
            return local(
                source[kind].at[index, tall], stage.at[j % 2, tall, pl.ds(0, widths[kind])], s_stage.at[n, j % 2]
            )

        def keep(j):
            _, _, kind, index, cut = where[j]
            at = (index, pl.ds(cut.start, cut.stop - cut.start))
            return local(mines[kind].at[at], sums[kind].at[at], s_keep.at[j])

        def add_stage(j, stage):
            _, _, kind, index, cut = where[j]
            mines[kind][index, cut] = (
                mines[kind][index, cut].astype(f32) + stage[j % 2, cut, 0 : widths[kind]].astype(f32)
            ).astype(bf16)

        def line_in(j):
            hop_in(j).wait_recv()
            staged(j, sums, stage_in, 0).start()
            staged(j, sums, stage_in, 0).wait()
            add_stage(j, stage_in)
            hop_across(j).start()

        def line_out(j):
            hop_across(j).wait_recv()
            staged(j, acrosses, stage_across, 1).start()
            staged(j, acrosses, stage_across, 1).wait()
            hop_across(j).wait_send()
            add_stage(j, stage_across)
            hop_out(j).start()
            keep(j).start()

        of_unit = [[j for j in range(count) if where[j][0] == u] for u in range(units)]

        def gradients(u):
            transfer(u, 0).wait_recv()
            transfer(u, 2).start()
            transfer(u, 1).wait_recv()
            transfer(u, 2).wait_recv()
            start(table_copies(u))
            wait(table_copies(u))
            for j in of_unit[u]:
                _, spans, kind, index, cut = where[j]
                filled = 0
                for which, at, w in spans:
                    mines[kind][index, cut, filled : filled + w] = dot_nn(
                        feature_t[which, cut], table[:, at : at + w]
                    ).astype(bf16)
                    filled += w

                @pl.when(jnp.logical_not(middle))
                def _(j=j):
                    if j >= 3:
                        hop_in(j - 3).wait_send()
                    hop_in(j).start()

        def feed(k):
            far_near(k).wait_recv()
            for which in range(3):
                if k == 0:
                    near(which).wait_recv()
                start(weight_copies(k, which))
            wait(weight_copies(k, 0))
            gate_w, up_w, down_w = (weights.at[:, pl.ds(n * width, width)] for n in range(3))
            gate = dot_nn(row_two[...], gate_w[...])
            wait(weight_copies(k, 1))
            up = dot_nn(row_two[...], up_w[...])
            wait(weight_copies(k, 2))
            d_active = dot_nn(row_fall[...], down_w[...])
            sigmoid = jax.nn.sigmoid(gate)
            swish = gate * sigmoid
            stage = acts_stage.at[k % 2]
            stage[:, 2 * width :] = (swish * up).astype(bf16)
            stage[:, :width] = (d_active * up * sigmoid * (1.0 + gate * (1.0 - sigmoid))).astype(bf16)
            stage[:, width : 2 * width] = (d_active * swish).astype(bf16)
            own_copy(k).start()
            d_part = contract_last(stage[:, :width], gate_w[...]) + contract_last(
                stage[:, width : 2 * width], up_w[...]
            )
            out_part = contract_last(stage[:, 2 * width :], down_w[...])
            if k == 0:
                d_sum[...] = d_part
                out_sum[...] = out_part
            else:
                d_sum[...] += d_part
                out_sum[...] += out_part

        def swap(n):
            return remote(y_send.at[n], y_land.at[n], send_y.at[n], recv_y.at[n], "tensor", 1 - side)

        for n, ref in enumerate(gain_refs):
            gains_ref[n : n + 1, :] = ref[...].astype(f32).reshape(1, features)
        at = 0
        for ref in bias_refs:
            biases_ref[:, at : at + ref.shape[0]] = ref[...].astype(f32).reshape(1, ref.shape[0])
            at += ref.shape[0]
        for r in range(size):
            gains_v[:, r * own_rows : (r + 1) * own_rows] = gains_ref[:, block_of(r)]
        gain_one, gain_two = gains_v[0:1, :], gains_v[1:2, :]

        def mean_scale(field):
            return lax.rsqrt(jnp.mean(field * field, -1, keepdims=True) + EPSILON)

        spans_of_rows = [slice(n, n + part) for n in range(0, rows, part)]

        def row_valid(span):
            at = lax.broadcasted_iota(jnp.int32, (part, 1), 0) + (place * rows + span.start)
            return (at < length_ref[0]).astype(f32)

        def keep_gain(which, value):
            for r in range(size):
                at = pl.multiple_of(partner[r] * own_rows + which * features, 128)
                vec[:, pl.ds(at, own_rows)] = value[:, r * own_rows : (r + 1) * own_rows]

        pl.semaphore_wait(barrier, size - 1 + 3 + 1)
        attention_send(0)
        attention_send(2)
        attention_send(1)
        attention_send(3)
        far_send(0)
        wait(ins[0])
        for span in spans_of_rows:
            field = tokens_rel[span, :].astype(f32)
            row_normed[span, :] = (field * mean_scale(field) * gain_one).astype(bf16)
        wait(ins[1])
        for span in spans_of_rows:
            row_fall[span, :] = (row_fall[span, :].astype(f32) * row_valid(span)).astype(bf16)
        for r in (2, 3, 1):
            trade(1, r).start()
        far_send(1)
        far_send(2)
        attention_wait(0).wait_recv()
        attention_send(6)
        bias[...] = key_bias_table(place, length_ref[0], keys, rows)
        attention_wait(1).wait_recv()
        attention_send(7)
        attention_arrived(6)
        attention_send(4)
        near(0).start()
        attention_wait(2).wait_recv()
        attention_wait(4).wait_recv()
        start(attention_copies(0))
        wait(rest)
        wait(attention_copies(0))
        queries = dot_nn(row_normed[...], weights[:, 0:heads_width]) + biases_ref[:, 0:heads_width]
        for head in range(heads):
            at = slice(head * HEAD_DIM, (head + 1) * HEAD_DIM)
            query_v[:, at] = turn(queries[:, at], cos_ref[...], sin_ref[...]).astype(bf16)
        others = dot_nn(row_normed[...], weights[:, heads_width:projected]) + biases_ref[:, heads_width:projected]
        pair_v[0:rows, :HEAD_DIM] = turn(others[:, :HEAD_DIM], cos_ref[...], sin_ref[...]).astype(bf16)
        pair_v[0:rows, HEAD_DIM:] = others[:, HEAD_DIM:].astype(bf16)

        def lend(s):
            return remote(
                pair_v.at[pl.ds(0, rows), :], pair_v.at[pl.ds(s * rows, rows), :], send_p.at[s - 1], recv_p.at[s - 1],
                "context", place + s,
            )

        for s in range(1, 4):
            pl.when(place + s <= 3)(lend(s).start)

            @pl.when(place < s)
            def _(s=s):
                pair_v[s * rows : (s + 1) * rows, :] = jnp.zeros((rows, pair_width), bf16)

        attention_arrived(7)
        attention_send(5)
        near(1).start()
        near(2).start()
        for s in range(1, 4):
            pl.when(place >= s)(lend(s).wait_recv)
        weight_straight(0)
        key_t[...] = pair_v[:, HEAD_DIM:].T
        for head in range(heads):
            at = slice(head * HEAD_DIM, (head + 1) * HEAD_DIM)
            scores = contract_last(pair_v[:, :HEAD_DIM], query_v[:, at]) * scale + bias[...]
            top = jnp.max(scores, 0, keepdims=True)
            raised = jnp.exp(scores - top)
            total = jnp.sum(raised, 0, keepdims=True)
            lse_ref[head : head + 1, :] = top + jnp.log(total)
            probs = (raised * (1.0 / total)).astype(bf16)
            mixed_at = slice(projected + head * HEAD_DIM, projected + (head + 1) * HEAD_DIM)
            last_v[:, mixed_at] = dot_nn(key_t[...], probs).T.astype(bf16)
        attention_wait(3).wait_recv()
        attention_wait(5).wait_recv()
        start(attention_copies(1))
        wait(attention_copies(1))
        y_send[3] = contract_last(last_v[:, projected:], weights[:, projected:attention_width]).astype(bf16)
        swap(3).start()
        weight_round(0)
        weight_straight(1)
        swap(3).wait_recv()
        for span in spans_of_rows:
            field = tokens_rel[span, :].astype(f32) + (
                y_send[3, span, :].astype(f32) + y_land[3, span, :].astype(f32)
            )
            hidden_rel[span, :] = field
            row_two[span, :] = (field * mean_scale(field) * gain_two).astype(bf16)
        def share(r):
            return remote(vec, vec_land.at[me], send_v.at[r - 1], recv_v.at[r - 1], "dp", partner[r])

        def spread(s):
            return remote(
                vec, total_land.at[place], send_w.at[s - 1], recv_w.at[s - 1], "context", lax.rem(place + s, 4)
            )

        far_send(3)
        feed(0)
        for r in (2, 3, 1):
            trade(0, r).start()
        begin(0)
        weight_straight(2)
        weight_straight(3)
        weight_round(1)
        feed(1)
        far_send(4)
        begin(1)
        turn_features(1)
        weight_round(3)
        turn_features(0)
        weight_round(2)
        gradients(0)

        @pl.when(middle)
        def _():
            line_in(0)
            line_in(1)

        feed(2)

        @pl.when(middle)
        def _():
            line_in(2)

        weight_straight(4)

        @pl.when(middle)
        def _():
            line_out(0)
            line_out(1)
            line_in(3)
            line_in(4)

        far_send(5)

        @pl.when(middle)
        def _():
            line_in(5)

        begin(2)

        @pl.when(middle)
        def _():
            line_out(2)
            line_out(3)

        gradients(1)

        @pl.when(middle)
        def _():
            line_out(4)
            line_out(5)
            line_in(6)

        feed(3)
        begin(3)

        @pl.when(middle)
        def _():
            line_in(7)

        weight_round(4)
        weight_straight(5)

        @pl.when(middle)
        def _():
            line_out(6)

        feed(4)

        @pl.when(middle)
        def _():
            line_in(8)
            line_out(7)

        gradients(2)
        begin(4)

        @pl.when(middle)
        def _():
            line_out(8)
            line_in(9)

        gradients(3)

        @pl.when(middle)
        def _():
            line_in(10)
            line_out(9)

        far_send(6)
        weight_round(5)

        @pl.when(middle)
        def _():
            line_in(11)
            line_out(10)
            line_in(12)

        feed(5)

        @pl.when(middle)
        def _():
            line_out(11)
            line_in(13)
            line_out(12)

        gradients(4)

        @pl.when(middle)
        def _():
            line_in(14)

        begin(5)

        @pl.when(middle)
        def _():
            line_out(13)

        weight_straight(6)
        weight_round(6)

        @pl.when(middle)
        def _():
            line_in(15)

        feed(6)

        @pl.when(middle)
        def _():
            line_out(14)

        for r in (2, 3, 1):
            trade(2, r).start()
        y_send[0] = d_sum[...].astype(bf16)
        swap(0).start()
        start(attention_copies(0) + attention_copies(1))

        @pl.when(middle)
        def _():
            line_in(16)

        begin(6)

        @pl.when(middle)
        def _():
            line_out(15)

        gradients(5)

        @pl.when(middle)
        def _():
            line_in(17)
            line_out(16)

        y_send[1] = out_sum[...].astype(bf16)
        swap(0).wait_recv()
        swap(1).start()
        gain_sum = jnp.zeros((1, features), f32)
        for span in spans_of_rows:
            d_normed = y_send[0, span, :].astype(f32) + y_land[0, span, :].astype(f32)
            field = hidden_rel[span, :]
            r2 = mean_scale(field)
            gain_sum = gain_sum + jnp.sum(d_normed * field * r2, 0, keepdims=True)
            weighted = d_normed * gain_two
            d_hidden = (
                row_fall[span, :].astype(f32)
                + r2 * weighted
                - field * (r2 * r2 * r2) * jnp.mean(field * weighted, -1, keepdims=True)
            )
            d_sum[span, :] = d_hidden
            row_branch[span, :] = d_hidden.astype(bf16)
        keep_gain(1, gain_sum)
        for r in (2, 3, 1):
            trade(3, r).start()
        wait(attention_copies(0) + attention_copies(1))
        d_mixed[...] = dot_nn(row_branch[...], weights[:, projected:attention_width]).astype(bf16)

        @pl.when(middle)
        def _():
            line_in(18)
            line_out(17)

        key_t[...] = pair_v[:, :HEAD_DIM].T
        for head in range(heads):
            at = slice(head * HEAD_DIM, (head + 1) * HEAD_DIM)
            scores = contract_last(pair_v[:, :HEAD_DIM], query_v[:, at]) * scale + bias[...]
            probs = jnp.exp(scores - lse_ref[head : head + 1, :])
            d_probs = contract_last(pair_v[:, HEAD_DIM:], d_mixed[:, at])
            inside = jnp.sum(d_probs * probs, 0, keepdims=True)
            d_scores = (probs * (d_probs - inside)).astype(bf16)
            d_query = (dot_nn(key_t[...], d_scores) * scale).T
            last_v[:, at] = turn(d_query, cos_ref[...], -sin_ref[...]).astype(bf16)
            more_key = dot_nn(d_scores, query_v[:, at])
            more_value = dot_nn(probs.astype(bf16), d_mixed[:, at])
            if head == 0:
                d_key[...] = more_key
                d_value[...] = more_value
            else:
                d_key[...] += more_key
                d_value[...] += more_value
        d_rest[:, :HEAD_DIM] = (d_key[rows:, :] * scale).astype(bf16)
        d_rest[:, HEAD_DIM:] = d_value[rows:, :].astype(bf16)

        def give(s):
            return remote(
                d_rest.at[pl.ds((s - 1) * rows, rows), :], d_land.at[s - 1], send_k.at[s - 1], recv_k.at[s - 1],
                "context", place - s,
            )

        for s in range(1, 4):
            pl.when(place >= s)(give(s).start)

        @pl.when(middle)
        def _():
            line_in(19)
            line_in(20)
            line_out(18)

        gradients(6)

        @pl.when(middle)
        def _():
            line_out(19)
            line_in(21)

        turn_features(2)
        d_key[0:rows, :] = d_key[0:rows, :] * scale
        for s in range(1, 4):

            @pl.when(place + s <= 3)
            def _(s=s):
                give(s).wait_recv()
                d_key[0:rows, :] += d_land[s - 1, :, :HEAD_DIM].astype(f32)
                d_value[0:rows, :] += d_land[s - 1, :, HEAD_DIM:].astype(f32)

        last_v[:, heads_width : heads_width + HEAD_DIM] = turn(
            d_key[0:rows, :], cos_ref[...], -sin_ref[...]
        ).astype(bf16)
        last_v[:, heads_width + HEAD_DIM : projected] = d_value[0:rows, :].astype(bf16)
        own_copy(chunks).start()
        begin(chunks)
        swap(1).wait_recv()
        swap(1).wait_send()
        for span in spans_of_rows:
            whole = y_send[1, span, :].astype(f32) + y_land[1, span, :].astype(f32)
            y_land[1, span, :] = (row_valid(span) * (hidden_rel[span, :] + whole)).astype(bf16)

        def stored(n, target):
            return [
                local(y_land.at[n, :, cols(r)], target.at[:, block_of(r)], s_store.at[n, r]) for r in range(size)
            ]

        start(stored(1, output_hbm))

        @pl.when(middle)
        def _():
            line_out(20)

        y_send[2] = contract_last(last_v[:, 0:projected], weights[:, 0:projected]).astype(bf16)
        swap(2).start()
        vec[:, 2 * features :] = jnp.sum(last_v[:, 0:projected].astype(f32), 0, keepdims=True)

        @pl.when(middle)
        def _():
            line_in(22)

        turn_features(3)

        @pl.when(middle)
        def _():
            line_out(21)
            line_in(23)
            line_out(22)

        gradients(7)

        @pl.when(middle)
        def _():
            line_in(24)
            line_in(25)
            line_out(23)

        swap(2).wait_recv()
        swap(2).wait_send()
        gain_sum = jnp.zeros((1, features), f32)
        for span in spans_of_rows:
            d_normed = y_send[2, span, :].astype(f32) + y_land[2, span, :].astype(f32)
            field = tokens_rel[span, :].astype(f32)
            r1 = mean_scale(field)
            gain_sum = gain_sum + jnp.sum(d_normed * field * r1, 0, keepdims=True)
            weighted = d_normed * gain_one
            y_land[2, span, :] = (
                d_sum[span, :]
                + r1 * weighted
                - field * (r1 * r1 * r1) * jnp.mean(field * weighted, -1, keepdims=True)
            ).astype(bf16)
        start(stored(2, grad_tokens_hbm))
        keep_gain(0, gain_sum)


        @pl.when(middle)
        def _():
            line_in(26)
            line_out(24)
            line_out(25)

        for r in range(1, size):
            share(r).start()
        vec_land[me] = vec[...]

        @pl.when(middle)
        def _():
            line_in(27)
            line_in(28)
            line_out(26)
            line_out(27)

        for r in range(1, size):
            share(r).wait()
        vec[...] = vec_land[0] + vec_land[1] + vec_land[2] + vec_land[3]
        for s in range(1, 4):
            spread(s).start()
        total_land[place] = vec[...]

        @pl.when(middle)
        def _():
            line_in(29)
            line_out(28)
            line_in(30)
            line_out(29)
            line_out(30)

        for s in range(1, 4):
            spread(s).wait()
        small_ref[...] = total_land[0] + total_land[1] + total_land[2] + total_land[3]

        @pl.when(middle)
        def _():
            for j in range(count):
                hop_out(j).wait_send()
                keep(j).wait()

        @pl.when(jnp.logical_not(middle))
        def _():
            for j in range(count - 3, count):
                hop_in(j).wait_send()
            for j in range(count):
                hop_out(j).wait_recv()

        wait(stored(1, output_hbm))
        wait(stored(2, grad_tokens_hbm))
        swap(0).wait_send()
        swap(3).wait_send()
        for n in range(8):
            attention_wait(n).wait_send()
        for which in range(3):
            near(which).wait_send()
        for k in range(chunks):
            far_wait(k).wait_send()
            if parts_of_x[k] < 6:
                far_round(k).wait_send()
            far_near(k).wait_send()
        for s in range(1, 4):
            pl.when(place >= s)(give(s).wait_send)
            pl.when(place + s <= 3)(lend(s).wait_send)
        for w in range(4):
            for r in range(1, size):
                trade(w, r).wait_send()
        for u in range(units):
            for n in range(3):
                transfer(u, n).wait_send()

    dma = pltpu.SemaphoreType.DMA
    shape = jax.ShapeDtypeStruct
    wide, last = (3 * chunks, own_rows, width), (last_width // halfway, own_rows, halfway)
    results = pl.pallas_call(
        kernel,
        out_shape=(
            shape((rows, features), bf16),
            shape((rows, features), bf16),
            shape((1, small_width), f32),
            shape(wide, bf16),
            shape(last, bf16),
            shape((size - 1, units, rows, 3 * width), bf16),
            shape((units, rows, 3 * width), bf16),
            shape(wide, bf16),
            shape(last, bf16),
            shape((size - 1, own_rows, attention_width), bf16),
            shape((3, own_rows, units_all), bf16),
            shape((2, chunks, own_rows, 3 * width), bf16),
        ),
        in_specs=[SMEM] + [VMEM] * 5 + [ANY] * (3 + 4 + 3),
        out_specs=(ANY, ANY, VMEM) + (ANY,) * 9,
        scratch_shapes=[
            pltpu.VMEM(wide, bf16),
            pltpu.VMEM(last, bf16),
            pltpu.VMEM((2, own_rows, max(widths)), bf16),
            pltpu.VMEM((2, own_rows, max(widths)), bf16),
            pltpu.VMEM((tokens_all, 3 * width), bf16),
            pltpu.VMEM((features, 3 * width), bf16),
            pltpu.VMEM((4, own_rows, tokens_all), bf16),
            pltpu.VMEM((4, size - 1, rows, own_rows), bf16),
            pltpu.VMEM((rows, features), bf16),
            pltpu.VMEM((rows, features), bf16),
            pltpu.VMEM((rows, features), bf16),
            pltpu.VMEM((rows, features), bf16),
            pltpu.VMEM((rows, features), f32),
            pltpu.VMEM((rows, features), bf16),
            pltpu.VMEM((rows, features), f32),
            pltpu.VMEM((rows, features), f32),
            pltpu.VMEM((4, rows, features), bf16),
            pltpu.VMEM((4, rows, features), bf16),
            pltpu.VMEM((2, rows, 3 * width), bf16),
            pltpu.VMEM((rows, heads_width), bf16),
            pltpu.VMEM((keys, pair_width), bf16),
            pltpu.VMEM((rows, last_width), bf16),
            pltpu.VMEM((keys, rows), f32),
            pltpu.VMEM((HEAD_DIM, keys), bf16),
            pltpu.VMEM((keys, HEAD_DIM), f32),
            pltpu.VMEM((keys, HEAD_DIM), f32),
            pltpu.VMEM((rows, heads_width), bf16),
            pltpu.VMEM((keys - rows, pair_width), bf16),
            pltpu.VMEM((3, rows, pair_width), bf16),
            pltpu.VMEM((1, small_width), f32),
            pltpu.VMEM((4, 1, small_width), f32),
            pltpu.VMEM((4, 1, small_width), f32),
            pltpu.VMEM((2, features), f32),
            pltpu.VMEM((2, rows, HEAD_DIM), f32),
            pltpu.VMEM((8, rows), f32),
            pltpu.VMEM((2, features), f32),
            pltpu.VMEM((1, projected), f32),
            dma((2, size)),
            dma((3, size)),
            dma((units,)),
            dma((1,)),
            dma((3, units)),
            dma((3, units)),
            dma((count,)),
            dma((count,)),
            dma((count,)),
            dma((count,)),
            dma((2, 2)),
            dma((count,)),
            dma((size,)),
            dma((4, size - 1)),
            dma((4, size - 1)),
            dma((4,)),
            dma((4,)),
            dma((3,)),
            dma((3,)),
            dma((size - 1,)),
            dma((size - 1,)),
            dma((3,)),
            dma((3,)),
            dma((3, size)),
            dma((8,)),
            dma((8,)),
            dma((3,)),
            dma((3,)),
            dma((chunks,)),
            dma((chunks,)),
            dma((chunks,)),
            dma((chunks,)),
            dma((chunks,)),
            dma((chunks,)),
            dma((3,)),
            dma((3,)),
            dma((4,)),
        ],
        compiler_params=pltpu.CompilerParams(
            collective_id=0, has_side_effects=True, vmem_limit_bytes=60 << 20
        ),
        name="layer",
    )(
        length, *gains, *biases, tokens, grad_out, tables, *attention_own, *feed_own,
    )
    return results[:5]


def finish(wide, last, output, grad_tokens, small, spans, small_spans):
    blocks, own_rows, width = wide.shape
    halfway = last.shape[2]
    chunks = blocks // 3
    row_steps = 4
    f32 = jnp.float32

    def kernel(wide_ref, last_ref, small_ref, output_ref, tokens_ref, *refs):
        outs = refs
        at = pl.program_id(0)
        block = last_ref[0].astype(f32)
        for (start, size), out in zip(spans, outs[3:]):
            if size % halfway == 0:
                first, count = start // halfway, size // halfway

                @pl.when((at >= first) & (at < first + count))
                def _(out=out):
                    out[...] = block

            else:

                @pl.when(at == start // halfway)
                def _(out=out, low=start % halfway, size=size):
                    out[...] = block[:, low : low + size]

        @pl.when(at < row_steps)
        def _():
            outs[-2][...] = output_ref[...]
            outs[-1][...] = tokens_ref[...]

        @pl.when(at == 0)
        def _():
            for (start, size), out in zip(small_spans, outs[3 + len(spans) :]):
                out[...] = small_ref[0, start : start + size]

        for n in range(3):
            outs[n][...] = wide_ref[n].astype(f32)

    def whole(shape):
        return pl.BlockSpec(shape, lambda k: (0,) * len(shape))

    def by_span(start, size):
        if size % halfway:
            return whole((own_rows, size))
        first, count = start // halfway, size // halfway
        return pl.BlockSpec((own_rows, halfway), lambda k: (0, jnp.clip(k - first, 0, count - 1)))

    by_rows = pl.BlockSpec(
        (output.shape[0] // row_steps, output.shape[1]), lambda k: (jnp.minimum(k, row_steps - 1), 0)
    )

    shape = jax.ShapeDtypeStruct
    return pl.pallas_call(
        kernel,
        grid=(chunks,),
        out_shape=[shape((own_rows, chunks * width), f32)] * 3
        + [shape((own_rows, size), f32) for _, size in spans]
        + [shape((size,), f32) for _, size in small_spans]
        + [shape(output.shape, output.dtype)] * 2,
        in_specs=[
            pl.BlockSpec((3, own_rows, width), lambda k: (k, 0, 0)),
            pl.BlockSpec((1, own_rows, halfway), lambda k: (jnp.minimum(k, last.shape[0] - 1), 0, 0)),
            whole(small.shape),
            by_rows,
            by_rows,
        ],
        out_specs=[pl.BlockSpec((own_rows, width), lambda k: (0, k))] * 3
        + [by_span(start, size) for start, size in spans]
        + [whole((size,)) for _, size in small_spans]
        + [by_rows] * 2,
        compiler_params=plain_params(60 << 20),
        name="finish",
    )(wide, last, small, output, grad_tokens)


def rotary_tables(position_count):
    half = HEAD_DIM // 2
    inverse = np.exp(np.arange(half) * (-2.0 * math.log(ROPE_BASE) / HEAD_DIM))
    angles = np.arange(position_count)[:, None] * inverse[None, :]
    cosine, sine = np.cos(angles), np.sin(angles)
    return np.stack(
        [np.concatenate([cosine, cosine], 1), np.concatenate([-sine, sine], 1)]
    ).astype(np.float32)


PARTS_OF_X = (3, 3, 3, 3, 4, 4, 6)


def chunk_edges(columns):
    tiles = columns // 128
    count = next((n for n in (7, 5, 4, 6, 3, 2) if tiles % n == 0), 1)
    width = columns // count
    return [(n * width, width) for n in range(count)]


def local(
    tokens,
    lengths,
    gain_one,
    w_query,
    b_query,
    key_weight,
    key_bias,
    value_weight,
    value_bias,
    w_out,
    gain_two,
    w_gate,
    w_up,
    w_down,
    grad_out,
):
    bf16, f32 = jnp.bfloat16, jnp.float32
    seq_count, block_len, model_width = tokens.shape
    row_count = seq_count * block_len
    query_cols = w_query.shape[1]
    key_cols = key_weight.shape[1]
    unit_cols = w_gate.shape[1]
    own_rows = w_query.shape[0]
    head_count = query_cols // HEAD_DIM
    kv_count = key_cols // HEAD_DIM
    query_group_width = head_count // kv_count
    size = lax.axis_size("dp")
    me = lax.axis_index("dp")
    blocks_along = lax.axis_size("context")
    place = lax.axis_index("context")
    parity = place % 2 if blocks_along % 2 == 0 and own_rows % 32 == 0 else None

    edges = chunk_edges(unit_cols)
    if (
        size == 4
        and blocks_along == 4
        and lax.axis_size("tensor") == 2
        and own_rows % 384 == 0
        and row_count % 64 == 0
        and len(edges) == len(PARTS_OF_X)
        and kv_count == 1
        and seq_count == 1
    ):
        output, grad_tokens, small, feed_sums, last_sums = layer(
            lengths,
            tokens.reshape(row_count, model_width),
            grad_out.reshape(row_count, model_width),
            (gain_one, gain_two),
            (b_query, key_bias, value_bias),
            rotary_tables(block_len * blocks_along),
            (w_query, key_weight, value_weight, w_out),
            (w_gate, w_up, w_down),
            edges[0][1],
            PARTS_OF_X,
        )
        turned_at, at = query_cols + key_cols, 2 * model_width
        *grads, output, grad_tokens = finish(
            feed_sums,
            last_sums,
            output,
            grad_tokens,
            small,
            [(0, query_cols), (query_cols, key_cols), (turned_at, key_cols), (turned_at + key_cols, query_cols)],
            [
                (0, model_width),
                (at, query_cols),
                (at + query_cols, key_cols),
                (at + turned_at, key_cols),
                (model_width, model_width),
            ],
        )
        return (
            output.reshape(seq_count, block_len, model_width),
            grad_tokens.reshape(seq_count, block_len, model_width),
            grads[7],
            grads[3],
            grads[8],
            grads[4],
            grads[9],
            grads[5],
            grads[10],
            grads[6],
            grads[11],
            *grads[:3],
        )

    def relative(field):
        return swap_blocks([field[:, n * own_rows : (n + 1) * own_rows] for n in range(size)], me)

    def absolute(blocks):
        return jnp.concatenate(swap_blocks(blocks, me), 1)

    def dot_rows(blocks, weights):
        return jnp.dot(
            jnp.concatenate(blocks, 1), jnp.concatenate(weights, 0), preferred_element_type=f32
        )

    lanes = {name: Lane() for name in ("x", "z", "hop1", "hop2", "hop3")}
    attention_weights = gather_pieces(
        jnp.concatenate([w_query, key_weight, value_weight], 1), size, lanes
    )
    out_weights = gather_pieces(w_out, size, lanes, parity)
    edges = chunk_edges(unit_cols)
    feed_weights = []
    early = len(edges) - 2

    feed_own = (w_gate, w_up, w_down)
    feed_near = tuple(lax.ppermute(w, "dp", xor_pairs(size, 1)) for w in feed_own)

    def fetch(start, width):
        own = jnp.concatenate([w[:, start : start + width] for w in feed_own], 1)
        far = far_pieces(own, size, lanes, parity)
        sources = []
        for r in range(size):
            if r < 2:
                sources.append(feed_own if r == 0 else feed_near)
            elif r % 2 == 0:
                sources.append((far[r],))
            else:
                sources.append((lax.ppermute(far[r - 1], "dp", xor_pairs(size, 1)),))
        feed_weights.append(sources)

    for start, width in edges[:early]:
        fetch(start, width)

    positions = place * block_len + jnp.arange(block_len, dtype=jnp.int32)
    position_count = block_len * blocks_along
    valid_rows = (positions[None, :] < lengths[:, None]).astype(f32).reshape(row_count, 1)
    facts = jnp.stack([place.astype(jnp.int32), lengths[0]])
    half = HEAD_DIM // 2
    inverse = jnp.exp(jnp.arange(half, dtype=f32) * (-2.0 * math.log(ROPE_BASE) / HEAD_DIM))
    angles = positions.astype(f32)[:, None] * inverse[None, :]
    cosine = jnp.concatenate([jnp.cos(angles)] * 2, 1)
    sine = jnp.concatenate([-jnp.sin(angles), jnp.sin(angles)], 1)
    gain_first = gain_one.astype(f32)
    gain_second = gain_two.astype(f32)
    inputs = tokens.reshape(row_count, model_width).astype(f32)
    scale_one = lax.rsqrt(jnp.mean(inputs * inputs, -1, keepdims=True) + EPSILON)
    normalized_input = (inputs * scale_one * gain_first).astype(bf16)
    normed_blocks = relative(normalized_input)
    projected = dot_rows(normed_blocks, attention_weights) + jnp.concatenate(
        [b_query, key_bias, value_bias]
    ).astype(f32)
    turned = query_cols + key_cols

    def turn_heads(field, sine_rows):
        grid = field.reshape(row_count, field.shape[1] // HEAD_DIM, HEAD_DIM)
        swapped = jnp.concatenate([grid[..., half:], grid[..., :half]], -1)
        grid = grid * cosine[:, None, :] + swapped * sine_rows[:, None, :]
        return grid.reshape(field.shape).astype(bf16)

    turned_rows = turn_heads(projected[:, :turned], sine)
    query_rot = turned_rows[:, :query_cols]
    pair_rows = jnp.concatenate([turned_rows[:, query_cols:], projected[:, turned:].astype(bf16)], 1)
    pair_all = [pair_rows]
    for shift in range(1, blocks_along):
        pair_all.append(
            lax.ppermute(
                pair_rows, "context", [(n, n + shift) for n in range(blocks_along - shift)]
            )
        )
    pair_all = jnp.concatenate(pair_all, 0)
    mixed_heads, lse = attend(facts, query_rot, pair_all)
    full_out = jnp.concatenate(out_weights, 0)
    branch = contract_last(mixed_heads, full_out)
    branch = absolute([branch[:, r * own_rows : (r + 1) * own_rows] for r in range(size)])
    hidden = inputs + tensor_sum(branch)
    scale_two = lax.rsqrt(jnp.mean(hidden * hidden, -1, keepdims=True) + EPSILON)
    normed_two = (hidden * scale_two * gain_second).astype(bf16)
    fall_grad = grad_out.reshape(row_count, model_width).astype(f32) * valid_rows
    fall_low = fall_grad.astype(bf16)
    fall_blocks = relative(fall_low)
    two_blocks = relative(normed_two)
    traded_early = trade_blocks(
        [jnp.concatenate([a, b], 1) for a, b in zip(normed_blocks, fall_blocks)], size
    )
    traded_early = jnp.concatenate(traded_early, 0).T
    normed_features, fall_features = traded_early[:own_rows], traded_early[own_rows:]
    two_features = jnp.concatenate(trade_blocks(two_blocks, size), 0).T
    two_row = jnp.concatenate(two_blocks, 1)
    fall_row = jnp.concatenate(fall_blocks, 1)

    feed_out, d_normed_two = None, None
    feed_units = []
    for turn_at, (start, width) in enumerate(edges):
        acts, d_normed_two, feed_out = feed_chunk(
            two_row, fall_row, feed_weights[turn_at], start, width, d_normed_two, feed_out
        )
        if turn_at < 0:
            acts = gather_pieces(acts, size, lanes)
        feed_units.append(acts)
        if turn_at == 0:
            for edge in edges[early:]:
                fetch(*edge)

    def split(field):
        return [field[:, r * own_rows : (r + 1) * own_rows] for r in range(size)]

    d_normed_two = tensor_sum(absolute(split(d_normed_two)))
    result = valid_rows * (hidden + tensor_sum(absolute(split(feed_out))))
    output = result.astype(bf16).reshape(seq_count, block_len, model_width)
    gain_two_grad = jnp.sum(d_normed_two * hidden * scale_two, 0)
    d_hidden = fall_grad + norm_back(hidden, scale_two, gain_second, d_normed_two)
    d_branch = d_hidden.astype(bf16)
    branch_blocks = relative(d_branch)
    branch_features = jnp.concatenate(trade_blocks(branch_blocks, size), 0).T
    d_mixed = jnp.dot(
        jnp.concatenate(branch_blocks, 1), full_out, preferred_element_type=f32
    ).astype(bf16)
    d_query_low, d_own, d_rest = attend_back(
        facts, query_rot, pair_all, lse, d_mixed, cosine, sine
    )
    for shift in range(1, blocks_along):
        d_own = d_own + lax.ppermute(
            d_rest[(shift - 1) * block_len : shift * block_len],
            "context",
            [(n, n - shift) for n in range(shift, blocks_along)],
        ).astype(f32)
    d_key_low = turn_heads(d_own[:, :key_cols], -sine)
    d_value_low = d_own[:, key_cols:].astype(bf16)
    d_projected = jnp.concatenate([d_query_low, d_key_low, d_value_low], 1)
    d_normed = contract_last(d_projected, jnp.concatenate(attention_weights, 0))
    d_normed = tensor_sum(absolute(split(d_normed)))
    gain_one_grad = jnp.sum(d_normed * inputs * scale_one, 0)
    d_inputs = d_hidden + norm_back(inputs, scale_one, gain_first, d_normed)
    grad_tokens = d_inputs.astype(bf16).reshape(seq_count, block_len, model_width)
    gain_two_grad = small_total(gain_two_grad)
    small = small_total(
        jnp.concatenate([gain_one_grad, jnp.sum(d_projected.astype(f32), 0)])
    )
    projected_width = d_projected.shape[1]
    last = jnp.concatenate([d_projected, mixed_heads], 1)
    halfway = last.shape[1] // 2
    blocks = [
        [[(0, 0, width)], [(0, width, width)], [(1, 2 * width, width)]] for _, width in edges
    ] + [
        [
            [(2, 0, halfway)],
            [(2, halfway, projected_width - halfway), (3, projected_width, query_cols)],
        ]
    ]
    sums = gather_and_sum(
        feed_units + [last],
        [two_features, fall_features, normed_features, branch_features],
        blocks,
        size,
    )

    def columns(which):
        stack = sums[which][0]
        return jnp.concatenate(
            [stack[3 * n + which].astype(f32) for n in range(len(edges))], 1
        )

    stack = sums[-1][0]
    last_grad = jnp.concatenate([stack[0], stack[1]], 1).astype(f32)
    projected_grad, out_grad = last_grad[:, :projected_width], last_grad[:, projected_width:]

    low, high = model_width + query_cols, model_width + query_cols + key_cols
    return (
        output,
        grad_tokens,
        small[:model_width],
        projected_grad[:, :query_cols],
        small[model_width:low],
        projected_grad[:, query_cols : query_cols + key_cols],
        small[low:high],
        projected_grad[:, query_cols + key_cols :],
        small[high:],
        out_grad,
        gain_two_grad,
        columns(0),
        columns(1),
        columns(2),
    )


def solution(mesh):
    in_specs = (
        P("dp", "context", None),
        P("dp"),
        P(),
        P("dp", "tensor"),
        P("tensor"),
        P("dp", "tensor"),
        P("tensor"),
        P("dp", "tensor"),
        P("tensor"),
        P("dp", "tensor"),
        P(),
        P("dp", "tensor"),
        P("dp", "tensor"),
        P("dp", "tensor"),
        P("dp", "context", None),
    )
    out_specs = (
        P("dp", "context", None),
        P("dp", "context", None),
        P(),
        P("dp", "tensor"),
        P("tensor"),
        P("dp", "tensor"),
        P("tensor"),
        P("dp", "tensor"),
        P("tensor"),
        P("dp", "tensor"),
        P(),
        P("dp", "tensor"),
        P("dp", "tensor"),
        P("dp", "tensor"),
    )
    return jax.shard_map(local, mesh=mesh, in_specs=in_specs, out_specs=out_specs, check_vma=False)
```
